32 devices in a mesh: batch: 8 (over z, y), tp: 4 (over x, core).
Axes of the slice: x: 2, y: 2, z: 4, core: 2. Of those that a mesh axis runs over, the one named last changes fastest.
Arguments:
- tokens: bfloat16 [2, 8192, 768], P(None, ('batch', 'tp')), may hold values from -6 to 6
- passage_lengths: int32 [2, 32], P(None, 'batch'), may hold values from 1 to 256, 5120 in all within a row
- cotangent: bfloat16 [2, 8192, 768], P(None, ('batch', 'tp')), may hold values from -6 to 6
- w_qkv: bfloat16 [768, 3, 768], P(None, None, 'tp'), may hold values from -0.21875 to 0.21875
- b_query: float32 [768], P('tp'), may hold values from -3 to 3
- b_value: float32 [768], P('tp'), may hold values from -3 to 3
- w_out: bfloat16 [768, 768], P('tp'), may hold values from -0.625 to 0.625
- b_out: float32 [768], replicated, may hold values from -2 to 2
- gain_one: float32 [768], replicated, may hold values from 0.5 to 1.5
- shift_one: float32 [768], replicated, may hold values from -2 to 2
- w_in: bfloat16 [768, 3072], P(None, 'tp'), may hold values from -0.21875 to 0.21875
- b_in: bfloat16 [3072], P('tp'), may hold values from -3 to 3
- w_back: bfloat16 [3072, 768], P('tp'), may hold values from -0.109375 to 0.109375
- b_back: float32 [768], replicated, may hold values from -2 to 2
- gain_two: float32 [768], replicated, may hold values from 0.5 to 1.5
- shift_two: float32 [768], replicated, may hold values from -2 to 2
Outputs:
- layer_out: bfloat16 [2, 8192, 768], P(None, ('batch', 'tp'))
- grad_tokens: float32 [2, 8192, 768], P(None, ('batch', 'tp'))
- grad_qkv: float32 [768, 3, 768], P(None, None, 'tp')
- grad_query_bias: float32 [768], P('tp')
- grad_value_bias: float32 [768], P('tp')
- grad_out: float32 [768, 768], P('tp')
- grad_out_bias: float32 [768], replicated
- grad_gain_one: float32 [768], replicated
- grad_shift_one: float32 [768], replicated
- grad_in: float32 [768, 3072], P(None, 'tp')
- grad_in_bias: float32 [3072], P('tp')
- grad_back: float32 [3072, 768], P('tp')
- grad_back_bias: float32 [768], replicated
- grad_gain_two: float32 [768], replicated
- grad_shift_two: float32 [768], replicated
The draws below stay inside these ranges and needn't reach their ends.
Inputs may be any that keep to these rules, and one draw needn't show every extreme that they name: `passage_lengths`: each micro-batch's lengths, over all its passages together, sum to 5/8 of its 8192 slots, and some passage of every micro-batch fills all 256 slots.
All inputs are finite; a program needn't handle non-finite values. No bound on the sum of `passage_lengths` on one device may be relied on, other than what follows from the above.
Results may differ from the reference program's by a relative error of at most 0.013.
The reference program's roundings to bfloat16 on the way count: a program that leaves them out, or rounds other values in their place, can miss the bound.
Values may be sent and summed in bfloat16 or wider, within the bound.
No kernel may reach another device: no remote copies, remote signals or barrier semaphores. Data moves between devices by JAX's collectives and lax.ppermute only.
A program may use at most 128 MiB of HBM per device.

```python
import math
import jax
import jax.numpy as jnp
import numpy as np
from jax import lax

D = 768
HEADS = 12
DH = 64
FF = 3072
PLEN = 256
MICRO = 2
PASS_MB = 4
PASSAGES_MB = 32
TOK_MB = 8192
N_BATCH = 8


def shard_levels(rng, shape, pieces, smallest, top_value):
    def one(position, parts):
        draws = jax.random.uniform(jax.random.fold_in(jax.random.fold_in(rng, 6), position), (parts,), jnp.float32, smallest / len(pieces), top_value / len(pieces))
        return jnp.repeat(jnp.exp(draws), shape[position] // parts).reshape((-1,) + (1,) * (len(shape) - position - 1))

    loudness = one(*pieces[0])
    for cut in pieces[1:]:
        loudness = loudness * one(*cut)
    return loudness


def profile(amount, total, most, slope):
    weights = [(1 << 20) // math.isqrt(rank ** slope) + 1 for rank in range(2, amount + 1)]
    spare, given = total - most - (amount - 1), [1] * (amount - 1)
    while spare > 0:
        candidates = [i for i in range(amount - 1) if given[i] < most]
        mass, budget = sum([weights[i] for i in candidates]), spare
        for i in candidates:
            addition = min(most - given[i], max(1, budget * weights[i] // mass), spare)
            given[i] = given[i] + addition
            spare = spare - addition
    return np.array([most] + given)


def uneven_parts(rng, count, total, most, lean):
    if count == 2:
        one = jax.random.randint(rng, (), max(1, total - most), min(most, total - 1) + 1)
        return jnp.stack([one, total - one])
    sizes = jnp.asarray(profile(count, total, most, lean), jnp.int32)
    couples = (count - 1) // 2
    donor, receiver = sizes[1:1 + 2 * couples:2], sizes[2:2 + 2 * couples:2]
    margin = jnp.minimum(donor - 1, most - receiver)
    shifted = jax.random.randint(jax.random.fold_in(rng, 1), (couples,), 0, 1 << 20) % (margin + 1)
    sizes = sizes.at[1:1 + 2 * couples:2].set(donor - shifted).at[2:2 + 2 * couples:2].set(receiver + shifted)
    return sizes[jax.random.permutation(jax.random.fold_in(rng, 2), count)]


def bell_draw(key, dims, deviation, limit, split=(), held_as=jnp.bfloat16):
    gain = shard_levels(key, dims, split, -0.22, 0.18) if split else 1.0
    drawn = jax.random.normal(key, dims, jnp.float32) * deviation * gain
    return jnp.minimum(jnp.maximum(drawn, -limit), limit).astype(held_as)


def setup_inputs(seed: int = 0) -> dict:
    streams_of = jax.random.split(jax.random.key(seed), 17)
    return {
        "tokens": bell_draw(streams_of[0], (MICRO, TOK_MB, D), 1.0, 6.0, ((1, 32),)),
        "passage_lengths": jax.vmap(lambda own: uneven_parts(own, PASSAGES_MB, PASS_MB * N_BATCH * PLEN * 5 // 8, PLEN, 2))(jax.random.split(streams_of[1], MICRO)).reshape((MICRO, PASSAGES_MB)).astype(jnp.int32),
        "cotangent": bell_draw(streams_of[2], (MICRO, TOK_MB, D), 1.0, 6.0, ((1, 32),)),
        "w_qkv": bell_draw(streams_of[3], (D, 3, D), D ** -0.5, 0.21875, ((2, 4),)),
        "b_query": bell_draw(streams_of[4], (D,), 0.5, 3.0, ((0, 4),), jnp.float32),
        "b_value": bell_draw(streams_of[5], (D,), 0.5, 3.0, ((0, 4),), jnp.float32),
        "w_out": bell_draw(streams_of[6], (D, D), (D // 8) ** -0.5, 0.625, ((0, 4),)),
        "b_out": bell_draw(streams_of[7], (D,), 0.3, 2.0, (), jnp.float32),
        "gain_one": jnp.clip(1.0 + 0.1 * jax.random.normal(streams_of[8], (D,), jnp.float32), 0.5, 1.5),
        "shift_one": bell_draw(streams_of[9], (D,), 0.3, 2.0, (), jnp.float32),
        "w_in": bell_draw(streams_of[10], (D, FF), D ** -0.5, 0.21875, ((1, 4),)),
        "b_in": bell_draw(streams_of[11], (FF,), 0.5, 3.0, ((0, 4),)),
        "w_back": bell_draw(streams_of[12], (FF, D), FF ** -0.5, 0.109375, ((0, 4),)),
        "b_back": bell_draw(streams_of[13], (D,), 0.3, 2.0, (), jnp.float32),
        "gain_two": jnp.clip(1.0 + 0.1 * jax.random.normal(streams_of[14], (D,), jnp.float32), 0.5, 1.5),
        "shift_two": bell_draw(streams_of[15], (D,), 0.3, 2.0, (), jnp.float32),
    }


epsilon = 1e-05
highest = lax.Precision.HIGHEST

@jax.custom_vjp
def low(v):
    return lax.optimization_barrier(v.astype(jnp.bfloat16)).astype(jnp.float32)

@jax.custom_vjp
def low_back(v):
    return v

def low_keep(v):
    return (low(v), None)

def low_pass(kept, grad):
    return (grad,)

def back_keep(v):
    return (v, None)

def back_low(kept, grad):
    return (low(grad),)
low.defvjp(low_keep, low_pass)
low_back.defvjp(back_keep, back_low)

def layer_norm(values_in, gain_vec, shift_vec):
    middle = lax.optimization_barrier(jnp.mean(values_in, axis=-1, keepdims=True))
    centred = values_in - middle
    spread = lax.optimization_barrier(jnp.mean(centred * centred, axis=-1, keepdims=True))
    return centred * lax.rsqrt(spread + epsilon) * gain_vec + shift_vec

def attend(packed):
    block_qkv, key_keep = packed
    queries = block_qkv[:, :, 0]
    key_rows = block_qkv[:, :, 1]
    value_rows = block_qkv[:, :, 2]
    scores = jnp.einsum('pqhd,pkhd->phqk', queries, key_rows, precision=highest) * (1.0 / math.sqrt(DH))
    scores = low_back(scores)
    scores = jnp.where(key_keep[:, None, None, :], scores, -1000000000.0)
    row_max = lax.optimization_barrier(jnp.max(scores, axis=-1, keepdims=True))
    exponent = jnp.exp(scores - row_max)
    attn_probs = low(exponent / lax.optimization_barrier(jnp.sum(exponent, axis=-1, keepdims=True)))
    return jnp.einsum('phqk,pkhd->pqhd', attn_probs, value_rows, precision=highest)

def forward(tokens, w_qkv, b_query, b_value, w_out, b_out, gain_one, shift_one, w_in, b_in, w_back, b_back, gain_two, shift_two, key_blocks):
    n_rows = tokens.shape[0]
    qkv_bias = jnp.stack([b_query, jnp.zeros_like(b_query), b_value])
    projected = jnp.dot(tokens, w_qkv.reshape(D, 3 * D), precision=highest).reshape(n_rows, 3, D) + qkv_bias
    projected = low(low_back(projected))
    qkv_blocks = projected.reshape(n_rows // (PASS_MB * PLEN), PASS_MB, PLEN, 3, HEADS, DH)
    context = lax.map(jax.checkpoint(attend), (qkv_blocks, key_blocks))
    context = low(low_back(context.reshape(n_rows, D)))
    attn_out = low_back(jnp.dot(context, w_out, precision=highest)) + b_out
    normed_one = layer_norm(tokens + attn_out, gain_one, shift_one)
    preact = low_back(jnp.dot(low(normed_one), w_in, precision=highest) + b_in)
    activation = low(jax.nn.gelu(preact, approximate=False))
    ffn_out = low_back(jnp.dot(activation, w_back, precision=highest)) + b_back
    return layer_norm(normed_one + ffn_out, gain_two, shift_two)

def reference(tokens, passage_lengths, cotangent, w_qkv, b_query, b_value, w_out, b_out, gain_one, shift_one, w_in, b_in, w_back, b_back, gain_two, shift_two):
    all_rows = MICRO * N_BATCH * PASS_MB * PLEN
    positions = jnp.arange(PLEN, dtype=jnp.int32)
    key_keep = positions[None, None, :] < passage_lengths.astype(jnp.int32)[:, :, None]
    keep_rows = key_keep.reshape(all_rows).astype(jnp.float32)
    key_blocks = key_keep.reshape(MICRO * N_BATCH, PASS_MB, PLEN)
    float_args = [value_arg.astype(jnp.float32) for value_arg in (tokens, w_qkv, b_query, b_value, w_out, b_out, gain_one, shift_one, w_in, b_in, w_back, b_back, gain_two, shift_two)]

    def run_layer(*params):
        return forward(params[0].reshape(all_rows, D), *params[1:], key_blocks)
    layer_out, pullback = jax.vjp(run_layer, *float_args)
    seed_grad = cotangent.astype(jnp.float32).reshape(all_rows, D) * keep_rows[:, None]
    gradients = pullback(seed_grad)
    return (layer_out.reshape(MICRO, all_rows // MICRO, D).astype(jnp.bfloat16), gradients[0].reshape(MICRO, all_rows // MICRO, D), gradients[1], gradients[2], gradients[3], gradients[4], gradients[5], gradients[6], gradients[7], gradients[8], gradients[9], gradients[10], gradients[11], gradients[12], gradients[13])
```

```python
import math

import jax
import jax.numpy as jnp
from jax import lax
from jax.sharding import PartitionSpec as P

DH = 64
AXES = ("batch", "tp")
epsilon = 1e-05
F32 = jnp.float32
BF16 = jnp.bfloat16


def norm_forward(values_in, gain_vec, shift_vec):
    middle = jnp.mean(values_in, axis=-1, keepdims=True)
    centred = values_in - middle
    spread = jnp.mean(centred * centred, axis=-1, keepdims=True)
    inverse = lax.rsqrt(spread + epsilon)
    unit_rows = centred * inverse
    return (unit_rows * gain_vec + shift_vec, unit_rows, inverse)


def norm_backward(grad_rows, unit_rows, inverse, gain_vec):
    scaled = grad_rows * gain_vec
    mean_one = jnp.mean(scaled, axis=-1, keepdims=True)
    mean_two = jnp.mean(scaled * unit_rows, axis=-1, keepdims=True)
    return inverse * (scaled - mean_one - unit_rows * mean_two)


def gelu_slope(preact):
    normal_cdf = 0.5 * (1.0 + lax.erf(preact * (1.0 / math.sqrt(2.0))))
    density = jnp.exp(-0.5 * preact * preact) * (1.0 / math.sqrt(2.0 * math.pi))
    return normal_cdf + preact * density


def attend_forward(qkv_blocks, key_keep, score_scale):
    queries = qkv_blocks[:, :, 0]
    key_rows = qkv_blocks[:, :, 1]
    value_rows = qkv_blocks[:, :, 2]
    scores = (
        jnp.einsum("pqhd,pkhd->phqk", queries, key_rows, preferred_element_type=F32)
        * score_scale
    )
    scores = jnp.where(key_keep[:, None, None, :], scores, -1000000000.0)
    row_max = jnp.max(scores, axis=-1, keepdims=True)
    exponent = jnp.exp(scores - row_max)
    row_total = jnp.sum(exponent, axis=-1, keepdims=True)
    attn_probs = exponent / row_total
    log_total = row_max + jnp.log(row_total)
    context = jnp.einsum(
        "phqk,pkhd->pqhd", attn_probs.astype(BF16), value_rows, preferred_element_type=F32
    )
    return (context.astype(BF16), log_total)


def attend_backward(qkv_blocks, key_keep, log_total, grad_context, score_scale):
    queries = qkv_blocks[:, :, 0]
    key_rows = qkv_blocks[:, :, 1]
    value_rows = qkv_blocks[:, :, 2]
    scores = (
        jnp.einsum("pqhd,pkhd->phqk", queries, key_rows, preferred_element_type=F32)
        * score_scale
    )
    scores = jnp.where(key_keep[:, None, None, :], scores, -1000000000.0)
    attn_probs = jnp.exp(scores - log_total)
    grad_values = jnp.einsum(
        "phqk,pqhd->pkhd", attn_probs.astype(BF16), grad_context, preferred_element_type=F32
    )
    grad_probs = jnp.einsum(
        "pqhd,pkhd->phqk", grad_context, value_rows, preferred_element_type=F32
    )
    row_delta = jnp.sum(attn_probs * grad_probs, axis=-1, keepdims=True)
    grad_scores = (attn_probs * (grad_probs - row_delta)).astype(BF16)
    grad_queries = (
        jnp.einsum("phqk,pkhd->pqhd", grad_scores, key_rows, preferred_element_type=F32)
        * score_scale
    )
    grad_keys = (
        jnp.einsum("phqk,pqhd->pkhd", grad_scores, queries, preferred_element_type=F32)
        * score_scale
    )
    return jnp.stack([grad_queries, grad_keys, grad_values], axis=2).astype(BF16)


def flat_perm(move):
    pairs = []
    for z in range(4):
        for y in range(2):
            for x in range(2):
                for c in range(2):
                    to = move(z, y, x, c)
                    if to is not None:
                        z2, y2, x2, c2 = to
                        pairs.append(
                            (((z * 2 + y) * 2 + x) * 2 + c, ((z2 * 2 + y2) * 2 + x2) * 2 + c2)
                        )
    return pairs


class GridMoves:
    def __init__(self):
        self.row = lax.axis_index("batch") % 2
        self.layer = lax.axis_index("batch") // 2
        self.outer = (self.layer == 0) | (self.layer == 3)
        self.to_core = flat_perm(lambda z, y, x, c: (z, y, x, 1 - c))
        self.to_x = flat_perm(lambda z, y, x, c: (z, y, 1 - x, c))
        self.to_y = flat_perm(lambda z, y, x, c: (z, 1 - y, x, c))
        self.to_inner = flat_perm(
            lambda z, y, x, c: {0: (1, y, x, c), 3: (2, y, x, c)}.get(z)
        )
        self.across = flat_perm(
            lambda z, y, x, c: {1: (2, y, x, c), 2: (1, y, x, c)}.get(z)
        )
        self.to_outer = flat_perm(
            lambda z, y, x, c: {1: (0, y, x, c), 2: (3, y, x, c)}.get(z)
        )

    def send(self, value, pairs):
        return lax.ppermute(value, AXES, pairs)

    def half(self, value, which):
        rows = value.shape[0] // 2
        return lax.dynamic_slice_in_dim(value, which * rows, rows, axis=0)

    def order(self, mine, other):
        return jnp.where(
            self.row == 0,
            jnp.concatenate([mine, other], axis=0),
            jnp.concatenate([other, mine], axis=0),
        )

    def gather(self, own):
        first = self.send(self.half(own, self.row), self.to_x)
        second = self.send(first, self.to_y)
        far = self.order(first, second)
        return [own, self.send(own, self.to_core), far, self.send(far, self.to_core)]

    def gather_small(self, own):
        pair = jnp.stack([own, self.send(own, self.to_core)])
        far = self.send(pair, self.to_x)
        return [pair[0], pair[1], far[0], far[1]]

    def add(self, one, two):
        return (one.astype(F32) + two.astype(F32)).astype(BF16)

    def reduce(self, parts):
        low = [part.astype(BF16) for part in parts]
        got = self.send(jnp.stack([low[1], low[3]]), self.to_core)
        far = (parts[2] + got[1].astype(F32)).astype(BF16)
        near = (parts[0] + got[0].astype(F32)).astype(BF16)
        got = self.send(far, self.to_x)
        pass_on = self.add(self.half(near, 1 - self.row), self.half(got, 1 - self.row))
        keep = self.add(self.half(near, self.row), self.half(got, self.row))
        keep = self.add(keep, self.send(pass_on, self.to_y))
        keep = self.add(keep, self.send(keep, self.to_inner))
        keep = self.add(keep, self.send(keep, self.across))
        keep = jnp.where(self.outer, self.send(keep, self.to_outer), keep)
        other = self.send(keep, self.to_y)
        return self.order(keep, other).astype(F32)

    def reduce_all(self, value):
        for pairs in (self.to_core, self.to_x, self.to_y, self.to_inner, self.across):
            value = value + self.send(value, pairs)
        return jnp.where(self.outer, self.send(value, self.to_outer), value)


class PlainMoves:
    def gather(self, own):
        whole = lax.all_gather(own, "tp", axis=0)
        return [whole[i] for i in range(whole.shape[0])]

    gather_small = gather

    def reduce(self, parts):
        mine = lax.psum_scatter(jnp.stack(parts), "tp", scatter_dimension=0, tiled=False)
        return lax.psum(mine, "batch")

    def reduce_all(self, value):
        return lax.psum(value, AXES)

def body(
    tokens,
    passage_lengths,
    cotangent,
    w_qkv,
    b_query,
    b_value,
    w_out,
    b_out,
    gain_one,
    shift_one,
    w_in,
    b_in,
    w_back,
    b_back,
    gain_two,
    shift_two,
):
    micro_count, own_rows, model_width = tokens.shape
    tp_count = lax.axis_size("tp")
    batch_count = lax.axis_size("batch")
    passage_len = own_rows * tp_count // passage_lengths.shape[1]
    own_passages = own_rows // passage_len
    assert own_passages * passage_len == own_rows
    grid = (batch_count, tp_count) == (8, 4)
    moves = GridMoves() if grid else PlainMoves()
    width = w_qkv.shape[2]
    heads = width // DH
    units = w_in.shape[1]
    score_scale = 1.0 / math.sqrt(DH)
    rows = micro_count * own_rows
    position = lax.axis_index("tp")

    small = jnp.concatenate([b_query, b_value, b_in.astype(F32)])
    small_parts = moves.gather_small(small)
    qkv_parts = moves.gather(w_qkv.reshape(model_width, 3 * width))
    out_parts = moves.gather(w_out)
    in_parts = moves.gather(w_in)
    back_parts = moves.gather(w_back)

    lengths = lax.dynamic_slice_in_dim(
        passage_lengths, position * own_passages, own_passages, axis=1
    ).reshape(micro_count * own_passages)
    slots = jnp.arange(passage_len, dtype=jnp.int32)
    key_keep = slots[None, :] < lengths[:, None]
    keep_rows = key_keep.reshape(rows, 1).astype(F32)
    x = tokens.reshape(rows, model_width)
    dy = cotangent.reshape(rows, model_width)

    qkv_rows, contexts, log_totals = [], [], []
    attn_out = 0.0
    for part in range(tp_count):
        bias_q = small_parts[part][:width]
        bias_v = small_parts[part][width : 2 * width]
        bias = jnp.concatenate([bias_q, jnp.zeros_like(bias_q), bias_v])
        projected = (
            jnp.dot(x, qkv_parts[part], preferred_element_type=F32) + bias
        ).astype(BF16)
        blocks = projected.reshape(-1, passage_len, 3, heads, DH)
        context, log_total = attend_forward(blocks, key_keep, score_scale)
        context = context.reshape(rows, width)
        qkv_rows.append(blocks)
        contexts.append(context)
        log_totals.append(log_total)
        attn_out = attn_out + jnp.dot(context, out_parts[part], preferred_element_type=F32)
    normed_one, unit_one, inverse_one = norm_forward(
        x.astype(F32) + attn_out + b_out, gain_one, shift_one
    )
    normed_low = normed_one.astype(BF16)
    preacts, activations = [], []
    ffn_out = 0.0
    for part in range(tp_count):
        preact = (
            jnp.dot(normed_low, in_parts[part], preferred_element_type=F32)
            + small_parts[part][2 * width :]
        )
        activation = jax.nn.gelu(preact, approximate=False).astype(BF16)
        preacts.append(preact)
        activations.append(activation)
        ffn_out = ffn_out + jnp.dot(activation, back_parts[part], preferred_element_type=F32)
    result, unit_two, inverse_two = norm_forward(normed_one + ffn_out + b_back, gain_two, shift_two)
    layer_out = result.astype(BF16).reshape(tokens.shape)

    grad_y = dy.astype(F32) * keep_rows
    g_gain_two = jnp.sum(grad_y * unit_two, axis=0)
    g_shift_two = jnp.sum(grad_y, axis=0)
    grad_two = norm_backward(grad_y, unit_two, inverse_two, gain_two)
    g_back_bias = jnp.sum(grad_two, axis=0)
    grad_ffn = grad_two.astype(BF16)
    g_back = moves.reduce(
        [
            jnp.einsum("rf,rd->fd", activations[part], grad_ffn, preferred_element_type=F32)
            for part in range(tp_count)
        ]
    )
    grad_preacts, g_in_bias = [], []
    grad_normed = grad_two
    for part in range(tp_count):
        grad_act = jnp.einsum(
            "rd,fd->rf", grad_ffn, back_parts[part], preferred_element_type=F32
        )
        grad_preact = (grad_act * gelu_slope(preacts[part])).astype(BF16)
        grad_preacts.append(grad_preact)
        g_in_bias.append(jnp.sum(grad_preact.astype(F32), axis=0))
    g_in = moves.reduce(
        [
            jnp.einsum("rd,rf->df", normed_low, grad_preacts[part], preferred_element_type=F32)
            for part in range(tp_count)
        ]
    )
    for part in range(tp_count):
        grad_normed = grad_normed + jnp.einsum(
            "rf,df->rd", grad_preacts[part], in_parts[part], preferred_element_type=F32
        )
    g_gain_one = jnp.sum(grad_normed * unit_one, axis=0)
    g_shift_one = jnp.sum(grad_normed, axis=0)
    grad_one = norm_backward(grad_normed, unit_one, inverse_one, gain_one)
    g_out_bias = jnp.sum(grad_one, axis=0)
    grad_attn = grad_one.astype(BF16)
    g_out = moves.reduce(
        [
            jnp.einsum("rc,rd->cd", contexts[part], grad_attn, preferred_element_type=F32)
            for part in range(tp_count)
        ]
    )
    grad_flats, g_query, g_value = [], [], []
    grad_x = grad_one
    for part in range(tp_count):
        grad_context = jnp.einsum(
            "rd,cd->rc", grad_attn, out_parts[part], preferred_element_type=F32
        ).astype(BF16)
        grad_blocks = attend_backward(
            qkv_rows[part],
            key_keep,
            log_totals[part],
            grad_context.reshape(-1, passage_len, heads, DH),
            score_scale,
        )
        grad_flat = grad_blocks.reshape(rows, 3 * width)
        grad_flats.append(grad_flat)
        sums = jnp.sum(grad_flat.astype(F32), axis=0)
        g_query.append(sums[:width])
        g_value.append(sums[2 * width :])
    g_qkv = moves.reduce(
        [
            jnp.einsum("rd,rc->dc", x, grad_flats[part], preferred_element_type=F32)
            for part in range(tp_count)
        ]
    )
    for part in range(tp_count):
        grad_x = grad_x + jnp.einsum(
            "rc,dc->rd", grad_flats[part], qkv_parts[part], preferred_element_type=F32
        )
    sharded = jnp.stack(
        [
            jnp.concatenate([g_query[part], g_value[part], g_in_bias[part]])
            for part in range(tp_count)
        ]
    )
    if grid:
        slots_of = jnp.bitwise_xor(jnp.arange(tp_count, dtype=jnp.int32), position)
        pick = (slots_of[:, None] == jnp.arange(tp_count, dtype=jnp.int32)[None, :]).astype(F32)
        sharded = jnp.sum(pick[:, :, None] * sharded[None, :, :], axis=1)
    common = jnp.concatenate(
        [g_out_bias, g_gain_one, g_shift_one, g_back_bias, g_gain_two, g_shift_two]
    )
    total = moves.reduce_all(jnp.concatenate([sharded.reshape(-1), common]))
    mine = lax.dynamic_slice_in_dim(
        total[: sharded.size].reshape(tp_count, -1), position, 1, axis=0
    )[0]
    tail = total[sharded.size :].reshape(6, model_width)
    return (
        layer_out,
        grad_x.reshape(tokens.shape),
        g_qkv.reshape(model_width, 3, width),
        mine[:width],
        mine[width : 2 * width],
        g_out,
        tail[0],
        tail[1],
        tail[2],
        g_in,
        mine[2 * width :],
        g_back,
        tail[3],
        tail[4],
        tail[5],
    )


def solution(mesh):
    in_specs = (
        P(None, ("batch", "tp"), None),
        P(None, "batch"),
        P(None, ("batch", "tp"), None),
        P(None, None, "tp"),
        P("tp"),
        P("tp"),
        P("tp", None),
        P(),
        P(),
        P(),
        P(None, "tp"),
        P("tp"),
        P("tp", None),
        P(),
        P(),
        P(),
    )
    out_specs = (
        P(None, ("batch", "tp"), None),
        P(None, ("batch", "tp"), None),
        P(None, None, "tp"),
        P("tp"),
        P("tp"),
        P("tp", None),
        P(),
        P(),
        P(),
        P(None, "tp"),
        P("tp"),
        P("tp", None),
        P(),
        P(),
        P(),
    )
    return jax.shard_map(body, mesh=mesh, in_specs=in_specs, out_specs=out_specs, check_vma=False)
```

```python
import math

import jax
import jax.numpy as jnp
from jax import lax
from jax.sharding import PartitionSpec as P

DH = 64
AXES = ("batch", "tp")
epsilon = 1e-05
F32 = jnp.float32
BF16 = jnp.bfloat16


def norm_forward(values_in, gain_vec, shift_vec):
    middle = jnp.mean(values_in, axis=-1, keepdims=True)
    centred = values_in - middle
    spread = jnp.mean(centred * centred, axis=-1, keepdims=True)
    inverse = lax.rsqrt(spread + epsilon)
    unit_rows = centred * inverse
    return (unit_rows * gain_vec + shift_vec, unit_rows, inverse)


def norm_backward(grad_rows, unit_rows, inverse, gain_vec):
    scaled = grad_rows * gain_vec
    mean_one = jnp.mean(scaled, axis=-1, keepdims=True)
    mean_two = jnp.mean(scaled * unit_rows, axis=-1, keepdims=True)
    return inverse * (scaled - mean_one - unit_rows * mean_two)


def gelu_slope(preact):
    normal_cdf = 0.5 * (1.0 + lax.erf(preact * (1.0 / math.sqrt(2.0))))
    density = jnp.exp(-0.5 * preact * preact) * (1.0 / math.sqrt(2.0 * math.pi))
    return normal_cdf + preact * density


def attend_forward(qkv_blocks, key_keep, score_scale):
    queries = qkv_blocks[:, :, 0]
    key_rows = qkv_blocks[:, :, 1]
    value_rows = qkv_blocks[:, :, 2]
    scores = (
        jnp.einsum("pqhd,pkhd->phqk", queries, key_rows, preferred_element_type=F32)
        * score_scale
    )
    scores = jnp.where(key_keep[:, None, None, :], scores, -1000000000.0)
    row_max = jnp.max(scores, axis=-1, keepdims=True)
    exponent = jnp.exp(scores - row_max)
    row_total = jnp.sum(exponent, axis=-1, keepdims=True)
    attn_probs = exponent / row_total
    log_total = row_max + jnp.log(row_total)
    context = jnp.einsum(
        "phqk,pkhd->pqhd", attn_probs.astype(BF16), value_rows, preferred_element_type=F32
    )
    return (context.astype(BF16), log_total)


def attend_backward(qkv_blocks, key_keep, log_total, grad_context, score_scale):
    queries = qkv_blocks[:, :, 0]
    key_rows = qkv_blocks[:, :, 1]
    value_rows = qkv_blocks[:, :, 2]
    scores = (
        jnp.einsum("pqhd,pkhd->phqk", queries, key_rows, preferred_element_type=F32)
        * score_scale
    )
    scores = jnp.where(key_keep[:, None, None, :], scores, -1000000000.0)
    attn_probs = jnp.exp(scores - log_total)
    grad_values = jnp.einsum(
        "phqk,pqhd->pkhd", attn_probs.astype(BF16), grad_context, preferred_element_type=F32
    )
    grad_probs = jnp.einsum(
        "pqhd,pkhd->phqk", grad_context, value_rows, preferred_element_type=F32
    )
    row_delta = jnp.sum(attn_probs * grad_probs, axis=-1, keepdims=True)
    grad_scores = (attn_probs * (grad_probs - row_delta)).astype(BF16)
    grad_queries = (
        jnp.einsum("phqk,pkhd->pqhd", grad_scores, key_rows, preferred_element_type=F32)
        * score_scale
    )
    grad_keys = (
        jnp.einsum("phqk,pqhd->pkhd", grad_scores, queries, preferred_element_type=F32)
        * score_scale
    )
    return jnp.stack([grad_queries, grad_keys, grad_values], axis=2).astype(BF16)


def flat_perm(move):
    pairs = []
    for z in range(4):
        for y in range(2):
            for x in range(2):
                for c in range(2):
                    to = move(z, y, x, c)
                    if to is not None:
                        z2, y2, x2, c2 = to
                        pairs.append(
                            (((z * 2 + y) * 2 + x) * 2 + c, ((z2 * 2 + y2) * 2 + x2) * 2 + c2)
                        )
    return pairs


class GridMoves:
    def __init__(self):
        self.row = lax.axis_index("batch") % 2
        self.layer = lax.axis_index("batch") // 2
        self.outer = (self.layer == 0) | (self.layer == 3)
        self.to_core = flat_perm(lambda z, y, x, c: (z, y, x, 1 - c))
        self.to_x = flat_perm(lambda z, y, x, c: (z, y, 1 - x, c))
        self.to_y = flat_perm(lambda z, y, x, c: (z, 1 - y, x, c))
        self.to_inner = flat_perm(
            lambda z, y, x, c: {0: (1, y, x, c), 3: (2, y, x, c)}.get(z)
        )
        self.across = flat_perm(
            lambda z, y, x, c: {1: (2, y, x, c), 2: (1, y, x, c)}.get(z)
        )
        self.to_outer = flat_perm(
            lambda z, y, x, c: {1: (0, y, x, c), 2: (3, y, x, c)}.get(z)
        )

    def send(self, value, pairs):
        return lax.ppermute(value, AXES, pairs)

    def half(self, value, which):
        rows = value.shape[0] // 2
        return lax.dynamic_slice_in_dim(value, which * rows, rows, axis=0)

    def order(self, mine, other):
        return jnp.where(
            self.row == 0,
            jnp.concatenate([mine, other], axis=0),
            jnp.concatenate([other, mine], axis=0),
        )

    def gather(self, own):
        first = self.send(self.half(own, self.row), self.to_x)
        second = self.send(first, self.to_y)
        far = self.order(first, second)
        return [own, self.send(own, self.to_core), far, self.send(far, self.to_core)]

    def gather_small(self, own):
        pair = jnp.stack([own, self.send(own, self.to_core)])
        far = self.send(pair, self.to_x)
        return [pair[0], pair[1], far[0], far[1]]

    def add(self, one, two):
        return (one.astype(F32) + two.astype(F32)).astype(BF16)

    def reduce(self, parts):
        low = [part.astype(BF16) for part in parts]
        got = self.send(jnp.stack([low[1], low[3]]), self.to_core)
        far = (parts[2] + got[1].astype(F32)).astype(BF16)
        near = (parts[0] + got[0].astype(F32)).astype(BF16)
        got = self.send(far, self.to_x)
        pass_on = self.add(self.half(near, 1 - self.row), self.half(got, 1 - self.row))
        keep = self.add(self.half(near, self.row), self.half(got, self.row))
        keep = self.add(keep, self.send(pass_on, self.to_y))
        keep = self.add(keep, self.send(keep, self.to_inner))
        keep = self.add(keep, self.send(keep, self.across))
        keep = jnp.where(self.outer, self.send(keep, self.to_outer), keep)
        other = self.send(keep, self.to_y)
        return self.order(keep, other).astype(F32)

    def reduce_all(self, value):
        for pairs in (self.to_core, self.to_x, self.to_y, self.to_inner, self.across):
            value = value + self.send(value, pairs)
        return jnp.where(self.outer, self.send(value, self.to_outer), value)


class PlainMoves:
    def gather(self, own):
        whole = lax.all_gather(own, "tp", axis=0)
        return [whole[i] for i in range(whole.shape[0])]

    gather_small = gather

    def reduce(self, parts):
        mine = lax.psum_scatter(jnp.stack(parts), "tp", scatter_dimension=0, tiled=False)
        return lax.psum(mine, "batch")

    def reduce_all(self, value):
        return lax.psum(value, AXES)

def body(
    tokens,
    passage_lengths,
    cotangent,
    w_qkv,
    b_query,
    b_value,
    w_out,
    b_out,
    gain_one,
    shift_one,
    w_in,
    b_in,
    w_back,
    b_back,
    gain_two,
    shift_two,
):
    micro_count, own_rows, model_width = tokens.shape
    tp_count = lax.axis_size("tp")
    batch_count = lax.axis_size("batch")
    passage_len = own_rows * tp_count // passage_lengths.shape[1]
    own_passages = own_rows // passage_len
    assert own_passages * passage_len == own_rows
    grid = (batch_count, tp_count) == (8, 4)
    moves = GridMoves() if grid else PlainMoves()
    width = w_qkv.shape[2]
    heads = width // DH
    units = w_in.shape[1]
    score_scale = 1.0 / math.sqrt(DH)
    rows = micro_count * own_rows
    position = lax.axis_index("tp")

    small = jnp.concatenate([b_query, b_value, b_in.astype(F32)])
    small_parts = moves.gather_small(small)
    qkv_parts = moves.gather(w_qkv.reshape(model_width, 3 * width))
    out_parts = moves.gather(w_out)
    in_parts = moves.gather(w_in)
    back_parts = moves.gather(w_back)

    lengths = lax.dynamic_slice_in_dim(
        passage_lengths, position * own_passages, own_passages, axis=1
    ).reshape(micro_count * own_passages)
    slots = jnp.arange(passage_len, dtype=jnp.int32)
    key_keep = slots[None, :] < lengths[:, None]
    keep_rows = key_keep.reshape(rows, 1).astype(F32)
    x = tokens.reshape(rows, model_width)
    dy = cotangent.reshape(rows, model_width)

    qkv_rows, contexts, log_totals = [], [], []
    attn_out = 0.0
    for part in range(tp_count):
        bias_q = small_parts[part][:width]
        bias_v = small_parts[part][width : 2 * width]
        bias = jnp.concatenate([bias_q, jnp.zeros_like(bias_q), bias_v])
        projected = (
            jnp.dot(x, qkv_parts[part], preferred_element_type=F32) + bias
        ).astype(BF16)
        blocks = projected.reshape(-1, passage_len, 3, heads, DH)
        context, log_total = attend_forward(blocks, key_keep, score_scale)
        context = context.reshape(rows, width)
        qkv_rows.append(blocks)
        contexts.append(context)
        log_totals.append(log_total)
        attn_out = attn_out + jnp.dot(context, out_parts[part], preferred_element_type=F32)
    normed_one, unit_one, inverse_one = norm_forward(
        x.astype(F32) + attn_out + b_out, gain_one, shift_one
    )
    normed_low = normed_one.astype(BF16)
    preacts, activations = [], []
    ffn_out = 0.0
    for part in range(tp_count):
        preact = (
            jnp.dot(normed_low, in_parts[part], preferred_element_type=F32)
            + small_parts[part][2 * width :]
        )
        activation = jax.nn.gelu(preact, approximate=False).astype(BF16)
        preacts.append(preact)
        activations.append(activation)
        ffn_out = ffn_out + jnp.dot(activation, back_parts[part], preferred_element_type=F32)
    result, unit_two, inverse_two = norm_forward(normed_one + ffn_out + b_back, gain_two, shift_two)
    layer_out = result.astype(BF16).reshape(tokens.shape)

    grad_y = dy.astype(F32) * keep_rows
    g_gain_two = jnp.sum(grad_y * unit_two, axis=0)
    g_shift_two = jnp.sum(grad_y, axis=0)
    grad_two = norm_backward(grad_y, unit_two, inverse_two, gain_two)
    g_back_bias = jnp.sum(grad_two, axis=0)
    grad_ffn = grad_two.astype(BF16)
    back_terms = [
        jnp.einsum("rf,rd->fd", activations[part], grad_ffn, preferred_element_type=F32)
        for part in range(tp_count)
    ]
    grad_preacts, g_in_bias = [], []
    back_terms, grad_ffn = lax.optimization_barrier((back_terms, grad_ffn))
    g_back = moves.reduce(back_terms)
    grad_normed = grad_two
    for part in range(tp_count):
        grad_act = jnp.einsum(
            "rd,fd->rf", grad_ffn, back_parts[part], preferred_element_type=F32
        )
        grad_preact = (grad_act * gelu_slope(preacts[part])).astype(BF16)
        grad_preacts.append(grad_preact)
        g_in_bias.append(jnp.sum(grad_preact.astype(F32), axis=0))
    in_terms = [
        jnp.einsum("rd,rf->df", normed_low, grad_preacts[part], preferred_element_type=F32)
        for part in range(tp_count)
    ]
    in_terms, grad_preacts = lax.optimization_barrier((in_terms, grad_preacts))
    g_in = moves.reduce(in_terms)
    for part in range(tp_count):
        grad_normed = grad_normed + jnp.einsum(
            "rf,df->rd", grad_preacts[part], in_parts[part], preferred_element_type=F32
        )
    g_gain_one = jnp.sum(grad_normed * unit_one, axis=0)
    g_shift_one = jnp.sum(grad_normed, axis=0)
    grad_one = norm_backward(grad_normed, unit_one, inverse_one, gain_one)
    g_out_bias = jnp.sum(grad_one, axis=0)
    grad_attn = grad_one.astype(BF16)
    out_terms = [
        jnp.einsum("rc,rd->cd", contexts[part], grad_attn, preferred_element_type=F32)
        for part in range(tp_count)
    ]
    out_terms, grad_attn = lax.optimization_barrier((out_terms, grad_attn))
    g_out = moves.reduce(out_terms)
    grad_flats, g_query, g_value = [], [], []
    grad_x = grad_one
    for part in range(tp_count):
        grad_context = jnp.einsum(
            "rd,cd->rc", grad_attn, out_parts[part], preferred_element_type=F32
        ).astype(BF16)
        grad_blocks = attend_backward(
            qkv_rows[part],
            key_keep,
            log_totals[part],
            grad_context.reshape(-1, passage_len, heads, DH),
            score_scale,
        )
        grad_flat = grad_blocks.reshape(rows, 3 * width)
        grad_flats.append(grad_flat)
        sums = jnp.sum(grad_flat.astype(F32), axis=0)
        g_query.append(sums[:width])
        g_value.append(sums[2 * width :])
    g_qkv = moves.reduce(
        [
            jnp.einsum("rd,rc->dc", x, grad_flats[part], preferred_element_type=F32)
            for part in range(tp_count)
        ]
    )
    for part in range(tp_count):
        grad_x = grad_x + jnp.einsum(
            "rc,dc->rd", grad_flats[part], qkv_parts[part], preferred_element_type=F32
        )
    sharded = jnp.stack(
        [
            jnp.concatenate([g_query[part], g_value[part], g_in_bias[part]])
            for part in range(tp_count)
        ]
    )
    if grid:
        slots_of = jnp.bitwise_xor(jnp.arange(tp_count, dtype=jnp.int32), position)
        pick = (slots_of[:, None] == jnp.arange(tp_count, dtype=jnp.int32)[None, :]).astype(F32)
        sharded = jnp.sum(pick[:, :, None] * sharded[None, :, :], axis=1)
    common = jnp.concatenate(
        [g_out_bias, g_gain_one, g_shift_one, g_back_bias, g_gain_two, g_shift_two]
    )
    total = moves.reduce_all(jnp.concatenate([sharded.reshape(-1), common]))
    mine = lax.dynamic_slice_in_dim(
        total[: sharded.size].reshape(tp_count, -1), position, 1, axis=0
    )[0]
    tail = total[sharded.size :].reshape(6, model_width)
    return (
        layer_out,
        grad_x.reshape(tokens.shape),
        g_qkv.reshape(model_width, 3, width),
        mine[:width],
        mine[width : 2 * width],
        g_out,
        tail[0],
        tail[1],
        tail[2],
        g_in,
        mine[2 * width :],
        g_back,
        tail[3],
        tail[4],
        tail[5],
    )


def solution(mesh):
    in_specs = (
        P(None, ("batch", "tp"), None),
        P(None, "batch"),
        P(None, ("batch", "tp"), None),
        P(None, None, "tp"),
        P("tp"),
        P("tp"),
        P("tp", None),
        P(),
        P(),
        P(),
        P(None, "tp"),
        P("tp"),
        P("tp", None),
        P(),
        P(),
        P(),
    )
    out_specs = (
        P(None, ("batch", "tp"), None),
        P(None, ("batch", "tp"), None),
        P(None, None, "tp"),
        P("tp"),
        P("tp"),
        P("tp", None),
        P(),
        P(),
        P(),
        P(None, "tp"),
        P("tp"),
        P("tp", None),
        P(),
        P(),
        P(),
    )
    return jax.shard_map(body, mesh=mesh, in_specs=in_specs, out_specs=out_specs, check_vma=False)
```

```python
import math

import jax
import jax.numpy as jnp
from jax import lax
from jax.experimental import pallas as pl
from jax.experimental.pallas import tpu as pltpu
from jax.sharding import PartitionSpec as P

DH = 64
AXES = ("batch", "tp")
epsilon = 1e-05
F32 = jnp.float32
BF16 = jnp.bfloat16


def nt(a, b):
    return lax.dot_general(a, b, (((1,), (1,)), ((), ())), preferred_element_type=F32)


def tn(a, b):
    return lax.dot_general(a, b, (((0,), (0,)), ((), ())), preferred_element_type=F32)


def nn(a, b):
    return jnp.dot(a, b, preferred_element_type=F32)


HBM = pl.BlockSpec(memory_space=pl.ANY)
WHOLE = pl.BlockSpec(memory_space=pltpu.VMEM)
SCALARS = pl.BlockSpec(memory_space=pltpu.SMEM)


class Copies:
    def __init__(self, sems):
        self.sems, self.used = sems, 0
        self.pending = []

    def start(self, src, dst):
        copy = pltpu.make_async_copy(src, dst, self.sems.at[self.used])
        self.used += 1
        copy.start()
        return copy

    def out(self, src, dst):
        self.pending.append(self.start(src, dst))

    def drain(self):
        for copy in self.pending:
            copy.wait()


def call(kernel, name, inputs, outputs, scratch, copies, cost):
    in_specs = [spec for spec, _ in inputs]
    return pl.pallas_call(
        kernel,
        name=name,
        in_specs=in_specs,
        out_specs=tuple(spec for spec, _ in outputs),
        out_shape=tuple(shape for _, shape in outputs),
        scratch_shapes=list(scratch) + [pltpu.SemaphoreType.DMA((copies,))],
        cost_estimate=pl.CostEstimate(flops=cost, transcendentals=0, bytes_accessed=0),
    )(*[value for _, value in inputs])


def shape(dims, dtype):
    return jax.ShapeDtypeStruct(dims, dtype)


def block(i, size):
    return pl.ds(pl.multiple_of(i * size, size), size)


def unit_norm(v):
    middle = jnp.mean(v, axis=-1, keepdims=True)
    centred = v - middle
    inverse = lax.rsqrt(jnp.mean(centred * centred, axis=-1, keepdims=True) + epsilon)
    return centred * inverse, inverse


def norm_grad(scaled, unit, inverse):
    mean_one = jnp.mean(scaled, axis=-1, keepdims=True)
    mean_two = jnp.mean(scaled * unit, axis=-1, keepdims=True)
    return inverse * (scaled - mean_one - unit * mean_two)


STEP = 128


def attend_pair(x, plen, w_pair, bias, lengths, acc=None, vectors=None):
    rows, model = x.shape
    passages = rows // plen
    width = w_pair[0].shape[0] // 4
    heads = width // DH
    last = acc is not None

    def kernel(len_ref, x_hbm, wa, wb, bias_ref, *rest):
        if last:
            acc_hbm, vec_ref = rest[:2]
            rest = rest[2:]
            qkv_hbm, ctx_hbm, p_hbm, unit_hbm, inv_hbm, low_hbm = rest[:6]
            rest = rest[6:]
            x_s, w_s, qkv_s, ctx_s, p_s, acc_s, inv_s, low_s, sems = rest
        else:
            qkv_hbm, ctx_hbm, p_hbm, acc_out = rest[:4]
            rest = rest[4:]
            x_s, w_s, qkv_s, ctx_s, p_s, acc_s, sems = rest
        copies = Copies(sems)
        first = [copies.start(x_hbm, x_s), copies.start(wa, w_s.at[0])]
        second = [copies.start(wb, w_s.at[1])]
        if last:
            first.append(copies.start(acc_hbm, acc_s))
        for j, waits in ((0, first), (1, second)):
            for copy in waits:
                copy.wait()

            def one(g, carry, j=j):
                at = block(g, plen)
                qkv = (nt(x_s[at, :], w_s[j, : 3 * width, :]) + bias_ref[j : j + 1, :]).astype(BF16)
                qkv_s[j, at, :] = qkv
                keep = lax.broadcasted_iota(jnp.int32, (1, plen), 1) < len_ref[g]
                ctx = []
                for h in range(heads):
                    q = qkv[:, h * DH : (h + 1) * DH] * (1.0 / math.sqrt(DH))
                    k = qkv[:, width + h * DH : width + (h + 1) * DH]
                    v = qkv[:, 2 * width + h * DH : 2 * width + (h + 1) * DH]
                    s = jnp.where(keep, nt(q.astype(BF16), k), -1000000000.0)
                    e = jnp.exp(s - jnp.max(s, axis=-1, keepdims=True))
                    p = (e * (1.0 / jnp.sum(e, axis=-1, keepdims=True))).astype(BF16)
                    p_s[j, g * heads + h] = p
                    ctx.append(nn(p, v))
                ctx = jnp.concatenate(ctx, axis=1).astype(BF16)
                ctx_s[j, at, :] = ctx
                term = nn(ctx, w_s[j, 3 * width :, :])
                if j == 0 and not last:
                    acc_s[at, :] = term
                else:
                    acc_s[at, :] = acc_s[at, :] + term
                return carry

            lax.fori_loop(0, passages, one, 0)
            copies.out(qkv_s.at[j], qkv_hbm.at[j])
            copies.out(ctx_s.at[j], ctx_hbm.at[j])
            copies.out(p_s.at[j], p_hbm.at[j])
        if last:

            def finish(i, carry):
                at = block(i, STEP)
                v = x_s[at, :].astype(F32) + acc_s[at, :] + vec_ref[0:1, :]
                unit, inverse = unit_norm(v)
                acc_s[at, :] = unit
                inv_s[at, :] = jnp.broadcast_to(inverse, (STEP, 128))
                low_s[at, :] = (unit * vec_ref[1:2, :] + vec_ref[2:3, :]).astype(BF16)
                return carry

            lax.fori_loop(0, rows // STEP, finish, 0)
            copies.out(acc_s, unit_hbm)
            copies.out(inv_s, inv_hbm)
            copies.out(low_s, low_hbm)
        else:
            copies.out(acc_s, acc_out)
        copies.drain()

    inputs = [(SCALARS, lengths), (HBM, x), (HBM, w_pair[0]), (HBM, w_pair[1])]
    inputs += [(WHOLE, bias)]
    dims = [(2, rows, 3 * width), (2, rows, width), (2, passages * heads, plen, plen)]
    outputs = [(HBM, shape(d, BF16)) for d in dims]
    scratch = [pltpu.VMEM((rows, model), BF16), pltpu.VMEM((2, 4 * width, model), BF16)]
    scratch += [pltpu.VMEM(d, BF16) for d in dims]
    scratch += [pltpu.VMEM((rows, model), F32)]
    if last:
        inputs += [(HBM, acc), (WHOLE, vectors)]
        outputs += [(HBM, shape((rows, model), F32)), (HBM, shape((rows, 128), F32))]
        outputs += [(HBM, shape((rows, model), BF16))]
        scratch += [pltpu.VMEM((rows, 128), F32), pltpu.VMEM((rows, model), BF16)]
    else:
        outputs += [(HBM, shape((rows, model), F32))]
    return call(kernel, "attend_pair", inputs, outputs, scratch, 16, 1000)


def feed_pair(low, in_pair, back_pair, bias):
    rows, model = low.shape
    units = in_pair[0].shape[1]
    cut = units // 3 if units % 3 == 0 and (units // 3) % 128 == 0 else units

    def kernel(low_hbm, ia, ib, ba, bb, bias_ref, *rest):
        act_hbm, slope_hbm, acc_hbm, low_s, i_s, b_s, act_s, slope_s, acc_s, sems = rest
        copies = Copies(sems)
        first = [copies.start(low_hbm, low_s), copies.start(ia, i_s.at[0]), copies.start(ba, b_s.at[0])]
        second = [copies.start(ib, i_s.at[1]), copies.start(bb, b_s.at[1])]
        for j, waits in ((0, first), (1, second)):
            for copy in waits:
                copy.wait()

            def one(i, carry, j=j):
                at = block(i, 256)
                rows_in = low_s[at, :]
                total = acc_s[at, :] if j else 0.0
                for c in range(units // cut):
                    cols = slice(c * cut, (c + 1) * cut)
                    t = nn(rows_in, i_s[j, :, cols]) + bias_ref[j : j + 1, cols]
                    cdf = 0.5 * (1.0 + lax.erf(t * (1.0 / math.sqrt(2.0))))
                    pdf = jnp.exp(-0.5 * t * t) * (1.0 / math.sqrt(2.0 * math.pi))
                    act = (t * cdf).astype(BF16)
                    act_s[j, at, cols] = act
                    slope_s[j, at, cols] = (cdf + t * pdf).astype(BF16)
                    total = total + nn(act, b_s[j, cols, :])
                acc_s[at, :] = total
                return carry

            lax.fori_loop(0, rows // 256, one, 0)
            copies.out(act_s.at[j], act_hbm.at[j])
            copies.out(slope_s.at[j], slope_hbm.at[j])
        copies.out(acc_s, acc_hbm)
        copies.drain()

    inputs = [(HBM, v) for v in (low, *in_pair, *back_pair)] + [(WHOLE, bias)]
    outputs = [(HBM, shape((2, rows, units), BF16))] * 2 + [(HBM, shape((rows, model), F32))]
    scratch = [pltpu.VMEM((rows, model), BF16), pltpu.VMEM((2, model, units), BF16)]
    scratch += [pltpu.VMEM((2, units, model), BF16)] + [pltpu.VMEM((2, rows, units), BF16)] * 2
    scratch += [pltpu.VMEM((rows, model), F32)]
    return call(kernel, "feed_pair", inputs, outputs, scratch, 12, 1000)


def turn(unit, acc_one, acc_two, dy, lengths, vectors, plen):
    rows, model = unit.shape

    def kernel(len_ref, unit_ref, one_ref, two_ref, dy_ref, vec_ref, out_ref, grad_ref, ffn_ref, sum_ref):
        sum_ref[...] = jnp.zeros_like(sum_ref)

        def step(i, carry):
            at = block(i, STEP)
            normed = unit_ref[at, :] * vec_ref[0:1, :] + vec_ref[1:2, :]
            v = normed + (one_ref[at, :] + two_ref[at, :]) + vec_ref[2:3, :]
            u, inverse = unit_norm(v)
            out_ref[at, :] = (u * vec_ref[3:4, :] + vec_ref[4:5, :]).astype(BF16)
            slot = lax.broadcasted_iota(jnp.int32, (STEP, 1), 0) + (i * STEP) % plen
            keep = slot < len_ref[(i * STEP) // plen]
            grad_y = jnp.where(keep, dy_ref[at, :].astype(F32), 0.0)
            grad = norm_grad(grad_y * vec_ref[3:4, :], u, inverse)
            grad_ref[at, :] = grad
            ffn_ref[at, :] = grad.astype(BF16)
            sum_ref[0:1, :] += jnp.sum(grad_y * u, axis=0, keepdims=True)
            sum_ref[1:2, :] += jnp.sum(grad_y, axis=0, keepdims=True)
            sum_ref[2:3, :] += jnp.sum(grad, axis=0, keepdims=True)
            return carry

        lax.fori_loop(0, rows // STEP, step, 0)

    return pl.pallas_call(
        kernel,
        name="turn",
        in_specs=[SCALARS] + [WHOLE] * 5,
        out_specs=(WHOLE,) * 4,
        out_shape=(
            shape((rows, model), BF16),
            shape((rows, model), F32),
            shape((rows, model), BF16),
            shape((8, model), F32),
        ),
        cost_estimate=pl.CostEstimate(flops=1000, transcendentals=0, bytes_accessed=0),
    )(lengths, unit, acc_one, acc_two, dy, vectors)


def outer_pair(acts, grad_ffn):
    _, rows, units = acts.shape
    model = grad_ffn.shape[1]

    def kernel(act_hbm, g_hbm, oa, ob, act_s, g_s, out_s, sems):
        copies = Copies(sems)
        whole = copies.start(g_hbm, g_s)
        waits = [copies.start(act_hbm.at[j], act_s.at[j]) for j in (1, 0)]
        whole.wait()
        for j, wait, out in ((1, waits[0], ob), (0, waits[1], oa)):
            wait.wait()
            for c in range(0, units, 256):
                out_s[j, c : c + 256, :] = tn(act_s[j, :, c : c + 256], g_s[...]).astype(BF16)
            copies.out(out_s.at[j], out)
        copies.drain()

    inputs = [(HBM, acts), (HBM, grad_ffn)]
    outputs = [(HBM, shape((units, model), BF16))] * 2
    scratch = [pltpu.VMEM((2, rows, units), BF16), pltpu.VMEM((rows, model), BF16)]
    scratch += [pltpu.VMEM((2, units, model), BF16)]
    return call(kernel, "outer_pair", inputs, outputs, scratch, 8, 1000)


def feed_back_pair(grad_ffn, slopes, in_pair, back_pair, low, start, unit=None, inverse=None, gain=None):
    rows, model = grad_ffn.shape
    units = slopes.shape[2]
    last = unit is not None

    def kernel(g_hbm, slope_hbm, ia, ib, ba, bb, low_hbm, start_hbm, *rest):
        if last:
            unit_hbm, inv_hbm, gain_ref = rest[:3]
            rest = rest[3:]
            oa, ob, bias_ref, one_hbm, attn_hbm, sum_ref = rest[:6]
            g_s, slope_s, i_s, b_s, low_s, acc_s, pre_s, out_s, unit_s, inv_s, attn_s, sems = rest[6:]
        else:
            oa, ob, bias_ref, acc_out = rest[:4]
            g_s, slope_s, i_s, b_s, low_s, acc_s, pre_s, out_s, sems = rest[4:]
        copies = Copies(sems)
        weights = {1: (bb, ib), 0: (ba, ia)}
        early = copies.start(g_hbm, g_s)
        waits = {}
        for j in (1, 0):
            waits[j] = [copies.start(weights[j][0], b_s.at[j]), copies.start(slope_hbm.at[j], slope_s.at[j])]
            waits[j].append(copies.start(weights[j][1], i_s.at[j]))
            if j == 1:
                waits[j] += [copies.start(start_hbm, acc_s), copies.start(low_hbm, low_s)]
        if last:
            late = [copies.start(unit_hbm, unit_s), copies.start(inv_hbm, inv_s)]
        early.wait()
        for j, out in ((1, ob), (0, oa)):
            for wait in waits[j]:
                wait.wait()
            bias_ref[j : j + 1, :] = jnp.zeros((1, units), F32)

            def one(i, carry, j=j):
                at = block(i, 256)
                pre = (nt(g_s[at, :], b_s[j]) * slope_s[j, at, :].astype(F32)).astype(BF16)
                pre_s[at, :] = pre
                bias_ref[j : j + 1, :] += jnp.sum(pre.astype(F32), axis=0, keepdims=True)
                acc_s[at, :] = acc_s[at, :] + nt(pre, i_s[j])
                return carry

            lax.fori_loop(0, rows // 256, one, 0)
            for c in range(0, model, 256):
                out_s[j, c : c + 256, :] = tn(low_s[:, c : c + 256], pre_s[...]).astype(BF16)
            copies.out(out_s.at[j], out)
        if last:
            for wait in late:
                wait.wait()
            sum_ref[...] = jnp.zeros_like(sum_ref)

            def finish(i, carry):
                at = block(i, STEP)
                normed = acc_s[at, :]
                u = unit_s[at, :]
                grad = norm_grad(normed * gain_ref[0:1, :], u, inv_s[at, 0:1])
                sum_ref[0:1, :] += jnp.sum(grad, axis=0, keepdims=True)
                sum_ref[1:2, :] += jnp.sum(normed * u, axis=0, keepdims=True)
                sum_ref[2:3, :] += jnp.sum(normed, axis=0, keepdims=True)
                acc_s[at, :] = grad
                attn_s[at, :] = grad.astype(BF16)
                return carry

            lax.fori_loop(0, rows // STEP, finish, 0)
            copies.out(acc_s, one_hbm)
            copies.out(attn_s, attn_hbm)
        else:
            copies.out(acc_s, acc_out)
        copies.drain()

    inputs = [(HBM, v) for v in (grad_ffn, slopes, *in_pair, *back_pair, low, start)]
    outputs = [(HBM, shape((model, units), BF16))] * 2 + [(WHOLE, shape((2, units), F32))]
    outputs += [(HBM, shape((rows, model), F32))]
    scratch = [pltpu.VMEM((rows, model), BF16), pltpu.VMEM((2, rows, units), BF16)]
    scratch += [pltpu.VMEM((2, model, units), BF16), pltpu.VMEM((2, units, model), BF16)]
    scratch += [pltpu.VMEM((rows, model), BF16), pltpu.VMEM((rows, model), F32)]
    scratch += [pltpu.VMEM((rows, units), BF16), pltpu.VMEM((2, model, units), BF16)]
    if last:
        inputs += [(HBM, unit), (HBM, inverse), (WHOLE, gain)]
        outputs += [(HBM, shape((rows, model), BF16)), (WHOLE, shape((8, model), F32))]
        scratch += [pltpu.VMEM((rows, model), F32), pltpu.VMEM((rows, 128), F32)]
        scratch += [pltpu.VMEM((rows, model), BF16)]
    return call(kernel, "feed_back_pair", inputs, outputs, scratch, 20, 1000)


def attend_back_pair(x, plen, grad_attn, qkvs, ctxs, probs, w_pair, start):
    rows, model = x.shape
    passages = rows // plen
    width = ctxs.shape[2]
    heads = width // DH

    def kernel(x_hbm, g_hbm, qkv_hbm, ctx_hbm, p_hbm, wa, wb, start_hbm, *rest):
        oa, ob, sum_ref, acc_out = rest[:4]
        x_s, g_s, qkv_s, ctx_s, p_s, w_s, acc_s, grow_s, out_s, sems = rest[4:]
        copies = Copies(sems)
        early = [copies.start(g_hbm, g_s)]
        w_of = {0: wa, 1: wb}
        waits = {}
        for j in (1, 0):
            waits[j] = [copies.start(w_of[j], w_s.at[j]), copies.start(ctx_hbm.at[j], ctx_s.at[j])]
            waits[j] += [copies.start(qkv_hbm.at[j], qkv_s.at[j]), copies.start(p_hbm.at[j], p_s.at[j])]
            if j == 1:
                waits[j] += [copies.start(start_hbm, acc_s), copies.start(x_hbm, x_s)]
        for wait in early:
            wait.wait()
        for j, out in ((1, ob), (0, oa)):
            for wait in waits[j]:
                wait.wait()
            sum_ref[j : j + 1, :] = jnp.zeros((1, 3 * width), F32)
            out_s[j, 3 * width :, :] = tn(ctx_s[j], g_s[...]).astype(BF16)

            def one(g, carry, j=j):
                at = block(g, plen)
                qkv = qkv_s[j, at, :]
                grad_ctx = nt(g_s[at, :], w_s[j, 3 * width :, :]).astype(BF16)
                gq, gk, gv = [], [], []
                for h in range(heads):
                    q = qkv[:, h * DH : (h + 1) * DH]
                    k = qkv[:, width + h * DH : width + (h + 1) * DH]
                    v = qkv[:, 2 * width + h * DH : 2 * width + (h + 1) * DH]
                    gc = grad_ctx[:, h * DH : (h + 1) * DH]
                    low = p_s[j, g * heads + h]
                    p = low.astype(F32)
                    gp = nt(gc, v)
                    delta = jnp.sum(p * gp, axis=-1, keepdims=True)
                    gs = (p * (gp - delta)).astype(BF16)
                    gq.append(nn(gs, k) * (1.0 / math.sqrt(DH)))
                    gk.append(tn(gs, q) * (1.0 / math.sqrt(DH)))
                    gv.append(tn(low, gc))
                grow = jnp.concatenate(gq + gk + gv, axis=1).astype(BF16)
                grow_s[at, :] = grow
                sum_ref[j : j + 1, :] += jnp.sum(grow.astype(F32), axis=0, keepdims=True)
                acc_s[at, :] = acc_s[at, :] + nn(grow, w_s[j, : 3 * width, :])
                return carry

            lax.fori_loop(0, passages, one, 0)
            for c in range(0, 3 * width, width):
                out_s[j, c : c + width, :] = tn(grow_s[:, c : c + width], x_s[...]).astype(BF16)
            copies.out(out_s.at[j], out)
        copies.out(acc_s, acc_out)
        copies.drain()

    inputs = [(HBM, v) for v in (x, grad_attn, qkvs, ctxs, probs, *w_pair, start)]
    outputs = [(HBM, shape((4 * width, model), BF16))] * 2
    outputs += [(WHOLE, shape((2, 3 * width), F32)), (HBM, shape((rows, model), F32))]
    scratch = [pltpu.VMEM((rows, model), BF16), pltpu.VMEM((rows, model), BF16)]
    scratch += [pltpu.VMEM(v.shape, BF16) for v in (qkvs, ctxs, probs)]
    scratch += [pltpu.VMEM((2, 4 * width, model), BF16), pltpu.VMEM((rows, model), F32)]
    scratch += [pltpu.VMEM((rows, 3 * width), BF16), pltpu.VMEM((2, 4 * width, model), BF16)]
    return call(kernel, "attend_back_pair", inputs, outputs, scratch, 20, 1000)


def tie(value, *others):
    return lax.optimization_barrier((value, *others))[0]


def flat_perm(move):
    pairs = []
    for z in range(4):
        for y in range(2):
            for x in range(2):
                for c in range(2):
                    z2, y2, x2, c2 = move(z, y, x, c)
                    pairs.append((((z * 2 + y) * 2 + x) * 2 + c, ((z2 * 2 + y2) * 2 + x2) * 2 + c2))
    return pairs


def add(one, two):
    return (one.astype(F32) + two.astype(F32)).astype(BF16)


class GridMoves:
    def __init__(self):
        self.row = lax.axis_index("batch") % 2
        self.layer = lax.axis_index("batch") // 2 % 2
        self.to_core = flat_perm(lambda z, y, x, c: (z, y, x, 1 - c))
        self.to_x = flat_perm(lambda z, y, x, c: (z, y, 1 - x, c))
        self.to_y = flat_perm(lambda z, y, x, c: (z, 1 - y, x, c))
        self.to_z = flat_perm(lambda z, y, x, c: (z ^ 1, y, x, c))
        self.to_zz = flat_perm(lambda z, y, x, c: (z ^ 2, y, x, c))
        self.mark = None

    def send(self, value, pairs):
        return lax.ppermute(value, AXES, pairs)

    def half(self, value, which):
        rows = value.shape[0] // 2
        return lax.dynamic_slice_in_dim(value, which * rows, rows, axis=0)

    def order(self, mine, other, bit):
        low = jnp.where(bit == 0, mine, other)
        high = jnp.where(bit == 0, other, mine)
        return jnp.concatenate([low, high], axis=0)

    def gather(self, own):
        first = self.send(self.half(own, self.row), self.to_x)
        second = self.send(first, self.to_y)
        far = self.order(first, second, self.row)
        return [own, self.send(own, self.to_core), far, self.send(far, self.to_core)]

    def gather_small(self, own):
        pair = jnp.stack([own, self.send(own, self.to_core)])
        far = self.send(pair, self.to_x)
        return [pair[0], pair[1], far[0], far[1]]

    def after(self, value):
        if self.mark is not None:
            value = tie(value, self.mark)
        return value

    def chain(self, near, got):
        got = self.after(got)
        pass_on = add(self.half(near, 1 - self.row), self.half(got, 1 - self.row))
        keep = add(self.half(near, self.row), self.half(got, self.row))
        got = self.send(pass_on, self.to_y)
        yield pass_on
        got = self.after(got)
        keep = add(keep, got)
        pass_on = self.half(keep, 1 - self.layer)
        keep = self.half(keep, self.layer)
        got = self.send(pass_on, self.to_z)
        yield pass_on
        keep = add(keep, self.after(got))
        got = self.send(keep, self.to_zz)
        yield keep
        keep = add(keep, self.after(got))
        got = self.send(keep, self.to_z)
        yield keep
        keep = self.order(keep, self.after(got), self.layer)
        got = self.send(keep, self.to_y)
        yield keep
        yield self.order(keep, self.after(got), self.row).astype(F32)

    def chain_small(self, value):
        for pairs in (self.to_core, self.to_x, self.to_y, self.to_z, self.to_zz):
            got = self.send(value, pairs)
            yield value
            value = value + self.after(got)
        yield value

    def step(self, chain):
        self.mark = next(chain)
        return self.mark


def body(
    tokens,
    passage_lengths,
    cotangent,
    w_qkv,
    b_query,
    b_value,
    w_out,
    b_out,
    gain_one,
    shift_one,
    w_in,
    b_in,
    w_back,
    b_back,
    gain_two,
    shift_two,
):
    micro_count, own_rows, model = tokens.shape
    tp_count = lax.axis_size("tp")
    batch_count = lax.axis_size("batch")
    plen = own_rows * tp_count // passage_lengths.shape[1]
    own_passages = own_rows // plen
    assert own_passages * plen == own_rows and tp_count == 4
    grid = (batch_count, tp_count) == (8, 4)
    width = w_qkv.shape[2]
    rows = micro_count * own_rows
    position = lax.axis_index("tp")

    qkvo = jnp.concatenate([jnp.transpose(w_qkv, (1, 2, 0)).reshape(3 * width, model), w_out], axis=0)
    small = jnp.concatenate([b_query, jnp.zeros_like(b_query), b_value, b_in.astype(F32)])
    if grid:
        moves = GridMoves()
        att = moves.gather(qkvo)
        smalls = moves.gather_small(small)
        ins = moves.gather(w_in)
        backs = moves.gather(w_back)
    else:
        att, smalls, ins, backs = [
            list(lax.all_gather(v, "tp", axis=0)) for v in (qkvo, small, w_in, w_back)
        ]
    bias_qkv = [jnp.stack([smalls[i][: 3 * width], smalls[i + 1][: 3 * width]]) for i in (0, 2)]
    bias_in = [jnp.stack([smalls[i][3 * width :], smalls[i + 1][3 * width :]]) for i in (0, 2)]

    lengths = lax.dynamic_slice_in_dim(
        passage_lengths, position * own_passages, own_passages, axis=1
    ).reshape(micro_count * own_passages)
    x = tokens.reshape(rows, model)
    dy = cotangent.reshape(rows, model)

    qkv_near, ctx_near, p_near, acc = attend_pair(x, plen, att[:2], bias_qkv[0], lengths)
    qkv_far, ctx_far, p_far, unit, inverse, low = attend_pair(
        x, plen, att[2:], bias_qkv[1], lengths, acc, jnp.stack([b_out, gain_one, shift_one])
    )
    act_near, slope_near, feed_near = feed_pair(low, ins[:2], backs[:2], bias_in[0])
    act_far, slope_far, feed_far = feed_pair(tie(low, feed_near), ins[2:], backs[2:], bias_in[1])
    layer_out, grad_two, grad_ffn, sums_two = turn(
        unit,
        feed_near,
        feed_far,
        dy,
        lengths,
        jnp.stack([gain_one, shift_one, b_back, gain_two, shift_two]),
        plen,
    )
    gain = gain_one.reshape(1, model)

    b_far, b_farc = outer_pair(act_far, grad_ffn)
    if grid:
        got_b3 = moves.send(b_farc, moves.to_core)
    b_own, b_core = outer_pair(act_near, tie(grad_ffn, b_far))
    if grid:
        got_b1 = moves.send(b_core, moves.to_core)
        b_far = add(b_far, tie(got_b3, b_own))
        got_bx = moves.send(b_far, moves.to_x)
        slope_far = tie(slope_far, b_far)
    i_far, i_farc, bias_far, normed = feed_back_pair(
        grad_ffn, slope_far, ins[2:], backs[2:], low, grad_two
    )
    if grid:
        got_i3 = moves.send(i_farc, moves.to_core)
        b_near = add(b_own, tie(got_b1, normed))
        normed = tie(normed, b_near)
    i_own, i_core, bias_near, grad_one, grad_attn, sums_one = feed_back_pair(
        grad_ffn, slope_near, ins[:2], backs[:2], low, normed, unit, inverse, gain
    )
    if grid:
        got_i1 = moves.send(i_core, moves.to_core)
        i_far = add(i_far, tie(got_i3, grad_attn))
        got_ix = moves.send(i_far, moves.to_x)
        grad_attn = tie(grad_attn, i_far)
    a_far, a_farc, sum_far, grad_x = attend_back_pair(
        x, plen, grad_attn, qkv_far, ctx_far, p_far, att[2:], grad_one
    )
    if grid:
        got_a3 = moves.send(a_farc, moves.to_core)
        i_near = add(i_own, tie(got_i1, grad_x))
        moves.mark = i_near
        chain_b = moves.chain(b_near, got_bx)
        moves.step(chain_b)
        grad_x = tie(grad_x, moves.mark)
    a_own, a_core, sum_near, grad_x = attend_back_pair(
        x, plen, grad_attn, qkv_near, ctx_near, p_near, att[:2], grad_x
    )
    sharded = jnp.stack(
        [
            jnp.concatenate([sums[j, :width], sums[j, 2 * width :], bias[j]])
            for sums, bias in ((sum_near, bias_near), (sum_far, bias_far))
            for j in (0, 1)
        ]
    )
    if grid:
        slots_of = jnp.bitwise_xor(jnp.arange(tp_count, dtype=jnp.int32), position)
        pick = (slots_of[:, None] == jnp.arange(tp_count, dtype=jnp.int32)[None, :]).astype(F32)
        sharded = jnp.sum(pick[:, :, None] * sharded[None, :, :], axis=1)
    common = jnp.concatenate([sums_one[:3].reshape(-1), sums_two[:3].reshape(-1)])
    packed = jnp.concatenate([sharded.reshape(-1), common])
    if grid:
        got_a1 = moves.send(a_core, moves.to_core)
        moves.mark = grad_x
        a_far = add(a_far, moves.after(got_a3))
        cut = a_far.shape[0] // 2
        got_ax = [moves.send(part, moves.to_x) for part in (a_far[:cut], a_far[cut:])]
        moves.mark = a_far
        chains = {"s": moves.chain_small(packed), "b": chain_b}
        done = {}
        for key in ("s", "b"):
            done[key] = moves.step(chains[key])
        a_near = add(a_own, moves.after(got_a1))
        moves.mark = a_near
        chains["i"] = moves.chain(i_near, got_ix)
        chains["u"] = moves.chain(a_near[:cut], got_ax[0])
        chains["v"] = moves.chain(a_near[cut:], got_ax[1])
        for key in "sibsubisbivusibuivusvuivuvv":
            done[key] = moves.step(chains[key])
        g_back, g_in, packed = done["b"], done["i"], done["s"]
        g_att = jnp.concatenate([done["u"], done["v"]], axis=0)
    else:
        g_back, g_in, g_att = [
            lax.psum(
                lax.psum_scatter(jnp.stack(parts).astype(F32), "tp", scatter_dimension=0), "batch"
            )
            for parts in (
                (b_own, b_core, b_far, b_farc),
                (i_own, i_core, i_far, i_farc),
                (a_own, a_core, a_far, a_farc),
            )
        ]
        packed = lax.psum(packed, AXES)
    mine = lax.dynamic_slice_in_dim(
        packed[: sharded.size].reshape(tp_count, -1), position, 1, axis=0
    )[0]
    ends = packed[sharded.size :].reshape(6, model)
    return (
        layer_out.reshape(tokens.shape),
        grad_x.reshape(tokens.shape),
        jnp.transpose(g_att[: 3 * width].reshape(3, width, model), (2, 0, 1)),
        mine[:width],
        mine[width : 2 * width],
        g_att[3 * width :],
        ends[0],
        ends[1],
        ends[2],
        g_in,
        mine[2 * width :],
        g_back,
        ends[5],
        ends[3],
        ends[4],
    )


def solution(mesh):
    in_specs = (
        P(None, ("batch", "tp"), None),
        P(None, "batch"),
        P(None, ("batch", "tp"), None),
        P(None, None, "tp"),
        P("tp"),
        P("tp"),
        P("tp", None),
        P(),
        P(),
        P(),
        P(None, "tp"),
        P("tp"),
        P("tp", None),
        P(),
        P(),
        P(),
    )
    out_specs = (
        P(None, ("batch", "tp"), None),
        P(None, ("batch", "tp"), None),
        P(None, None, "tp"),
        P("tp"),
        P("tp"),
        P("tp", None),
        P(),
        P(),
        P(),
        P(None, "tp"),
        P("tp"),
        P("tp", None),
        P(),
        P(),
        P(),
    )
    return jax.shard_map(body, mesh=mesh, in_specs=in_specs, out_specs=out_specs, check_vma=False)
```

```python
import math

import jax
import jax.numpy as jnp
from jax import lax
from jax.experimental import pallas as pl
from jax.experimental.pallas import tpu as pltpu
from jax.sharding import PartitionSpec as P

DH = 64
AXES = ("batch", "tp")
epsilon = 1e-05
F32 = jnp.float32
BF16 = jnp.bfloat16


def nt(a, b):
    return lax.dot_general(a, b, (((1,), (1,)), ((), ())), preferred_element_type=F32)


def tn(a, b):
    return lax.dot_general(a, b, (((0,), (0,)), ((), ())), preferred_element_type=F32)


def nn(a, b):
    return jnp.dot(a, b, preferred_element_type=F32)


HBM = pl.BlockSpec(memory_space=pl.ANY)
WHOLE = pl.BlockSpec(memory_space=pltpu.VMEM)
SCALARS = pl.BlockSpec(memory_space=pltpu.SMEM)


class Copies:
    def __init__(self, sems):
        self.sems, self.used = sems, 0
        self.pending = []

    def start(self, src, dst):
        copy = pltpu.make_async_copy(src, dst, self.sems.at[self.used])
        self.used += 1
        copy.start()
        return copy

    def out(self, src, dst):
        self.pending.append(self.start(src, dst))

    def drain(self):
        for copy in self.pending:
            copy.wait()


def call(kernel, name, inputs, outputs, scratch, copies, cost=1000):
    in_specs = [spec for spec, _ in inputs]
    return pl.pallas_call(
        kernel,
        name=name,
        in_specs=in_specs,
        out_specs=tuple(spec for spec, _ in outputs),
        out_shape=tuple(shape for _, shape in outputs),
        scratch_shapes=list(scratch) + [pltpu.SemaphoreType.DMA((copies,))],
        cost_estimate=pl.CostEstimate(flops=cost, transcendentals=0, bytes_accessed=0),
    )(*[value for _, value in inputs])


def shape(dims, dtype):
    return jax.ShapeDtypeStruct(dims, dtype)


def block(i, size):
    return pl.ds(pl.multiple_of(i * size, size), size)


def unit_norm(v):
    middle = jnp.mean(v, axis=-1, keepdims=True)
    centred = v - middle
    inverse = lax.rsqrt(jnp.mean(centred * centred, axis=-1, keepdims=True) + epsilon)
    return centred * inverse, inverse


def norm_grad(scaled, unit, inverse):
    mean_one = jnp.mean(scaled, axis=-1, keepdims=True)
    mean_two = jnp.mean(scaled * unit, axis=-1, keepdims=True)
    return inverse * (scaled - mean_one - unit * mean_two)


STEP = 128


def row_of(part, meta_ref, kind):
    return 2 * jnp.bitwise_xor(part, meta_ref[meta_ref.shape[0] - 1]) + kind


def attend_pair(x, plen, w_pair, smalls, meta, acc=None, vectors=None):
    rows, model = x.shape
    passages = rows // plen
    width = w_pair[0].shape[0] // 4
    heads = width // DH
    units = smalls[0].shape[1] - 3 * width
    last = acc is not None

    def kernel(meta_ref, x_hbm, wa, wb, bias_a, bias_b, *rest):
        if last:
            acc_hbm, b_out, gain, shift = rest[:4]
            qkv_hbm, ctx_hbm, p_hbm, unit_hbm, inv_hbm, low_hbm = rest[4:10]
            x_s, w_s, qkv_s, ctx_s, p_s, acc_s, inv_s, low_s, sems = rest[10:]
        else:
            qkv_hbm, ctx_hbm, p_hbm, acc_out = rest[:4]
            x_s, w_s, qkv_s, ctx_s, p_s, acc_s, sems = rest[4:]
        copies = Copies(sems)
        first = [copies.start(x_hbm, x_s), copies.start(wa, w_s.at[0])]
        second = [copies.start(wb, w_s.at[1])]
        if last:
            first.append(copies.start(acc_hbm, acc_s))
        for j, waits, bias in ((0, first, bias_a), (1, second, bias_b)):
            for copy in waits:
                copy.wait()
            qkv_s[j] = (nt(x_s[...], w_s[j, : 3 * width, :]) + bias[0:1, units:]).astype(BF16)
            copies.out(qkv_s.at[j], qkv_hbm.at[j])

            def one(g, carry, j=j):
                at = block(g, plen)
                qkv = qkv_s[j, at, :]
                keep = lax.broadcasted_iota(jnp.int32, (1, plen), 1) < meta_ref[g]
                ctx = []
                for h in range(heads):
                    q = qkv[:, h * DH : (h + 1) * DH] * (1.0 / math.sqrt(DH))
                    k = qkv[:, width + h * DH : width + (h + 1) * DH]
                    v = qkv[:, 2 * width + h * DH : 2 * width + (h + 1) * DH]
                    s = jnp.where(keep, nt(q.astype(BF16), k), -1000000000.0)
                    e = jnp.exp(s - jnp.max(s, axis=-1, keepdims=True))
                    p = (e * (1.0 / jnp.sum(e, axis=-1, keepdims=True))).astype(BF16)
                    p_s[j, g * heads + h] = p
                    ctx.append(nn(p, v))
                ctx_s[j, at, :] = jnp.concatenate(ctx, axis=1).astype(BF16)
                return carry

            lax.fori_loop(0, passages, one, 0)
            copies.out(ctx_s.at[j], ctx_hbm.at[j])
            copies.out(p_s.at[j], p_hbm.at[j])
            term = nn(ctx_s[j], w_s[j, 3 * width :, :])
            acc_s[...] = term if j == 0 and not last else acc_s[...] + term
        if last:

            def finish(i, carry):
                at = block(i, STEP)
                v = x_s[at, :].astype(F32) + acc_s[at, :] + b_out[...]
                unit, inverse = unit_norm(v)
                acc_s[at, :] = unit
                inv_s[at, :] = jnp.broadcast_to(inverse, (STEP, 128))
                low_s[at, :] = (unit * gain[...] + shift[...]).astype(BF16)
                return carry

            lax.fori_loop(0, rows // STEP, finish, 0)
            copies.out(acc_s, unit_hbm)
            copies.out(inv_s, inv_hbm)
            copies.out(low_s, low_hbm)
        else:
            copies.out(acc_s, acc_out)
        copies.drain()

    inputs = [(SCALARS, meta), (HBM, x), (HBM, w_pair[0]), (HBM, w_pair[1])]
    inputs += [(WHOLE, v) for v in smalls]
    dims = [(2, rows, 3 * width), (2, rows, width), (2, passages * heads, plen, plen)]
    outputs = [(HBM, shape(d, BF16)) for d in dims]
    scratch = [pltpu.VMEM((rows, model), BF16), pltpu.VMEM((2, 4 * width, model), BF16)]
    scratch += [pltpu.VMEM(d, BF16) for d in dims]
    scratch += [pltpu.VMEM((rows, model), F32)]
    if last:
        inputs += [(HBM, acc)] + [(WHOLE, v) for v in vectors]
        outputs += [(HBM, shape((rows, model), F32)), (HBM, shape((rows, 128), F32))]
        outputs += [(HBM, shape((rows, model), BF16))]
        scratch += [pltpu.VMEM((rows, 128), F32), pltpu.VMEM((rows, model), BF16)]
    else:
        outputs += [(HBM, shape((rows, model), F32))]
    return call(kernel, "attend_pair", inputs, outputs, scratch, 16)


def feed(j, low_s, i_s, b_s, bias, act_s, slope_s):
    units = act_s.shape[2]
    for c in range(0, units, 256):
        cols = slice(c, c + 256)
        t = nn(low_s[...], i_s[j, :, cols]) + bias[0:1, cols]
        cdf = 0.5 * (1.0 + lax.erf(t * (1.0 / math.sqrt(2.0))))
        pdf = jnp.exp(-0.5 * t * t) * (1.0 / math.sqrt(2.0 * math.pi))
        act_s[j, :, cols] = (t * cdf).astype(BF16)
        slope_s[j, :, cols] = (cdf + t * pdf).astype(BF16)
    return nn(act_s[j], b_s[j])


def feed_pair(low, in_pair, back_pair, smalls):
    rows, model = low.shape
    units = in_pair[0].shape[1]

    def kernel(low_hbm, ia, ib, ba, bb, bias_a, bias_b, *rest):
        act_hbm, slope_hbm, acc_hbm, low_s, i_s, b_s, act_s, slope_s, acc_s, sems = rest
        copies = Copies(sems)
        first = [copies.start(low_hbm, low_s), copies.start(ia, i_s.at[0]), copies.start(ba, b_s.at[0])]
        second = [copies.start(ib, i_s.at[1]), copies.start(bb, b_s.at[1])]
        for j, waits, bias in ((0, first, bias_a), (1, second, bias_b)):
            for copy in waits:
                copy.wait()
            term = feed(j, low_s, i_s, b_s, bias, act_s, slope_s)
            copies.out(act_s.at[j], act_hbm.at[j])
            copies.out(slope_s.at[j], slope_hbm.at[j])
            acc_s[...] = acc_s[...] + term if j else term
        copies.out(acc_s, acc_hbm)
        copies.drain()

    inputs = [(HBM, v) for v in (low, *in_pair, *back_pair)] + [(WHOLE, v) for v in smalls]
    outputs = [(HBM, shape((2, rows, units), BF16))] * 2 + [(HBM, shape((rows, model), F32))]
    scratch = [pltpu.VMEM((rows, model), BF16), pltpu.VMEM((2, model, units), BF16)]
    scratch += [pltpu.VMEM((2, units, model), BF16)] + [pltpu.VMEM((2, rows, units), BF16)] * 2
    scratch += [pltpu.VMEM((rows, model), F32)]
    return call(kernel, "feed_pair", inputs, outputs, scratch, 12)


def turn_pair(low, in_pair, back_pair, smalls, unit, acc, dy, meta, vectors, plen):
    rows, model = low.shape
    units = in_pair[0].shape[1]

    def kernel(meta_ref, low_hbm, ia, ib, ba, bb, unit_hbm, acc_hbm, dy_hbm, bias_a, bias_b, *rest):
        gain_one, shift_one, b_back, gain_two, shift_two = rest[:5]
        out_hbm, grad_hbm, ffn_hbm, sum_ref, slope_hbm, oa, ob = rest[5:12]
        low_s, i_s, b_s, act_s, slope_s, acc_s, unit_s, dy_s, out_s, grad_s, ffn_s, g_s, sems = rest[12:]
        copies = Copies(sems)
        first = [copies.start(low_hbm, low_s), copies.start(ia, i_s.at[0]), copies.start(ba, b_s.at[0])]
        second = [copies.start(ib, i_s.at[1]), copies.start(bb, b_s.at[1]), copies.start(acc_hbm, acc_s)]
        third = [copies.start(unit_hbm, unit_s), copies.start(dy_hbm, dy_s)]
        for copy in first:
            copy.wait()
        term = feed(0, low_s, i_s, b_s, bias_a, act_s, slope_s)
        copies.out(slope_s.at[0], slope_hbm.at[0])
        for copy in second:
            copy.wait()
        acc_s[...] = acc_s[...] + term
        acc_s[...] = acc_s[...] + feed(1, low_s, i_s, b_s, bias_b, act_s, slope_s)
        copies.out(slope_s.at[1], slope_hbm.at[1])
        for copy in third:
            copy.wait()
        sum_ref[...] = jnp.zeros_like(sum_ref)

        def step(i, carry):
            at = block(i, STEP)
            normed = unit_s[at, :] * gain_one[...] + shift_one[...]
            u, inverse = unit_norm(normed + acc_s[at, :] + b_back[...])
            out_s[at, :] = (u * gain_two[...] + shift_two[...]).astype(BF16)
            slot = lax.broadcasted_iota(jnp.int32, (STEP, 1), 0) + (i * STEP) % plen
            keep = slot < meta_ref[(i * STEP) // plen]
            grad_y = jnp.where(keep, dy_s[at, :].astype(F32), 0.0)
            grad = norm_grad(grad_y * gain_two[...], u, inverse)
            grad_s[at, :] = grad
            ffn_s[at, :] = grad.astype(BF16)
            sum_ref[8:9, :] += jnp.sum(grad_y * u, axis=0, keepdims=True)
            sum_ref[9:10, :] += jnp.sum(grad_y, axis=0, keepdims=True)
            sum_ref[10:11, :] += jnp.sum(grad, axis=0, keepdims=True)
            return carry

        lax.fori_loop(0, rows // STEP, step, 0)
        copies.out(out_s, out_hbm)
        copies.out(grad_s, grad_hbm)
        copies.out(ffn_s, ffn_hbm)
        for j, out in ((1, ob), (0, oa)):
            g_s[j] = tn(act_s[j], ffn_s[...]).astype(BF16)
            copies.out(g_s.at[j], out)
        copies.drain()

    inputs = [(SCALARS, meta)] + [(HBM, v) for v in (low, *in_pair, *back_pair, unit, acc, dy)]
    inputs += [(WHOLE, v) for v in (*smalls, *vectors)]
    outputs = [(HBM, shape((rows, model), d)) for d in (BF16, F32, BF16)]
    outputs += [(WHOLE, shape((16, model), F32)), (HBM, shape((2, rows, units), BF16))]
    outputs += [(HBM, shape((units, model), BF16))] * 2
    scratch = [pltpu.VMEM((rows, model), BF16), pltpu.VMEM((2, model, units), BF16)]
    scratch += [pltpu.VMEM((2, units, model), BF16)] + [pltpu.VMEM((2, rows, units), BF16)] * 2
    scratch += [pltpu.VMEM((rows, model), d) for d in (F32, F32, BF16, BF16, F32, BF16)]
    scratch += [pltpu.VMEM((2, units, model), BF16)]
    return call(kernel, "turn_pair", inputs, outputs, scratch, 20)


def outer_pair(acts, grad_ffn):
    _, rows, units = acts.shape
    model = grad_ffn.shape[1]

    def kernel(act_hbm, g_hbm, oa, ob, act_s, g_s, out_s, sems):
        copies = Copies(sems)
        whole = copies.start(g_hbm, g_s)
        waits = [copies.start(act_hbm.at[j], act_s.at[j]) for j in (1, 0)]
        whole.wait()
        for j, wait, out in ((1, waits[0], ob), (0, waits[1], oa)):
            wait.wait()
            out_s[j] = tn(act_s[j], g_s[...]).astype(BF16)
            copies.out(out_s.at[j], out)
        copies.drain()

    inputs = [(HBM, acts), (HBM, grad_ffn)]
    outputs = [(HBM, shape((units, model), BF16))] * 2
    scratch = [pltpu.VMEM((2, rows, units), BF16), pltpu.VMEM((rows, model), BF16)]
    scratch += [pltpu.VMEM((2, units, model), BF16)]
    return call(kernel, "outer_pair", inputs, outputs, scratch, 8)


def feed_back_pair(grad_ffn, slopes, in_pair, back_pair, low, start, part, sums, meta, unit=None, inverse=None, gain=None):
    rows, model = grad_ffn.shape
    units = slopes.shape[2]
    last = unit is not None

    def kernel(meta_ref, before, g_hbm, slope_hbm, ia, ib, ba, bb, low_hbm, start_hbm, *rest):
        if last:
            unit_hbm, inv_hbm, gain_ref = rest[:3]
            rest = rest[3:]
            oa, ob, sum_ref, one_hbm, attn_hbm = rest[:5]
            g_s, slope_s, i_s, b_s, low_s, acc_s, pre_s, out_s, line, unit_s, inv_s, attn_s, sems = rest[5:]
        else:
            oa, ob, sum_ref, acc_out = rest[:4]
            g_s, slope_s, i_s, b_s, low_s, acc_s, pre_s, out_s, line, sems = rest[4:]
        copies = Copies(sems)
        sum_ref[...] = before[...]
        weights = {1: (bb, ib), 0: (ba, ia)}
        early = copies.start(g_hbm, g_s)
        waits = {}
        for j in (1, 0):
            waits[j] = [copies.start(weights[j][0], b_s.at[j]), copies.start(slope_hbm.at[j], slope_s.at[j])]
            waits[j].append(copies.start(weights[j][1], i_s.at[j]))
            if j == 1:
                waits[j] += [copies.start(start_hbm, acc_s), copies.start(low_hbm, low_s)]
        if last:
            late = [copies.start(unit_hbm, unit_s), copies.start(inv_hbm, inv_s)]
        early.wait()
        for j, out in ((1, ob), (0, oa)):
            for wait in waits[j]:
                wait.wait()
            for c in range(0, units, 256):
                cols = slice(c, c + 256)
                pre = nt(g_s[...], b_s[j, cols, :]) * slope_s[j, :, cols].astype(F32)
                pre = pre.astype(BF16)
                pre_s[:, cols] = pre
                line[:, cols] = jnp.sum(pre.astype(F32), axis=0, keepdims=True)
            sum_ref[pl.ds(row_of(part + j, meta_ref, 0), 1), :] = line[...]
            acc_s[...] = acc_s[...] + nt(pre_s[...], i_s[j])
            out_s[j] = tn(low_s[...], pre_s[...]).astype(BF16)
            copies.out(out_s.at[j], out)
        if last:
            for wait in late:
                wait.wait()

            def finish(i, carry):
                at = block(i, STEP)
                normed = acc_s[at, :]
                u = unit_s[at, :]
                grad = norm_grad(normed * gain_ref[0:1, :], u, inv_s[at, 0:1])
                sum_ref[11:12, :] += jnp.sum(grad, axis=0, keepdims=True)
                sum_ref[12:13, :] += jnp.sum(normed * u, axis=0, keepdims=True)
                sum_ref[13:14, :] += jnp.sum(normed, axis=0, keepdims=True)
                acc_s[at, :] = grad
                attn_s[at, :] = grad.astype(BF16)
                return carry

            lax.fori_loop(0, rows // STEP, finish, 0)
            copies.out(acc_s, one_hbm)
            copies.out(attn_s, attn_hbm)
        else:
            copies.out(acc_s, acc_out)
        copies.drain()

    inputs = [(SCALARS, meta), (WHOLE, sums)]
    inputs += [(HBM, v) for v in (grad_ffn, slopes, *in_pair, *back_pair, low, start)]
    outputs = [(HBM, shape((model, units), BF16))] * 2 + [(WHOLE, shape((16, model), F32))]
    outputs += [(HBM, shape((rows, model), F32))]
    scratch = [pltpu.VMEM((rows, model), BF16), pltpu.VMEM((2, rows, units), BF16)]
    scratch += [pltpu.VMEM((2, model, units), BF16), pltpu.VMEM((2, units, model), BF16)]
    scratch += [pltpu.VMEM((rows, model), BF16), pltpu.VMEM((rows, model), F32)]
    scratch += [pltpu.VMEM((rows, units), BF16), pltpu.VMEM((2, model, units), BF16)]
    scratch += [pltpu.VMEM((1, units), F32)]
    if last:
        inputs += [(HBM, unit), (HBM, inverse), (WHOLE, gain)]
        outputs += [(HBM, shape((rows, model), BF16))]
        scratch += [pltpu.VMEM((rows, model), F32), pltpu.VMEM((rows, 128), F32)]
        scratch += [pltpu.VMEM((rows, model), BF16)]
    return call(kernel, "feed_back_pair", inputs, outputs, scratch, 20)


def attend_back_pair(x, plen, grad_attn, qkvs, ctxs, probs, w_pair, start, part, sums, meta):
    rows, model = x.shape
    passages = rows // plen
    width = ctxs.shape[2]
    heads = width // DH

    def kernel(meta_ref, before, x_hbm, g_hbm, qkv_hbm, ctx_hbm, p_hbm, wa, wb, start_hbm, *rest):
        oa, ob, sum_ref, acc_out = rest[:4]
        x_s, g_s, qkv_s, ctx_s, p_s, w_s, acc_s, grow_s, out_s, gc_s, sems = rest[4:]
        copies = Copies(sems)
        sum_ref[...] = before[...]
        early = [copies.start(g_hbm, g_s)]
        w_of = {0: wa, 1: wb}
        waits = {}
        for j in (1, 0):
            waits[j] = [copies.start(w_of[j], w_s.at[j]), copies.start(ctx_hbm.at[j], ctx_s.at[j])]
            waits[j] += [copies.start(qkv_hbm.at[j], qkv_s.at[j]), copies.start(p_hbm.at[j], p_s.at[j])]
            if j == 1:
                waits[j] += [copies.start(start_hbm, acc_s), copies.start(x_hbm, x_s)]
        for wait in early:
            wait.wait()
        for j, out in ((1, ob), (0, oa)):
            for wait in waits[j]:
                wait.wait()
            gc_s[...] = nt(g_s[...], w_s[j, 3 * width :, :]).astype(BF16)
            out_s[j, 3 * width :, :] = tn(ctx_s[j], g_s[...]).astype(BF16)

            def one(g, carry, j=j):
                at = block(g, plen)
                qkv = qkv_s[j, at, :]
                grad_ctx = gc_s[at, :]
                gq, gk, gv = [], [], []
                for h in range(heads):
                    q = qkv[:, h * DH : (h + 1) * DH]
                    k = qkv[:, width + h * DH : width + (h + 1) * DH]
                    v = qkv[:, 2 * width + h * DH : 2 * width + (h + 1) * DH]
                    gc = grad_ctx[:, h * DH : (h + 1) * DH]
                    low = p_s[j, g * heads + h]
                    p = low.astype(F32)
                    gp = nt(gc, v)
                    delta = jnp.sum(p * gp, axis=-1, keepdims=True)
                    gs = (p * (gp - delta)).astype(BF16)
                    gq.append(nn(gs, k) * (1.0 / math.sqrt(DH)))
                    gk.append(tn(gs, q) * (1.0 / math.sqrt(DH)))
                    gv.append(tn(low, gc))
                grow = jnp.concatenate(gq + gk + gv, axis=1).astype(BF16)
                grow_s[at, :] = grow
                return carry + jnp.sum(grow.astype(F32), axis=0, keepdims=True)

            line = lax.fori_loop(0, passages, one, jnp.zeros((1, 3 * width), F32))
            line = jnp.concatenate([line, jnp.zeros((1, model - 3 * width), F32)], axis=1)
            sum_ref[pl.ds(row_of(part + j, meta_ref, 1), 1), :] = line
            out_s[j, : 3 * width, :] = tn(grow_s[...], x_s[...]).astype(BF16)
            copies.out(out_s.at[j], out)
            acc_s[...] = acc_s[...] + nn(grow_s[...], w_s[j, : 3 * width, :])
        copies.out(acc_s, acc_out)
        copies.drain()

    inputs = [(SCALARS, meta), (WHOLE, sums)]
    inputs += [(HBM, v) for v in (x, grad_attn, qkvs, ctxs, probs, *w_pair, start)]
    outputs = [(HBM, shape((4 * width, model), BF16))] * 2
    outputs += [(WHOLE, shape((16, model), F32)), (HBM, shape((rows, model), F32))]
    scratch = [pltpu.VMEM((rows, model), BF16), pltpu.VMEM((rows, model), BF16)]
    scratch += [pltpu.VMEM(v.shape, BF16) for v in (qkvs, ctxs, probs)]
    scratch += [pltpu.VMEM((2, 4 * width, model), BF16), pltpu.VMEM((rows, model), F32)]
    scratch += [pltpu.VMEM((rows, 3 * width), BF16), pltpu.VMEM((2, 4 * width, model), BF16)]
    scratch += [pltpu.VMEM((rows, width), BF16)]
    return call(kernel, "attend_back_pair", inputs, outputs, scratch, 20)


def tie(value, *others):
    return lax.optimization_barrier((value, *others))[0]


def flat_perm(move):
    pairs = []
    for z in range(4):
        for y in range(2):
            for x in range(2):
                for c in range(2):
                    z2, y2, x2, c2 = move(z, y, x, c)
                    pairs.append((((z * 2 + y) * 2 + x) * 2 + c, ((z2 * 2 + y2) * 2 + x2) * 2 + c2))
    return pairs


def add(one, two):
    return (one.astype(F32) + two.astype(F32)).astype(BF16)


class GridMoves:
    def __init__(self):
        self.row = lax.axis_index("batch") % 2
        self.layer = lax.axis_index("batch") // 2 % 2
        self.to_core = flat_perm(lambda z, y, x, c: (z, y, x, 1 - c))
        self.to_x = flat_perm(lambda z, y, x, c: (z, y, 1 - x, c))
        self.to_y = flat_perm(lambda z, y, x, c: (z, 1 - y, x, c))
        self.to_z = flat_perm(lambda z, y, x, c: (z ^ 1, y, x, c))
        self.to_zz = flat_perm(lambda z, y, x, c: (z ^ 2, y, x, c))
        self.mark = None

    def send(self, value, pairs):
        return lax.ppermute(value, AXES, pairs)

    def half(self, value, which):
        rows = value.shape[0] // 2
        return lax.dynamic_slice_in_dim(value, which * rows, rows, axis=0)

    def order(self, mine, other, bit):
        low = jnp.where(bit == 0, mine, other)
        high = jnp.where(bit == 0, other, mine)
        return jnp.concatenate([low, high], axis=0)

    def after(self, value):
        if self.mark is not None:
            value = tie(value, self.mark)
        return value

    def chain(self, near, got):
        got = self.after(got)
        pass_on = add(self.half(near, 1 - self.row), self.half(got, 1 - self.row))
        keep = add(self.half(near, self.row), self.half(got, self.row))
        got = self.send(pass_on, self.to_y)
        yield pass_on
        got = self.after(got)
        keep = add(keep, got)
        pass_on = self.half(keep, 1 - self.layer)
        keep = self.half(keep, self.layer)
        got = self.send(pass_on, self.to_z)
        yield pass_on
        keep = add(keep, self.after(got))
        got = self.send(keep, self.to_zz)
        yield keep
        keep = add(keep, self.after(got))
        got = self.send(keep, self.to_z)
        yield keep
        keep = self.order(keep, self.after(got), self.layer)
        got = self.send(keep, self.to_y)
        yield keep
        yield self.order(keep, self.after(got), self.row).astype(F32)

    def chain_small(self, value):
        for pairs in (self.to_core, self.to_x, self.to_y, self.to_z, self.to_zz):
            got = self.send(value, pairs)
            yield value
            value = value + self.after(got)
        yield value

    def step(self, chain):
        self.mark = next(chain)
        return self.mark


def body(
    tokens,
    passage_lengths,
    cotangent,
    w_qkv,
    b_query,
    b_value,
    w_out,
    b_out,
    gain_one,
    shift_one,
    w_in,
    b_in,
    w_back,
    b_back,
    gain_two,
    shift_two,
):
    micro_count, own_rows, model = tokens.shape
    tp_count = lax.axis_size("tp")
    batch_count = lax.axis_size("batch")
    plen = own_rows * tp_count // passage_lengths.shape[1]
    own_passages = own_rows // plen
    assert own_passages * plen == own_rows and tp_count == 4
    grid = (batch_count, tp_count) == (8, 4)
    width = w_qkv.shape[2]
    rows = micro_count * own_rows
    position = lax.axis_index("tp")

    vector = lambda v: v.reshape(1, -1)
    x = tokens.reshape(rows, model)
    dy = cotangent.reshape(rows, model)
    lengths = lax.dynamic_slice_in_dim(
        passage_lengths, position * own_passages, own_passages, axis=1
    ).reshape(micro_count * own_passages)
    meta = jnp.concatenate([lengths, (position if grid else 0 * position).reshape(1)])
    qkvo = jnp.concatenate([jnp.transpose(w_qkv, (1, 2, 0)).reshape(3 * width, model), w_out], axis=0)
    small = vector(jnp.concatenate([b_in.astype(F32), b_query, jnp.zeros_like(b_query), b_value]))
    if grid:
        m = moves = GridMoves()
        x_att = m.send(m.half(qkvo, m.row), m.to_x)
        c_att = m.send(qkvo, m.to_core)
        c_small = m.send(small, m.to_core)
        x_small = m.send(small, m.to_x)
        att, smalls = [qkvo, c_att], [small, c_small]
    else:
        att, smalls, ins, backs = [
            list(lax.all_gather(v, "tp", axis=0)) for v in (qkvo, small, w_in, w_back)
        ]
    qkv_near, ctx_near, p_near, acc = attend_pair(x, plen, att[:2], smalls[:2], meta)
    y = x
    if grid:
        x_att = tie(x_att, acc)
        y_att = m.send(x_att, m.to_y)
        x_in = m.send(tie(m.half(w_in, m.row), x_att), m.to_x)
        c_in = m.send(tie(w_in, x_att), m.to_core)
        c_back = m.send(tie(w_back, x_att), m.to_core)
        smalls += [x_small, m.send(tie(x_small, x_att), m.to_core)]
        f_att = m.order(x_att, y_att, m.row)
        att += [f_att, m.send(f_att, m.to_core)]
        x_in = tie(x_in, f_att)
        y_in = m.send(x_in, m.to_y)
        x_back = m.send(tie(m.half(w_back, m.row), x_in), m.to_x)
        y = tie(x, x_in)
    qkv_far, ctx_far, p_far, unit, inverse, low = attend_pair(
        y, plen, att[2:], smalls[2:], meta, acc, [vector(v) for v in (b_out, gain_one, shift_one)]
    )
    if grid:
        y_in = tie(y_in, low)
        f_in = m.order(x_in, y_in, m.row)
        ins = [w_in, c_in, f_in, m.send(f_in, m.to_core)]
        x_back = tie(x_back, f_in)
        y_back = m.send(x_back, m.to_y)
        backs = [w_back, c_back]
        low = tie(low, x_back)
    act_near, slope_near, feed_near = feed_pair(low, ins[:2], backs[:2], smalls[:2])
    if grid:
        y_back = tie(y_back, feed_near)
        f_back = m.order(x_back, y_back, m.row)
        backs += [f_back, m.send(f_back, m.to_core)]
    layer_out, grad_two, grad_ffn, sums, slope_far, b_far, b_farc = turn_pair(
        low,
        ins[2:],
        backs[2:],
        smalls[2:],
        unit,
        feed_near,
        dy,
        meta,
        [vector(v) for v in (gain_one, shift_one, b_back, gain_two, shift_two)],
        plen,
    )
    if grid:
        got_b3 = m.send(b_farc, m.to_core)
    b_own, b_core = outer_pair(act_near, grad_ffn)
    if grid:
        got_b1 = m.send(b_core, m.to_core)
        b_far = add(b_far, tie(got_b3, b_own))
        got_bx = m.send(b_far, m.to_x)
        slope_far = tie(slope_far, b_far)
    i_far, i_farc, sums, normed = feed_back_pair(
        grad_ffn, slope_far, ins[2:], backs[2:], low, grad_two, 2, sums, meta
    )
    if grid:
        got_i3 = m.send(i_farc, m.to_core)
        b_near = add(b_own, tie(got_b1, normed))
        normed = tie(normed, b_near)
    i_own, i_core, sums, grad_one, grad_attn = feed_back_pair(
        grad_ffn,
        slope_near,
        ins[:2],
        backs[:2],
        low,
        normed,
        0,
        sums,
        meta,
        unit,
        inverse,
        vector(gain_one),
    )
    if grid:
        got_i1 = m.send(i_core, m.to_core)
        i_far = add(i_far, tie(got_i3, grad_attn))
        got_ix = m.send(i_far, m.to_x)
        m.mark = i_far
        chain_b = m.chain(b_near, got_bx)
        m.step(chain_b)
        grad_attn = tie(grad_attn, m.mark)
    a_far, a_farc, sums, grad_x = attend_back_pair(
        x, plen, grad_attn, qkv_far, ctx_far, p_far, att[2:], grad_one, 2, sums, meta
    )
    if grid:
        got_a3 = m.send(a_farc, m.to_core)
        i_near = add(i_own, tie(got_i1, grad_x))
        m.mark = i_near
        m.step(chain_b)
        a_far = add(a_far, m.after(got_a3))
        cut = a_far.shape[0] // 2
        got_ax = [m.send(part, m.to_x) for part in (a_far[:cut], a_far[cut:])]
        grad_x = tie(grad_x, a_far)
    a_own, a_core, packed, grad_x = attend_back_pair(
        x, plen, grad_attn, qkv_near, ctx_near, p_near, att[:2], grad_x, 0, sums, meta
    )
    if grid:
        got_a1 = m.send(a_core, m.to_core)
        m.mark = grad_x
        chains = {"s": moves.chain_small(packed), "b": chain_b, "i": moves.chain(i_near, got_ix)}
        done = {}
        for key in "sbi":
            done[key] = moves.step(chains[key])
        a_near = add(a_own, moves.after(got_a1))
        moves.mark = a_near
        chains["u"] = moves.chain(a_near[:cut], got_ax[0])
        chains["v"] = moves.chain(a_near[cut:], got_ax[1])
        for key in "sisubivsubivsbiuvsiuvuvuv":
            done[key] = moves.step(chains[key])
        g_back, g_in, packed = done["b"], done["i"], done["s"]
        g_att = jnp.concatenate([done["u"], done["v"]], axis=0)
    else:
        g_back, g_in, g_att = [
            lax.psum(
                lax.psum_scatter(jnp.stack(parts).astype(F32), "tp", scatter_dimension=0), "batch"
            )
            for parts in (
                (b_own, b_core, b_far, b_farc),
                (i_own, i_core, i_far, i_farc),
                (a_own, a_core, a_far, a_farc),
            )
        ]
        packed = lax.psum(packed, AXES)
    mine = lax.dynamic_slice_in_dim(packed, 2 * position, 2, axis=0)
    return (
        layer_out.reshape(tokens.shape),
        grad_x.reshape(tokens.shape),
        jnp.transpose(g_att[: 3 * width].reshape(3, width, model), (2, 0, 1)),
        mine[1, :width],
        mine[1, 2 * width : 3 * width],
        g_att[3 * width :],
        packed[11],
        packed[12],
        packed[13],
        g_in,
        mine[0],
        g_back,
        packed[10],
        packed[8],
        packed[9],
    )


def solution(mesh):
    in_specs = (
        P(None, ("batch", "tp"), None),
        P(None, "batch"),
        P(None, ("batch", "tp"), None),
        P(None, None, "tp"),
        P("tp"),
        P("tp"),
        P("tp", None),
        P(),
        P(),
        P(),
        P(None, "tp"),
        P("tp"),
        P("tp", None),
        P(),
        P(),
        P(),
    )
    out_specs = (
        P(None, ("batch", "tp"), None),
        P(None, ("batch", "tp"), None),
        P(None, None, "tp"),
        P("tp"),
        P("tp"),
        P("tp", None),
        P(),
        P(),
        P(),
        P(None, "tp"),
        P("tp"),
        P("tp", None),
        P(),
        P(),
        P(),
    )
    return jax.shard_map(body, mesh=mesh, in_specs=in_specs, out_specs=out_specs, check_vma=False)
```

```python
import math

import jax
import jax.numpy as jnp
from jax import lax
from jax.experimental import pallas as pl
from jax.experimental.pallas import tpu as pltpu
from jax.sharding import PartitionSpec as P

DH = 64
AXES = ("batch", "tp")
epsilon = 1e-05
F32 = jnp.float32
BF16 = jnp.bfloat16


def nt(a, b):
    return lax.dot_general(a, b, (((1,), (1,)), ((), ())), preferred_element_type=F32)


def tn(a, b):
    return lax.dot_general(a, b, (((0,), (0,)), ((), ())), preferred_element_type=F32)


def nn(a, b):
    return jnp.dot(a, b, preferred_element_type=F32)


HBM = pl.BlockSpec(memory_space=pl.ANY)
WHOLE = pl.BlockSpec(memory_space=pltpu.VMEM)
SCALARS = pl.BlockSpec(memory_space=pltpu.SMEM)


class Copies:
    def __init__(self, sems):
        self.sems, self.used = sems, 0
        self.pending = []

    def start(self, src, dst):
        copy = pltpu.make_async_copy(src, dst, self.sems.at[self.used])
        self.used += 1
        copy.start()
        return copy

    def out(self, src, dst):
        self.pending.append(self.start(src, dst))

    def drain(self):
        for copy in self.pending:
            copy.wait()


def call(kernel, name, inputs, outputs, scratch, copies, cost=200 * 10**9):
    in_specs = [spec for spec, _ in inputs]
    return pl.pallas_call(
        kernel,
        name=name,
        in_specs=in_specs,
        out_specs=tuple(spec for spec, _ in outputs),
        out_shape=tuple(shape for _, shape in outputs),
        scratch_shapes=list(scratch) + [pltpu.SemaphoreType.DMA((copies,))],
        cost_estimate=pl.CostEstimate(flops=cost, transcendentals=0, bytes_accessed=0),
    )(*[value for _, value in inputs])


def shape(dims, dtype):
    return jax.ShapeDtypeStruct(dims, dtype)


def block(i, size):
    return pl.ds(pl.multiple_of(i * size, size), size)


def unit_norm(v):
    middle = jnp.mean(v, axis=-1, keepdims=True)
    centred = v - middle
    inverse = lax.rsqrt(jnp.mean(centred * centred, axis=-1, keepdims=True) + epsilon)
    return centred * inverse, inverse


def norm_grad(scaled, unit, inverse):
    mean_one = jnp.mean(scaled, axis=-1, keepdims=True)
    mean_two = jnp.mean(scaled * unit, axis=-1, keepdims=True)
    return inverse * (scaled - mean_one - unit * mean_two)


STEP = 128


def row_of(part, meta_ref, kind):
    return 2 * jnp.bitwise_xor(part, meta_ref[meta_ref.shape[0] - 1]) + kind


def attend_pair(x, plen, w_pair, smalls, meta, acc=None, vectors=None):
    rows, model = x.shape
    passages = rows // plen
    width = w_pair[0].shape[0] // 4
    heads = width // DH
    units = smalls[0].shape[1] - 3 * width
    last = acc is not None

    def kernel(meta_ref, x_hbm, wa, wb, bias_a, bias_b, *rest):
        if last:
            acc_hbm, b_out, gain, shift = rest[:4]
            qkv_hbm, ctx_hbm, p_hbm, unit_hbm, inv_hbm, low_hbm = rest[4:10]
            x_s, w_s, qkv_s, ctx_s, p_s, acc_s, inv_s, low_s, sems = rest[10:]
        else:
            qkv_hbm, ctx_hbm, p_hbm, acc_out = rest[:4]
            x_s, w_s, qkv_s, ctx_s, p_s, acc_s, sems = rest[4:]
        copies = Copies(sems)
        first = [copies.start(x_hbm, x_s), copies.start(wa, w_s.at[0])]
        second = [copies.start(wb, w_s.at[1])]
        if last:
            first.append(copies.start(acc_hbm, acc_s))
        for j, waits, bias in ((0, first, bias_a), (1, second, bias_b)):
            for copy in waits:
                copy.wait()
            qkv_s[j] = (nt(x_s[...], w_s[j, : 3 * width, :]) + bias[0:1, units:]).astype(BF16)
            copies.out(qkv_s.at[j], qkv_hbm.at[j])

            def one(g, carry, j=j):
                at = block(g, plen)
                qkv = qkv_s[j, at, :]
                keep = lax.broadcasted_iota(jnp.int32, (1, plen), 1) < meta_ref[g]
                ctx = []
                for h in range(heads):
                    q = qkv[:, h * DH : (h + 1) * DH] * (1.0 / math.sqrt(DH))
                    k = qkv[:, width + h * DH : width + (h + 1) * DH]
                    v = qkv[:, 2 * width + h * DH : 2 * width + (h + 1) * DH]
                    s = jnp.where(keep, nt(q.astype(BF16), k), -1000000000.0)
                    e = jnp.exp(s - jnp.max(s, axis=-1, keepdims=True))
                    p = (e * (1.0 / jnp.sum(e, axis=-1, keepdims=True))).astype(BF16)
                    p_s[j, g * heads + h] = p
                    ctx.append(nn(p, v))
                ctx_s[j, at, :] = jnp.concatenate(ctx, axis=1).astype(BF16)
                return carry

            lax.fori_loop(0, passages, one, 0)
            copies.out(ctx_s.at[j], ctx_hbm.at[j])
            copies.out(p_s.at[j], p_hbm.at[j])
            term = nn(ctx_s[j], w_s[j, 3 * width :, :])
            acc_s[...] = term if j == 0 and not last else acc_s[...] + term
        if last:

            def finish(i, carry):
                at = block(i, STEP)
                v = x_s[at, :].astype(F32) + acc_s[at, :] + b_out[...]
                unit, inverse = unit_norm(v)
                acc_s[at, :] = unit
                inv_s[at, :] = jnp.broadcast_to(inverse, (STEP, 128))
                low_s[at, :] = (unit * gain[...] + shift[...]).astype(BF16)
                return carry

            lax.fori_loop(0, rows // STEP, finish, 0)
            copies.out(acc_s, unit_hbm)
            copies.out(inv_s, inv_hbm)
            copies.out(low_s, low_hbm)
        else:
            copies.out(acc_s, acc_out)
        copies.drain()

    inputs = [(SCALARS, meta), (HBM, x), (HBM, w_pair[0]), (HBM, w_pair[1])]
    inputs += [(WHOLE, v) for v in smalls]
    dims = [(2, rows, 3 * width), (2, rows, width), (2, passages * heads, plen, plen)]
    outputs = [(HBM, shape(d, BF16)) for d in dims]
    scratch = [pltpu.VMEM((rows, model), BF16), pltpu.VMEM((2, 4 * width, model), BF16)]
    scratch += [pltpu.VMEM(d, BF16) for d in dims]
    scratch += [pltpu.VMEM((rows, model), F32)]
    if last:
        inputs += [(HBM, acc)] + [(WHOLE, v) for v in vectors]
        outputs += [(HBM, shape((rows, model), F32)), (HBM, shape((rows, 128), F32))]
        outputs += [(HBM, shape((rows, model), BF16))]
        scratch += [pltpu.VMEM((rows, 128), F32), pltpu.VMEM((rows, model), BF16)]
    else:
        outputs += [(HBM, shape((rows, model), F32))]
    return call(kernel, "attend_pair", inputs, outputs, scratch, 16)


def feed(j, low_s, i_s, b_s, bias, act_s, slope_s):
    units = act_s.shape[2]
    for c in range(0, units, 256):
        cols = slice(c, c + 256)
        t = nn(low_s[...], i_s[j, :, cols]) + bias[0:1, cols]
        cdf = 0.5 * (1.0 + lax.erf(t * (1.0 / math.sqrt(2.0))))
        pdf = jnp.exp(-0.5 * t * t) * (1.0 / math.sqrt(2.0 * math.pi))
        act_s[j, :, cols] = (t * cdf).astype(BF16)
        slope_s[j, :, cols] = (cdf + t * pdf).astype(BF16)
    return nn(act_s[j], b_s[j])


def feed_pair(low, in_pair, back_pair, smalls):
    rows, model = low.shape
    units = in_pair[0].shape[1]

    def kernel(low_hbm, ia, ib, ba, bb, bias_a, bias_b, *rest):
        act_hbm, slope_hbm, acc_hbm, low_s, i_s, b_s, act_s, slope_s, acc_s, sems = rest
        copies = Copies(sems)
        first = [copies.start(low_hbm, low_s), copies.start(ia, i_s.at[0]), copies.start(ba, b_s.at[0])]
        second = [copies.start(ib, i_s.at[1]), copies.start(bb, b_s.at[1])]
        for j, waits, bias in ((0, first, bias_a), (1, second, bias_b)):
            for copy in waits:
                copy.wait()
            term = feed(j, low_s, i_s, b_s, bias, act_s, slope_s)
            copies.out(act_s.at[j], act_hbm.at[j])
            copies.out(slope_s.at[j], slope_hbm.at[j])
            acc_s[...] = acc_s[...] + term if j else term
        copies.out(acc_s, acc_hbm)
        copies.drain()

    inputs = [(HBM, v) for v in (low, *in_pair, *back_pair)] + [(WHOLE, v) for v in smalls]
    outputs = [(HBM, shape((2, rows, units), BF16))] * 2 + [(HBM, shape((rows, model), F32))]
    scratch = [pltpu.VMEM((rows, model), BF16), pltpu.VMEM((2, model, units), BF16)]
    scratch += [pltpu.VMEM((2, units, model), BF16)] + [pltpu.VMEM((2, rows, units), BF16)] * 2
    scratch += [pltpu.VMEM((rows, model), F32)]
    return call(kernel, "feed_pair", inputs, outputs, scratch, 12)


def turn_pair(low, in_pair, back_pair, smalls, unit, acc, dy, meta, vectors, plen):
    rows, model = low.shape
    units = in_pair[0].shape[1]

    def kernel(meta_ref, low_hbm, ia, ib, ba, bb, unit_hbm, acc_hbm, dy_hbm, bias_a, bias_b, *rest):
        gain_one, shift_one, b_back, gain_two, shift_two = rest[:5]
        out_hbm, grad_hbm, ffn_hbm, sum_ref, slope_hbm, oa, ob = rest[5:12]
        low_s, i_s, b_s, act_s, slope_s, acc_s, unit_s, dy_s, out_s, grad_s, ffn_s, g_s, sems = rest[12:]
        copies = Copies(sems)
        first = [copies.start(low_hbm, low_s), copies.start(ia, i_s.at[0]), copies.start(ba, b_s.at[0])]
        second = [copies.start(ib, i_s.at[1]), copies.start(bb, b_s.at[1]), copies.start(acc_hbm, acc_s)]
        third = [copies.start(unit_hbm, unit_s), copies.start(dy_hbm, dy_s)]
        for copy in first:
            copy.wait()
        term = feed(0, low_s, i_s, b_s, bias_a, act_s, slope_s)
        copies.out(slope_s.at[0], slope_hbm.at[0])
        for copy in second:
            copy.wait()
        acc_s[...] = acc_s[...] + term
        acc_s[...] = acc_s[...] + feed(1, low_s, i_s, b_s, bias_b, act_s, slope_s)
        copies.out(slope_s.at[1], slope_hbm.at[1])
        for copy in third:
            copy.wait()
        sum_ref[...] = jnp.zeros_like(sum_ref)

        def step(i, carry):
            at = block(i, STEP)
            normed = unit_s[at, :] * gain_one[...] + shift_one[...]
            u, inverse = unit_norm(normed + acc_s[at, :] + b_back[...])
            out_s[at, :] = (u * gain_two[...] + shift_two[...]).astype(BF16)
            slot = lax.broadcasted_iota(jnp.int32, (STEP, 1), 0) + (i * STEP) % plen
            keep = slot < meta_ref[(i * STEP) // plen]
            grad_y = jnp.where(keep, dy_s[at, :].astype(F32), 0.0)
            grad = norm_grad(grad_y * gain_two[...], u, inverse)
            grad_s[at, :] = grad
            ffn_s[at, :] = grad.astype(BF16)
            sum_ref[8:9, :] += jnp.sum(grad_y * u, axis=0, keepdims=True)
            sum_ref[9:10, :] += jnp.sum(grad_y, axis=0, keepdims=True)
            sum_ref[10:11, :] += jnp.sum(grad, axis=0, keepdims=True)
            return carry

        lax.fori_loop(0, rows // STEP, step, 0)
        copies.out(out_s, out_hbm)
        copies.out(grad_s, grad_hbm)
        copies.out(ffn_s, ffn_hbm)
        for j, out in ((1, ob), (0, oa)):
            g_s[j] = tn(act_s[j], ffn_s[...]).astype(BF16)
            copies.out(g_s.at[j], out)
        copies.drain()

    inputs = [(SCALARS, meta)] + [(HBM, v) for v in (low, *in_pair, *back_pair, unit, acc, dy)]
    inputs += [(WHOLE, v) for v in (*smalls, *vectors)]
    outputs = [(HBM, shape((rows, model), d)) for d in (BF16, F32, BF16)]
    outputs += [(WHOLE, shape((16, model), F32)), (HBM, shape((2, rows, units), BF16))]
    outputs += [(HBM, shape((units, model), BF16))] * 2
    scratch = [pltpu.VMEM((rows, model), BF16), pltpu.VMEM((2, model, units), BF16)]
    scratch += [pltpu.VMEM((2, units, model), BF16)] + [pltpu.VMEM((2, rows, units), BF16)] * 2
    scratch += [pltpu.VMEM((rows, model), d) for d in (F32, F32, BF16, BF16, F32, BF16)]
    scratch += [pltpu.VMEM((2, units, model), BF16)]
    return call(kernel, "turn_pair", inputs, outputs, scratch, 20)


def outer_pair(acts, grad_ffn):
    _, rows, units = acts.shape
    model = grad_ffn.shape[1]

    def kernel(act_hbm, g_hbm, oa, ob, act_s, g_s, out_s, sems):
        copies = Copies(sems)
        whole = copies.start(g_hbm, g_s)
        waits = [copies.start(act_hbm.at[j], act_s.at[j]) for j in (1, 0)]
        whole.wait()
        for j, wait, out in ((1, waits[0], ob), (0, waits[1], oa)):
            wait.wait()
            out_s[j] = tn(act_s[j], g_s[...]).astype(BF16)
            copies.out(out_s.at[j], out)
        copies.drain()

    inputs = [(HBM, acts), (HBM, grad_ffn)]
    outputs = [(HBM, shape((units, model), BF16))] * 2
    scratch = [pltpu.VMEM((2, rows, units), BF16), pltpu.VMEM((rows, model), BF16)]
    scratch += [pltpu.VMEM((2, units, model), BF16)]
    return call(kernel, "outer_pair", inputs, outputs, scratch, 8)


def feed_back_pair(grad_ffn, slopes, in_pair, back_pair, low, start, part, sums, meta, unit=None, inverse=None, gain=None):
    rows, model = grad_ffn.shape
    units = slopes.shape[2]
    last = unit is not None

    def kernel(meta_ref, before, g_hbm, slope_hbm, ia, ib, ba, bb, low_hbm, start_hbm, *rest):
        if last:
            unit_hbm, inv_hbm, gain_ref = rest[:3]
            rest = rest[3:]
            oa, ob, sum_ref, one_hbm, attn_hbm = rest[:5]
            g_s, slope_s, i_s, b_s, low_s, acc_s, pre_s, out_s, line, unit_s, inv_s, attn_s, sems = rest[5:]
        else:
            oa, ob, sum_ref, acc_out = rest[:4]
            g_s, slope_s, i_s, b_s, low_s, acc_s, pre_s, out_s, line, sems = rest[4:]
        copies = Copies(sems)
        sum_ref[...] = before[...]
        weights = {1: (bb, ib), 0: (ba, ia)}
        early = copies.start(g_hbm, g_s)
        waits = {}
        for j in (1, 0):
            waits[j] = [copies.start(weights[j][0], b_s.at[j]), copies.start(slope_hbm.at[j], slope_s.at[j])]
            waits[j].append(copies.start(weights[j][1], i_s.at[j]))
            if j == 1:
                waits[j] += [copies.start(start_hbm, acc_s), copies.start(low_hbm, low_s)]
        if last:
            late = [copies.start(unit_hbm, unit_s), copies.start(inv_hbm, inv_s)]
        early.wait()
        for j, out in ((1, ob), (0, oa)):
            for wait in waits[j]:
                wait.wait()
            for c in range(0, units, 256):
                cols = slice(c, c + 256)
                pre = nt(g_s[...], b_s[j, cols, :]) * slope_s[j, :, cols].astype(F32)
                pre = pre.astype(BF16)
                pre_s[:, cols] = pre
                line[:, cols] = jnp.sum(pre.astype(F32), axis=0, keepdims=True)
            sum_ref[pl.ds(row_of(part + j, meta_ref, 0), 1), :] = line[...]
            acc_s[...] = acc_s[...] + nt(pre_s[...], i_s[j])
            out_s[j] = tn(low_s[...], pre_s[...]).astype(BF16)
            copies.out(out_s.at[j], out)
        if last:
            for wait in late:
                wait.wait()

            def finish(i, carry):
                at = block(i, STEP)
                normed = acc_s[at, :]
                u = unit_s[at, :]
                grad = norm_grad(normed * gain_ref[0:1, :], u, inv_s[at, 0:1])
                sum_ref[11:12, :] += jnp.sum(grad, axis=0, keepdims=True)
                sum_ref[12:13, :] += jnp.sum(normed * u, axis=0, keepdims=True)
                sum_ref[13:14, :] += jnp.sum(normed, axis=0, keepdims=True)
                acc_s[at, :] = grad
                attn_s[at, :] = grad.astype(BF16)
                return carry

            lax.fori_loop(0, rows // STEP, finish, 0)
            copies.out(acc_s, one_hbm)
            copies.out(attn_s, attn_hbm)
        else:
            copies.out(acc_s, acc_out)
        copies.drain()

    inputs = [(SCALARS, meta), (WHOLE, sums)]
    inputs += [(HBM, v) for v in (grad_ffn, slopes, *in_pair, *back_pair, low, start)]
    outputs = [(HBM, shape((model, units), BF16))] * 2 + [(WHOLE, shape((16, model), F32))]
    outputs += [(HBM, shape((rows, model), F32))]
    scratch = [pltpu.VMEM((rows, model), BF16), pltpu.VMEM((2, rows, units), BF16)]
    scratch += [pltpu.VMEM((2, model, units), BF16), pltpu.VMEM((2, units, model), BF16)]
    scratch += [pltpu.VMEM((rows, model), BF16), pltpu.VMEM((rows, model), F32)]
    scratch += [pltpu.VMEM((rows, units), BF16), pltpu.VMEM((2, model, units), BF16)]
    scratch += [pltpu.VMEM((1, units), F32)]
    if last:
        inputs += [(HBM, unit), (HBM, inverse), (WHOLE, gain)]
        outputs += [(HBM, shape((rows, model), BF16))]
        scratch += [pltpu.VMEM((rows, model), F32), pltpu.VMEM((rows, 128), F32)]
        scratch += [pltpu.VMEM((rows, model), BF16)]
    return call(kernel, "feed_back_pair", inputs, outputs, scratch, 20)


def attend_back_pair(x, plen, grad_attn, qkvs, ctxs, probs, w_pair, start, part, sums, meta):
    rows, model = x.shape
    passages = rows // plen
    width = ctxs.shape[2]
    heads = width // DH

    def kernel(meta_ref, before, x_hbm, g_hbm, qkv_hbm, ctx_hbm, p_hbm, wa, wb, start_hbm, *rest):
        oa, ob, sum_ref, acc_out = rest[:4]
        x_s, g_s, qkv_s, ctx_s, p_s, w_s, acc_s, grow_s, out_s, gc_s, sems = rest[4:]
        copies = Copies(sems)
        sum_ref[...] = before[...]
        early = [copies.start(g_hbm, g_s)]
        w_of = {0: wa, 1: wb}
        waits = {}
        for j in (1, 0):
            waits[j] = [copies.start(w_of[j], w_s.at[j]), copies.start(ctx_hbm.at[j], ctx_s.at[j])]
            waits[j] += [copies.start(qkv_hbm.at[j], qkv_s.at[j]), copies.start(p_hbm.at[j], p_s.at[j])]
            if j == 1:
                waits[j] += [copies.start(start_hbm, acc_s), copies.start(x_hbm, x_s)]
        for wait in early:
            wait.wait()
        for j, out in ((1, ob), (0, oa)):
            for wait in waits[j]:
                wait.wait()
            gc_s[...] = nt(g_s[...], w_s[j, 3 * width :, :]).astype(BF16)
            out_s[j, 3 * width :, :] = tn(ctx_s[j], g_s[...]).astype(BF16)

            def one(g, carry, j=j):
                at = block(g, plen)
                qkv = qkv_s[j, at, :]
                grad_ctx = gc_s[at, :]
                gq, gk, gv = [], [], []
                for h in range(heads):
                    q = qkv[:, h * DH : (h + 1) * DH]
                    k = qkv[:, width + h * DH : width + (h + 1) * DH]
                    v = qkv[:, 2 * width + h * DH : 2 * width + (h + 1) * DH]
                    gc = grad_ctx[:, h * DH : (h + 1) * DH]
                    low = p_s[j, g * heads + h]
                    p = low.astype(F32)
                    gp = nt(gc, v)
                    delta = jnp.sum(p * gp, axis=-1, keepdims=True)
                    gs = (p * (gp - delta)).astype(BF16)
                    gq.append(nn(gs, k) * (1.0 / math.sqrt(DH)))
                    gk.append(tn(gs, q) * (1.0 / math.sqrt(DH)))
                    gv.append(tn(low, gc))
                grow = jnp.concatenate(gq + gk + gv, axis=1).astype(BF16)
                grow_s[at, :] = grow
                return carry + jnp.sum(grow.astype(F32), axis=0, keepdims=True)

            line = lax.fori_loop(0, passages, one, jnp.zeros((1, 3 * width), F32))
            line = jnp.concatenate([line, jnp.zeros((1, model - 3 * width), F32)], axis=1)
            sum_ref[pl.ds(row_of(part + j, meta_ref, 1), 1), :] = line
            out_s[j, : 3 * width, :] = tn(grow_s[...], x_s[...]).astype(BF16)
            copies.out(out_s.at[j], out)
            acc_s[...] = acc_s[...] + nn(grow_s[...], w_s[j, : 3 * width, :])
        copies.out(acc_s, acc_out)
        copies.drain()

    inputs = [(SCALARS, meta), (WHOLE, sums)]
    inputs += [(HBM, v) for v in (x, grad_attn, qkvs, ctxs, probs, *w_pair, start)]
    outputs = [(HBM, shape((4 * width, model), BF16))] * 2
    outputs += [(WHOLE, shape((16, model), F32)), (HBM, shape((rows, model), F32))]
    scratch = [pltpu.VMEM((rows, model), BF16), pltpu.VMEM((rows, model), BF16)]
    scratch += [pltpu.VMEM(v.shape, BF16) for v in (qkvs, ctxs, probs)]
    scratch += [pltpu.VMEM((2, 4 * width, model), BF16), pltpu.VMEM((rows, model), F32)]
    scratch += [pltpu.VMEM((rows, 3 * width), BF16), pltpu.VMEM((2, 4 * width, model), BF16)]
    scratch += [pltpu.VMEM((rows, width), BF16)]
    return call(kernel, "attend_back_pair", inputs, outputs, scratch, 20)


def tie(value, *others):
    return lax.optimization_barrier((value, *others))[0]


def flat_perm(move):
    pairs = []
    for z in range(4):
        for y in range(2):
            for x in range(2):
                for c in range(2):
                    z2, y2, x2, c2 = move(z, y, x, c)
                    pairs.append((((z * 2 + y) * 2 + x) * 2 + c, ((z2 * 2 + y2) * 2 + x2) * 2 + c2))
    return pairs


def add(one, two):
    return (one.astype(F32) + two.astype(F32)).astype(BF16)


ORDER = "vsbisuvibsuvibsuvisuvuviuv"


class GridMoves:
    def __init__(self):
        self.row = lax.axis_index("batch") % 2
        self.layer = lax.axis_index("batch") // 2 % 2
        self.to_core = flat_perm(lambda z, y, x, c: (z, y, x, 1 - c))
        self.to_x = flat_perm(lambda z, y, x, c: (z, y, 1 - x, c))
        self.to_y = flat_perm(lambda z, y, x, c: (z, 1 - y, x, c))
        self.to_z = flat_perm(lambda z, y, x, c: (z ^ 1, y, x, c))
        self.to_zz = flat_perm(lambda z, y, x, c: (z ^ 2, y, x, c))
        self.mark = None

    def send(self, value, pairs):
        return lax.ppermute(value, AXES, pairs)

    def half(self, value, which):
        if isinstance(value, tuple):
            return jnp.where(which == 0, value[0], value[1])
        rows = value.shape[0] // 2
        return lax.dynamic_slice_in_dim(value, which * rows, rows, axis=0)

    def order(self, mine, other, bit):
        low = jnp.where(bit == 0, mine, other)
        high = jnp.where(bit == 0, other, mine)
        return jnp.concatenate([low, high], axis=0)

    def after(self, value):
        if self.mark is not None:
            value = tie(value, self.mark)
        return value

    def halves(self, value):
        rows = value.shape[0] // 2
        return value[:rows], value[rows:]

    def chain(self, near, got):
        got = tuple(self.after(part) for part in got)
        got = got if len(got) == 2 else got[0]
        pass_on = add(self.half(near, 1 - self.row), self.half(got, 1 - self.row))
        keep = add(self.half(near, self.row), self.half(got, self.row))
        got = self.send(pass_on, self.to_y)
        yield pass_on
        yield from self.chain_z(add(keep, self.after(got)))

    def chain_y(self, near, far):
        pass_on = jnp.concatenate(
            [self.half(near, 1 - self.row), self.half(far, 1 - self.row)], axis=0
        )
        got = self.send(pass_on, self.to_y)
        yield pass_on
        got = self.halves(self.after(got))
        far = add(self.half(far, self.row), got[1])
        keep = add(self.half(near, self.row), got[0])
        got = self.send(far, self.to_x)
        yield far
        yield from self.chain_z(add(keep, self.after(got)))

    def chain_z(self, keep):
        pass_on = self.half(keep, 1 - self.layer)
        keep = self.half(keep, self.layer)
        got = self.send(pass_on, self.to_z)
        yield pass_on
        keep = add(keep, self.after(got))
        got = self.send(keep, self.to_zz)
        yield keep
        keep = add(keep, self.after(got))
        got = self.send(keep, self.to_z)
        yield keep
        keep = self.order(keep, self.after(got), self.layer)
        got = self.send(keep, self.to_y)
        yield keep
        yield self.order(keep, self.after(got), self.row).astype(F32)

    def chain_small(self, value):
        for pairs in (self.to_core, self.to_x, self.to_y, self.to_z, self.to_zz):
            got = self.send(value, pairs)
            yield value
            value = value + self.after(got)
        yield value

    def step(self, chain):
        self.mark = next(chain)
        return self.mark


def body(
    tokens,
    passage_lengths,
    cotangent,
    w_qkv,
    b_query,
    b_value,
    w_out,
    b_out,
    gain_one,
    shift_one,
    w_in,
    b_in,
    w_back,
    b_back,
    gain_two,
    shift_two,
):
    micro_count, own_rows, model = tokens.shape
    tp_count = lax.axis_size("tp")
    batch_count = lax.axis_size("batch")
    plen = own_rows * tp_count // passage_lengths.shape[1]
    own_passages = own_rows // plen
    assert own_passages * plen == own_rows and tp_count == 4
    grid = (batch_count, tp_count) == (8, 4)
    width = w_qkv.shape[2]
    rows = micro_count * own_rows
    position = lax.axis_index("tp")

    vector = lambda v: v.reshape(1, -1)
    x = tokens.reshape(rows, model)
    dy = cotangent.reshape(rows, model)
    lengths = lax.dynamic_slice_in_dim(
        passage_lengths, position * own_passages, own_passages, axis=1
    ).reshape(micro_count * own_passages)
    meta = jnp.concatenate([lengths, (position if grid else 0 * position).reshape(1)])
    qkvo = jnp.concatenate([jnp.transpose(w_qkv, (1, 2, 0)).reshape(3 * width, model), w_out], axis=0)
    small = vector(jnp.concatenate([b_in.astype(F32), b_query, jnp.zeros_like(b_query), b_value]))
    if grid:
        m = moves = GridMoves()
        x_att = m.send(m.half(qkvo, m.row), m.to_x)
        c_att = m.send(qkvo, m.to_core)
        c_small = m.send(small, m.to_core)
        x_small = m.send(small, m.to_x)
        att, smalls = [qkvo, c_att], [small, c_small]
    else:
        att, smalls, ins, backs = [
            list(lax.all_gather(v, "tp", axis=0)) for v in (qkvo, small, w_in, w_back)
        ]
    qkv_near, ctx_near, p_near, acc = attend_pair(x, plen, att[:2], smalls[:2], meta)
    y = x
    if grid:
        x_att = tie(x_att, acc)
        y_att = m.send(x_att, m.to_y)
        x_in = m.send(tie(m.half(w_in, m.row), x_att), m.to_x)
        c_in = m.send(tie(w_in, x_att), m.to_core)
        c_back = m.send(tie(w_back, x_att), m.to_core)
        smalls += [x_small, m.send(tie(x_small, x_att), m.to_core)]
        f_att = m.order(x_att, y_att, m.row)
        att += [f_att, m.send(f_att, m.to_core)]
        x_in = tie(x_in, f_att)
        y_in = m.send(x_in, m.to_y)
        x_back = m.send(tie(m.half(w_back, m.row), x_in), m.to_x)
        y = tie(x, x_in)
    qkv_far, ctx_far, p_far, unit, inverse, low = attend_pair(
        y, plen, att[2:], smalls[2:], meta, acc, [vector(v) for v in (b_out, gain_one, shift_one)]
    )
    if grid:
        y_in = tie(y_in, low)
        f_in = m.order(x_in, y_in, m.row)
        ins = [w_in, c_in, f_in, m.send(f_in, m.to_core)]
        x_back = tie(x_back, f_in)
        y_back = m.send(x_back, m.to_y)
        backs = [w_back, c_back]
        low = tie(low, x_back)
    act_near, slope_near, feed_near = feed_pair(low, ins[:2], backs[:2], smalls[:2])
    if grid:
        y_back = tie(y_back, feed_near)
        f_back = m.order(x_back, y_back, m.row)
        backs += [f_back, m.send(f_back, m.to_core)]
    layer_out, grad_two, grad_ffn, sums, slope_far, b_far, b_farc = turn_pair(
        low,
        ins[2:],
        backs[2:],
        smalls[2:],
        unit,
        feed_near,
        dy,
        meta,
        [vector(v) for v in (gain_one, shift_one, b_back, gain_two, shift_two)],
        plen,
    )
    if grid:
        got_b3 = m.send(b_farc, m.to_core)
    b_own, b_core = outer_pair(act_near, grad_ffn)
    if grid:
        got_b1 = m.send(b_core, m.to_core)
        b_far = add(b_far, tie(got_b3, b_own))
        got_bx = [m.send(part, m.to_x) for part in m.halves(b_far)]
        slope_far = tie(slope_far, b_far)
    i_far, i_farc, sums, normed = feed_back_pair(
        grad_ffn, slope_far, ins[2:], backs[2:], low, grad_two, 2, sums, meta
    )
    if grid:
        got_i3 = m.send(i_farc, m.to_core)
        b_near = add(b_own, tie(got_b1, normed))
        got_bx[0] = tie(got_bx[0], b_near)
        normed = tie(normed, got_bx[0])
    i_own, i_core, sums, grad_one, grad_attn = feed_back_pair(
        grad_ffn,
        slope_near,
        ins[:2],
        backs[:2],
        low,
        normed,
        0,
        sums,
        meta,
        unit,
        inverse,
        vector(gain_one),
    )
    if grid:
        got_i1 = m.send(i_core, m.to_core)
        i_far = add(i_far, tie(got_i3, grad_attn))
        got_ix = [m.send(part, m.to_x) for part in m.halves(i_far)]
        m.mark = i_far
        chain_b = m.chain(b_near, got_bx)
        m.step(chain_b)
        grad_attn = tie(grad_attn, m.mark)
    a_far, a_farc, sums, grad_x = attend_back_pair(
        x, plen, grad_attn, qkv_far, ctx_far, p_far, att[2:], grad_one, 2, sums, meta
    )
    if grid:
        got_a3 = m.send(a_farc, m.to_core)
        i_near = add(i_own, tie(got_i1, grad_x))
        m.mark = i_near
        m.step(chain_b)
        got_ix[0] = m.after(got_ix[0])
        grad_x = tie(grad_x, got_ix[0])
    a_own, a_core, packed, grad_x = attend_back_pair(
        x, plen, grad_attn, qkv_near, ctx_near, p_near, att[:2], grad_x, 0, sums, meta
    )
    if grid:
        got_a1 = m.send(a_core, m.to_core)
        m.mark = grad_x
        a_far = m.halves(add(a_far, m.after(got_a3)))
        got_ax = m.send(a_far[0], m.to_x)
        m.mark = a_far[0]
        chains = {"s": m.chain_small(packed), "b": chain_b, "i": m.chain(i_near, got_ix)}
        done = {}
        for key in "ibs":
            done[key] = m.step(chains[key])
        a_near = m.halves(add(a_own, m.after(got_a1)))
        m.mark = a_near[0]
        chains["v"] = m.chain_y(a_near[1], a_far[1])
        chains["u"] = m.chain(a_near[0], [got_ax])
        for key in ORDER:
            done[key] = m.step(chains[key])
        g_back, g_in, packed = done["b"], done["i"], done["s"]
        g_att = jnp.concatenate([done["u"], done["v"]], axis=0)
    else:
        g_back, g_in, g_att = [
            lax.psum(
                lax.psum_scatter(jnp.stack(parts).astype(F32), "tp", scatter_dimension=0), "batch"
            )
            for parts in (
                (b_own, b_core, b_far, b_farc),
                (i_own, i_core, i_far, i_farc),
                (a_own, a_core, a_far, a_farc),
            )
        ]
        packed = lax.psum(packed, AXES)
    mine = lax.dynamic_slice_in_dim(packed, 2 * position, 2, axis=0)
    return (
        layer_out.reshape(tokens.shape),
        grad_x.reshape(tokens.shape),
        jnp.transpose(g_att[: 3 * width].reshape(3, width, model), (2, 0, 1)),
        mine[1, :width],
        mine[1, 2 * width : 3 * width],
        g_att[3 * width :],
        packed[11],
        packed[12],
        packed[13],
        g_in,
        mine[0],
        g_back,
        packed[10],
        packed[8],
        packed[9],
    )


def solution(mesh):
    in_specs = (
        P(None, ("batch", "tp"), None),
        P(None, "batch"),
        P(None, ("batch", "tp"), None),
        P(None, None, "tp"),
        P("tp"),
        P("tp"),
        P("tp", None),
        P(),
        P(),
        P(),
        P(None, "tp"),
        P("tp"),
        P("tp", None),
        P(),
        P(),
        P(),
    )
    out_specs = (
        P(None, ("batch", "tp"), None),
        P(None, ("batch", "tp"), None),
        P(None, None, "tp"),
        P("tp"),
        P("tp"),
        P("tp", None),
        P(),
        P(),
        P(),
        P(None, "tp"),
        P("tp"),
        P("tp", None),
        P(),
        P(),
        P(),
    )
    return jax.shard_map(body, mesh=mesh, in_specs=in_specs, out_specs=out_specs, check_vma=False)
```

```python
import math

import jax
import jax.numpy as jnp
from jax import lax
from jax.experimental import pallas as pl
from jax.experimental.pallas import tpu as pltpu
from jax.sharding import PartitionSpec as P

DH = 64
AXES = ("batch", "tp")
epsilon = 1e-05
F32 = jnp.float32
BF16 = jnp.bfloat16


def nt(a, b):
    return lax.dot_general(a, b, (((1,), (1,)), ((), ())), preferred_element_type=F32)


def tn(a, b):
    return lax.dot_general(a, b, (((0,), (0,)), ((), ())), preferred_element_type=F32)


def nn(a, b):
    return jnp.dot(a, b, preferred_element_type=F32)


HBM = pl.BlockSpec(memory_space=pl.ANY)
WHOLE = pl.BlockSpec(memory_space=pltpu.VMEM)
SCALARS = pl.BlockSpec(memory_space=pltpu.SMEM)


class Copies:
    def __init__(self, sems):
        self.sems, self.used = sems, 0
        self.pending = []

    def start(self, src, dst):
        copy = pltpu.make_async_copy(src, dst, self.sems.at[self.used])
        self.used += 1
        copy.start()
        return copy

    def out(self, src, dst):
        self.pending.append(self.start(src, dst))

    def drain(self):
        for copy in self.pending:
            copy.wait()


def call(kernel, name, inputs, outputs, scratch, copies, cost=1000):
    in_specs = [spec for spec, _ in inputs]
    return pl.pallas_call(
        kernel,
        name=name,
        in_specs=in_specs,
        out_specs=tuple(spec for spec, _ in outputs),
        out_shape=tuple(shape for _, shape in outputs),
        scratch_shapes=list(scratch) + [pltpu.SemaphoreType.DMA((copies,))],
        cost_estimate=pl.CostEstimate(flops=cost, transcendentals=0, bytes_accessed=0),
    )(*[value for _, value in inputs])


def shape(dims, dtype):
    return jax.ShapeDtypeStruct(dims, dtype)


def block(i, size):
    return pl.ds(pl.multiple_of(i * size, size), size)


def unit_norm(v):
    middle = jnp.mean(v, axis=-1, keepdims=True)
    centred = v - middle
    inverse = lax.rsqrt(jnp.mean(centred * centred, axis=-1, keepdims=True) + epsilon)
    return centred * inverse, inverse


def norm_grad(scaled, unit, inverse):
    mean_one = jnp.mean(scaled, axis=-1, keepdims=True)
    mean_two = jnp.mean(scaled * unit, axis=-1, keepdims=True)
    return inverse * (scaled - mean_one - unit * mean_two)


STEP = 128


def row_of(part, meta_ref, kind):
    return 2 * jnp.bitwise_xor(part, meta_ref[meta_ref.shape[0] - 1]) + kind


def attend_pair(x, plen, w_pair, smalls, meta, acc=None, vectors=None):
    rows, model = x.shape
    passages = rows // plen
    width = w_pair[0].shape[0] // 4
    heads = width // DH
    units = smalls[0].shape[1] - 3 * width
    last = acc is not None

    def kernel(meta_ref, x_hbm, wa, wb, bias_a, bias_b, *rest):
        if last:
            acc_hbm, b_out, gain, shift = rest[:4]
            qkv_hbm, ctx_hbm, p_hbm, unit_hbm, inv_hbm, low_hbm = rest[4:10]
            x_s, w_s, qkv_s, ctx_s, p_s, acc_s, inv_s, low_s, sems = rest[10:]
        else:
            qkv_hbm, ctx_hbm, p_hbm, acc_out = rest[:4]
            x_s, w_s, qkv_s, ctx_s, p_s, acc_s, sems = rest[4:]
        copies = Copies(sems)
        first = [copies.start(x_hbm, x_s), copies.start(wa, w_s.at[0])]
        second = [copies.start(wb, w_s.at[1])]
        if last:
            held = copies.start(acc_hbm, acc_s)
        for j, waits, bias in ((0, first, bias_a), (1, second, bias_b)):
            for copy in waits:
                copy.wait()
            qkv_s[j] = (nt(x_s[...], w_s[j, : 3 * width, :]) + bias[0:1, units:]).astype(BF16)
            copies.out(qkv_s.at[j], qkv_hbm.at[j])

            def one(g, carry, j=j):
                at = block(g, plen)
                qkv = qkv_s[j, at, :]
                keep = lax.broadcasted_iota(jnp.int32, (1, plen), 1) < meta_ref[g]
                ctx = []
                for h in range(heads):
                    q = qkv[:, h * DH : (h + 1) * DH] * (1.0 / math.sqrt(DH))
                    k = qkv[:, width + h * DH : width + (h + 1) * DH]
                    v = qkv[:, 2 * width + h * DH : 2 * width + (h + 1) * DH]
                    s = jnp.where(keep, nt(q.astype(BF16), k), -1000000000.0)
                    e = jnp.exp(s - jnp.max(s, axis=-1, keepdims=True))
                    p = (e * (1.0 / jnp.sum(e, axis=-1, keepdims=True))).astype(BF16)
                    p_s[j, g * heads + h] = p
                    ctx.append(nn(p, v))
                ctx_s[j, at, :] = jnp.concatenate(ctx, axis=1).astype(BF16)
                return carry

            lax.fori_loop(0, passages, one, 0)
            copies.out(ctx_s.at[j], ctx_hbm.at[j])
            copies.out(p_s.at[j], p_hbm.at[j])
            term = nn(ctx_s[j], w_s[j, 3 * width :, :])
            if last and j == 0:
                held.wait()
            acc_s[...] = term if j == 0 and not last else acc_s[...] + term
        if last:

            def finish(i, carry):
                at = block(i, STEP)
                v = x_s[at, :].astype(F32) + acc_s[at, :] + b_out[...]
                unit, inverse = unit_norm(v)
                acc_s[at, :] = unit
                inv_s[at, :] = jnp.broadcast_to(inverse, (STEP, 128))
                low_s[at, :] = (unit * gain[...] + shift[...]).astype(BF16)
                return carry

            lax.fori_loop(0, rows // STEP, finish, 0)
            copies.out(acc_s, unit_hbm)
            copies.out(inv_s, inv_hbm)
            copies.out(low_s, low_hbm)
        else:
            copies.out(acc_s, acc_out)
        copies.drain()

    inputs = [(SCALARS, meta), (HBM, x), (HBM, w_pair[0]), (HBM, w_pair[1])]
    inputs += [(WHOLE, v) for v in smalls]
    dims = [(2, rows, 3 * width), (2, rows, width), (2, passages * heads, plen, plen)]
    outputs = [(HBM, shape(d, BF16)) for d in dims]
    scratch = [pltpu.VMEM((rows, model), BF16), pltpu.VMEM((2, 4 * width, model), BF16)]
    scratch += [pltpu.VMEM(d, BF16) for d in dims]
    scratch += [pltpu.VMEM((rows, model), F32)]
    if last:
        inputs += [(HBM, acc)] + [(WHOLE, v) for v in vectors]
        outputs += [(HBM, shape((rows, model), F32)), (HBM, shape((rows, 128), F32))]
        outputs += [(HBM, shape((rows, model), BF16))]
        scratch += [pltpu.VMEM((rows, 128), F32), pltpu.VMEM((rows, model), BF16)]
    else:
        outputs += [(HBM, shape((rows, model), F32))]
    return call(kernel, "attend_pair", inputs, outputs, scratch, 16)


def feed(j, low_s, i_s, b_s, bias, act_s, slope_s):
    units = act_s.shape[2]
    for c in range(0, units, 256):
        cols = slice(c, c + 256)
        t = nn(low_s[...], i_s[j, :, cols]) + bias[0:1, cols]
        cdf = 0.5 * (1.0 + lax.erf(t * (1.0 / math.sqrt(2.0))))
        pdf = jnp.exp(-0.5 * t * t) * (1.0 / math.sqrt(2.0 * math.pi))
        act_s[j, :, cols] = (t * cdf).astype(BF16)
        slope_s[j, :, cols] = (cdf + t * pdf).astype(BF16)
    return nn(act_s[j], b_s[j])


def feed_pair(low, in_pair, back_pair, smalls):
    rows, model = low.shape
    units = in_pair[0].shape[1]

    def kernel(low_hbm, ia, ib, ba, bb, bias_a, bias_b, *rest):
        act_hbm, slope_hbm, acc_hbm, low_s, i_s, b_s, act_s, slope_s, acc_s, sems = rest
        copies = Copies(sems)
        first = [copies.start(low_hbm, low_s), copies.start(ia, i_s.at[0]), copies.start(ba, b_s.at[0])]
        second = [copies.start(ib, i_s.at[1]), copies.start(bb, b_s.at[1])]
        for j, waits, bias in ((0, first, bias_a), (1, second, bias_b)):
            for copy in waits:
                copy.wait()
            term = feed(j, low_s, i_s, b_s, bias, act_s, slope_s)
            copies.out(act_s.at[j], act_hbm.at[j])
            copies.out(slope_s.at[j], slope_hbm.at[j])
            acc_s[...] = acc_s[...] + term if j else term
        copies.out(acc_s, acc_hbm)
        copies.drain()

    inputs = [(HBM, v) for v in (low, *in_pair, *back_pair)] + [(WHOLE, v) for v in smalls]
    outputs = [(HBM, shape((2, rows, units), BF16))] * 2 + [(HBM, shape((rows, model), F32))]
    scratch = [pltpu.VMEM((rows, model), BF16), pltpu.VMEM((2, model, units), BF16)]
    scratch += [pltpu.VMEM((2, units, model), BF16)] + [pltpu.VMEM((2, rows, units), BF16)] * 2
    scratch += [pltpu.VMEM((rows, model), F32)]
    return call(kernel, "feed_pair", inputs, outputs, scratch, 12)


def turn_pair(low, in_pair, back_pair, smalls, unit, acc, dy, meta, vectors, plen):
    rows, model = low.shape
    units = in_pair[0].shape[1]

    def kernel(meta_ref, low_hbm, ia, ib, ba, bb, unit_hbm, acc_hbm, dy_hbm, bias_a, bias_b, *rest):
        gain_one, shift_one, b_back, gain_two, shift_two = rest[:5]
        out_hbm, grad_hbm, ffn_hbm, sum_ref, slope_hbm, oa, ob = rest[5:12]
        low_s, i_s, b_s, act_s, slope_s, acc_s, unit_s, dy_s, out_s, grad_s, ffn_s, g_s, sems = rest[12:]
        copies = Copies(sems)
        first = [copies.start(low_hbm, low_s), copies.start(ia, i_s.at[0]), copies.start(ba, b_s.at[0])]
        second = [copies.start(ib, i_s.at[1]), copies.start(bb, b_s.at[1]), copies.start(acc_hbm, acc_s)]
        third = [copies.start(unit_hbm, unit_s), copies.start(dy_hbm, dy_s)]
        for copy in first:
            copy.wait()
        term = feed(0, low_s, i_s, b_s, bias_a, act_s, slope_s)
        copies.out(slope_s.at[0], slope_hbm.at[0])
        for copy in second:
            copy.wait()
        acc_s[...] = acc_s[...] + term
        acc_s[...] = acc_s[...] + feed(1, low_s, i_s, b_s, bias_b, act_s, slope_s)
        copies.out(slope_s.at[1], slope_hbm.at[1])
        for copy in third:
            copy.wait()
        sum_ref[...] = jnp.zeros_like(sum_ref)

        def step(i, carry):
            at = block(i, STEP)
            normed = unit_s[at, :] * gain_one[...] + shift_one[...]
            u, inverse = unit_norm(normed + acc_s[at, :] + b_back[...])
            out_s[at, :] = (u * gain_two[...] + shift_two[...]).astype(BF16)
            slot = lax.broadcasted_iota(jnp.int32, (STEP, 1), 0) + (i * STEP) % plen
            keep = slot < meta_ref[(i * STEP) // plen]
            grad_y = jnp.where(keep, dy_s[at, :].astype(F32), 0.0)
            grad = norm_grad(grad_y * gain_two[...], u, inverse)
            grad_s[at, :] = grad
            ffn_s[at, :] = grad.astype(BF16)
            sum_ref[8:9, :] += jnp.sum(grad_y * u, axis=0, keepdims=True)
            sum_ref[9:10, :] += jnp.sum(grad_y, axis=0, keepdims=True)
            sum_ref[10:11, :] += jnp.sum(grad, axis=0, keepdims=True)
            return carry

        lax.fori_loop(0, rows // STEP, step, 0)
        copies.out(out_s, out_hbm)
        copies.out(grad_s, grad_hbm)
        copies.out(ffn_s, ffn_hbm)
        for j, out in ((1, ob), (0, oa)):
            g_s[j] = tn(act_s[j], ffn_s[...]).astype(BF16)
            copies.out(g_s.at[j], out)
        copies.drain()

    inputs = [(SCALARS, meta)] + [(HBM, v) for v in (low, *in_pair, *back_pair, unit, acc, dy)]
    inputs += [(WHOLE, v) for v in (*smalls, *vectors)]
    outputs = [(HBM, shape((rows, model), d)) for d in (BF16, F32, BF16)]
    outputs += [(WHOLE, shape((16, model), F32)), (HBM, shape((2, rows, units), BF16))]
    outputs += [(HBM, shape((units, model), BF16))] * 2
    scratch = [pltpu.VMEM((rows, model), BF16), pltpu.VMEM((2, model, units), BF16)]
    scratch += [pltpu.VMEM((2, units, model), BF16)] + [pltpu.VMEM((2, rows, units), BF16)] * 2
    scratch += [pltpu.VMEM((rows, model), d) for d in (F32, F32, BF16, BF16, F32, BF16)]
    scratch += [pltpu.VMEM((2, units, model), BF16)]
    return call(kernel, "turn_pair", inputs, outputs, scratch, 20)


def outer_pair(acts, grad_ffn):
    _, rows, units = acts.shape
    model = grad_ffn.shape[1]

    def kernel(act_hbm, g_hbm, oa, ob, act_s, g_s, out_s, sems):
        copies = Copies(sems)
        whole = copies.start(g_hbm, g_s)
        waits = [copies.start(act_hbm.at[j], act_s.at[j]) for j in (1, 0)]
        whole.wait()
        for j, wait, out in ((1, waits[0], ob), (0, waits[1], oa)):
            wait.wait()
            out_s[j] = tn(act_s[j], g_s[...]).astype(BF16)
            copies.out(out_s.at[j], out)
        copies.drain()

    inputs = [(HBM, acts), (HBM, grad_ffn)]
    outputs = [(HBM, shape((units, model), BF16))] * 2
    scratch = [pltpu.VMEM((2, rows, units), BF16), pltpu.VMEM((rows, model), BF16)]
    scratch += [pltpu.VMEM((2, units, model), BF16)]
    return call(kernel, "outer_pair", inputs, outputs, scratch, 8, 200 * 10**9)


def feed_back_pair(grad_ffn, slopes, in_pair, back_pair, low, start, part, sums, meta, unit=None, inverse=None, gain=None):
    rows, model = grad_ffn.shape
    units = slopes.shape[2]
    last = unit is not None

    def kernel(meta_ref, before, g_hbm, slope_hbm, ia, ib, ba, bb, low_hbm, start_hbm, *rest):
        if last:
            unit_hbm, inv_hbm, gain_ref = rest[:3]
            rest = rest[3:]
            oa, ob, sum_ref, one_hbm, attn_hbm = rest[:5]
            g_s, slope_s, i_s, b_s, low_s, acc_s, pre_s, out_s, line, unit_s, inv_s, attn_s, sems = rest[5:]
        else:
            oa, ob, sum_ref, acc_out = rest[:4]
            g_s, slope_s, i_s, b_s, low_s, acc_s, pre_s, out_s, line, sems = rest[4:]
        copies = Copies(sems)
        sum_ref[...] = before[...]
        weights = {1: (bb, ib), 0: (ba, ia)}
        early = copies.start(g_hbm, g_s)
        waits, later = {}, {}
        for j in (1, 0):
            waits[j] = [copies.start(weights[j][0], b_s.at[j]), copies.start(slope_hbm.at[j], slope_s.at[j])]
            later[j] = [copies.start(weights[j][1], i_s.at[j])]
            if j == 1:
                later[j] += [copies.start(low_hbm, low_s), copies.start(start_hbm, acc_s)]
        if last:
            late = [copies.start(unit_hbm, unit_s), copies.start(inv_hbm, inv_s)]
        early.wait()
        for j, out in ((1, ob), (0, oa)):
            for wait in waits[j]:
                wait.wait()
            for c in range(0, units, 256):
                cols = slice(c, c + 256)
                pre = nt(g_s[...], b_s[j, cols, :]) * slope_s[j, :, cols].astype(F32)
                pre = pre.astype(BF16)
                pre_s[:, cols] = pre
                line[:, cols] = jnp.sum(pre.astype(F32), axis=0, keepdims=True)
            sum_ref[pl.ds(row_of(part + j, meta_ref, 0), 1), :] = line[...]
            for wait in later[j]:
                wait.wait()
            acc_s[...] = acc_s[...] + nt(pre_s[...], i_s[j])
            out_s[j] = tn(low_s[...], pre_s[...]).astype(BF16)
            copies.out(out_s.at[j], out)
        if last:
            for wait in late:
                wait.wait()

            def finish(i, carry):
                at = block(i, STEP)
                normed = acc_s[at, :]
                u = unit_s[at, :]
                grad = norm_grad(normed * gain_ref[0:1, :], u, inv_s[at, 0:1])
                sum_ref[11:12, :] += jnp.sum(grad, axis=0, keepdims=True)
                sum_ref[12:13, :] += jnp.sum(normed * u, axis=0, keepdims=True)
                sum_ref[13:14, :] += jnp.sum(normed, axis=0, keepdims=True)
                acc_s[at, :] = grad
                attn_s[at, :] = grad.astype(BF16)
                return carry

            lax.fori_loop(0, rows // STEP, finish, 0)
            copies.out(acc_s, one_hbm)
            copies.out(attn_s, attn_hbm)
        else:
            copies.out(acc_s, acc_out)
        copies.drain()

    inputs = [(SCALARS, meta), (WHOLE, sums)]
    inputs += [(HBM, v) for v in (grad_ffn, slopes, *in_pair, *back_pair, low, start)]
    outputs = [(HBM, shape((model, units), BF16))] * 2 + [(WHOLE, shape((16, model), F32))]
    outputs += [(HBM, shape((rows, model), F32))]
    scratch = [pltpu.VMEM((rows, model), BF16), pltpu.VMEM((2, rows, units), BF16)]
    scratch += [pltpu.VMEM((2, model, units), BF16), pltpu.VMEM((2, units, model), BF16)]
    scratch += [pltpu.VMEM((rows, model), BF16), pltpu.VMEM((rows, model), F32)]
    scratch += [pltpu.VMEM((rows, units), BF16), pltpu.VMEM((2, model, units), BF16)]
    scratch += [pltpu.VMEM((1, units), F32)]
    if last:
        inputs += [(HBM, unit), (HBM, inverse), (WHOLE, gain)]
        outputs += [(HBM, shape((rows, model), BF16))]
        scratch += [pltpu.VMEM((rows, model), F32), pltpu.VMEM((rows, 128), F32)]
        scratch += [pltpu.VMEM((rows, model), BF16)]
    return call(kernel, "feed_back_pair", inputs, outputs, scratch, 20, 200 * 10**9)


def attend_back_pair(x, plen, grad_attn, qkvs, ctxs, probs, w_pair, start, part, sums, meta):
    rows, model = x.shape
    passages = rows // plen
    width = ctxs.shape[2]
    heads = width // DH

    def kernel(meta_ref, before, x_hbm, g_hbm, qkv_hbm, ctx_hbm, p_hbm, wa, wb, start_hbm, *rest):
        oa, ob, sum_ref, acc_out = rest[:4]
        x_s, g_s, qkv_s, ctx_s, p_s, w_s, acc_s, grow_s, out_s, gc_s, sems = rest[4:]
        copies = Copies(sems)
        sum_ref[...] = before[...]
        early = [copies.start(g_hbm, g_s)]
        w_of = {0: wa, 1: wb}
        waits, middle, later = {}, {}, {}
        for j in (1, 0):
            waits[j] = [copies.start(w_of[j], w_s.at[j]), copies.start(ctx_hbm.at[j], ctx_s.at[j])]
            middle[j] = [copies.start(qkv_hbm.at[j], qkv_s.at[j]), copies.start(p_hbm.at[j], p_s.at[j])]
            later[j] = []
            if j == 1:
                later[j] = [copies.start(x_hbm, x_s), copies.start(start_hbm, acc_s)]
        for wait in early:
            wait.wait()
        for j, out in ((1, ob), (0, oa)):
            for wait in waits[j]:
                wait.wait()
            gc_s[...] = nt(g_s[...], w_s[j, 3 * width :, :]).astype(BF16)
            out_s[j, 3 * width :, :] = tn(ctx_s[j], g_s[...]).astype(BF16)
            for wait in middle[j]:
                wait.wait()

            def one(g, carry, j=j):
                at = block(g, plen)
                qkv = qkv_s[j, at, :]
                grad_ctx = gc_s[at, :]
                gq, gk, gv = [], [], []
                for h in range(heads):
                    q = qkv[:, h * DH : (h + 1) * DH]
                    k = qkv[:, width + h * DH : width + (h + 1) * DH]
                    v = qkv[:, 2 * width + h * DH : 2 * width + (h + 1) * DH]
                    gc = grad_ctx[:, h * DH : (h + 1) * DH]
                    low = p_s[j, g * heads + h]
                    p = low.astype(F32)
                    gp = nt(gc, v)
                    delta = jnp.sum(p * gp, axis=-1, keepdims=True)
                    gs = (p * (gp - delta)).astype(BF16)
                    gq.append(nn(gs, k) * (1.0 / math.sqrt(DH)))
                    gk.append(tn(gs, q) * (1.0 / math.sqrt(DH)))
                    gv.append(tn(low, gc))
                grow = jnp.concatenate(gq + gk + gv, axis=1).astype(BF16)
                grow_s[at, :] = grow
                return carry + jnp.sum(grow.astype(F32), axis=0, keepdims=True)

            line = lax.fori_loop(0, passages, one, jnp.zeros((1, 3 * width), F32))
            line = jnp.concatenate([line, jnp.zeros((1, model - 3 * width), F32)], axis=1)
            sum_ref[pl.ds(row_of(part + j, meta_ref, 1), 1), :] = line
            for wait in later[j]:
                wait.wait()
            out_s[j, : 3 * width, :] = tn(grow_s[...], x_s[...]).astype(BF16)
            copies.out(out_s.at[j], out)
            acc_s[...] = acc_s[...] + nn(grow_s[...], w_s[j, : 3 * width, :])
        copies.out(acc_s, acc_out)
        copies.drain()

    inputs = [(SCALARS, meta), (WHOLE, sums)]
    inputs += [(HBM, v) for v in (x, grad_attn, qkvs, ctxs, probs, *w_pair, start)]
    outputs = [(HBM, shape((4 * width, model), BF16))] * 2
    outputs += [(WHOLE, shape((16, model), F32)), (HBM, shape((rows, model), F32))]
    scratch = [pltpu.VMEM((rows, model), BF16), pltpu.VMEM((rows, model), BF16)]
    scratch += [pltpu.VMEM(v.shape, BF16) for v in (qkvs, ctxs, probs)]
    scratch += [pltpu.VMEM((2, 4 * width, model), BF16), pltpu.VMEM((rows, model), F32)]
    scratch += [pltpu.VMEM((rows, 3 * width), BF16), pltpu.VMEM((2, 4 * width, model), BF16)]
    scratch += [pltpu.VMEM((rows, width), BF16)]
    return call(kernel, "attend_back_pair", inputs, outputs, scratch, 20, 200 * 10**9)


def tie(value, *others):
    return lax.optimization_barrier((value, *others))[0]


def flat_perm(move):
    pairs = []
    for z in range(4):
        for y in range(2):
            for x in range(2):
                for c in range(2):
                    z2, y2, x2, c2 = move(z, y, x, c)
                    pairs.append((((z * 2 + y) * 2 + x) * 2 + c, ((z2 * 2 + y2) * 2 + x2) * 2 + c2))
    return pairs


def add(one, two):
    return (one.astype(F32) + two.astype(F32)).astype(BF16)


ORDER = "vssibsvuivbuvsuivsuvisubvui"


class GridMoves:
    def __init__(self):
        self.row = lax.axis_index("batch") % 2
        self.layer = lax.axis_index("batch") // 2 % 2
        self.side = (self.row + self.layer) % 2
        self.to_core = flat_perm(lambda z, y, x, c: (z, y, x, 1 - c))
        self.to_x = flat_perm(lambda z, y, x, c: (z, y, 1 - x, c))
        self.to_y = flat_perm(lambda z, y, x, c: (z, 1 - y, x, c))
        self.to_z = flat_perm(lambda z, y, x, c: (z ^ 1, y, x, c))
        self.to_zz = flat_perm(lambda z, y, x, c: (z ^ 2, y, x, c))
        self.mark = None

    def send(self, value, pairs):
        return lax.ppermute(value, AXES, pairs)

    def half(self, value, which):
        if isinstance(value, tuple):
            return jnp.where(which == 0, value[0], value[1])
        rows = value.shape[0] // 2
        return lax.dynamic_slice_in_dim(value, which * rows, rows, axis=0)

    def order(self, mine, other, bit):
        low = jnp.where(bit == 0, mine, other)
        high = jnp.where(bit == 0, other, mine)
        return jnp.concatenate([low, high], axis=0)

    def after(self, value):
        if self.mark is not None:
            value = tie(value, self.mark)
        return value

    def pieces(self, mine):
        first, second = self.halves(mine)
        return [self.send(first, self.to_y), self.send(second, self.to_z)]

    def whole(self, mine, pieces):
        return self.order(mine, jnp.concatenate(pieces, axis=0), self.side)

    def halves(self, value):
        rows = value.shape[0] // 2
        return value[:rows], value[rows:]

    def chain(self, near, got):
        got = tuple(self.after(part) for part in got)
        got = got if len(got) == 2 else got[0]
        pass_on = add(self.half(near, 1 - self.row), self.half(got, 1 - self.row))
        keep = add(self.half(near, self.row), self.half(got, self.row))
        got = self.send(pass_on, self.to_y)
        yield pass_on
        yield from self.chain_z(add(keep, self.after(got)))

    def chain_zy(self, near, got):
        got = tuple(self.after(part) for part in got)
        pass_on = add(self.half(near, 1 - self.layer), self.half(got, 1 - self.layer))
        keep = add(self.half(near, self.layer), self.half(got, self.layer))
        got = self.send(pass_on, self.to_z)
        yield pass_on
        keep = add(keep, self.after(got))
        pass_on = self.half(keep, 1 - self.row)
        keep = self.half(keep, self.row)
        got = self.send(pass_on, self.to_y)
        yield pass_on
        keep = add(keep, self.after(got))
        got = self.send(keep, self.to_zz)
        yield keep
        keep = add(keep, self.after(got))
        got = self.send(keep, self.to_y)
        yield keep
        keep = self.order(keep, self.after(got), self.row)
        got = self.send(keep, self.to_z)
        yield keep
        yield self.order(keep, self.after(got), self.layer).astype(F32)

    def chain_y(self, near, far):
        pass_on = jnp.concatenate(
            [self.half(near, 1 - self.row), self.half(far, 1 - self.row)], axis=0
        )
        got = self.send(pass_on, self.to_y)
        yield pass_on
        got = self.halves(self.after(got))
        far = add(self.half(far, self.row), got[1])
        keep = add(self.half(near, self.row), got[0])
        got = self.send(far, self.to_x)
        yield far
        yield from self.chain_z(add(keep, self.after(got)))

    def chain_z(self, keep):
        pass_on = self.half(keep, 1 - self.layer)
        keep = self.half(keep, self.layer)
        got = self.send(pass_on, self.to_z)
        yield pass_on
        keep = add(keep, self.after(got))
        got = self.send(keep, self.to_zz)
        yield keep
        keep = add(keep, self.after(got))
        got = self.send(keep, self.to_z)
        yield keep
        keep = self.order(keep, self.after(got), self.layer)
        got = self.send(keep, self.to_y)
        yield keep
        yield self.order(keep, self.after(got), self.row).astype(F32)

    def chain_small(self, value):
        for pairs in (self.to_core, self.to_x, self.to_y, self.to_z, self.to_zz):
            got = self.send(value, pairs)
            yield value
            value = value + self.after(got)
        yield value

    def step(self, chain):
        self.mark = next(chain)
        return self.mark


def body(
    tokens,
    passage_lengths,
    cotangent,
    w_qkv,
    b_query,
    b_value,
    w_out,
    b_out,
    gain_one,
    shift_one,
    w_in,
    b_in,
    w_back,
    b_back,
    gain_two,
    shift_two,
):
    micro_count, own_rows, model = tokens.shape
    tp_count = lax.axis_size("tp")
    batch_count = lax.axis_size("batch")
    plen = own_rows * tp_count // passage_lengths.shape[1]
    own_passages = own_rows // plen
    assert own_passages * plen == own_rows and tp_count == 4
    grid = (batch_count, tp_count) == (8, 4)
    width = w_qkv.shape[2]
    rows = micro_count * own_rows
    position = lax.axis_index("tp")

    vector = lambda v: v.reshape(1, -1)
    x = tokens.reshape(rows, model)
    dy = cotangent.reshape(rows, model)
    lengths = lax.dynamic_slice_in_dim(
        passage_lengths, position * own_passages, own_passages, axis=1
    ).reshape(micro_count * own_passages)
    meta = jnp.concatenate([lengths, (position if grid else 0 * position).reshape(1)])
    qkvo = jnp.concatenate([jnp.transpose(w_qkv, (1, 2, 0)).reshape(3 * width, model), w_out], axis=0)
    small = vector(jnp.concatenate([b_in.astype(F32), b_query, jnp.zeros_like(b_query), b_value]))
    if grid:
        m = moves = GridMoves()
        x_att = m.send(m.half(qkvo, m.side), m.to_x)
        c_att = m.send(qkvo, m.to_core)
        c_small = m.send(small, m.to_core)
        x_small = m.send(small, m.to_x)
        half_in = m.half(w_in, m.side)
        meta = tie(meta, x_small, half_in)
        att, smalls = [qkvo, c_att], [small, c_small]
    else:
        att, smalls, ins, backs = [
            list(lax.all_gather(v, "tp", axis=0)) for v in (qkvo, small, w_in, w_back)
        ]
    qkv_near, ctx_near, p_near, acc = attend_pair(x, plen, att[:2], smalls[:2], meta)
    y = x
    if grid:
        x_att = tie(x_att, acc)
        y_att = m.send(x_att, m.to_y)
        half_back = m.half(w_back, m.side)
        x_in = m.send(tie(half_in, x_att), m.to_x)
        smalls += [x_small, m.send(tie(x_small, x_att), m.to_core)]
        y_att = tie(y_att, half_back)
        f_att = m.order(x_att, y_att, m.side)
        att += [f_att, m.send(f_att, m.to_core)]
        c_in = m.send(tie(w_in, f_att), m.to_core)
        c_back = m.send(tie(w_back, f_att), m.to_core)
        x_in = tie(x_in, f_att)
        y_in = m.send(x_in, m.to_y)
        x_back = m.send(tie(half_back, x_in), m.to_x)
        y = tie(x, x_in)
    qkv_far, ctx_far, p_far, unit, inverse, low = attend_pair(
        y, plen, att[2:], smalls[2:], meta, acc, [vector(v) for v in (b_out, gain_one, shift_one)]
    )
    if grid:
        y_in = tie(y_in, low)
        f_in = m.order(x_in, y_in, m.side)
        ins = [w_in, c_in, f_in, m.send(f_in, m.to_core)]
        x_back = tie(x_back, f_in)
        p_back = m.pieces(x_back)
        backs = [w_back, c_back]
        low = tie(low, x_back)
    act_near, slope_near, feed_near = feed_pair(low, ins[:2], backs[:2], smalls[:2])
    if grid:
        p_back[0] = tie(p_back[0], feed_near)
        f_back = m.whole(x_back, p_back)
        backs += [f_back, m.send(f_back, m.to_core)]
    layer_out, grad_two, grad_ffn, sums, slope_far, b_far, b_farc = turn_pair(
        low,
        ins[2:],
        backs[2:],
        smalls[2:],
        unit,
        feed_near,
        dy,
        meta,
        [vector(v) for v in (gain_one, shift_one, b_back, gain_two, shift_two)],
        plen,
    )
    if grid:
        got_b3 = m.send(b_farc, m.to_core)
    b_own, b_core = outer_pair(act_near, grad_ffn)
    if grid:
        got_b1 = m.send(b_core, m.to_core)
        b_far = add(b_far, tie(got_b3, b_own))
        got_bx = [m.send(part, m.to_x) for part in m.halves(b_far)]
        slope_far = tie(slope_far, b_far)
    i_far, i_farc, sums, normed = feed_back_pair(
        grad_ffn, slope_far, ins[2:], backs[2:], low, grad_two, 2, sums, meta
    )
    if grid:
        got_i3 = m.send(i_farc, m.to_core)
        b_near = add(b_own, tie(got_b1, normed))
        got_bx[0] = tie(got_bx[0], b_near)
        normed = tie(normed, got_bx[0])
    i_own, i_core, sums, grad_one, grad_attn = feed_back_pair(
        grad_ffn,
        slope_near,
        ins[:2],
        backs[:2],
        low,
        normed,
        0,
        sums,
        meta,
        unit,
        inverse,
        vector(gain_one),
    )
    if grid:
        got_i1 = m.send(i_core, m.to_core)
        i_far = add(i_far, tie(got_i3, grad_attn))
        got_ix = [m.send(part, m.to_x) for part in m.halves(i_far)]
        m.mark = i_far
        chain_b = m.chain(b_near, got_bx)
        m.step(chain_b)
        grad_attn = tie(grad_attn, m.mark)
    a_far, a_farc, sums, grad_x = attend_back_pair(
        x, plen, grad_attn, qkv_far, ctx_far, p_far, att[2:], grad_one, 2, sums, meta
    )
    if grid:
        got_a3 = m.send(a_farc, m.to_core)
        i_near = add(i_own, tie(got_i1, grad_x))
        m.mark = i_near
        m.step(chain_b)
        got_ix[0] = m.after(got_ix[0])
        grad_x = tie(grad_x, got_ix[0])
    a_own, a_core, packed, grad_x = attend_back_pair(
        x, plen, grad_attn, qkv_near, ctx_near, p_near, att[:2], grad_x, 0, sums, meta
    )
    if grid:
        got_a1 = m.send(a_core, m.to_core)
        m.mark = grad_x
        a_far = m.halves(add(a_far, m.after(got_a3)))
        got_ax = m.send(a_far[0], m.to_x)
        m.mark = a_far[0]
        chains = {"s": m.chain_small(packed), "b": chain_b, "i": m.chain_zy(i_near, got_ix)}
        done = {}
        for key in "ib":
            done[key] = m.step(chains[key])
        a_near = m.halves(add(a_own, m.after(got_a1)))
        m.mark = a_near[0]
        chains["v"] = m.chain_y(a_near[1], a_far[1])
        chains["u"] = m.chain(a_near[0], [got_ax])
        for key in ORDER:
            done[key] = m.step(chains[key])
        g_back, g_in, packed = done["b"], done["i"], done["s"]
        g_att = jnp.concatenate([done["u"], done["v"]], axis=0)
    else:
        g_back, g_in, g_att = [
            lax.psum(
                lax.psum_scatter(jnp.stack(parts).astype(F32), "tp", scatter_dimension=0), "batch"
            )
            for parts in (
                (b_own, b_core, b_far, b_farc),
                (i_own, i_core, i_far, i_farc),
                (a_own, a_core, a_far, a_farc),
            )
        ]
        packed = lax.psum(packed, AXES)
    mine = lax.dynamic_slice_in_dim(packed, 2 * position, 2, axis=0)
    return (
        layer_out.reshape(tokens.shape),
        grad_x.reshape(tokens.shape),
        jnp.transpose(g_att[: 3 * width].reshape(3, width, model), (2, 0, 1)),
        mine[1, :width],
        mine[1, 2 * width : 3 * width],
        g_att[3 * width :],
        packed[11],
        packed[12],
        packed[13],
        g_in,
        mine[0],
        g_back,
        packed[10],
        packed[8],
        packed[9],
    )


def solution(mesh):
    in_specs = (
        P(None, ("batch", "tp"), None),
        P(None, "batch"),
        P(None, ("batch", "tp"), None),
        P(None, None, "tp"),
        P("tp"),
        P("tp"),
        P("tp", None),
        P(),
        P(),
        P(),
        P(None, "tp"),
        P("tp"),
        P("tp", None),
        P(),
        P(),
        P(),
    )
    out_specs = (
        P(None, ("batch", "tp"), None),
        P(None, ("batch", "tp"), None),
        P(None, None, "tp"),
        P("tp"),
        P("tp"),
        P("tp", None),
        P(),
        P(),
        P(),
        P(None, "tp"),
        P("tp"),
        P("tp", None),
        P(),
        P(),
        P(),
    )
    return jax.shard_map(body, mesh=mesh, in_specs=in_specs, out_specs=out_specs, check_vma=False)
```

```python
import math

import jax
import jax.numpy as jnp
from jax import lax
from jax.experimental import pallas as pl
from jax.experimental.pallas import tpu as pltpu
from jax.sharding import PartitionSpec as P

DH = 64
AXES = ("batch", "tp")
epsilon = 1e-05
F32 = jnp.float32
BF16 = jnp.bfloat16


def nt(a, b):
    return lax.dot_general(a, b, (((1,), (1,)), ((), ())), preferred_element_type=F32)


def tn(a, b):
    return lax.dot_general(a, b, (((0,), (0,)), ((), ())), preferred_element_type=F32)


def nn(a, b):
    return jnp.dot(a, b, preferred_element_type=F32)


HBM = pl.BlockSpec(memory_space=pl.ANY)
WHOLE = pl.BlockSpec(memory_space=pltpu.VMEM)
SCALARS = pl.BlockSpec(memory_space=pltpu.SMEM)


class Copies:
    def __init__(self, sems):
        self.sems, self.used = sems, 0
        self.pending = []

    def start(self, src, dst):
        copy = pltpu.make_async_copy(src, dst, self.sems.at[self.used])
        self.used += 1
        copy.start()
        return copy

    def out(self, src, dst):
        self.pending.append(self.start(src, dst))

    def drain(self):
        for copy in self.pending:
            copy.wait()


def call(kernel, name, inputs, outputs, scratch, copies, cost=1000):
    in_specs = [spec for spec, _ in inputs]
    return pl.pallas_call(
        kernel,
        name=name,
        in_specs=in_specs,
        out_specs=tuple(spec for spec, _ in outputs),
        out_shape=tuple(shape for _, shape in outputs),
        scratch_shapes=list(scratch) + [pltpu.SemaphoreType.DMA((copies,))],
        cost_estimate=pl.CostEstimate(flops=cost, transcendentals=0, bytes_accessed=0),
    )(*[value for _, value in inputs])


def shape(dims, dtype):
    return jax.ShapeDtypeStruct(dims, dtype)


def block(i, size):
    return pl.ds(pl.multiple_of(i * size, size), size)


def unit_norm(v):
    middle = jnp.mean(v, axis=-1, keepdims=True)
    centred = v - middle
    inverse = lax.rsqrt(jnp.mean(centred * centred, axis=-1, keepdims=True) + epsilon)
    return centred * inverse, inverse


def norm_grad(scaled, unit, inverse):
    mean_one = jnp.mean(scaled, axis=-1, keepdims=True)
    mean_two = jnp.mean(scaled * unit, axis=-1, keepdims=True)
    return inverse * (scaled - mean_one - unit * mean_two)


STEP = 128


def row_of(part, meta_ref, kind):
    return 2 * jnp.bitwise_xor(part, meta_ref[meta_ref.shape[0] - 1]) + kind


def attend_pair(x, plen, w_pair, smalls, meta, acc=None, vectors=None):
    rows, model = x.shape
    passages = rows // plen
    width = w_pair[0].shape[0] // 4
    heads = width // DH
    units = smalls[0].shape[1] - 3 * width
    last = acc is not None

    def kernel(meta_ref, x_hbm, wa, wb, bias_a, bias_b, *rest):
        if last:
            acc_hbm, b_out, gain, shift = rest[:4]
            qkv_hbm, ctx_hbm, p_hbm, unit_hbm, inv_hbm, low_hbm = rest[4:10]
            x_s, w_s, qkv_s, ctx_s, p_s, acc_s, inv_s, low_s, sems = rest[10:]
        else:
            qkv_hbm, ctx_hbm, p_hbm, acc_out = rest[:4]
            x_s, w_s, qkv_s, ctx_s, p_s, acc_s, sems = rest[4:]
        copies = Copies(sems)
        first = [copies.start(x_hbm, x_s), copies.start(wa, w_s.at[0])]
        second = [copies.start(wb, w_s.at[1])]
        if last:
            held = copies.start(acc_hbm, acc_s)
        for j, waits, bias in ((0, first, bias_a), (1, second, bias_b)):
            for copy in waits:
                copy.wait()
            qkv_s[j] = (nt(x_s[...], w_s[j, : 3 * width, :]) + bias[0:1, units:]).astype(BF16)
            copies.out(qkv_s.at[j], qkv_hbm.at[j])

            def one(g, carry, j=j):
                at = block(g, plen)
                qkv = qkv_s[j, at, :]
                keep = lax.broadcasted_iota(jnp.int32, (1, plen), 1) < meta_ref[g]
                ctx = []
                for h in range(heads):
                    q = qkv[:, h * DH : (h + 1) * DH] * (1.0 / math.sqrt(DH))
                    k = qkv[:, width + h * DH : width + (h + 1) * DH]
                    v = qkv[:, 2 * width + h * DH : 2 * width + (h + 1) * DH]
                    s = jnp.where(keep, nt(q.astype(BF16), k), -1000000000.0)
                    e = jnp.exp(s - jnp.max(s, axis=-1, keepdims=True))
                    p = (e * (1.0 / jnp.sum(e, axis=-1, keepdims=True))).astype(BF16)
                    p_s[j, g * heads + h] = p
                    ctx.append(nn(p, v))
                ctx_s[j, at, :] = jnp.concatenate(ctx, axis=1).astype(BF16)
                return carry

            lax.fori_loop(0, passages, one, 0)
            copies.out(ctx_s.at[j], ctx_hbm.at[j])
            copies.out(p_s.at[j], p_hbm.at[j])
            term = nn(ctx_s[j], w_s[j, 3 * width :, :])
            if last and j == 0:
                held.wait()
            acc_s[...] = term if j == 0 and not last else acc_s[...] + term
        if last:

            def finish(i, carry):
                at = block(i, STEP)
                v = x_s[at, :].astype(F32) + acc_s[at, :] + b_out[...]
                unit, inverse = unit_norm(v)
                acc_s[at, :] = unit
                inv_s[at, :] = jnp.broadcast_to(inverse, (STEP, 128))
                low_s[at, :] = (unit * gain[...] + shift[...]).astype(BF16)
                return carry

            lax.fori_loop(0, rows // STEP, finish, 0)
            copies.out(acc_s, unit_hbm)
            copies.out(inv_s, inv_hbm)
            copies.out(low_s, low_hbm)
        else:
            copies.out(acc_s, acc_out)
        copies.drain()

    inputs = [(SCALARS, meta), (HBM, x), (HBM, w_pair[0]), (HBM, w_pair[1])]
    inputs += [(WHOLE, v) for v in smalls]
    dims = [(2, rows, 3 * width), (2, rows, width), (2, passages * heads, plen, plen)]
    outputs = [(HBM, shape(d, BF16)) for d in dims]
    scratch = [pltpu.VMEM((rows, model), BF16), pltpu.VMEM((2, 4 * width, model), BF16)]
    scratch += [pltpu.VMEM(d, BF16) for d in dims]
    scratch += [pltpu.VMEM((rows, model), F32)]
    if last:
        inputs += [(HBM, acc)] + [(WHOLE, v) for v in vectors]
        outputs += [(HBM, shape((rows, model), F32)), (HBM, shape((rows, 128), F32))]
        outputs += [(HBM, shape((rows, model), BF16))]
        scratch += [pltpu.VMEM((rows, 128), F32), pltpu.VMEM((rows, model), BF16)]
    else:
        outputs += [(HBM, shape((rows, model), F32))]
    return call(kernel, "attend_pair", inputs, outputs, scratch, 16, 1000 if last else 200 * 10**9)


def feed(j, low_s, i_s, b_s, bias, act_s, slope_s):
    units = act_s.shape[2]
    for c in range(0, units, 256):
        cols = slice(c, c + 256)
        t = nn(low_s[...], i_s[j, :, cols]) + bias[0:1, cols]
        cdf = 0.5 * (1.0 + lax.erf(t * (1.0 / math.sqrt(2.0))))
        pdf = jnp.exp(-0.5 * t * t) * (1.0 / math.sqrt(2.0 * math.pi))
        act_s[j, :, cols] = (t * cdf).astype(BF16)
        slope_s[j, :, cols] = (cdf + t * pdf).astype(BF16)
    return nn(act_s[j], b_s[j])


def feed_pair(low, in_pair, back_pair, smalls):
    rows, model = low.shape
    units = in_pair[0].shape[1]

    def kernel(low_hbm, ia, ib, ba, bb, bias_a, bias_b, *rest):
        act_hbm, slope_hbm, acc_hbm, low_s, i_s, b_s, act_s, slope_s, acc_s, sems = rest
        copies = Copies(sems)
        first = [copies.start(low_hbm, low_s), copies.start(ia, i_s.at[0]), copies.start(ba, b_s.at[0])]
        second = [copies.start(ib, i_s.at[1]), copies.start(bb, b_s.at[1])]
        for j, waits, bias in ((0, first, bias_a), (1, second, bias_b)):
            for copy in waits:
                copy.wait()
            term = feed(j, low_s, i_s, b_s, bias, act_s, slope_s)
            copies.out(act_s.at[j], act_hbm.at[j])
            copies.out(slope_s.at[j], slope_hbm.at[j])
            acc_s[...] = acc_s[...] + term if j else term
        copies.out(acc_s, acc_hbm)
        copies.drain()

    inputs = [(HBM, v) for v in (low, *in_pair, *back_pair)] + [(WHOLE, v) for v in smalls]
    outputs = [(HBM, shape((2, rows, units), BF16))] * 2 + [(HBM, shape((rows, model), F32))]
    scratch = [pltpu.VMEM((rows, model), BF16), pltpu.VMEM((2, model, units), BF16)]
    scratch += [pltpu.VMEM((2, units, model), BF16)] + [pltpu.VMEM((2, rows, units), BF16)] * 2
    scratch += [pltpu.VMEM((rows, model), F32)]
    return call(kernel, "feed_pair", inputs, outputs, scratch, 12)


def turn_pair(low, in_pair, back_pair, smalls, unit, acc, dy, meta, vectors, plen):
    rows, model = low.shape
    units = in_pair[0].shape[1]

    def kernel(meta_ref, low_hbm, ia, ib, ba, bb, unit_hbm, acc_hbm, dy_hbm, bias_a, bias_b, *rest):
        gain_one, shift_one, b_back, gain_two, shift_two = rest[:5]
        out_hbm, grad_hbm, ffn_hbm, sum_ref, slope_hbm, oa, ob = rest[5:12]
        low_s, i_s, b_s, act_s, slope_s, acc_s, unit_s, dy_s, out_s, grad_s, ffn_s, g_s, sems = rest[12:]
        copies = Copies(sems)
        first = [copies.start(low_hbm, low_s), copies.start(ia, i_s.at[0]), copies.start(ba, b_s.at[0])]
        second = [copies.start(ib, i_s.at[1]), copies.start(bb, b_s.at[1]), copies.start(acc_hbm, acc_s)]
        third = [copies.start(unit_hbm, unit_s), copies.start(dy_hbm, dy_s)]
        for copy in first:
            copy.wait()
        term = feed(0, low_s, i_s, b_s, bias_a, act_s, slope_s)
        copies.out(slope_s.at[0], slope_hbm.at[0])
        for copy in second:
            copy.wait()
        acc_s[...] = acc_s[...] + term
        acc_s[...] = acc_s[...] + feed(1, low_s, i_s, b_s, bias_b, act_s, slope_s)
        copies.out(slope_s.at[1], slope_hbm.at[1])
        for copy in third:
            copy.wait()
        sum_ref[...] = jnp.zeros_like(sum_ref)

        def step(i, carry):
            at = block(i, STEP)
            normed = unit_s[at, :] * gain_one[...] + shift_one[...]
            u, inverse = unit_norm(normed + acc_s[at, :] + b_back[...])
            out_s[at, :] = (u * gain_two[...] + shift_two[...]).astype(BF16)
            slot = lax.broadcasted_iota(jnp.int32, (STEP, 1), 0) + (i * STEP) % plen
            keep = slot < meta_ref[(i * STEP) // plen]
            grad_y = jnp.where(keep, dy_s[at, :].astype(F32), 0.0)
            grad = norm_grad(grad_y * gain_two[...], u, inverse)
            grad_s[at, :] = grad
            ffn_s[at, :] = grad.astype(BF16)
            sum_ref[8:9, :] += jnp.sum(grad_y * u, axis=0, keepdims=True)
            sum_ref[9:10, :] += jnp.sum(grad_y, axis=0, keepdims=True)
            sum_ref[10:11, :] += jnp.sum(grad, axis=0, keepdims=True)
            return carry

        lax.fori_loop(0, rows // STEP, step, 0)
        copies.out(out_s, out_hbm)
        copies.out(grad_s, grad_hbm)
        copies.out(ffn_s, ffn_hbm)
        for j, out in ((1, ob), (0, oa)):
            g_s[j] = tn(act_s[j], ffn_s[...]).astype(BF16)
            copies.out(g_s.at[j], out)
        copies.drain()

    inputs = [(SCALARS, meta)] + [(HBM, v) for v in (low, *in_pair, *back_pair, unit, acc, dy)]
    inputs += [(WHOLE, v) for v in (*smalls, *vectors)]
    outputs = [(HBM, shape((rows, model), d)) for d in (BF16, F32, BF16)]
    outputs += [(WHOLE, shape((16, model), F32)), (HBM, shape((2, rows, units), BF16))]
    outputs += [(HBM, shape((units, model), BF16))] * 2
    scratch = [pltpu.VMEM((rows, model), BF16), pltpu.VMEM((2, model, units), BF16)]
    scratch += [pltpu.VMEM((2, units, model), BF16)] + [pltpu.VMEM((2, rows, units), BF16)] * 2
    scratch += [pltpu.VMEM((rows, model), d) for d in (F32, F32, BF16, BF16, F32, BF16)]
    scratch += [pltpu.VMEM((2, units, model), BF16)]
    return call(kernel, "turn_pair", inputs, outputs, scratch, 20)


def outer_pair(acts, grad_ffn):
    _, rows, units = acts.shape
    model = grad_ffn.shape[1]

    def kernel(act_hbm, g_hbm, oa, ob, act_s, g_s, out_s, sems):
        copies = Copies(sems)
        whole = copies.start(g_hbm, g_s)
        waits = [copies.start(act_hbm.at[j], act_s.at[j]) for j in (1, 0)]
        whole.wait()
        for j, wait, out in ((1, waits[0], ob), (0, waits[1], oa)):
            wait.wait()
            out_s[j] = tn(act_s[j], g_s[...]).astype(BF16)
            copies.out(out_s.at[j], out)
        copies.drain()

    inputs = [(HBM, acts), (HBM, grad_ffn)]
    outputs = [(HBM, shape((units, model), BF16))] * 2
    scratch = [pltpu.VMEM((2, rows, units), BF16), pltpu.VMEM((rows, model), BF16)]
    scratch += [pltpu.VMEM((2, units, model), BF16)]
    return call(kernel, "outer_pair", inputs, outputs, scratch, 8, 200 * 10**9)


def feed_back_pair(grad_ffn, slopes, which, in_pair, back_pair, low, start, parts, sums, meta, unit=None, inverse=None, gain=None):
    rows, model = grad_ffn.shape
    units = slopes[0].shape[2]
    last = unit is not None

    def kernel(meta_ref, before, g_hbm, sa, sb, ia, ib, ba, bb, low_hbm, start_hbm, *rest):
        if last:
            unit_hbm, inv_hbm, gain_ref = rest[:3]
            rest = rest[3:]
            oa, ob, sum_ref, one_hbm, attn_hbm = rest[:5]
            g_s, slope_s, i_s, b_s, low_s, acc_s, pre_s, out_s, line, unit_s, inv_s, attn_s, sems = rest[5:]
        else:
            oa, ob, sum_ref, acc_out = rest[:4]
            g_s, slope_s, i_s, b_s, low_s, acc_s, pre_s, out_s, line, sems = rest[4:]
        copies = Copies(sems)
        sum_ref[...] = before[...]
        weights = {1: (bb, ib, sb.at[which]), 0: (ba, ia, sa.at[which])}
        early = copies.start(g_hbm, g_s)
        waits, later = {}, {}
        for j in (1, 0):
            waits[j] = [copies.start(weights[j][0], b_s.at[j]), copies.start(weights[j][2], slope_s.at[j])]
            later[j] = [copies.start(weights[j][1], i_s.at[j])]
            if j == 1:
                later[j] += [copies.start(low_hbm, low_s), copies.start(start_hbm, acc_s)]
        if last:
            late = [copies.start(unit_hbm, unit_s), copies.start(inv_hbm, inv_s)]
        early.wait()
        for j, out in ((1, ob), (0, oa)):
            for wait in waits[j]:
                wait.wait()
            for c in range(0, units, 256):
                cols = slice(c, c + 256)
                pre = nt(g_s[...], b_s[j, cols, :]) * slope_s[j, :, cols].astype(F32)
                pre = pre.astype(BF16)
                pre_s[:, cols] = pre
                line[:, cols] = jnp.sum(pre.astype(F32), axis=0, keepdims=True)
            sum_ref[pl.ds(row_of(parts[j], meta_ref, 0), 1), :] = line[...]
            for wait in later[j]:
                wait.wait()
            acc_s[...] = acc_s[...] + nt(pre_s[...], i_s[j])
            out_s[j] = tn(low_s[...], pre_s[...]).astype(BF16)
            copies.out(out_s.at[j], out)
        if last:
            for wait in late:
                wait.wait()

            def finish(i, carry):
                at = block(i, STEP)
                normed = acc_s[at, :]
                u = unit_s[at, :]
                grad = norm_grad(normed * gain_ref[0:1, :], u, inv_s[at, 0:1])
                sum_ref[11:12, :] += jnp.sum(grad, axis=0, keepdims=True)
                sum_ref[12:13, :] += jnp.sum(normed * u, axis=0, keepdims=True)
                sum_ref[13:14, :] += jnp.sum(normed, axis=0, keepdims=True)
                acc_s[at, :] = grad
                attn_s[at, :] = grad.astype(BF16)
                return carry

            lax.fori_loop(0, rows // STEP, finish, 0)
            copies.out(acc_s, one_hbm)
            copies.out(attn_s, attn_hbm)
        else:
            copies.out(acc_s, acc_out)
        copies.drain()

    inputs = [(SCALARS, meta), (WHOLE, sums)]
    inputs += [(HBM, v) for v in (grad_ffn, *slopes, *in_pair, *back_pair, low, start)]
    outputs = [(HBM, shape((model, units), BF16))] * 2 + [(WHOLE, shape((16, model), F32))]
    outputs += [(HBM, shape((rows, model), F32))]
    scratch = [pltpu.VMEM((rows, model), BF16), pltpu.VMEM((2, rows, units), BF16)]
    scratch += [pltpu.VMEM((2, model, units), BF16), pltpu.VMEM((2, units, model), BF16)]
    scratch += [pltpu.VMEM((rows, model), BF16), pltpu.VMEM((rows, model), F32)]
    scratch += [pltpu.VMEM((rows, units), BF16), pltpu.VMEM((2, model, units), BF16)]
    scratch += [pltpu.VMEM((1, units), F32)]
    if last:
        inputs += [(HBM, unit), (HBM, inverse), (WHOLE, gain)]
        outputs += [(HBM, shape((rows, model), BF16))]
        scratch += [pltpu.VMEM((rows, model), F32), pltpu.VMEM((rows, 128), F32)]
        scratch += [pltpu.VMEM((rows, model), BF16)]
    return call(kernel, "feed_back_pair", inputs, outputs, scratch, 20, 200 * 10**9)


def attend_back_pair(x, plen, grad_attn, qkvs, ctxs, probs, which, w_pair, start, parts, sums, meta):
    rows, model = x.shape
    passages = rows // plen
    width = ctxs[0].shape[2]
    heads = width // DH

    def kernel(meta_ref, before, x_hbm, g_hbm, qa, qb, ca, cb, pa, pb, wa, wb, start_hbm, *rest):
        oa, ob, sum_ref, acc_out = rest[:4]
        x_s, g_s, qkv_s, ctx_s, p_s, w_s, acc_s, grow_s, out_s, gc_s, sems = rest[4:]
        copies = Copies(sems)
        sum_ref[...] = before[...]
        early = [copies.start(g_hbm, g_s)]
        of = {0: (wa, ca, qa, pa), 1: (wb, cb, qb, pb)}
        waits, middle, later = {}, {}, {}
        for j in (1, 0):
            waits[j] = [copies.start(of[j][0], w_s.at[j]), copies.start(of[j][1].at[which], ctx_s.at[j])]
            middle[j] = [copies.start(of[j][2].at[which], qkv_s.at[j]), copies.start(of[j][3].at[which], p_s.at[j])]
            later[j] = []
            if j == 1:
                later[j] = [copies.start(x_hbm, x_s), copies.start(start_hbm, acc_s)]
        for wait in early:
            wait.wait()
        for j, out in ((1, ob), (0, oa)):
            for wait in waits[j]:
                wait.wait()
            gc_s[...] = nt(g_s[...], w_s[j, 3 * width :, :]).astype(BF16)
            out_s[j, 3 * width :, :] = tn(ctx_s[j], g_s[...]).astype(BF16)
            for wait in middle[j]:
                wait.wait()

            def one(g, carry, j=j):
                at = block(g, plen)
                qkv = qkv_s[j, at, :]
                grad_ctx = gc_s[at, :]
                gq, gk, gv = [], [], []
                for h in range(heads):
                    q = qkv[:, h * DH : (h + 1) * DH]
                    k = qkv[:, width + h * DH : width + (h + 1) * DH]
                    v = qkv[:, 2 * width + h * DH : 2 * width + (h + 1) * DH]
                    gc = grad_ctx[:, h * DH : (h + 1) * DH]
                    low = p_s[j, g * heads + h]
                    p = low.astype(F32)
                    gp = nt(gc, v)
                    delta = jnp.sum(p * gp, axis=-1, keepdims=True)
                    gs = (p * (gp - delta)).astype(BF16)
                    gq.append(nn(gs, k) * (1.0 / math.sqrt(DH)))
                    gk.append(tn(gs, q) * (1.0 / math.sqrt(DH)))
                    gv.append(tn(low, gc))
                grow = jnp.concatenate(gq + gk + gv, axis=1).astype(BF16)
                grow_s[at, :] = grow
                return carry + jnp.sum(grow.astype(F32), axis=0, keepdims=True)

            line = lax.fori_loop(0, passages, one, jnp.zeros((1, 3 * width), F32))
            line = jnp.concatenate([line, jnp.zeros((1, model - 3 * width), F32)], axis=1)
            sum_ref[pl.ds(row_of(parts[j], meta_ref, 1), 1), :] = line
            for wait in later[j]:
                wait.wait()
            out_s[j, : 3 * width, :] = tn(grow_s[...], x_s[...]).astype(BF16)
            copies.out(out_s.at[j], out)
            acc_s[...] = acc_s[...] + nn(grow_s[...], w_s[j, : 3 * width, :])
        copies.out(acc_s, acc_out)
        copies.drain()

    inputs = [(SCALARS, meta), (WHOLE, sums)]
    inputs += [(HBM, v) for v in (x, grad_attn, *qkvs, *ctxs, *probs, *w_pair, start)]
    outputs = [(HBM, shape((4 * width, model), BF16))] * 2
    outputs += [(WHOLE, shape((16, model), F32)), (HBM, shape((rows, model), F32))]
    scratch = [pltpu.VMEM((rows, model), BF16), pltpu.VMEM((rows, model), BF16)]
    scratch += [pltpu.VMEM(v[0].shape, BF16) for v in (qkvs, ctxs, probs)]
    scratch += [pltpu.VMEM((2, 4 * width, model), BF16), pltpu.VMEM((rows, model), F32)]
    scratch += [pltpu.VMEM((rows, 3 * width), BF16), pltpu.VMEM((2, 4 * width, model), BF16)]
    scratch += [pltpu.VMEM((rows, width), BF16)]
    return call(kernel, "attend_back_pair", inputs, outputs, scratch, 20, 200 * 10**9)


def tie(value, *others):
    return lax.optimization_barrier((value, *others))[0]


def flat_perm(move):
    pairs = []
    for z in range(4):
        for y in range(2):
            for x in range(2):
                for c in range(2):
                    z2, y2, x2, c2 = move(z, y, x, c)
                    pairs.append((((z * 2 + y) * 2 + x) * 2 + c, ((z2 * 2 + y2) * 2 + x2) * 2 + c2))
    return pairs


def add(one, two):
    return (one.astype(F32) + two.astype(F32)).astype(BF16)


ORDER = "uvibsuvibusvsisubsvuivusvi"


class GridMoves:
    def __init__(self):
        self.row = lax.axis_index("batch") % 2
        self.layer = lax.axis_index("batch") // 2 % 2
        self.side = (self.row + self.layer) % 2
        self.to_core = flat_perm(lambda z, y, x, c: (z, y, x, 1 - c))
        self.to_x = flat_perm(lambda z, y, x, c: (z, y, 1 - x, c))
        self.to_y = flat_perm(lambda z, y, x, c: (z, 1 - y, x, c))
        self.to_z = flat_perm(lambda z, y, x, c: (z ^ 1, y, x, c))
        self.to_zz = flat_perm(lambda z, y, x, c: (z ^ 2, y, x, c))
        self.mark = None

    def send(self, value, pairs):
        return lax.ppermute(value, AXES, pairs)

    def half(self, value, which):
        if isinstance(value, tuple):
            return jnp.where(which == 0, value[0], value[1])
        rows = value.shape[0] // 2
        return lax.dynamic_slice_in_dim(value, which * rows, rows, axis=0)

    def order(self, mine, other, bit):
        low = jnp.where(bit == 0, mine, other)
        high = jnp.where(bit == 0, other, mine)
        return jnp.concatenate([low, high], axis=0)

    def after(self, value):
        if self.mark is not None:
            value = tie(value, self.mark)
        return value

    def pieces(self, mine):
        first, second = self.halves(mine)
        return [self.send(first, self.to_y), self.send(second, self.to_z)]

    def whole(self, mine, pieces):
        return self.order(mine, jnp.concatenate(pieces, axis=0), self.side)

    def halves(self, value):
        rows = value.shape[0] // 2
        return value[:rows], value[rows:]

    def chain(self, near, got):
        got = tuple(self.after(part) for part in got)
        got = got if len(got) == 2 else got[0]
        pass_on = add(self.half(near, 1 - self.row), self.half(got, 1 - self.row))
        keep = add(self.half(near, self.row), self.half(got, self.row))
        got = self.send(pass_on, self.to_y)
        yield pass_on
        yield from self.chain_z(add(keep, self.after(got)))

    def chain_zy(self, near, got):
        got = tuple(self.after(part) for part in got)
        pass_on = add(self.half(near, 1 - self.layer), self.half(got, 1 - self.layer))
        keep = add(self.half(near, self.layer), self.half(got, self.layer))
        got = self.send(pass_on, self.to_z)
        yield pass_on
        keep = add(keep, self.after(got))
        pass_on = self.half(keep, 1 - self.row)
        keep = self.half(keep, self.row)
        got = self.send(pass_on, self.to_y)
        yield pass_on
        keep = add(keep, self.after(got))
        got = self.send(keep, self.to_zz)
        yield keep
        keep = add(keep, self.after(got))
        got = self.send(keep, self.to_y)
        yield keep
        keep = self.order(keep, self.after(got), self.row)
        got = self.send(keep, self.to_z)
        yield keep
        yield self.order(keep, self.after(got), self.layer).astype(F32)

    def chain_y(self, near, far):
        pass_on = jnp.concatenate(
            [self.half(near, 1 - self.row), self.half(far, 1 - self.row)], axis=0
        )
        got = self.send(pass_on, self.to_y)
        yield pass_on
        got = self.halves(self.after(got))
        far = add(self.half(far, self.row), got[1])
        keep = add(self.half(near, self.row), got[0])
        got = self.send(far, self.to_x)
        yield far
        yield from self.chain_z(add(keep, self.after(got)))

    def chain_z(self, keep):
        pass_on = self.half(keep, 1 - self.layer)
        keep = self.half(keep, self.layer)
        got = self.send(pass_on, self.to_z)
        yield pass_on
        keep = add(keep, self.after(got))
        got = self.send(keep, self.to_zz)
        yield keep
        keep = add(keep, self.after(got))
        got = self.send(keep, self.to_z)
        yield keep
        keep = self.order(keep, self.after(got), self.layer)
        got = self.send(keep, self.to_y)
        yield keep
        yield self.order(keep, self.after(got), self.row).astype(F32)

    def chain_small(self, value):
        for pairs in (self.to_core, self.to_x, self.to_y, self.to_z, self.to_zz):
            got = self.send(value, pairs)
            yield value
            value = value + self.after(got)
        yield value

    def step(self, chain):
        self.mark = next(chain)
        return self.mark


def body(
    tokens,
    passage_lengths,
    cotangent,
    w_qkv,
    b_query,
    b_value,
    w_out,
    b_out,
    gain_one,
    shift_one,
    w_in,
    b_in,
    w_back,
    b_back,
    gain_two,
    shift_two,
):
    micro_count, own_rows, model = tokens.shape
    tp_count = lax.axis_size("tp")
    batch_count = lax.axis_size("batch")
    plen = own_rows * tp_count // passage_lengths.shape[1]
    own_passages = own_rows // plen
    assert own_passages * plen == own_rows and tp_count == 4
    grid = (batch_count, tp_count) == (8, 4)
    width = w_qkv.shape[2]
    rows = micro_count * own_rows
    position = lax.axis_index("tp")

    vector = lambda v: v.reshape(1, -1)
    x = tokens.reshape(rows, model)
    dy = cotangent.reshape(rows, model)
    lengths = lax.dynamic_slice_in_dim(
        passage_lengths, position * own_passages, own_passages, axis=1
    ).reshape(micro_count * own_passages)
    meta = jnp.concatenate([lengths, (position if grid else 0 * position).reshape(1)])
    qkvo = jnp.concatenate([jnp.transpose(w_qkv, (1, 2, 0)).reshape(3 * width, model), w_out], axis=0)
    small = vector(jnp.concatenate([b_in.astype(F32), b_query, jnp.zeros_like(b_query), b_value]))
    if grid:
        m = moves = GridMoves()
        x_att = m.send(m.half(qkvo, m.side), m.to_x)
        c_att = m.send(qkvo, m.to_core)
        c_small = m.send(small, m.to_core)
        x_small = m.send(small, m.to_x)
        half_in = m.half(w_in, m.side)
        meta = tie(meta, half_in)
        att, smalls = [qkvo, c_att], [small, c_small]
    else:
        att, smalls, ins, backs = [
            list(lax.all_gather(v, "tp", axis=0)) for v in (qkvo, small, w_in, w_back)
        ]
    qkv_near, ctx_near, p_near, acc = attend_pair(x, plen, att[:2], smalls[:2], meta)
    y = x
    if grid:
        x_att, x_small = tie(x_att, acc), tie(x_small, acc)
        y_att = m.send(x_att, m.to_y)
        half_back = m.half(w_back, m.side)
        x_in = m.send(tie(half_in, x_att), m.to_x)
        smalls += [x_small, m.send(x_small, m.to_core)]
        y_att = tie(y_att, half_back, smalls[3])
        f_att = m.order(x_att, y_att, m.side)
        att += [f_att, m.send(f_att, m.to_core)]
        c_in = m.send(tie(w_in, f_att), m.to_core)
        c_back = m.send(tie(w_back, f_att), m.to_core)
        x_in = tie(x_in, f_att)
        y_in = m.send(x_in, m.to_y)
        x_back = m.send(tie(half_back, x_in), m.to_x)
        y = tie(x, x_in)
    qkv_far, ctx_far, p_far, unit, inverse, low = attend_pair(
        y, plen, att[2:], smalls[2:], meta, acc, [vector(v) for v in (b_out, gain_one, shift_one)]
    )
    if grid:
        y_in = tie(y_in, low)
        f_in = m.order(x_in, y_in, m.side)
        ins = [w_in, c_in, f_in, m.send(f_in, m.to_core)]
        x_back = tie(x_back, f_in)
        p_back = m.pieces(x_back)
        backs = [w_back, c_back]
        low = tie(low, x_back)
    act_near, slope_near, feed_near = feed_pair(low, ins[:2], backs[:2], smalls[:2])
    if grid:
        p_back[0] = tie(p_back[0], feed_near)
        f_back = m.whole(x_back, p_back)
        backs += [f_back, m.send(f_back, m.to_core)]
    layer_out, grad_two, grad_ffn, sums, slope_far, b_far, b_farc = turn_pair(
        low,
        ins[2:],
        backs[2:],
        smalls[2:],
        unit,
        feed_near,
        dy,
        meta,
        [vector(v) for v in (gain_one, shift_one, b_back, gain_two, shift_two)],
        plen,
    )
    if grid:
        got_b3 = m.send(b_farc, m.to_core)
    b_own, b_core = outer_pair(act_near, grad_ffn)
    if grid:
        got_b1 = m.send(b_core, m.to_core)
        b_far = add(b_far, tie(got_b3, b_own))
        got_bx = [m.send(part, m.to_x) for part in m.halves(b_far)]
        grad_ffn = tie(grad_ffn, b_far)
    slopes = (slope_near, slope_far)
    feed_sent = [(v[1], v[3]) for v in (ins, backs)]
    feed_kept = [(v[0], v[2]) for v in (ins, backs)]
    i_core, i_farc, sums, normed = feed_back_pair(
        grad_ffn, slopes, 1, *feed_sent, low, grad_two, (1, 3), sums, meta
    )
    if grid:
        got_i1, got_i3 = [m.send(v, m.to_core) for v in (i_core, i_farc)]
        b_near = add(b_own, tie(got_b1, normed))
        got_bx[0] = tie(got_bx[0], b_near)
        normed = tie(normed, got_bx[0])
    i_own, i_far, sums, grad_one, grad_attn = feed_back_pair(
        grad_ffn,
        slopes,
        0,
        *feed_kept,
        low,
        normed,
        (0, 2),
        sums,
        meta,
        unit,
        inverse,
        vector(gain_one),
    )
    if grid:
        i_far = add(i_far, tie(got_i3, grad_attn))
        got_ix = [m.send(part, m.to_x) for part in m.halves(i_far)]
        m.mark = i_far
        chain_b = m.chain(b_near, got_bx)
        m.step(chain_b)
        grad_attn = tie(grad_attn, m.mark)
    kept = [(qkv_near, qkv_far), (ctx_near, ctx_far), (p_near, p_far)]
    a_core, a_farc, sums, grad_x = attend_back_pair(
        x, plen, grad_attn, *kept, 1, (att[1], att[3]), grad_one, (1, 3), sums, meta
    )
    if grid:
        got_a1, got_a3 = [m.send(v, m.to_core) for v in (a_core, a_farc)]
        i_near = add(i_own, tie(got_i1, grad_x))
        m.mark = i_near
        m.step(chain_b)
        got_ix[0] = m.after(got_ix[0])
        grad_x = tie(grad_x, got_ix[0])
    a_own, a_far, packed, grad_x = attend_back_pair(
        x, plen, grad_attn, *kept, 0, (att[0], att[2]), grad_x, (0, 2), sums, meta
    )
    if grid:
        m.mark = grad_x
        a_far = m.halves(add(a_far, m.after(got_a3)))
        got_ax = m.send(a_far[0], m.to_x)
        m.mark = a_far[0]
        a_near = m.halves(add(a_own, m.after(got_a1)))
        m.mark = a_near[0]
        chains = {"b": chain_b, "i": m.chain_zy(i_near, got_ix), "v": m.chain_y(a_near[1], a_far[1])}
        done = {}
        for key in "vib":
            done[key] = m.step(chains[key])
        chains["u"] = m.chain(a_near[0], [got_ax])
        chains["s"] = m.chain_small(m.after(packed))
        for key in ORDER:
            done[key] = m.step(chains[key])
        g_back, g_in, packed = done["b"], done["i"], done["s"]
        g_att = jnp.concatenate([done["u"], done["v"]], axis=0)
    else:
        g_back, g_in, g_att = [
            lax.psum(
                lax.psum_scatter(jnp.stack(parts).astype(F32), "tp", scatter_dimension=0), "batch"
            )
            for parts in (
                (b_own, b_core, b_far, b_farc),
                (i_own, i_core, i_far, i_farc),
                (a_own, a_core, a_far, a_farc),
            )
        ]
        packed = lax.psum(packed, AXES)
    mine = lax.dynamic_slice_in_dim(packed, 2 * position, 2, axis=0)
    return (
        layer_out.reshape(tokens.shape),
        grad_x.reshape(tokens.shape),
        jnp.transpose(g_att[: 3 * width].reshape(3, width, model), (2, 0, 1)),
        mine[1, :width],
        mine[1, 2 * width : 3 * width],
        g_att[3 * width :],
        packed[11],
        packed[12],
        packed[13],
        g_in,
        mine[0],
        g_back,
        packed[10],
        packed[8],
        packed[9],
    )


def solution(mesh):
    in_specs = (
        P(None, ("batch", "tp"), None),
        P(None, "batch"),
        P(None, ("batch", "tp"), None),
        P(None, None, "tp"),
        P("tp"),
        P("tp"),
        P("tp", None),
        P(),
        P(),
        P(),
        P(None, "tp"),
        P("tp"),
        P("tp", None),
        P(),
        P(),
        P(),
    )
    out_specs = (
        P(None, ("batch", "tp"), None),
        P(None, ("batch", "tp"), None),
        P(None, None, "tp"),
        P("tp"),
        P("tp"),
        P("tp", None),
        P(),
        P(),
        P(),
        P(None, "tp"),
        P("tp"),
        P("tp", None),
        P(),
        P(),
        P(),
    )
    return jax.shard_map(body, mesh=mesh, in_specs=in_specs, out_specs=out_specs, check_vma=False)
```

```python
import math

import jax
import jax.numpy as jnp
from jax import lax
from jax.experimental import pallas as pl
from jax.experimental.pallas import tpu as pltpu
from jax.sharding import PartitionSpec as P

DH = 64
AXES = ("batch", "tp")
epsilon = 1e-05
F32 = jnp.float32
BF16 = jnp.bfloat16


def nt(a, b):
    return lax.dot_general(a, b, (((1,), (1,)), ((), ())), preferred_element_type=F32)


def tn(a, b):
    return lax.dot_general(a, b, (((0,), (0,)), ((), ())), preferred_element_type=F32)


def nn(a, b):
    return jnp.dot(a, b, preferred_element_type=F32)


HBM = pl.BlockSpec(memory_space=pl.ANY)
WHOLE = pl.BlockSpec(memory_space=pltpu.VMEM)
SCALARS = pl.BlockSpec(memory_space=pltpu.SMEM)


class Copies:
    def __init__(self, sems):
        self.sems, self.used = sems, 0
        self.pending = []

    def start(self, src, dst):
        copy = pltpu.make_async_copy(src, dst, self.sems.at[self.used])
        self.used += 1
        copy.start()
        return copy

    def out(self, src, dst):
        self.pending.append(self.start(src, dst))

    def drain(self):
        for copy in self.pending:
            copy.wait()


def call(kernel, name, inputs, outputs, scratch, copies, cost=1000):
    in_specs = [spec for spec, _ in inputs]
    return pl.pallas_call(
        kernel,
        name=name,
        in_specs=in_specs,
        out_specs=tuple(spec for spec, _ in outputs),
        out_shape=tuple(shape for _, shape in outputs),
        scratch_shapes=list(scratch) + [pltpu.SemaphoreType.DMA((copies,))],
        cost_estimate=pl.CostEstimate(flops=cost, transcendentals=0, bytes_accessed=0),
    )(*[value for _, value in inputs])


def shape(dims, dtype):
    return jax.ShapeDtypeStruct(dims, dtype)


def block(i, size):
    return pl.ds(pl.multiple_of(i * size, size), size)


def unit_norm(v):
    middle = jnp.mean(v, axis=-1, keepdims=True)
    centred = v - middle
    inverse = lax.rsqrt(jnp.mean(centred * centred, axis=-1, keepdims=True) + epsilon)
    return centred * inverse, inverse


def norm_grad(scaled, unit, inverse):
    mean_one = jnp.mean(scaled, axis=-1, keepdims=True)
    mean_two = jnp.mean(scaled * unit, axis=-1, keepdims=True)
    return inverse * (scaled - mean_one - unit * mean_two)


STEP = 128


def row_of(part, meta_ref, kind):
    return 2 * jnp.bitwise_xor(part, meta_ref[meta_ref.shape[0] - 1]) + kind


def attend_pair(x, plen, w_pair, smalls, meta, acc=None, vectors=None):
    rows, model = x.shape
    passages = rows // plen
    width = w_pair[0].shape[0] // 4
    heads = width // DH
    units = smalls[0].shape[1] - 3 * width
    last = acc is not None

    def kernel(meta_ref, x_hbm, wa, wb, bias_a, bias_b, *rest):
        if last:
            acc_hbm, b_out, gain, shift = rest[:4]
            qkv_hbm, ctx_hbm, p_hbm, unit_hbm, inv_hbm, low_hbm = rest[4:10]
            x_s, w_s, qkv_s, ctx_s, p_s, acc_s, inv_s, low_s, sems = rest[10:]
        else:
            qkv_hbm, ctx_hbm, p_hbm, acc_out = rest[:4]
            x_s, w_s, qkv_s, ctx_s, p_s, acc_s, sems = rest[4:]
        copies = Copies(sems)
        first = [copies.start(x_hbm, x_s), copies.start(wa, w_s.at[0])]
        second = [copies.start(wb, w_s.at[1])]
        if last:
            held = copies.start(acc_hbm, acc_s)
        for j, waits, bias in ((0, first, bias_a), (1, second, bias_b)):
            for copy in waits:
                copy.wait()
            qkv_s[j] = (nt(x_s[...], w_s[j, : 3 * width, :]) + bias[0:1, units:]).astype(BF16)
            copies.out(qkv_s.at[j], qkv_hbm.at[j])

            def one(g, carry, j=j):
                at = block(g, plen)
                qkv = qkv_s[j, at, :]
                keep = lax.broadcasted_iota(jnp.int32, (1, plen), 1) < meta_ref[g]
                ctx = []
                for h in range(heads):
                    q = qkv[:, h * DH : (h + 1) * DH] * (1.0 / math.sqrt(DH))
                    k = qkv[:, width + h * DH : width + (h + 1) * DH]
                    v = qkv[:, 2 * width + h * DH : 2 * width + (h + 1) * DH]
                    s = jnp.where(keep, nt(q.astype(BF16), k), -1000000000.0)
                    e = jnp.exp(s - jnp.max(s, axis=-1, keepdims=True))
                    p = (e * (1.0 / jnp.sum(e, axis=-1, keepdims=True))).astype(BF16)
                    p_s[j, g * heads + h] = p
                    ctx.append(nn(p, v))
                ctx_s[j, at, :] = jnp.concatenate(ctx, axis=1).astype(BF16)
                return carry

            lax.fori_loop(0, passages, one, 0)
            copies.out(ctx_s.at[j], ctx_hbm.at[j])
            copies.out(p_s.at[j], p_hbm.at[j])
            term = nn(ctx_s[j], w_s[j, 3 * width :, :])
            if last and j == 0:
                held.wait()
            acc_s[...] = term if j == 0 and not last else acc_s[...] + term
        if last:

            def finish(i, carry):
                at = block(i, STEP)
                v = x_s[at, :].astype(F32) + acc_s[at, :] + b_out[...]
                unit, inverse = unit_norm(v)
                acc_s[at, :] = unit
                inv_s[at, :] = jnp.broadcast_to(inverse, (STEP, 128))
                low_s[at, :] = (unit * gain[...] + shift[...]).astype(BF16)
                return carry

            lax.fori_loop(0, rows // STEP, finish, 0)
            copies.out(acc_s, unit_hbm)
            copies.out(inv_s, inv_hbm)
            copies.out(low_s, low_hbm)
        else:
            copies.out(acc_s, acc_out)
        copies.drain()

    inputs = [(SCALARS, meta), (HBM, x), (HBM, w_pair[0]), (HBM, w_pair[1])]
    inputs += [(WHOLE, v) for v in smalls]
    dims = [(2, rows, 3 * width), (2, rows, width), (2, passages * heads, plen, plen)]
    outputs = [(HBM, shape(d, BF16)) for d in dims]
    scratch = [pltpu.VMEM((rows, model), BF16), pltpu.VMEM((2, 4 * width, model), BF16)]
    scratch += [pltpu.VMEM(d, BF16) for d in dims]
    scratch += [pltpu.VMEM((rows, model), F32)]
    if last:
        inputs += [(HBM, acc)] + [(WHOLE, v) for v in vectors]
        outputs += [(HBM, shape((rows, model), F32)), (HBM, shape((rows, 128), F32))]
        outputs += [(HBM, shape((rows, model), BF16))]
        scratch += [pltpu.VMEM((rows, 128), F32), pltpu.VMEM((rows, model), BF16)]
    else:
        outputs += [(HBM, shape((rows, model), F32))]
    return call(kernel, "attend_pair", inputs, outputs, scratch, 16, 1000 if last else 200 * 10**9)


def feed(j, low_s, i_s, b_s, bias, act_s, slope_s):
    units = act_s.shape[2]
    for c in range(0, units, 256):
        cols = slice(c, c + 256)
        t = nn(low_s[...], i_s[j, :, cols]) + bias[0:1, cols]
        cdf = 0.5 * (1.0 + lax.erf(t * (1.0 / math.sqrt(2.0))))
        pdf = jnp.exp(-0.5 * t * t) * (1.0 / math.sqrt(2.0 * math.pi))
        act_s[j, :, cols] = (t * cdf).astype(BF16)
        slope_s[j, :, cols] = (cdf + t * pdf).astype(BF16)
    return nn(act_s[j], b_s[j])


def feed_pair(low, in_pair, back_pair, smalls):
    rows, model = low.shape
    units = in_pair[0].shape[1]

    def kernel(low_hbm, ia, ib, ba, bb, bias_a, bias_b, *rest):
        act_hbm, slope_hbm, acc_hbm, low_s, i_s, b_s, act_s, slope_s, acc_s, sems = rest
        copies = Copies(sems)
        first = [copies.start(low_hbm, low_s), copies.start(ia, i_s.at[0]), copies.start(ba, b_s.at[0])]
        second = [copies.start(ib, i_s.at[1]), copies.start(bb, b_s.at[1])]
        for j, waits, bias in ((0, first, bias_a), (1, second, bias_b)):
            for copy in waits:
                copy.wait()
            term = feed(j, low_s, i_s, b_s, bias, act_s, slope_s)
            copies.out(act_s.at[j], act_hbm.at[j])
            copies.out(slope_s.at[j], slope_hbm.at[j])
            acc_s[...] = acc_s[...] + term if j else term
        copies.out(acc_s, acc_hbm)
        copies.drain()

    inputs = [(HBM, v) for v in (low, *in_pair, *back_pair)] + [(WHOLE, v) for v in smalls]
    outputs = [(HBM, shape((2, rows, units), BF16))] * 2 + [(HBM, shape((rows, model), F32))]
    scratch = [pltpu.VMEM((rows, model), BF16), pltpu.VMEM((2, model, units), BF16)]
    scratch += [pltpu.VMEM((2, units, model), BF16)] + [pltpu.VMEM((2, rows, units), BF16)] * 2
    scratch += [pltpu.VMEM((rows, model), F32)]
    return call(kernel, "feed_pair", inputs, outputs, scratch, 12)


def turn_pair(low, in_pair, back_pair, smalls, unit, acc, dy, meta, vectors, plen):
    rows, model = low.shape
    units = in_pair[0].shape[1]

    def kernel(meta_ref, low_hbm, ia, ib, ba, bb, unit_hbm, acc_hbm, dy_hbm, bias_a, bias_b, *rest):
        gain_one, shift_one, b_back, gain_two, shift_two = rest[:5]
        out_hbm, grad_hbm, ffn_hbm, sum_ref, slope_hbm, oa, ob = rest[5:12]
        low_s, i_s, b_s, act_s, slope_s, acc_s, unit_s, dy_s, out_s, grad_s, ffn_s, g_s, sems = rest[12:]
        copies = Copies(sems)
        first = [copies.start(low_hbm, low_s), copies.start(ia, i_s.at[0]), copies.start(ba, b_s.at[0])]
        second = [copies.start(ib, i_s.at[1]), copies.start(bb, b_s.at[1]), copies.start(acc_hbm, acc_s)]
        third = [copies.start(unit_hbm, unit_s), copies.start(dy_hbm, dy_s)]
        for copy in first:
            copy.wait()
        term = feed(0, low_s, i_s, b_s, bias_a, act_s, slope_s)
        copies.out(slope_s.at[0], slope_hbm.at[0])
        for copy in second:
            copy.wait()
        acc_s[...] = acc_s[...] + term
        acc_s[...] = acc_s[...] + feed(1, low_s, i_s, b_s, bias_b, act_s, slope_s)
        copies.out(slope_s.at[1], slope_hbm.at[1])
        for copy in third:
            copy.wait()
        sum_ref[...] = jnp.zeros_like(sum_ref)

        def step(i, carry):
            at = block(i, STEP)
            normed = unit_s[at, :] * gain_one[...] + shift_one[...]
            u, inverse = unit_norm(normed + acc_s[at, :] + b_back[...])
            out_s[at, :] = (u * gain_two[...] + shift_two[...]).astype(BF16)
            slot = lax.broadcasted_iota(jnp.int32, (STEP, 1), 0) + (i * STEP) % plen
            keep = slot < meta_ref[(i * STEP) // plen]
            grad_y = jnp.where(keep, dy_s[at, :].astype(F32), 0.0)
            grad = norm_grad(grad_y * gain_two[...], u, inverse)
            grad_s[at, :] = grad
            ffn_s[at, :] = grad.astype(BF16)
            sum_ref[8:9, :] += jnp.sum(grad_y * u, axis=0, keepdims=True)
            sum_ref[9:10, :] += jnp.sum(grad_y, axis=0, keepdims=True)
            sum_ref[10:11, :] += jnp.sum(grad, axis=0, keepdims=True)
            return carry

        lax.fori_loop(0, rows // STEP, step, 0)
        copies.out(out_s, out_hbm)
        copies.out(grad_s, grad_hbm)
        copies.out(ffn_s, ffn_hbm)
        for j, out in ((1, ob), (0, oa)):
            g_s[j] = tn(act_s[j], ffn_s[...]).astype(BF16)
            copies.out(g_s.at[j], out)
        copies.drain()

    inputs = [(SCALARS, meta)] + [(HBM, v) for v in (low, *in_pair, *back_pair, unit, acc, dy)]
    inputs += [(WHOLE, v) for v in (*smalls, *vectors)]
    outputs = [(HBM, shape((rows, model), d)) for d in (BF16, F32, BF16)]
    outputs += [(WHOLE, shape((16, model), F32)), (HBM, shape((2, rows, units), BF16))]
    outputs += [(HBM, shape((units, model), BF16))] * 2
    scratch = [pltpu.VMEM((rows, model), BF16), pltpu.VMEM((2, model, units), BF16)]
    scratch += [pltpu.VMEM((2, units, model), BF16)] + [pltpu.VMEM((2, rows, units), BF16)] * 2
    scratch += [pltpu.VMEM((rows, model), d) for d in (F32, F32, BF16, BF16, F32, BF16)]
    scratch += [pltpu.VMEM((2, units, model), BF16)]
    return call(kernel, "turn_pair", inputs, outputs, scratch, 20)


def outer_pair(acts, grad_ffn):
    _, rows, units = acts.shape
    model = grad_ffn.shape[1]

    def kernel(act_hbm, g_hbm, oa, ob, act_s, g_s, out_s, sems):
        copies = Copies(sems)
        whole = copies.start(g_hbm, g_s)
        waits = [copies.start(act_hbm.at[j], act_s.at[j]) for j in (1, 0)]
        whole.wait()
        for j, wait, out in ((1, waits[0], ob), (0, waits[1], oa)):
            wait.wait()
            out_s[j] = tn(act_s[j], g_s[...]).astype(BF16)
            copies.out(out_s.at[j], out)
        copies.drain()

    inputs = [(HBM, acts), (HBM, grad_ffn)]
    outputs = [(HBM, shape((units, model), BF16))] * 2
    scratch = [pltpu.VMEM((2, rows, units), BF16), pltpu.VMEM((rows, model), BF16)]
    scratch += [pltpu.VMEM((2, units, model), BF16)]
    return call(kernel, "outer_pair", inputs, outputs, scratch, 8, 200 * 10**9)


def feed_back_pair(grad_ffn, slopes, which, in_pair, back_pair, low, start, parts, sums, meta, unit=None, inverse=None, gain=None):
    rows, model = grad_ffn.shape
    units = slopes[0].shape[2]
    last = unit is not None

    def kernel(meta_ref, before, g_hbm, sa, sb, ia, ib, ba, bb, low_hbm, start_hbm, *rest):
        if last:
            unit_hbm, inv_hbm, gain_ref = rest[:3]
            rest = rest[3:]
            oa, ob, sum_ref, one_hbm, attn_hbm = rest[:5]
            g_s, slope_s, i_s, b_s, low_s, acc_s, pre_s, out_s, line, unit_s, inv_s, attn_s, sems = rest[5:]
        else:
            oa, ob, sum_ref, acc_out = rest[:4]
            g_s, slope_s, i_s, b_s, low_s, acc_s, pre_s, out_s, line, sems = rest[4:]
        copies = Copies(sems)
        sum_ref[...] = before[...]
        weights = {1: (bb, ib, sb.at[which]), 0: (ba, ia, sa.at[which])}
        early = copies.start(g_hbm, g_s)
        waits, later = {}, {}
        for j in (1, 0):
            waits[j] = [copies.start(weights[j][0], b_s.at[j]), copies.start(weights[j][2], slope_s.at[j])]
            later[j] = [copies.start(weights[j][1], i_s.at[j])]
            if j == 1:
                later[j] += [copies.start(low_hbm, low_s), copies.start(start_hbm, acc_s)]
        if last:
            late = [copies.start(unit_hbm, unit_s), copies.start(inv_hbm, inv_s)]
        early.wait()
        for j, out in ((1, ob), (0, oa)):
            for wait in waits[j]:
                wait.wait()
            for c in range(0, units, 256):
                cols = slice(c, c + 256)
                pre = nt(g_s[...], b_s[j, cols, :]) * slope_s[j, :, cols].astype(F32)
                pre = pre.astype(BF16)
                pre_s[:, cols] = pre
                line[:, cols] = jnp.sum(pre.astype(F32), axis=0, keepdims=True)
            sum_ref[pl.ds(row_of(parts[j], meta_ref, 0), 1), :] = line[...]
            for wait in later[j]:
                wait.wait()
            acc_s[...] = acc_s[...] + nt(pre_s[...], i_s[j])
            out_s[j] = tn(low_s[...], pre_s[...]).astype(BF16)
            copies.out(out_s.at[j], out)
        if last:
            for wait in late:
                wait.wait()

            def finish(i, carry):
                at = block(i, STEP)
                normed = acc_s[at, :]
                u = unit_s[at, :]
                grad = norm_grad(normed * gain_ref[0:1, :], u, inv_s[at, 0:1])
                sum_ref[11:12, :] += jnp.sum(grad, axis=0, keepdims=True)
                sum_ref[12:13, :] += jnp.sum(normed * u, axis=0, keepdims=True)
                sum_ref[13:14, :] += jnp.sum(normed, axis=0, keepdims=True)
                acc_s[at, :] = grad
                attn_s[at, :] = grad.astype(BF16)
                return carry

            lax.fori_loop(0, rows // STEP, finish, 0)
            copies.out(acc_s, one_hbm)
            copies.out(attn_s, attn_hbm)
        else:
            copies.out(acc_s, acc_out)
        copies.drain()

    inputs = [(SCALARS, meta), (WHOLE, sums)]
    inputs += [(HBM, v) for v in (grad_ffn, *slopes, *in_pair, *back_pair, low, start)]
    outputs = [(HBM, shape((model, units), BF16))] * 2 + [(WHOLE, shape((16, model), F32))]
    outputs += [(HBM, shape((rows, model), F32))]
    scratch = [pltpu.VMEM((rows, model), BF16), pltpu.VMEM((2, rows, units), BF16)]
    scratch += [pltpu.VMEM((2, model, units), BF16), pltpu.VMEM((2, units, model), BF16)]
    scratch += [pltpu.VMEM((rows, model), BF16), pltpu.VMEM((rows, model), F32)]
    scratch += [pltpu.VMEM((rows, units), BF16), pltpu.VMEM((2, model, units), BF16)]
    scratch += [pltpu.VMEM((1, units), F32)]
    if last:
        inputs += [(HBM, unit), (HBM, inverse), (WHOLE, gain)]
        outputs += [(HBM, shape((rows, model), BF16))]
        scratch += [pltpu.VMEM((rows, model), F32), pltpu.VMEM((rows, 128), F32)]
        scratch += [pltpu.VMEM((rows, model), BF16)]
    return call(kernel, "feed_back_pair", inputs, outputs, scratch, 20, 200 * 10**9)


def attend_back_pair(x, plen, grad_attn, qkvs, ctxs, probs, which, w_pair, start, parts, sums, meta):
    rows, model = x.shape
    passages = rows // plen
    width = ctxs[0].shape[2]
    heads = width // DH

    def kernel(meta_ref, before, x_hbm, g_hbm, qa, qb, ca, cb, pa, pb, wa, wb, start_hbm, *rest):
        oa, ob, sum_ref, acc_out = rest[:4]
        x_s, g_s, qkv_s, ctx_s, p_s, w_s, acc_s, grow_s, out_s, gc_s, sems = rest[4:]
        copies = Copies(sems)
        sum_ref[...] = before[...]
        early = [copies.start(g_hbm, g_s)]
        of = {0: (wa, ca, qa, pa), 1: (wb, cb, qb, pb)}
        waits, middle, later = {}, {}, {}
        for j in (1, 0):
            waits[j] = [copies.start(of[j][0], w_s.at[j]), copies.start(of[j][1].at[which], ctx_s.at[j])]
            middle[j] = [copies.start(of[j][2].at[which], qkv_s.at[j]), copies.start(of[j][3].at[which], p_s.at[j])]
            later[j] = []
            if j == 1:
                later[j] = [copies.start(x_hbm, x_s), copies.start(start_hbm, acc_s)]
        for wait in early:
            wait.wait()
        for j, out in ((1, ob), (0, oa)):
            for wait in waits[j]:
                wait.wait()
            gc_s[...] = nt(g_s[...], w_s[j, 3 * width :, :]).astype(BF16)
            out_s[j, 3 * width :, :] = tn(ctx_s[j], g_s[...]).astype(BF16)
            for wait in middle[j]:
                wait.wait()

            def one(g, carry, j=j):
                at = block(g, plen)
                qkv = qkv_s[j, at, :]
                grad_ctx = gc_s[at, :]
                gq, gk, gv = [], [], []
                for h in range(heads):
                    q = qkv[:, h * DH : (h + 1) * DH]
                    k = qkv[:, width + h * DH : width + (h + 1) * DH]
                    v = qkv[:, 2 * width + h * DH : 2 * width + (h + 1) * DH]
                    gc = grad_ctx[:, h * DH : (h + 1) * DH]
                    low = p_s[j, g * heads + h]
                    p = low.astype(F32)
                    gp = nt(gc, v)
                    delta = jnp.sum(p * gp, axis=-1, keepdims=True)
                    gs = (p * (gp - delta)).astype(BF16)
                    gq.append(nn(gs, k) * (1.0 / math.sqrt(DH)))
                    gk.append(tn(gs, q) * (1.0 / math.sqrt(DH)))
                    gv.append(tn(low, gc))
                grow = jnp.concatenate(gq + gk + gv, axis=1).astype(BF16)
                grow_s[at, :] = grow
                return carry + jnp.sum(grow.astype(F32), axis=0, keepdims=True)

            line = lax.fori_loop(0, passages, one, jnp.zeros((1, 3 * width), F32))
            line = jnp.concatenate([line, jnp.zeros((1, model - 3 * width), F32)], axis=1)
            sum_ref[pl.ds(row_of(parts[j], meta_ref, 1), 1), :] = line
            for wait in later[j]:
                wait.wait()
            out_s[j, : 3 * width, :] = tn(grow_s[...], x_s[...]).astype(BF16)
            copies.out(out_s.at[j], out)
            acc_s[...] = acc_s[...] + nn(grow_s[...], w_s[j, : 3 * width, :])
        copies.out(acc_s, acc_out)
        copies.drain()

    inputs = [(SCALARS, meta), (WHOLE, sums)]
    inputs += [(HBM, v) for v in (x, grad_attn, *qkvs, *ctxs, *probs, *w_pair, start)]
    outputs = [(HBM, shape((4 * width, model), BF16))] * 2
    outputs += [(WHOLE, shape((16, model), F32)), (HBM, shape((rows, model), F32))]
    scratch = [pltpu.VMEM((rows, model), BF16), pltpu.VMEM((rows, model), BF16)]
    scratch += [pltpu.VMEM(v[0].shape, BF16) for v in (qkvs, ctxs, probs)]
    scratch += [pltpu.VMEM((2, 4 * width, model), BF16), pltpu.VMEM((rows, model), F32)]
    scratch += [pltpu.VMEM((rows, 3 * width), BF16), pltpu.VMEM((2, 4 * width, model), BF16)]
    scratch += [pltpu.VMEM((rows, width), BF16)]
    return call(kernel, "attend_back_pair", inputs, outputs, scratch, 20, 200 * 10**9)


def tie(value, *others):
    return lax.optimization_barrier((value, *others))[0]


def flat_perm(move):
    pairs = []
    for z in range(4):
        for y in range(2):
            for x in range(2):
                for c in range(2):
                    z2, y2, x2, c2 = move(z, y, x, c)
                    pairs.append((((z * 2 + y) * 2 + x) * 2 + c, ((z2 * 2 + y2) * 2 + x2) * 2 + c2))
    return pairs


def add(*terms):
    return sum(term.astype(F32) for term in terms).astype(BF16)


ORDER = "susibuvibusvvibusvuisvusvi"


class GridMoves:
    def __init__(self):
        self.row = lax.axis_index("batch") % 2
        self.layer = lax.axis_index("batch") // 2 % 2
        self.side = (self.row + self.layer) % 2
        self.to_core = flat_perm(lambda z, y, x, c: (z, y, x, 1 - c))
        self.to_x = flat_perm(lambda z, y, x, c: (z, y, 1 - x, c))
        self.to_y = flat_perm(lambda z, y, x, c: (z, 1 - y, x, c))
        self.to_z = flat_perm(lambda z, y, x, c: (z ^ 1, y, x, c))
        self.to_zz = flat_perm(lambda z, y, x, c: (z ^ 2, y, x, c))
        self.mark = None

    def send(self, value, pairs):
        return lax.ppermute(value, AXES, pairs)

    def half(self, value, which):
        if isinstance(value, tuple):
            return jnp.where(which == 0, value[0], value[1])
        if isinstance(value, list):
            return add(*(self.half(term, which) for term in value))
        rows = value.shape[0] // 2
        return lax.dynamic_slice_in_dim(value, which * rows, rows, axis=0)

    def order(self, mine, other, bit):
        low = jnp.where(bit == 0, mine, other)
        high = jnp.where(bit == 0, other, mine)
        return jnp.concatenate([low, high], axis=0)

    def after(self, value):
        if self.mark is not None:
            value = tie(value, self.mark)
        return value

    def halves(self, value):
        rows = value.shape[0] // 2
        return value[:rows], value[rows:]

    def sums(self, one, two):
        return [add(a, b) for a, b in zip(self.halves(one), self.halves(two))]

    def chain(self, near, got):
        got = tuple(self.after(part) for part in got)
        got = got if len(got) == 2 else got[0]
        pass_on = self.half([*near, got], 1 - self.row)
        keep = self.half([*near, got], self.row)
        got = self.send(pass_on, self.to_y)
        yield pass_on
        yield from self.chain_z(add(keep, self.after(got)))

    def chain_zy(self, near, got):
        got = tuple(self.after(part) for part in got)
        pass_on = self.half([*near, got], 1 - self.layer)
        keep = self.half([*near, got], self.layer)
        got = self.send(pass_on, self.to_z)
        yield pass_on
        keep = add(keep, self.after(got))
        pass_on = self.half(keep, 1 - self.row)
        keep = self.half(keep, self.row)
        got = self.send(pass_on, self.to_y)
        yield pass_on
        keep = add(keep, self.after(got))
        got = self.send(keep, self.to_zz)
        yield keep
        keep = add(keep, self.after(got))
        got = self.send(keep, self.to_y)
        yield keep
        keep = self.order(keep, self.after(got), self.row)
        got = self.send(keep, self.to_z)
        yield keep
        yield self.order(keep, self.after(got), self.layer).astype(F32)

    def chain_y(self, near, far):
        pass_on = jnp.concatenate(
            [self.half(term, 1 - self.row) for term in (near, far)], axis=0
        )
        got = self.send(pass_on, self.to_y)
        yield pass_on
        got = self.halves(self.after(got))
        far = add(*(self.half(term, self.row) for term in far), got[1])
        keep = add(*(self.half(term, self.row) for term in near), got[0])
        got = self.send(far, self.to_x)
        yield far
        yield from self.chain_z(add(keep, self.after(got)))

    def chain_z(self, keep):
        pass_on = self.half(keep, 1 - self.layer)
        keep = self.half(keep, self.layer)
        got = self.send(pass_on, self.to_z)
        yield pass_on
        keep = add(keep, self.after(got))
        got = self.send(keep, self.to_zz)
        yield keep
        keep = add(keep, self.after(got))
        got = self.send(keep, self.to_z)
        yield keep
        keep = self.order(keep, self.after(got), self.layer)
        got = self.send(keep, self.to_y)
        yield keep
        yield self.order(keep, self.after(got), self.row).astype(F32)

    def chain_small(self, value):
        for pairs in (self.to_core, self.to_x, self.to_y, self.to_z, self.to_zz):
            got = self.send(value, pairs)
            yield value
            value = value + self.after(got)
        yield value

    def step(self, chain):
        self.mark = next(chain)
        return self.mark


def body(
    tokens,
    passage_lengths,
    cotangent,
    w_qkv,
    b_query,
    b_value,
    w_out,
    b_out,
    gain_one,
    shift_one,
    w_in,
    b_in,
    w_back,
    b_back,
    gain_two,
    shift_two,
):
    micro_count, own_rows, model = tokens.shape
    tp_count = lax.axis_size("tp")
    batch_count = lax.axis_size("batch")
    plen = own_rows * tp_count // passage_lengths.shape[1]
    own_passages = own_rows // plen
    assert own_passages * plen == own_rows and tp_count == 4
    grid = (batch_count, tp_count) == (8, 4)
    width = w_qkv.shape[2]
    rows = micro_count * own_rows
    position = lax.axis_index("tp")

    vector = lambda v: v.reshape(1, -1)
    x = tokens.reshape(rows, model)
    dy = cotangent.reshape(rows, model)
    lengths = lax.dynamic_slice_in_dim(
        passage_lengths, position * own_passages, own_passages, axis=1
    ).reshape(micro_count * own_passages)
    meta = jnp.concatenate([lengths, (position if grid else 0 * position).reshape(1)])
    qkvo = jnp.concatenate([jnp.transpose(w_qkv, (1, 2, 0)).reshape(3 * width, model), w_out], axis=0)
    small = vector(jnp.concatenate([b_in.astype(F32), b_query, jnp.zeros_like(b_query), b_value]))
    if grid:
        m = moves = GridMoves()
        x_att = m.send(m.half(qkvo, m.side), m.to_x)
        feed_half = jnp.concatenate([m.half(w_in, m.side), m.half(w_back, m.side)], axis=0)
        meta = tie(meta, feed_half)
        c_att = m.send(qkvo, m.to_core)
        c_small = m.send(small, m.to_core)
        x_feed = m.send(tie(feed_half, c_small), m.to_x)
        x_small = m.send(small, m.to_x)
        att, smalls = [qkvo, c_att], [small, c_small]
    else:
        att, smalls, ins, backs = [
            list(lax.all_gather(v, "tp", axis=0)) for v in (qkvo, small, w_in, w_back)
        ]
    qkv_near, ctx_near, p_near, acc = attend_pair(x, plen, att[:2], smalls[:2], meta)
    y = x
    if grid:
        x_att = tie(x_att, acc, x_small)
        y_att = m.send(x_att, m.to_y)
        xc_att = m.send(x_att, m.to_core)
        smalls += [x_small, m.send(x_small, m.to_core)]
        att += [m.order(v, w, m.side) for v, w in ((x_att, y_att), (xc_att, m.send(y_att, m.to_core)))]
        f_att = att[2]
        c_in = m.send(tie(w_in, f_att), m.to_core)
        c_back = m.send(tie(w_back, f_att), m.to_core)
        x_in, x_back = m.halves(tie(x_feed, f_att))
        y_in, z_back = m.send(x_in, m.to_y), m.send(x_back, m.to_z)
        y = tie(x, x_in)
    qkv_far, ctx_far, p_far, unit, inverse, low = attend_pair(
        y, plen, att[2:], smalls[2:], meta, acc, [vector(v) for v in (b_out, gain_one, shift_one)]
    )
    if grid:
        y_in, z_back = tie(y_in, low), tie(z_back, low)
        f_in, f_back = m.order(x_in, y_in, m.side), m.order(x_back, z_back, m.side)
        ins = [w_in, c_in, f_in, m.send(f_in, m.to_core)]
        backs = [w_back, c_back, f_back, m.send(f_back, m.to_core)]
        low = tie(low, f_in, f_back)
    act_near, slope_near, feed_near = feed_pair(low, ins[:2], backs[:2], smalls[:2])
    layer_out, grad_two, grad_ffn, sums, slope_far, b_far, b_farc = turn_pair(
        low,
        ins[2:],
        backs[2:],
        smalls[2:],
        unit,
        feed_near,
        dy,
        meta,
        [vector(v) for v in (gain_one, shift_one, b_back, gain_two, shift_two)],
        plen,
    )
    if grid:
        got_b3 = m.send(b_farc, m.to_core)
    b_own, b_core = outer_pair(act_near, grad_ffn)
    if grid:
        got_b1 = m.send(b_core, m.to_core)
        b_far = m.sums(b_far, tie(got_b3, b_own))
        got_bx = [m.send(part, m.to_x) for part in b_far]
        grad_ffn = tie(grad_ffn, *b_far)
    slopes = (slope_near, slope_far)
    feed_sent = [(v[1], v[3]) for v in (ins, backs)]
    feed_kept = [(v[0], v[2]) for v in (ins, backs)]
    i_core, i_farc, sums, normed = feed_back_pair(
        grad_ffn, slopes, 1, *feed_sent, low, grad_two, (1, 3), sums, meta
    )
    if grid:
        got_i1, got_i3 = [m.send(v, m.to_core) for v in (i_core, i_farc)]
        b_near = [b_own, tie(got_b1, normed)]
        got_bx[0] = tie(got_bx[0], normed)
        normed = tie(normed, got_bx[0])
    i_own, i_far, sums, grad_one, grad_attn = feed_back_pair(
        grad_ffn,
        slopes,
        0,
        *feed_kept,
        low,
        normed,
        (0, 2),
        sums,
        meta,
        unit,
        inverse,
        vector(gain_one),
    )
    if grid:
        i_far = m.sums(i_far, tie(got_i3, grad_attn))
        got_ix = [m.send(part, m.to_x) for part in i_far]
        m.mark = i_far[0]
        chain_b = m.chain(b_near, got_bx)
        m.step(chain_b)
        grad_attn = tie(grad_attn, m.mark)
    kept = [(qkv_near, qkv_far), (ctx_near, ctx_far), (p_near, p_far)]
    a_core, a_farc, sums, grad_x = attend_back_pair(
        x, plen, grad_attn, *kept, 1, (att[1], att[3]), grad_one, (1, 3), sums, meta
    )
    if grid:
        got_a1, got_a3 = [m.send(v, m.to_core) for v in (a_core, a_farc)]
        i_near = [i_own, got_i1]
        m.mark = grad_x
        m.step(chain_b)
        got_ix[0] = m.after(got_ix[0])
        grad_x = tie(grad_x, got_ix[0])
    a_own, a_far, packed, grad_x = attend_back_pair(
        x, plen, grad_attn, *kept, 0, (att[0], att[2]), grad_x, (0, 2), sums, meta
    )
    if grid:
        m.mark = grad_x
        low_far, high_far = zip(*(m.halves(v) for v in (a_far, m.after(got_a3))))
        low_near, high_near = zip(*(m.halves(v) for v in (a_own, got_a1)))
        low_far = add(*low_far)
        got_ax = m.send(low_far, m.to_x)
        m.mark = low_far
        chains = {"b": chain_b, "i": m.chain_zy(i_near, got_ix), "v": m.chain_y(list(high_near), list(high_far))}
        done = {}
        for key in "vib":
            done[key] = m.step(chains[key])
        chains["u"] = m.chain(low_near, [got_ax])
        chains["s"] = m.chain_small(m.after(packed))
        for key in ORDER:
            done[key] = m.step(chains[key])
        g_back, g_in, packed = done["b"], done["i"], done["s"]
        g_att = jnp.concatenate([done["u"], done["v"]], axis=0)
    else:
        g_back, g_in, g_att = [
            lax.psum(
                lax.psum_scatter(jnp.stack(parts).astype(F32), "tp", scatter_dimension=0), "batch"
            )
            for parts in (
                (b_own, b_core, b_far, b_farc),
                (i_own, i_core, i_far, i_farc),
                (a_own, a_core, a_far, a_farc),
            )
        ]
        packed = lax.psum(packed, AXES)
    mine = lax.dynamic_slice_in_dim(packed, 2 * position, 2, axis=0)
    return (
        layer_out.reshape(tokens.shape),
        grad_x.reshape(tokens.shape),
        jnp.transpose(g_att[: 3 * width].reshape(3, width, model), (2, 0, 1)),
        mine[1, :width],
        mine[1, 2 * width : 3 * width],
        g_att[3 * width :],
        packed[11],
        packed[12],
        packed[13],
        g_in,
        mine[0],
        g_back,
        packed[10],
        packed[8],
        packed[9],
    )


def solution(mesh):
    in_specs = (
        P(None, ("batch", "tp"), None),
        P(None, "batch"),
        P(None, ("batch", "tp"), None),
        P(None, None, "tp"),
        P("tp"),
        P("tp"),
        P("tp", None),
        P(),
        P(),
        P(),
        P(None, "tp"),
        P("tp"),
        P("tp", None),
        P(),
        P(),
        P(),
    )
    out_specs = (
        P(None, ("batch", "tp"), None),
        P(None, ("batch", "tp"), None),
        P(None, None, "tp"),
        P("tp"),
        P("tp"),
        P("tp", None),
        P(),
        P(),
        P(),
        P(None, "tp"),
        P("tp"),
        P("tp", None),
        P(),
        P(),
        P(),
    )
    return jax.shard_map(body, mesh=mesh, in_specs=in_specs, out_specs=out_specs, check_vma=False)
```

```python
import math

import jax
import jax.numpy as jnp
from jax import lax
from jax.experimental import pallas as pl
from jax.experimental.pallas import tpu as pltpu
from jax.sharding import PartitionSpec as P

DH = 64
AXES = ("batch", "tp")
epsilon = 1e-05
F32 = jnp.float32
BF16 = jnp.bfloat16


def nt(a, b):
    return lax.dot_general(a, b, (((1,), (1,)), ((), ())), preferred_element_type=F32)


def tn(a, b):
    return lax.dot_general(a, b, (((0,), (0,)), ((), ())), preferred_element_type=F32)


def nn(a, b):
    return jnp.dot(a, b, preferred_element_type=F32)


HBM = pl.BlockSpec(memory_space=pl.ANY)
WHOLE = pl.BlockSpec(memory_space=pltpu.VMEM)
SCALARS = pl.BlockSpec(memory_space=pltpu.SMEM)


class Copies:
    def __init__(self, sems):
        self.sems, self.used = sems, 0
        self.pending = []

    def start(self, src, dst):
        copy = pltpu.make_async_copy(src, dst, self.sems.at[self.used])
        self.used += 1
        copy.start()
        return copy

    def out(self, src, dst):
        self.pending.append(self.start(src, dst))

    def drain(self):
        for copy in self.pending:
            copy.wait()


def call(kernel, name, inputs, outputs, scratch, copies, cost=1000):
    in_specs = [spec for spec, _ in inputs]
    return pl.pallas_call(
        kernel,
        name=name,
        in_specs=in_specs,
        out_specs=tuple(spec for spec, _ in outputs),
        out_shape=tuple(shape for _, shape in outputs),
        scratch_shapes=list(scratch) + [pltpu.SemaphoreType.DMA((copies,))],
        cost_estimate=pl.CostEstimate(flops=cost, transcendentals=0, bytes_accessed=0),
    )(*[value for _, value in inputs])


def shape(dims, dtype):
    return jax.ShapeDtypeStruct(dims, dtype)


def block(i, size):
    return pl.ds(pl.multiple_of(i * size, size), size)


def unit_norm(v):
    middle = jnp.mean(v, axis=-1, keepdims=True)
    centred = v - middle
    inverse = lax.rsqrt(jnp.mean(centred * centred, axis=-1, keepdims=True) + epsilon)
    return centred * inverse, inverse


def norm_grad(scaled, unit, inverse):
    mean_one = jnp.mean(scaled, axis=-1, keepdims=True)
    mean_two = jnp.mean(scaled * unit, axis=-1, keepdims=True)
    return inverse * (scaled - mean_one - unit * mean_two)


STEP = 128


def row_of(part, meta_ref, kind):
    return 2 * jnp.bitwise_xor(part, meta_ref[meta_ref.shape[0] - 1]) + kind


def attend_pair(x, plen, w_pair, smalls, meta, acc=None, vectors=None):
    rows, model = x.shape
    passages = rows // plen
    width = w_pair[0].shape[0] // 4
    heads = width // DH
    units = smalls[0].shape[1] - 3 * width
    last = acc is not None

    def kernel(meta_ref, x_hbm, wa, wb, bias_a, bias_b, *rest):
        if last:
            acc_hbm, b_out, gain, shift = rest[:4]
            qkv_hbm, ctx_hbm, p_hbm, unit_hbm, inv_hbm, low_hbm = rest[4:10]
            x_s, w_s, qkv_s, ctx_s, p_s, acc_s, inv_s, low_s, sems = rest[10:]
        else:
            qkv_hbm, ctx_hbm, p_hbm, acc_out = rest[:4]
            x_s, w_s, qkv_s, ctx_s, p_s, acc_s, sems = rest[4:]
        copies = Copies(sems)
        first = [copies.start(x_hbm, x_s), copies.start(wa, w_s.at[0])]
        second = [copies.start(wb, w_s.at[1])]
        if last:
            held = copies.start(acc_hbm, acc_s)
        for j, waits, bias in ((0, first, bias_a), (1, second, bias_b)):
            for copy in waits:
                copy.wait()
            qkv_s[j] = (nt(x_s[...], w_s[j, : 3 * width, :]) + bias[0:1, units:]).astype(BF16)
            copies.out(qkv_s.at[j], qkv_hbm.at[j])

            def one(g, carry, j=j):
                at = block(g, plen)
                qkv = qkv_s[j, at, :]
                keep = lax.broadcasted_iota(jnp.int32, (1, plen), 1) < meta_ref[g]
                ctx = []
                for h in range(heads):
                    q = qkv[:, h * DH : (h + 1) * DH] * (1.0 / math.sqrt(DH))
                    k = qkv[:, width + h * DH : width + (h + 1) * DH]
                    v = qkv[:, 2 * width + h * DH : 2 * width + (h + 1) * DH]
                    s = jnp.where(keep, nt(q.astype(BF16), k), -1000000000.0)
                    e = jnp.exp(s - jnp.max(s, axis=-1, keepdims=True))
                    p = (e * (1.0 / jnp.sum(e, axis=-1, keepdims=True))).astype(BF16)
                    p_s[j, g * heads + h] = p
                    ctx.append(nn(p, v))
                ctx_s[j, at, :] = jnp.concatenate(ctx, axis=1).astype(BF16)
                return carry

            lax.fori_loop(0, passages, one, 0)
            copies.out(ctx_s.at[j], ctx_hbm.at[j])
            copies.out(p_s.at[j], p_hbm.at[j])
            term = nn(ctx_s[j], w_s[j, 3 * width :, :])
            if last and j == 0:
                held.wait()
            acc_s[...] = term if j == 0 and not last else acc_s[...] + term
        if last:

            def finish(i, carry):
                at = block(i, STEP)
                v = x_s[at, :].astype(F32) + acc_s[at, :] + b_out[...]
                unit, inverse = unit_norm(v)
                acc_s[at, :] = unit
                inv_s[at, :] = jnp.broadcast_to(inverse, (STEP, 128))
                low_s[at, :] = (unit * gain[...] + shift[...]).astype(BF16)
                return carry

            lax.fori_loop(0, rows // STEP, finish, 0)
            copies.out(acc_s, unit_hbm)
            copies.out(inv_s, inv_hbm)
            copies.out(low_s, low_hbm)
        else:
            copies.out(acc_s, acc_out)
        copies.drain()

    inputs = [(SCALARS, meta), (HBM, x), (HBM, w_pair[0]), (HBM, w_pair[1])]
    inputs += [(WHOLE, v) for v in smalls]
    dims = [(2, rows, 3 * width), (2, rows, width), (2, passages * heads, plen, plen)]
    outputs = [(HBM, shape(d, BF16)) for d in dims]
    scratch = [pltpu.VMEM((rows, model), BF16), pltpu.VMEM((2, 4 * width, model), BF16)]
    scratch += [pltpu.VMEM(d, BF16) for d in dims]
    scratch += [pltpu.VMEM((rows, model), F32)]
    if last:
        inputs += [(HBM, acc)] + [(WHOLE, v) for v in vectors]
        outputs += [(HBM, shape((rows, model), F32)), (HBM, shape((rows, 128), F32))]
        outputs += [(HBM, shape((rows, model), BF16))]
        scratch += [pltpu.VMEM((rows, 128), F32), pltpu.VMEM((rows, model), BF16)]
    else:
        outputs += [(HBM, shape((rows, model), F32))]
    return call(kernel, "attend_pair", inputs, outputs, scratch, 16, 1000 if last else 200 * 10**9)


def feed(j, low_s, i_s, b_s, bias, act_s, slope_s):
    units = act_s.shape[2]
    for c in range(0, units, 256):
        cols = slice(c, c + 256)
        t = nn(low_s[...], i_s[j, :, cols]) + bias[0:1, cols]
        cdf = 0.5 * (1.0 + lax.erf(t * (1.0 / math.sqrt(2.0))))
        pdf = jnp.exp(-0.5 * t * t) * (1.0 / math.sqrt(2.0 * math.pi))
        act_s[j, :, cols] = (t * cdf).astype(BF16)
        slope_s[j, :, cols] = (cdf + t * pdf).astype(BF16)
    return nn(act_s[j], b_s[j])


def feed_pair(low, in_pair, back_pair, smalls):
    rows, model = low.shape
    units = in_pair[0].shape[1]

    def kernel(low_hbm, ia, ib, ba, bb, bias_a, bias_b, *rest):
        act_hbm, slope_hbm, acc_hbm, low_s, i_s, b_s, act_s, slope_s, acc_s, sems = rest
        copies = Copies(sems)
        first = [copies.start(low_hbm, low_s), copies.start(ia, i_s.at[0]), copies.start(ba, b_s.at[0])]
        second = [copies.start(ib, i_s.at[1]), copies.start(bb, b_s.at[1])]
        for j, waits, bias in ((0, first, bias_a), (1, second, bias_b)):
            for copy in waits:
                copy.wait()
            term = feed(j, low_s, i_s, b_s, bias, act_s, slope_s)
            copies.out(act_s.at[j], act_hbm.at[j])
            copies.out(slope_s.at[j], slope_hbm.at[j])
            acc_s[...] = acc_s[...] + term if j else term
        copies.out(acc_s, acc_hbm)
        copies.drain()

    inputs = [(HBM, v) for v in (low, *in_pair, *back_pair)] + [(WHOLE, v) for v in smalls]
    outputs = [(HBM, shape((2, rows, units), BF16))] * 2 + [(HBM, shape((rows, model), F32))]
    scratch = [pltpu.VMEM((rows, model), BF16), pltpu.VMEM((2, model, units), BF16)]
    scratch += [pltpu.VMEM((2, units, model), BF16)] + [pltpu.VMEM((2, rows, units), BF16)] * 2
    scratch += [pltpu.VMEM((rows, model), F32)]
    return call(kernel, "feed_pair", inputs, outputs, scratch, 12)


def turn_pair(low, in_pair, back_pair, smalls, unit, acc, dy, meta, vectors, plen):
    rows, model = low.shape
    units = in_pair[0].shape[1]

    def kernel(meta_ref, low_hbm, ia, ib, ba, bb, unit_hbm, acc_hbm, dy_hbm, bias_a, bias_b, *rest):
        gain_one, shift_one, b_back, gain_two, shift_two = rest[:5]
        out_hbm, grad_hbm, ffn_hbm, sum_ref, slope_hbm, oa, ob = rest[5:12]
        low_s, i_s, b_s, act_s, slope_s, acc_s, unit_s, dy_s, out_s, grad_s, ffn_s, g_s, sems = rest[12:]
        copies = Copies(sems)
        first = [copies.start(low_hbm, low_s), copies.start(ia, i_s.at[0]), copies.start(ba, b_s.at[0])]
        second = [copies.start(ib, i_s.at[1]), copies.start(bb, b_s.at[1]), copies.start(acc_hbm, acc_s)]
        third = [copies.start(unit_hbm, unit_s), copies.start(dy_hbm, dy_s)]
        for copy in first:
            copy.wait()
        term = feed(0, low_s, i_s, b_s, bias_a, act_s, slope_s)
        copies.out(slope_s.at[0], slope_hbm.at[0])
        for copy in second:
            copy.wait()
        acc_s[...] = acc_s[...] + term
        acc_s[...] = acc_s[...] + feed(1, low_s, i_s, b_s, bias_b, act_s, slope_s)
        copies.out(slope_s.at[1], slope_hbm.at[1])
        for copy in third:
            copy.wait()
        sum_ref[...] = jnp.zeros_like(sum_ref)

        def step(i, carry):
            at = block(i, STEP)
            normed = unit_s[at, :] * gain_one[...] + shift_one[...]
            u, inverse = unit_norm(normed + acc_s[at, :] + b_back[...])
            out_s[at, :] = (u * gain_two[...] + shift_two[...]).astype(BF16)
            slot = lax.broadcasted_iota(jnp.int32, (STEP, 1), 0) + (i * STEP) % plen
            keep = slot < meta_ref[(i * STEP) // plen]
            grad_y = jnp.where(keep, dy_s[at, :].astype(F32), 0.0)
            grad = norm_grad(grad_y * gain_two[...], u, inverse)
            grad_s[at, :] = grad
            ffn_s[at, :] = grad.astype(BF16)
            sum_ref[8:9, :] += jnp.sum(grad_y * u, axis=0, keepdims=True)
            sum_ref[9:10, :] += jnp.sum(grad_y, axis=0, keepdims=True)
            sum_ref[10:11, :] += jnp.sum(grad, axis=0, keepdims=True)
            return carry

        lax.fori_loop(0, rows // STEP, step, 0)
        copies.out(out_s, out_hbm)
        copies.out(grad_s, grad_hbm)
        copies.out(ffn_s, ffn_hbm)
        for j, out in ((1, ob), (0, oa)):
            g_s[j] = tn(act_s[j], ffn_s[...]).astype(BF16)
            copies.out(g_s.at[j], out)
        copies.drain()

    inputs = [(SCALARS, meta)] + [(HBM, v) for v in (low, *in_pair, *back_pair, unit, acc, dy)]
    inputs += [(WHOLE, v) for v in (*smalls, *vectors)]
    outputs = [(HBM, shape((rows, model), d)) for d in (BF16, F32, BF16)]
    outputs += [(WHOLE, shape((16, model), F32)), (HBM, shape((2, rows, units), BF16))]
    outputs += [(HBM, shape((units, model), BF16))] * 2
    scratch = [pltpu.VMEM((rows, model), BF16), pltpu.VMEM((2, model, units), BF16)]
    scratch += [pltpu.VMEM((2, units, model), BF16)] + [pltpu.VMEM((2, rows, units), BF16)] * 2
    scratch += [pltpu.VMEM((rows, model), d) for d in (F32, F32, BF16, BF16, F32, BF16)]
    scratch += [pltpu.VMEM((2, units, model), BF16)]
    return call(kernel, "turn_pair", inputs, outputs, scratch, 20)


def outer_pair(acts, grad_ffn):
    _, rows, units = acts.shape
    model = grad_ffn.shape[1]

    def kernel(act_hbm, g_hbm, oa, ob, act_s, g_s, out_s, sems):
        copies = Copies(sems)
        whole = copies.start(g_hbm, g_s)
        waits = [copies.start(act_hbm.at[j], act_s.at[j]) for j in (1, 0)]
        whole.wait()
        for j, wait, out in ((1, waits[0], ob), (0, waits[1], oa)):
            wait.wait()
            out_s[j] = tn(act_s[j], g_s[...]).astype(BF16)
            copies.out(out_s.at[j], out)
        copies.drain()

    inputs = [(HBM, acts), (HBM, grad_ffn)]
    outputs = [(HBM, shape((units, model), BF16))] * 2
    scratch = [pltpu.VMEM((2, rows, units), BF16), pltpu.VMEM((rows, model), BF16)]
    scratch += [pltpu.VMEM((2, units, model), BF16)]
    return call(kernel, "outer_pair", inputs, outputs, scratch, 8, 200 * 10**9)


def feed_back_pair(grad_ffn, slopes, which, in_pair, back_pair, low, start, parts, sums, meta, unit=None, inverse=None, gain=None):
    rows, model = grad_ffn.shape
    units = slopes[0].shape[2]
    last = unit is not None

    def kernel(meta_ref, before, g_hbm, sa, sb, ia, ib, ba, bb, low_hbm, start_hbm, *rest):
        if last:
            unit_hbm, inv_hbm, gain_ref = rest[:3]
            rest = rest[3:]
            oa, ob, sum_ref, one_hbm, attn_hbm = rest[:5]
            g_s, slope_s, i_s, b_s, low_s, acc_s, pre_s, out_s, line, unit_s, inv_s, attn_s, sems = rest[5:]
        else:
            oa, ob, sum_ref, acc_out = rest[:4]
            g_s, slope_s, i_s, b_s, low_s, acc_s, pre_s, out_s, line, sems = rest[4:]
        copies = Copies(sems)
        sum_ref[...] = before[...]
        weights = {1: (bb, ib, sb.at[which]), 0: (ba, ia, sa.at[which])}
        early = copies.start(g_hbm, g_s)
        waits, later = {}, {}
        for j in (1, 0):
            waits[j] = [copies.start(weights[j][0], b_s.at[j]), copies.start(weights[j][2], slope_s.at[j])]
            later[j] = [copies.start(weights[j][1], i_s.at[j])]
            if j == 1:
                later[j] += [copies.start(low_hbm, low_s), copies.start(start_hbm, acc_s)]
        if last:
            late = [copies.start(unit_hbm, unit_s), copies.start(inv_hbm, inv_s)]
        early.wait()
        for j, out in ((1, ob), (0, oa)):
            for wait in waits[j]:
                wait.wait()
            for c in range(0, units, 256):
                cols = slice(c, c + 256)
                pre = nt(g_s[...], b_s[j, cols, :]) * slope_s[j, :, cols].astype(F32)
                pre = pre.astype(BF16)
                pre_s[:, cols] = pre
                line[:, cols] = jnp.sum(pre.astype(F32), axis=0, keepdims=True)
            sum_ref[pl.ds(row_of(parts[j], meta_ref, 0), 1), :] = line[...]
            for wait in later[j]:
                wait.wait()
            acc_s[...] = acc_s[...] + nt(pre_s[...], i_s[j])
            out_s[j] = tn(low_s[...], pre_s[...]).astype(BF16)
            copies.out(out_s.at[j], out)
        if last:
            for wait in late:
                wait.wait()

            def finish(i, carry):
                at = block(i, STEP)
                normed = acc_s[at, :]
                u = unit_s[at, :]
                grad = norm_grad(normed * gain_ref[0:1, :], u, inv_s[at, 0:1])
                sum_ref[11:12, :] += jnp.sum(grad, axis=0, keepdims=True)
                sum_ref[12:13, :] += jnp.sum(normed * u, axis=0, keepdims=True)
                sum_ref[13:14, :] += jnp.sum(normed, axis=0, keepdims=True)
                acc_s[at, :] = grad
                attn_s[at, :] = grad.astype(BF16)
                return carry

            lax.fori_loop(0, rows // STEP, finish, 0)
            copies.out(acc_s, one_hbm)
            copies.out(attn_s, attn_hbm)
        else:
            copies.out(acc_s, acc_out)
        copies.drain()

    inputs = [(SCALARS, meta), (WHOLE, sums)]
    inputs += [(HBM, v) for v in (grad_ffn, *slopes, *in_pair, *back_pair, low, start)]
    outputs = [(HBM, shape((model, units), BF16))] * 2 + [(WHOLE, shape((16, model), F32))]
    outputs += [(HBM, shape((rows, model), F32))]
    scratch = [pltpu.VMEM((rows, model), BF16), pltpu.VMEM((2, rows, units), BF16)]
    scratch += [pltpu.VMEM((2, model, units), BF16), pltpu.VMEM((2, units, model), BF16)]
    scratch += [pltpu.VMEM((rows, model), BF16), pltpu.VMEM((rows, model), F32)]
    scratch += [pltpu.VMEM((rows, units), BF16), pltpu.VMEM((2, model, units), BF16)]
    scratch += [pltpu.VMEM((1, units), F32)]
    if last:
        inputs += [(HBM, unit), (HBM, inverse), (WHOLE, gain)]
        outputs += [(HBM, shape((rows, model), BF16))]
        scratch += [pltpu.VMEM((rows, model), F32), pltpu.VMEM((rows, 128), F32)]
        scratch += [pltpu.VMEM((rows, model), BF16)]
    return call(kernel, "feed_back_pair", inputs, outputs, scratch, 20, 200 * 10**9)


def attend_back_pair(x, plen, grad_attn, qkvs, ctxs, probs, which, w_pair, start, parts, sums, meta):
    rows, model = x.shape
    passages = rows // plen
    width = ctxs[0].shape[2]
    heads = width // DH

    def kernel(meta_ref, before, x_hbm, g_hbm, qa, qb, ca, cb, pa, pb, wa, wb, start_hbm, *rest):
        oa, ob, sum_ref, acc_out = rest[:4]
        x_s, g_s, qkv_s, ctx_s, p_s, w_s, acc_s, grow_s, out_s, gc_s, sems = rest[4:]
        copies = Copies(sems)
        sum_ref[...] = before[...]
        early = [copies.start(g_hbm, g_s)]
        of = {0: (wa, ca, qa, pa), 1: (wb, cb, qb, pb)}
        waits, middle, later = {}, {}, {}
        for j in (1, 0):
            waits[j] = [copies.start(of[j][0], w_s.at[j]), copies.start(of[j][1].at[which], ctx_s.at[j])]
            middle[j] = [copies.start(of[j][2].at[which], qkv_s.at[j]), copies.start(of[j][3].at[which], p_s.at[j])]
            later[j] = []
            if j == 1:
                later[j] = [copies.start(x_hbm, x_s), copies.start(start_hbm, acc_s)]
        for wait in early:
            wait.wait()
        for j, out in ((1, ob), (0, oa)):
            for wait in waits[j]:
                wait.wait()
            gc_s[...] = nt(g_s[...], w_s[j, 3 * width :, :]).astype(BF16)
            out_s[j, 3 * width :, :] = tn(ctx_s[j], g_s[...]).astype(BF16)
            for wait in middle[j]:
                wait.wait()

            def one(g, carry, j=j):
                at = block(g, plen)
                qkv = qkv_s[j, at, :]
                grad_ctx = gc_s[at, :]
                gq, gk, gv = [], [], []
                for h in range(heads):
                    q = qkv[:, h * DH : (h + 1) * DH]
                    k = qkv[:, width + h * DH : width + (h + 1) * DH]
                    v = qkv[:, 2 * width + h * DH : 2 * width + (h + 1) * DH]
                    gc = grad_ctx[:, h * DH : (h + 1) * DH]
                    low = p_s[j, g * heads + h]
                    p = low.astype(F32)
                    gp = nt(gc, v)
                    delta = jnp.sum(p * gp, axis=-1, keepdims=True)
                    gs = (p * (gp - delta)).astype(BF16)
                    gq.append(nn(gs, k) * (1.0 / math.sqrt(DH)))
                    gk.append(tn(gs, q) * (1.0 / math.sqrt(DH)))
                    gv.append(tn(low, gc))
                grow = jnp.concatenate(gq + gk + gv, axis=1).astype(BF16)
                grow_s[at, :] = grow
                return carry + jnp.sum(grow.astype(F32), axis=0, keepdims=True)

            line = lax.fori_loop(0, passages, one, jnp.zeros((1, 3 * width), F32))
            line = jnp.concatenate([line, jnp.zeros((1, model - 3 * width), F32)], axis=1)
            sum_ref[pl.ds(row_of(parts[j], meta_ref, 1), 1), :] = line
            for wait in later[j]:
                wait.wait()
            out_s[j, : 3 * width, :] = tn(grow_s[...], x_s[...]).astype(BF16)
            copies.out(out_s.at[j], out)
            acc_s[...] = acc_s[...] + nn(grow_s[...], w_s[j, : 3 * width, :])
        copies.out(acc_s, acc_out)
        copies.drain()

    inputs = [(SCALARS, meta), (WHOLE, sums)]
    inputs += [(HBM, v) for v in (x, grad_attn, *qkvs, *ctxs, *probs, *w_pair, start)]
    outputs = [(HBM, shape((4 * width, model), BF16))] * 2
    outputs += [(WHOLE, shape((16, model), F32)), (HBM, shape((rows, model), F32))]
    scratch = [pltpu.VMEM((rows, model), BF16), pltpu.VMEM((rows, model), BF16)]
    scratch += [pltpu.VMEM(v[0].shape, BF16) for v in (qkvs, ctxs, probs)]
    scratch += [pltpu.VMEM((2, 4 * width, model), BF16), pltpu.VMEM((rows, model), F32)]
    scratch += [pltpu.VMEM((rows, 3 * width), BF16), pltpu.VMEM((2, 4 * width, model), BF16)]
    scratch += [pltpu.VMEM((rows, width), BF16)]
    return call(kernel, "attend_back_pair", inputs, outputs, scratch, 20, 200 * 10**9)


def tie(value, *others):
    return lax.optimization_barrier((value, *others))[0]


def flat_perm(move):
    pairs = []
    for z in range(4):
        for y in range(2):
            for x in range(2):
                for c in range(2):
                    z2, y2, x2, c2 = move(z, y, x, c)
                    pairs.append((((z * 2 + y) * 2 + x) * 2 + c, ((z2 * 2 + y2) * 2 + x2) * 2 + c2))
    return pairs


def add(*terms):
    return sum(term.astype(F32) for term in terms).astype(BF16)


ORDER = "susibuvibusvvibusvuisvusvi"


class GridMoves:
    def __init__(self):
        self.row = lax.axis_index("batch") % 2
        self.layer = lax.axis_index("batch") // 2 % 2
        self.side = (self.row + self.layer) % 2
        self.to_core = flat_perm(lambda z, y, x, c: (z, y, x, 1 - c))
        self.to_x = flat_perm(lambda z, y, x, c: (z, y, 1 - x, c))
        self.to_y = flat_perm(lambda z, y, x, c: (z, 1 - y, x, c))
        self.to_z = flat_perm(lambda z, y, x, c: (z ^ 1, y, x, c))
        self.to_zz = flat_perm(lambda z, y, x, c: (z ^ 2, y, x, c))
        self.mark = None

    def send(self, value, pairs):
        return lax.ppermute(value, AXES, pairs)

    def half(self, value, which):
        if isinstance(value, tuple):
            return jnp.where(which == 0, value[0], value[1])
        if isinstance(value, dict):
            rows = value["rows"] // 2
            at = value["at"] + which * rows
            return lax.dynamic_slice_in_dim(value["of"], at, rows, axis=0)
        if isinstance(value, list):
            return add(*(self.half(term, which) for term in value))
        rows = value.shape[0] // 2
        return lax.dynamic_slice_in_dim(value, which * rows, rows, axis=0)

    def order(self, mine, other, bit):
        low = jnp.where(bit == 0, mine, other)
        high = jnp.where(bit == 0, other, mine)
        return jnp.concatenate([low, high], axis=0)

    def after(self, value):
        if self.mark is not None:
            value = tie(value, self.mark)
        return value

    def pieces(self, mine):
        first, second = self.halves(mine)
        return [self.send(first, self.to_y), self.send(second, self.to_z)]

    def whole(self, mine, pieces):
        return self.order(mine, jnp.concatenate(pieces, axis=0), self.side)

    def halves(self, value):
        rows = value.shape[0] // 2
        return value[:rows], value[rows:]

    def sums(self, one, two):
        return [add(a, b) for a, b in zip(self.halves(one), self.halves(two))]

    def chain(self, near, got):
        got = tuple(self.after(part) for part in got)
        got = got if len(got) == 2 else got[0]
        pass_on = self.half([*near, got], 1 - self.row)
        keep = self.half([*near, got], self.row)
        got = self.send(pass_on, self.to_y)
        yield pass_on
        yield from self.chain_z(add(keep, self.after(got)))

    def chain_zy(self, near, got):
        got = tuple(self.after(part) for part in got)
        pass_on = self.half([*near, got], 1 - self.layer)
        keep = self.half([*near, got], self.layer)
        got = self.send(pass_on, self.to_z)
        yield pass_on
        keep = add(keep, self.after(got))
        pass_on = self.half(keep, 1 - self.row)
        keep = self.half(keep, self.row)
        got = self.send(pass_on, self.to_y)
        yield pass_on
        keep = add(keep, self.after(got))
        got = self.send(keep, self.to_zz)
        yield keep
        keep = add(keep, self.after(got))
        got = self.send(keep, self.to_y)
        yield keep
        keep = self.order(keep, self.after(got), self.row)
        got = self.send(keep, self.to_z)
        yield keep
        yield self.order(keep, self.after(got), self.layer).astype(F32)

    def chain_y(self, near, far):
        pass_on = jnp.concatenate(
            [self.half(term, 1 - self.row) for term in (near, far)], axis=0
        )
        got = self.send(pass_on, self.to_y)
        yield pass_on
        got = self.halves(self.after(got))
        far = add(*(self.half(term, self.row) for term in far), got[1])
        keep = add(*(self.half(term, self.row) for term in near), got[0])
        got = self.send(far, self.to_x)
        yield far
        yield from self.chain_z(add(keep, self.after(got)))

    def chain_z(self, keep):
        pass_on = self.half(keep, 1 - self.layer)
        keep = self.half(keep, self.layer)
        got = self.send(pass_on, self.to_z)
        yield pass_on
        keep = add(keep, self.after(got))
        got = self.send(keep, self.to_zz)
        yield keep
        keep = add(keep, self.after(got))
        got = self.send(keep, self.to_z)
        yield keep
        keep = self.order(keep, self.after(got), self.layer)
        got = self.send(keep, self.to_y)
        yield keep
        yield self.order(keep, self.after(got), self.row).astype(F32)

    def chain_small(self, value):
        for pairs in (self.to_core, self.to_x, self.to_y, self.to_z, self.to_zz):
            got = self.send(value, pairs)
            yield value
            value = value + self.after(got)
        yield value

    def step(self, chain):
        self.mark = next(chain)
        return self.mark


def body(
    tokens,
    passage_lengths,
    cotangent,
    w_qkv,
    b_query,
    b_value,
    w_out,
    b_out,
    gain_one,
    shift_one,
    w_in,
    b_in,
    w_back,
    b_back,
    gain_two,
    shift_two,
):
    micro_count, own_rows, model = tokens.shape
    tp_count = lax.axis_size("tp")
    batch_count = lax.axis_size("batch")
    plen = own_rows * tp_count // passage_lengths.shape[1]
    own_passages = own_rows // plen
    assert own_passages * plen == own_rows and tp_count == 4
    grid = (batch_count, tp_count) == (8, 4)
    width = w_qkv.shape[2]
    rows = micro_count * own_rows
    position = lax.axis_index("tp")

    vector = lambda v: v.reshape(1, -1)
    x = tokens.reshape(rows, model)
    dy = cotangent.reshape(rows, model)
    lengths = lax.dynamic_slice_in_dim(
        passage_lengths, position * own_passages, own_passages, axis=1
    ).reshape(micro_count * own_passages)
    meta = jnp.concatenate([lengths, (position if grid else 0 * position).reshape(1)])
    qkvo = jnp.concatenate([jnp.transpose(w_qkv, (1, 2, 0)).reshape(3 * width, model), w_out], axis=0)
    small = vector(jnp.concatenate([b_in.astype(F32), b_query, jnp.zeros_like(b_query), b_value]))
    if grid:
        m = moves = GridMoves()
        x_att = m.send(m.half(qkvo, m.side), m.to_x)
        c_att = m.send(qkvo, m.to_core)
        c_small = m.send(small, m.to_core)
        x_small = m.send(small, m.to_x)
        half_in = m.half(w_in, m.side)
        meta = tie(meta, half_in)
        att, smalls = [qkvo, c_att], [small, c_small]
    else:
        att, smalls, ins, backs = [
            list(lax.all_gather(v, "tp", axis=0)) for v in (qkvo, small, w_in, w_back)
        ]
    qkv_near, ctx_near, p_near, acc = attend_pair(x, plen, att[:2], smalls[:2], meta)
    y = x
    if grid:
        x_att, x_small = tie(x_att, acc), tie(x_small, acc)
        y_att = m.send(x_att, m.to_y)
        half_back = m.half(w_back, m.side)
        x_in = m.send(tie(half_in, x_att), m.to_x)
        smalls += [x_small, m.send(x_small, m.to_core)]
        y_att = tie(y_att, half_back, smalls[3])
        f_att = m.order(x_att, y_att, m.side)
        att += [f_att, m.send(f_att, m.to_core)]
        c_in = m.send(tie(w_in, f_att), m.to_core)
        c_back = m.send(tie(w_back, f_att), m.to_core)
        x_in = tie(x_in, f_att)
        y_in = m.send(x_in, m.to_y)
        x_back = m.send(tie(half_back, x_in), m.to_x)
        y = tie(x, x_in)
    qkv_far, ctx_far, p_far, unit, inverse, low = attend_pair(
        y, plen, att[2:], smalls[2:], meta, acc, [vector(v) for v in (b_out, gain_one, shift_one)]
    )
    if grid:
        y_in = tie(y_in, low)
        f_in = m.order(x_in, y_in, m.side)
        ins = [w_in, c_in, f_in, m.send(f_in, m.to_core)]
        x_back = tie(x_back, f_in)
        p_back = m.pieces(x_back)
        backs = [w_back, c_back]
        low = tie(low, x_back)
    act_near, slope_near, feed_near = feed_pair(low, ins[:2], backs[:2], smalls[:2])
    if grid:
        p_back[0] = tie(p_back[0], feed_near)
        f_back = m.whole(x_back, p_back)
        backs += [f_back, m.send(f_back, m.to_core)]
    layer_out, grad_two, grad_ffn, sums, slope_far, b_far, b_farc = turn_pair(
        low,
        ins[2:],
        backs[2:],
        smalls[2:],
        unit,
        feed_near,
        dy,
        meta,
        [vector(v) for v in (gain_one, shift_one, b_back, gain_two, shift_two)],
        plen,
    )
    if grid:
        got_b3 = m.send(b_farc, m.to_core)
    b_own, b_core = outer_pair(act_near, grad_ffn)
    if grid:
        got_b1 = m.send(b_core, m.to_core)
        b_far = m.sums(b_far, tie(got_b3, b_own))
        got_bx = [m.send(part, m.to_x) for part in b_far]
        grad_ffn = tie(grad_ffn, *b_far)
    slopes = (slope_near, slope_far)
    feed_sent = [(v[1], v[3]) for v in (ins, backs)]
    feed_kept = [(v[0], v[2]) for v in (ins, backs)]
    i_core, i_farc, sums, normed = feed_back_pair(
        grad_ffn, slopes, 1, *feed_sent, low, grad_two, (1, 3), sums, meta
    )
    if grid:
        got_i1, got_i3 = [m.send(v, m.to_core) for v in (i_core, i_farc)]
        b_near = [b_own, tie(got_b1, normed)]
        got_bx[0] = tie(got_bx[0], normed)
        normed = tie(normed, got_bx[0])
    i_own, i_far, sums, grad_one, grad_attn = feed_back_pair(
        grad_ffn,
        slopes,
        0,
        *feed_kept,
        low,
        normed,
        (0, 2),
        sums,
        meta,
        unit,
        inverse,
        vector(gain_one),
    )
    if grid:
        i_far = m.sums(i_far, tie(got_i3, grad_attn))
        got_ix = [m.send(part, m.to_x) for part in i_far]
        m.mark = i_far[0]
        chain_b = m.chain(b_near, got_bx)
        m.step(chain_b)
        grad_attn = tie(grad_attn, m.mark)
    kept = [(qkv_near, qkv_far), (ctx_near, ctx_far), (p_near, p_far)]
    a_core, a_farc, sums, grad_x = attend_back_pair(
        x, plen, grad_attn, *kept, 1, (att[1], att[3]), grad_one, (1, 3), sums, meta
    )
    if grid:
        got_a1, got_a3 = [m.send(v, m.to_core) for v in (a_core, a_farc)]
        i_near = [i_own, got_i1]
        m.mark = grad_x
        m.step(chain_b)
        got_ix[0] = m.after(got_ix[0])
        grad_x = tie(grad_x, got_ix[0])
    a_own, a_far, packed, grad_x = attend_back_pair(
        x, plen, grad_attn, *kept, 0, (att[0], att[2]), grad_x, (0, 2), sums, meta
    )
    if grid:
        m.mark = grad_x
        got_a3 = m.after(got_a3)
        rows_a = a_far.shape[0] // 2
        low_far = [v[:rows_a] for v in (a_far, got_a3)]
        low_far = add(*low_far)
        got_ax = m.send(low_far, m.to_x)
        m.mark = low_far
        got_a1 = m.after(got_a1)
        view = lambda v, at: {"of": v, "at": at, "rows": rows_a}
        low_near = [view(v, 0) for v in (a_own, got_a1)]
        high_near = [view(v, rows_a) for v in (a_own, got_a1)]
        high_far = [view(v, rows_a) for v in (a_far, got_a3)]
        chains = {"b": chain_b, "i": m.chain_zy(i_near, got_ix), "v": m.chain_y(high_near, high_far)}
        done = {}
        for key in "vib":
            done[key] = m.step(chains[key])
        chains["u"] = m.chain(low_near, [got_ax])
        chains["s"] = m.chain_small(m.after(packed))
        for key in ORDER:
            done[key] = m.step(chains[key])
        g_back, g_in, packed = done["b"], done["i"], done["s"]
        g_att = jnp.concatenate([done["u"], done["v"]], axis=0)
    else:
        g_back, g_in, g_att = [
            lax.psum(
                lax.psum_scatter(jnp.stack(parts).astype(F32), "tp", scatter_dimension=0), "batch"
            )
            for parts in (
                (b_own, b_core, b_far, b_farc),
                (i_own, i_core, i_far, i_farc),
                (a_own, a_core, a_far, a_farc),
            )
        ]
        packed = lax.psum(packed, AXES)
    mine = lax.dynamic_slice_in_dim(packed, 2 * position, 2, axis=0)
    return (
        layer_out.reshape(tokens.shape),
        grad_x.reshape(tokens.shape),
        jnp.transpose(g_att[: 3 * width].reshape(3, width, model), (2, 0, 1)),
        mine[1, :width],
        mine[1, 2 * width : 3 * width],
        g_att[3 * width :],
        packed[11],
        packed[12],
        packed[13],
        g_in,
        mine[0],
        g_back,
        packed[10],
        packed[8],
        packed[9],
    )


def solution(mesh):
    in_specs = (
        P(None, ("batch", "tp"), None),
        P(None, "batch"),
        P(None, ("batch", "tp"), None),
        P(None, None, "tp"),
        P("tp"),
        P("tp"),
        P("tp", None),
        P(),
        P(),
        P(),
        P(None, "tp"),
        P("tp"),
        P("tp", None),
        P(),
        P(),
        P(),
    )
    out_specs = (
        P(None, ("batch", "tp"), None),
        P(None, ("batch", "tp"), None),
        P(None, None, "tp"),
        P("tp"),
        P("tp"),
        P("tp", None),
        P(),
        P(),
        P(),
        P(None, "tp"),
        P("tp"),
        P("tp", None),
        P(),
        P(),
        P(),
    )
    return jax.shard_map(body, mesh=mesh, in_specs=in_specs, out_specs=out_specs, check_vma=False)
```

```python
import math

import jax
import jax.numpy as jnp
from jax import lax
from jax.experimental import pallas as pl
from jax.experimental.pallas import tpu as pltpu
from jax.sharding import PartitionSpec as P

DH = 64
AXES = ("batch", "tp")
epsilon = 1e-05
F32 = jnp.float32
BF16 = jnp.bfloat16


def nt(a, b):
    return lax.dot_general(a, b, (((1,), (1,)), ((), ())), preferred_element_type=F32)


def tn(a, b):
    return lax.dot_general(a, b, (((0,), (0,)), ((), ())), preferred_element_type=F32)


def nn(a, b):
    return jnp.dot(a, b, preferred_element_type=F32)


HBM = pl.BlockSpec(memory_space=pl.ANY)
WHOLE = pl.BlockSpec(memory_space=pltpu.VMEM)
SCALARS = pl.BlockSpec(memory_space=pltpu.SMEM)


class Copies:
    def __init__(self, sems):
        self.sems, self.used = sems, 0
        self.pending = []

    def start(self, src, dst):
        copy = pltpu.make_async_copy(src, dst, self.sems.at[self.used])
        self.used += 1
        copy.start()
        return copy

    def out(self, src, dst):
        self.pending.append(self.start(src, dst))

    def drain(self):
        for copy in self.pending:
            copy.wait()


def call(kernel, name, inputs, outputs, scratch, copies, cost=1000):
    in_specs = [spec for spec, _ in inputs]
    return pl.pallas_call(
        kernel,
        name=name,
        in_specs=in_specs,
        out_specs=tuple(spec for spec, _ in outputs),
        out_shape=tuple(shape for _, shape in outputs),
        scratch_shapes=list(scratch) + [pltpu.SemaphoreType.DMA((copies,))],
        cost_estimate=pl.CostEstimate(flops=cost, transcendentals=0, bytes_accessed=0),
    )(*[value for _, value in inputs])


def shape(dims, dtype):
    return jax.ShapeDtypeStruct(dims, dtype)


def block(i, size):
    return pl.ds(pl.multiple_of(i * size, size), size)


def unit_norm(v):
    middle = jnp.mean(v, axis=-1, keepdims=True)
    centred = v - middle
    inverse = lax.rsqrt(jnp.mean(centred * centred, axis=-1, keepdims=True) + epsilon)
    return centred * inverse, inverse


def norm_grad(scaled, unit, inverse):
    mean_one = jnp.mean(scaled, axis=-1, keepdims=True)
    mean_two = jnp.mean(scaled * unit, axis=-1, keepdims=True)
    return inverse * (scaled - mean_one - unit * mean_two)


STEP = 128


def row_of(part, meta_ref, kind):
    return 2 * jnp.bitwise_xor(part, meta_ref[meta_ref.shape[0] - 1]) + kind


def attend_pair(x, plen, w_pair, smalls, meta, acc=None, vectors=None):
    rows, model = x.shape
    passages = rows // plen
    width = w_pair[0].shape[0] // 4
    heads = width // DH
    units = smalls[0].shape[1] - 3 * width
    last = acc is not None

    def kernel(meta_ref, x_hbm, wa, wb, bias_a, bias_b, *rest):
        if last:
            acc_hbm, b_out, gain, shift = rest[:4]
            qkv_hbm, ctx_hbm, p_hbm, unit_hbm, inv_hbm, low_hbm = rest[4:10]
            x_s, w_s, qkv_s, ctx_s, p_s, acc_s, inv_s, low_s, sems = rest[10:]
        else:
            qkv_hbm, ctx_hbm, p_hbm, acc_out = rest[:4]
            x_s, w_s, qkv_s, ctx_s, p_s, acc_s, sems = rest[4:]
        copies = Copies(sems)
        first = [copies.start(x_hbm, x_s), copies.start(wa, w_s.at[0])]
        second = [copies.start(wb, w_s.at[1])]
        if last:
            held = copies.start(acc_hbm, acc_s)
        for j, waits, bias in ((0, first, bias_a), (1, second, bias_b)):
            for copy in waits:
                copy.wait()
            qkv_s[j] = (nt(x_s[...], w_s[j, : 3 * width, :]) + bias[0:1, units:]).astype(BF16)
            copies.out(qkv_s.at[j], qkv_hbm.at[j])

            def one(g, carry, j=j):
                at = block(g, plen)
                qkv = qkv_s[j, at, :]
                keep = lax.broadcasted_iota(jnp.int32, (1, plen), 1) < meta_ref[g]
                ctx = []
                for h in range(heads):
                    q = qkv[:, h * DH : (h + 1) * DH] * (1.0 / math.sqrt(DH))
                    k = qkv[:, width + h * DH : width + (h + 1) * DH]
                    v = qkv[:, 2 * width + h * DH : 2 * width + (h + 1) * DH]
                    s = jnp.where(keep, nt(q.astype(BF16), k), -1000000000.0)
                    e = jnp.exp(s - jnp.max(s, axis=-1, keepdims=True))
                    p = (e * (1.0 / jnp.sum(e, axis=-1, keepdims=True))).astype(BF16)
                    p_s[j, g * heads + h] = p
                    ctx.append(nn(p, v))
                ctx_s[j, at, :] = jnp.concatenate(ctx, axis=1).astype(BF16)
                return carry

            lax.fori_loop(0, passages, one, 0)
            copies.out(ctx_s.at[j], ctx_hbm.at[j])
            copies.out(p_s.at[j], p_hbm.at[j])
            term = nn(ctx_s[j], w_s[j, 3 * width :, :])
            if last and j == 0:
                held.wait()
            acc_s[...] = term if j == 0 and not last else acc_s[...] + term
        if last:

            def finish(i, carry):
                at = block(i, STEP)
                v = x_s[at, :].astype(F32) + acc_s[at, :] + b_out[...]
                unit, inverse = unit_norm(v)
                acc_s[at, :] = unit
                inv_s[at, :] = jnp.broadcast_to(inverse, (STEP, 128))
                low_s[at, :] = (unit * gain[...] + shift[...]).astype(BF16)
                return carry

            lax.fori_loop(0, rows // STEP, finish, 0)
            copies.out(acc_s, unit_hbm)
            copies.out(inv_s, inv_hbm)
            copies.out(low_s, low_hbm)
        else:
            copies.out(acc_s, acc_out)
        copies.drain()

    inputs = [(SCALARS, meta), (HBM, x), (HBM, w_pair[0]), (HBM, w_pair[1])]
    inputs += [(WHOLE, v) for v in smalls]
    dims = [(2, rows, 3 * width), (2, rows, width), (2, passages * heads, plen, plen)]
    outputs = [(HBM, shape(d, BF16)) for d in dims]
    scratch = [pltpu.VMEM((rows, model), BF16), pltpu.VMEM((2, 4 * width, model), BF16)]
    scratch += [pltpu.VMEM(d, BF16) for d in dims]
    scratch += [pltpu.VMEM((rows, model), F32)]
    if last:
        inputs += [(HBM, acc)] + [(WHOLE, v) for v in vectors]
        outputs += [(HBM, shape((rows, model), F32)), (HBM, shape((rows, 128), F32))]
        outputs += [(HBM, shape((rows, model), BF16))]
        scratch += [pltpu.VMEM((rows, 128), F32), pltpu.VMEM((rows, model), BF16)]
    else:
        outputs += [(HBM, shape((rows, model), F32))]
    return call(kernel, "attend_pair", inputs, outputs, scratch, 16, 1000 if last else 200 * 10**9)


def feed(j, low_s, i_s, b_s, bias, act_s, slope_s):
    units = act_s.shape[2]
    for c in range(0, units, 256):
        cols = slice(c, c + 256)
        t = nn(low_s[...], i_s[j, :, cols]) + bias[0:1, cols]
        cdf = 0.5 * (1.0 + lax.erf(t * (1.0 / math.sqrt(2.0))))
        pdf = jnp.exp(-0.5 * t * t) * (1.0 / math.sqrt(2.0 * math.pi))
        act_s[j, :, cols] = (t * cdf).astype(BF16)
        slope_s[j, :, cols] = (cdf + t * pdf).astype(BF16)
    return nn(act_s[j], b_s[j])


def feed_pair(low, in_pair, back_pair, smalls):
    rows, model = low.shape
    units = in_pair[0].shape[1]

    def kernel(low_hbm, ia, ib, ba, bb, bias_a, bias_b, *rest):
        act_hbm, slope_hbm, acc_hbm, low_s, i_s, b_s, act_s, slope_s, acc_s, sems = rest
        copies = Copies(sems)
        first = [copies.start(low_hbm, low_s), copies.start(ia, i_s.at[0]), copies.start(ba, b_s.at[0])]
        second = [copies.start(ib, i_s.at[1]), copies.start(bb, b_s.at[1])]
        for j, waits, bias in ((0, first, bias_a), (1, second, bias_b)):
            for copy in waits:
                copy.wait()
            term = feed(j, low_s, i_s, b_s, bias, act_s, slope_s)
            copies.out(act_s.at[j], act_hbm.at[j])
            copies.out(slope_s.at[j], slope_hbm.at[j])
            acc_s[...] = acc_s[...] + term if j else term
        copies.out(acc_s, acc_hbm)
        copies.drain()

    inputs = [(HBM, v) for v in (low, *in_pair, *back_pair)] + [(WHOLE, v) for v in smalls]
    outputs = [(HBM, shape((2, rows, units), BF16))] * 2 + [(HBM, shape((rows, model), F32))]
    scratch = [pltpu.VMEM((rows, model), BF16), pltpu.VMEM((2, model, units), BF16)]
    scratch += [pltpu.VMEM((2, units, model), BF16)] + [pltpu.VMEM((2, rows, units), BF16)] * 2
    scratch += [pltpu.VMEM((rows, model), F32)]
    return call(kernel, "feed_pair", inputs, outputs, scratch, 12)


def turn_pair(low, in_pair, back_pair, smalls, unit, acc, dy, meta, vectors, plen):
    rows, model = low.shape
    units = in_pair[0].shape[1]

    def kernel(meta_ref, low_hbm, ia, ib, ba, bb, unit_hbm, acc_hbm, dy_hbm, bias_a, bias_b, *rest):
        gain_one, shift_one, b_back, gain_two, shift_two = rest[:5]
        out_hbm, grad_hbm, ffn_hbm, sum_ref, slope_hbm, oa, ob = rest[5:12]
        low_s, i_s, b_s, act_s, slope_s, acc_s, unit_s, dy_s, out_s, grad_s, ffn_s, g_s, sems = rest[12:]
        copies = Copies(sems)
        first = [copies.start(low_hbm, low_s), copies.start(ia, i_s.at[0]), copies.start(ba, b_s.at[0])]
        second = [copies.start(ib, i_s.at[1]), copies.start(bb, b_s.at[1]), copies.start(acc_hbm, acc_s)]
        third = [copies.start(unit_hbm, unit_s), copies.start(dy_hbm, dy_s)]
        for copy in first:
            copy.wait()
        term = feed(0, low_s, i_s, b_s, bias_a, act_s, slope_s)
        copies.out(slope_s.at[0], slope_hbm.at[0])
        for copy in second:
            copy.wait()
        acc_s[...] = acc_s[...] + term
        acc_s[...] = acc_s[...] + feed(1, low_s, i_s, b_s, bias_b, act_s, slope_s)
        copies.out(slope_s.at[1], slope_hbm.at[1])
        for copy in third:
            copy.wait()
        sum_ref[...] = jnp.zeros_like(sum_ref)

        def step(i, carry):
            at = block(i, STEP)
            normed = unit_s[at, :] * gain_one[...] + shift_one[...]
            u, inverse = unit_norm(normed + acc_s[at, :] + b_back[...])
            out_s[at, :] = (u * gain_two[...] + shift_two[...]).astype(BF16)
            slot = lax.broadcasted_iota(jnp.int32, (STEP, 1), 0) + (i * STEP) % plen
            keep = slot < meta_ref[(i * STEP) // plen]
            grad_y = jnp.where(keep, dy_s[at, :].astype(F32), 0.0)
            grad = norm_grad(grad_y * gain_two[...], u, inverse)
            grad_s[at, :] = grad
            ffn_s[at, :] = grad.astype(BF16)
            sum_ref[8:9, :] += jnp.sum(grad_y * u, axis=0, keepdims=True)
            sum_ref[9:10, :] += jnp.sum(grad_y, axis=0, keepdims=True)
            sum_ref[10:11, :] += jnp.sum(grad, axis=0, keepdims=True)
            return carry

        lax.fori_loop(0, rows // STEP, step, 0)
        copies.out(out_s, out_hbm)
        copies.out(grad_s, grad_hbm)
        copies.out(ffn_s, ffn_hbm)
        for j, out in ((1, ob), (0, oa)):
            g_s[j] = tn(act_s[j], ffn_s[...]).astype(BF16)
            copies.out(g_s.at[j], out)
        copies.drain()

    inputs = [(SCALARS, meta)] + [(HBM, v) for v in (low, *in_pair, *back_pair, unit, acc, dy)]
    inputs += [(WHOLE, v) for v in (*smalls, *vectors)]
    outputs = [(HBM, shape((rows, model), d)) for d in (BF16, F32, BF16)]
    outputs += [(WHOLE, shape((16, model), F32)), (HBM, shape((2, rows, units), BF16))]
    outputs += [(HBM, shape((units, model), BF16))] * 2
    scratch = [pltpu.VMEM((rows, model), BF16), pltpu.VMEM((2, model, units), BF16)]
    scratch += [pltpu.VMEM((2, units, model), BF16)] + [pltpu.VMEM((2, rows, units), BF16)] * 2
    scratch += [pltpu.VMEM((rows, model), d) for d in (F32, F32, BF16, BF16, F32, BF16)]
    scratch += [pltpu.VMEM((2, units, model), BF16)]
    return call(kernel, "turn_pair", inputs, outputs, scratch, 20)


def outer_pair(acts, grad_ffn):
    _, rows, units = acts.shape
    model = grad_ffn.shape[1]

    def kernel(act_hbm, g_hbm, oa, ob, act_s, g_s, out_s, sems):
        copies = Copies(sems)
        whole = copies.start(g_hbm, g_s)
        waits = [copies.start(act_hbm.at[j], act_s.at[j]) for j in (1, 0)]
        whole.wait()
        for j, wait, out in ((1, waits[0], ob), (0, waits[1], oa)):
            wait.wait()
            out_s[j] = tn(act_s[j], g_s[...]).astype(BF16)
            copies.out(out_s.at[j], out)
        copies.drain()

    inputs = [(HBM, acts), (HBM, grad_ffn)]
    outputs = [(HBM, shape((units, model), BF16))] * 2
    scratch = [pltpu.VMEM((2, rows, units), BF16), pltpu.VMEM((rows, model), BF16)]
    scratch += [pltpu.VMEM((2, units, model), BF16)]
    return call(kernel, "outer_pair", inputs, outputs, scratch, 8, 200 * 10**9)


def feed_back_pair(grad_ffn, slopes, which, in_pair, back_pair, low, start, parts, sums, meta, unit=None, inverse=None, gain=None):
    rows, model = grad_ffn.shape
    units = slopes[0].shape[2]
    last = unit is not None

    def kernel(meta_ref, before, g_hbm, sa, sb, ia, ib, ba, bb, low_hbm, start_hbm, *rest):
        if last:
            unit_hbm, inv_hbm, gain_ref = rest[:3]
            rest = rest[3:]
            oa, ob, sum_ref, one_hbm, attn_hbm = rest[:5]
            g_s, slope_s, i_s, b_s, low_s, acc_s, pre_s, out_s, line, unit_s, inv_s, attn_s, sems = rest[5:]
        else:
            oa, ob, sum_ref, acc_out = rest[:4]
            g_s, slope_s, i_s, b_s, low_s, acc_s, pre_s, out_s, line, sems = rest[4:]
        copies = Copies(sems)
        sum_ref[...] = before[...]
        weights = {1: (bb, ib, sb.at[which]), 0: (ba, ia, sa.at[which])}
        early = copies.start(g_hbm, g_s)
        waits, later = {}, {}
        for j in (1, 0):
            waits[j] = [copies.start(weights[j][0], b_s.at[j]), copies.start(weights[j][2], slope_s.at[j])]
            later[j] = [copies.start(weights[j][1], i_s.at[j])]
            if j == 1:
                later[j] += [copies.start(low_hbm, low_s), copies.start(start_hbm, acc_s)]
        if last:
            late = [copies.start(unit_hbm, unit_s), copies.start(inv_hbm, inv_s)]
        early.wait()
        for j, out in ((1, ob), (0, oa)):
            for wait in waits[j]:
                wait.wait()
            for c in range(0, units, 256):
                cols = slice(c, c + 256)
                pre = nt(g_s[...], b_s[j, cols, :]) * slope_s[j, :, cols].astype(F32)
                pre = pre.astype(BF16)
                pre_s[:, cols] = pre
                line[:, cols] = jnp.sum(pre.astype(F32), axis=0, keepdims=True)
            sum_ref[pl.ds(row_of(parts[j], meta_ref, 0), 1), :] = line[...]
            for wait in later[j]:
                wait.wait()
            acc_s[...] = acc_s[...] + nt(pre_s[...], i_s[j])
            out_s[j] = tn(low_s[...], pre_s[...]).astype(BF16)
            copies.out(out_s.at[j], out)
        if last:
            for wait in late:
                wait.wait()

            def finish(i, carry):
                at = block(i, STEP)
                normed = acc_s[at, :]
                u = unit_s[at, :]
                grad = norm_grad(normed * gain_ref[0:1, :], u, inv_s[at, 0:1])
                sum_ref[11:12, :] += jnp.sum(grad, axis=0, keepdims=True)
                sum_ref[12:13, :] += jnp.sum(normed * u, axis=0, keepdims=True)
                sum_ref[13:14, :] += jnp.sum(normed, axis=0, keepdims=True)
                acc_s[at, :] = grad
                attn_s[at, :] = grad.astype(BF16)
                return carry

            lax.fori_loop(0, rows // STEP, finish, 0)
            copies.out(acc_s, one_hbm)
            copies.out(attn_s, attn_hbm)
        else:
            copies.out(acc_s, acc_out)
        copies.drain()

    inputs = [(SCALARS, meta), (WHOLE, sums)]
    inputs += [(HBM, v) for v in (grad_ffn, *slopes, *in_pair, *back_pair, low, start)]
    outputs = [(HBM, shape((model, units), BF16))] * 2 + [(WHOLE, shape((16, model), F32))]
    outputs += [(HBM, shape((rows, model), F32))]
    scratch = [pltpu.VMEM((rows, model), BF16), pltpu.VMEM((2, rows, units), BF16)]
    scratch += [pltpu.VMEM((2, model, units), BF16), pltpu.VMEM((2, units, model), BF16)]
    scratch += [pltpu.VMEM((rows, model), BF16), pltpu.VMEM((rows, model), F32)]
    scratch += [pltpu.VMEM((rows, units), BF16), pltpu.VMEM((2, model, units), BF16)]
    scratch += [pltpu.VMEM((1, units), F32)]
    if last:
        inputs += [(HBM, unit), (HBM, inverse), (WHOLE, gain)]
        outputs += [(HBM, shape((rows, model), BF16))]
        scratch += [pltpu.VMEM((rows, model), F32), pltpu.VMEM((rows, 128), F32)]
        scratch += [pltpu.VMEM((rows, model), BF16)]
    return call(kernel, "feed_back_pair", inputs, outputs, scratch, 20, 200 * 10**9)


def attend_back_pair(x, plen, grad_attn, qkvs, ctxs, probs, which, w_pair, start, parts, sums, meta):
    rows, model = x.shape
    passages = rows // plen
    width = ctxs[0].shape[2]
    heads = width // DH

    def kernel(meta_ref, before, x_hbm, g_hbm, qa, qb, ca, cb, pa, pb, wa, wb, start_hbm, *rest):
        oa, ob, sum_ref, acc_out = rest[:4]
        x_s, g_s, qkv_s, ctx_s, p_s, w_s, acc_s, grow_s, out_s, gc_s, sems = rest[4:]
        copies = Copies(sems)
        sum_ref[...] = before[...]
        early = [copies.start(g_hbm, g_s)]
        of = {0: (wa, ca, qa, pa), 1: (wb, cb, qb, pb)}
        waits, middle, later = {}, {}, {}
        for j in (1, 0):
            waits[j] = [copies.start(of[j][0], w_s.at[j]), copies.start(of[j][1].at[which], ctx_s.at[j])]
            middle[j] = [copies.start(of[j][2].at[which], qkv_s.at[j]), copies.start(of[j][3].at[which], p_s.at[j])]
            later[j] = []
            if j == 1:
                later[j] = [copies.start(x_hbm, x_s), copies.start(start_hbm, acc_s)]
        for wait in early:
            wait.wait()
        for j, out in ((1, ob), (0, oa)):
            for wait in waits[j]:
                wait.wait()
            gc_s[...] = nt(g_s[...], w_s[j, 3 * width :, :]).astype(BF16)
            out_s[j, 3 * width :, :] = tn(ctx_s[j], g_s[...]).astype(BF16)
            for wait in middle[j]:
                wait.wait()

            def one(g, carry, j=j):
                at = block(g, plen)
                qkv = qkv_s[j, at, :]
                grad_ctx = gc_s[at, :]
                gq, gk, gv = [], [], []
                for h in range(heads):
                    q = qkv[:, h * DH : (h + 1) * DH]
                    k = qkv[:, width + h * DH : width + (h + 1) * DH]
                    v = qkv[:, 2 * width + h * DH : 2 * width + (h + 1) * DH]
                    gc = grad_ctx[:, h * DH : (h + 1) * DH]
                    low = p_s[j, g * heads + h]
                    p = low.astype(F32)
                    gp = nt(gc, v)
                    delta = jnp.sum(p * gp, axis=-1, keepdims=True)
                    gs = (p * (gp - delta)).astype(BF16)
                    gq.append(nn(gs, k) * (1.0 / math.sqrt(DH)))
                    gk.append(tn(gs, q) * (1.0 / math.sqrt(DH)))
                    gv.append(tn(low, gc))
                grow = jnp.concatenate(gq + gk + gv, axis=1).astype(BF16)
                grow_s[at, :] = grow
                return carry + jnp.sum(grow.astype(F32), axis=0, keepdims=True)

            line = lax.fori_loop(0, passages, one, jnp.zeros((1, 3 * width), F32))
            line = jnp.concatenate([line, jnp.zeros((1, model - 3 * width), F32)], axis=1)
            sum_ref[pl.ds(row_of(parts[j], meta_ref, 1), 1), :] = line
            for wait in later[j]:
                wait.wait()
            out_s[j, : 3 * width, :] = tn(grow_s[...], x_s[...]).astype(BF16)
            copies.out(out_s.at[j], out)
            acc_s[...] = acc_s[...] + nn(grow_s[...], w_s[j, : 3 * width, :])
        copies.out(acc_s, acc_out)
        copies.drain()

    inputs = [(SCALARS, meta), (WHOLE, sums)]
    inputs += [(HBM, v) for v in (x, grad_attn, *qkvs, *ctxs, *probs, *w_pair, start)]
    outputs = [(HBM, shape((4 * width, model), BF16))] * 2
    outputs += [(WHOLE, shape((16, model), F32)), (HBM, shape((rows, model), F32))]
    scratch = [pltpu.VMEM((rows, model), BF16), pltpu.VMEM((rows, model), BF16)]
    scratch += [pltpu.VMEM(v[0].shape, BF16) for v in (qkvs, ctxs, probs)]
    scratch += [pltpu.VMEM((2, 4 * width, model), BF16), pltpu.VMEM((rows, model), F32)]
    scratch += [pltpu.VMEM((rows, 3 * width), BF16), pltpu.VMEM((2, 4 * width, model), BF16)]
    scratch += [pltpu.VMEM((rows, width), BF16)]
    return call(kernel, "attend_back_pair", inputs, outputs, scratch, 20, 200 * 10**9)


def tie(value, *others):
    return lax.optimization_barrier((value, *others))[0]


def flat_perm(move):
    pairs = []
    for z in range(4):
        for y in range(2):
            for x in range(2):
                for c in range(2):
                    z2, y2, x2, c2 = move(z, y, x, c)
                    pairs.append((((z * 2 + y) * 2 + x) * 2 + c, ((z2 * 2 + y2) * 2 + x2) * 2 + c2))
    return pairs


def add(*terms):
    return sum(term.astype(F32) for term in terms).astype(BF16)


ORDER = "svibusvisubvsuivsuvibuvsui"


class GridMoves:
    def __init__(self):
        self.row = lax.axis_index("batch") % 2
        self.layer = lax.axis_index("batch") // 2 % 2
        self.side = (self.row + self.layer) % 2
        self.to_core = flat_perm(lambda z, y, x, c: (z, y, x, 1 - c))
        self.to_x = flat_perm(lambda z, y, x, c: (z, y, 1 - x, c))
        self.to_y = flat_perm(lambda z, y, x, c: (z, 1 - y, x, c))
        self.to_z = flat_perm(lambda z, y, x, c: (z ^ 1, y, x, c))
        self.to_zz = flat_perm(lambda z, y, x, c: (z ^ 2, y, x, c))
        self.mark = None

    def send(self, value, pairs):
        return lax.ppermute(value, AXES, pairs)

    def half(self, value, which):
        if isinstance(value, tuple):
            return jnp.where(which == 0, value[0], value[1])
        if isinstance(value, dict):
            rows = value["rows"] // 2
            at = value["at"] + which * rows
            return lax.dynamic_slice_in_dim(value["of"], at, rows, axis=0)
        if isinstance(value, list):
            return add(*(self.half(term, which) for term in value))
        rows = value.shape[0] // 2
        return lax.dynamic_slice_in_dim(value, which * rows, rows, axis=0)

    def order(self, mine, other, bit):
        low = jnp.where(bit == 0, mine, other)
        high = jnp.where(bit == 0, other, mine)
        return jnp.concatenate([low, high], axis=0)

    def after(self, value):
        if self.mark is not None:
            value = tie(value, self.mark)
        return value

    def pieces(self, mine):
        first, second = self.halves(mine)
        return [self.send(first, self.to_y), self.send(second, self.to_z)]

    def whole(self, mine, pieces):
        return self.order(mine, jnp.concatenate(pieces, axis=0), self.side)

    def halves(self, value):
        rows = value.shape[0] // 2
        return value[:rows], value[rows:]

    def sums(self, one, two):
        return [add(a, b) for a, b in zip(self.halves(one), self.halves(two))]

    def chain(self, near, got):
        got = tuple(self.after(part) for part in got)
        got = got if len(got) == 2 else got[0]
        pass_on = self.half([*near, got], 1 - self.row)
        keep = self.half([*near, got], self.row)
        got = self.send(pass_on, self.to_y)
        yield pass_on
        yield from self.chain_z(add(keep, self.after(got)))

    def chain_zy(self, near, got):
        got = tuple(self.after(part) for part in got)
        pass_on = self.half([*near, got], 1 - self.layer)
        keep = self.half([*near, got], self.layer)
        got = self.send(pass_on, self.to_z)
        yield pass_on
        keep = add(keep, self.after(got))
        pass_on = self.half(keep, 1 - self.row)
        keep = self.half(keep, self.row)
        got = self.send(pass_on, self.to_y)
        yield pass_on
        keep = add(keep, self.after(got))
        got = self.send(keep, self.to_zz)
        yield keep
        keep = add(keep, self.after(got))
        got = self.send(keep, self.to_y)
        yield keep
        keep = self.order(keep, self.after(got), self.row)
        got = self.send(keep, self.to_z)
        yield keep
        yield self.order(keep, self.after(got), self.layer).astype(F32)

    def chain_y(self, near, far):
        pass_on = jnp.concatenate(
            [self.half(term, 1 - self.row) for term in (near, far)], axis=0
        )
        got = self.send(pass_on, self.to_y)
        yield pass_on
        got = self.halves(self.after(got))
        far = add(*(self.half(term, self.row) for term in far), got[1])
        keep = add(*(self.half(term, self.row) for term in near), got[0])
        got = self.send(far, self.to_x)
        yield far
        yield from self.chain_z(add(keep, self.after(got)))

    def chain_z(self, keep):
        pass_on = self.half(keep, 1 - self.layer)
        keep = self.half(keep, self.layer)
        got = self.send(pass_on, self.to_z)
        yield pass_on
        keep = add(keep, self.after(got))
        got = self.send(keep, self.to_zz)
        yield keep
        keep = add(keep, self.after(got))
        got = self.send(keep, self.to_z)
        yield keep
        keep = self.order(keep, self.after(got), self.layer)
        got = self.send(keep, self.to_y)
        yield keep
        yield self.order(keep, self.after(got), self.row).astype(F32)

    def chain_small(self, value):
        for pairs in (self.to_core, self.to_x, self.to_y, self.to_z, self.to_zz):
            got = self.send(value, pairs)
            yield value
            value = value + self.after(got)
        yield value

    def step(self, chain):
        self.mark = next(chain)
        return self.mark


def body(
    tokens,
    passage_lengths,
    cotangent,
    w_qkv,
    b_query,
    b_value,
    w_out,
    b_out,
    gain_one,
    shift_one,
    w_in,
    b_in,
    w_back,
    b_back,
    gain_two,
    shift_two,
):
    micro_count, own_rows, model = tokens.shape
    tp_count = lax.axis_size("tp")
    batch_count = lax.axis_size("batch")
    plen = own_rows * tp_count // passage_lengths.shape[1]
    own_passages = own_rows // plen
    assert own_passages * plen == own_rows and tp_count == 4
    grid = (batch_count, tp_count) == (8, 4)
    width = w_qkv.shape[2]
    rows = micro_count * own_rows
    position = lax.axis_index("tp")

    vector = lambda v: v.reshape(1, -1)
    x = tokens.reshape(rows, model)
    dy = cotangent.reshape(rows, model)
    lengths = lax.dynamic_slice_in_dim(
        passage_lengths, position * own_passages, own_passages, axis=1
    ).reshape(micro_count * own_passages)
    meta = jnp.concatenate([lengths, (position if grid else 0 * position).reshape(1)])
    qkvo = jnp.concatenate([jnp.transpose(w_qkv, (1, 2, 0)).reshape(3 * width, model), w_out], axis=0)
    small = vector(jnp.concatenate([b_in.astype(F32), b_query, jnp.zeros_like(b_query), b_value]))
    if grid:
        m = moves = GridMoves()
        x_att = m.send(m.half(qkvo, m.side), m.to_x)
        c_att = m.send(qkvo, m.to_core)
        c_small = m.send(small, m.to_core)
        x_small = m.send(small, m.to_x)
        half_in = m.half(w_in, m.side)
        meta = tie(meta, half_in)
        att, smalls = [qkvo, c_att], [small, c_small]
    else:
        att, smalls, ins, backs = [
            list(lax.all_gather(v, "tp", axis=0)) for v in (qkvo, small, w_in, w_back)
        ]
    qkv_near, ctx_near, p_near, acc = attend_pair(x, plen, att[:2], smalls[:2], meta)
    y = x
    if grid:
        x_att, x_small = tie(x_att, acc), tie(x_small, acc)
        y_att = m.send(x_att, m.to_y)
        half_back = m.half(w_back, m.side)
        x_in = m.send(tie(half_in, x_att), m.to_x)
        smalls += [x_small, m.send(x_small, m.to_core)]
        y_att = tie(y_att, half_back, smalls[3])
        f_att = m.order(x_att, y_att, m.side)
        att += [f_att, m.send(f_att, m.to_core)]
        c_in = m.send(tie(w_in, f_att), m.to_core)
        c_back = m.send(tie(w_back, f_att), m.to_core)
        x_in = tie(x_in, f_att)
        y_in = m.send(x_in, m.to_y)
        x_back = m.send(tie(half_back, x_in), m.to_x)
        y = tie(x, x_in)
    qkv_far, ctx_far, p_far, unit, inverse, low = attend_pair(
        y, plen, att[2:], smalls[2:], meta, acc, [vector(v) for v in (b_out, gain_one, shift_one)]
    )
    if grid:
        y_in = tie(y_in, low)
        f_in = m.order(x_in, y_in, m.side)
        ins = [w_in, c_in, f_in, m.send(f_in, m.to_core)]
        x_back = tie(x_back, f_in)
        p_back = m.pieces(x_back)
        backs = [w_back, c_back]
        low = tie(low, x_back)
    act_near, slope_near, feed_near = feed_pair(low, ins[:2], backs[:2], smalls[:2])
    if grid:
        p_back[0] = tie(p_back[0], feed_near)
        f_back = m.whole(x_back, p_back)
        backs += [f_back, m.send(f_back, m.to_core)]
    layer_out, grad_two, grad_ffn, sums, slope_far, b_far, b_farc = turn_pair(
        low,
        ins[2:],
        backs[2:],
        smalls[2:],
        unit,
        feed_near,
        dy,
        meta,
        [vector(v) for v in (gain_one, shift_one, b_back, gain_two, shift_two)],
        plen,
    )
    if grid:
        got_b3 = m.send(b_farc, m.to_core)
    b_own, b_core = outer_pair(act_near, grad_ffn)
    if grid:
        got_b1 = m.send(b_core, m.to_core)
        b_far = m.sums(b_far, tie(got_b3, b_own))
        got_bx = [m.send(part, m.to_x) for part in b_far]
        grad_ffn = tie(grad_ffn, *b_far)
    slopes = (slope_near, slope_far)
    feed_sent = [(v[1], v[3]) for v in (ins, backs)]
    feed_kept = [(v[0], v[2]) for v in (ins, backs)]
    i_core, i_farc, sums, normed = feed_back_pair(
        grad_ffn, slopes, 1, *feed_sent, low, grad_two, (1, 3), sums, meta
    )
    if grid:
        got_i1, got_i3 = [m.send(v, m.to_core) for v in (i_core, i_farc)]
        b_near = [b_own, tie(got_b1, normed)]
        got_bx[0] = tie(got_bx[0], normed)
        normed = tie(normed, got_bx[0])
    i_own, i_far, sums, grad_one, grad_attn = feed_back_pair(
        grad_ffn,
        slopes,
        0,
        *feed_kept,
        low,
        normed,
        (0, 2),
        sums,
        meta,
        unit,
        inverse,
        vector(gain_one),
    )
    if grid:
        i_far = m.sums(i_far, tie(got_i3, grad_attn))
        got_ix = [m.send(part, m.to_x) for part in i_far]
        m.mark = i_far[0]
        chain_b = m.chain(b_near, got_bx)
        m.step(chain_b)
        grad_attn = tie(grad_attn, m.mark)
    kept = [(qkv_near, qkv_far), (ctx_near, ctx_far), (p_near, p_far)]
    a_core, a_farc, sums, grad_x = attend_back_pair(
        x, plen, grad_attn, *kept, 1, (att[1], att[3]), grad_one, (1, 3), sums, meta
    )
    if grid:
        got_a1, got_a3 = [m.send(v, m.to_core) for v in (a_core, a_farc)]
        i_near = [i_own, got_i1]
        m.mark = grad_x
        m.step(chain_b)
        got_ix[0] = m.after(got_ix[0])
        grad_x = tie(grad_x, got_ix[0])
    a_own, a_far, packed, grad_x = attend_back_pair(
        x, plen, grad_attn, *kept, 0, (att[0], att[2]), grad_x, (0, 2), sums, meta
    )
    if grid:
        m.mark = grad_x
        got_a3 = m.after(got_a3)
        rows_a = a_far.shape[0] // 2
        low_far = [v[:rows_a] for v in (a_far, got_a3)]
        low_far = add(*low_far)
        got_ax = m.send(low_far, m.to_x)
        m.mark = low_far
        got_a1 = m.after(got_a1)
        view = lambda v, at: {"of": v, "at": at, "rows": rows_a}
        low_near = [view(v, 0) for v in (a_own, got_a1)]
        high_near = [view(v, rows_a) for v in (a_own, got_a1)]
        high_far = [view(v, rows_a) for v in (a_far, got_a3)]
        chains = {"b": chain_b, "i": m.chain_zy(i_near, got_ix), "v": m.chain_y(high_near, high_far)}
        done = {}
        for key in "vib":
            done[key] = m.step(chains[key])
        chains["u"] = m.chain(low_near, [got_ax])
        chains["s"] = m.chain_small(m.after(packed))
        for key in ORDER:
            done[key] = m.step(chains[key])
        g_back, g_in, packed = done["b"], done["i"], done["s"]
        g_att = jnp.concatenate([done["u"], done["v"]], axis=0)
    else:
        g_back, g_in, g_att = [
            lax.psum(
                lax.psum_scatter(jnp.stack(parts).astype(F32), "tp", scatter_dimension=0), "batch"
            )
            for parts in (
                (b_own, b_core, b_far, b_farc),
                (i_own, i_core, i_far, i_farc),
                (a_own, a_core, a_far, a_farc),
            )
        ]
        packed = lax.psum(packed, AXES)
    mine = lax.dynamic_slice_in_dim(packed, 2 * position, 2, axis=0)
    return (
        layer_out.reshape(tokens.shape),
        grad_x.reshape(tokens.shape),
        jnp.transpose(g_att[: 3 * width].reshape(3, width, model), (2, 0, 1)),
        mine[1, :width],
        mine[1, 2 * width : 3 * width],
        g_att[3 * width :],
        packed[11],
        packed[12],
        packed[13],
        g_in,
        mine[0],
        g_back,
        packed[10],
        packed[8],
        packed[9],
    )


def solution(mesh):
    in_specs = (
        P(None, ("batch", "tp"), None),
        P(None, "batch"),
        P(None, ("batch", "tp"), None),
        P(None, None, "tp"),
        P("tp"),
        P("tp"),
        P("tp", None),
        P(),
        P(),
        P(),
        P(None, "tp"),
        P("tp"),
        P("tp", None),
        P(),
        P(),
        P(),
    )
    out_specs = (
        P(None, ("batch", "tp"), None),
        P(None, ("batch", "tp"), None),
        P(None, None, "tp"),
        P("tp"),
        P("tp"),
        P("tp", None),
        P(),
        P(),
        P(),
        P(None, "tp"),
        P("tp"),
        P("tp", None),
        P(),
        P(),
        P(),
    )
    return jax.shard_map(body, mesh=mesh, in_specs=in_specs, out_specs=out_specs, check_vma=False)
```

```python
import math

import jax
import jax.numpy as jnp
from jax import lax
from jax.experimental import pallas as pl
from jax.experimental.pallas import tpu as pltpu
from jax.sharding import PartitionSpec as P

DH = 64
AXES = ("batch", "tp")
epsilon = 1e-05
F32 = jnp.float32
BF16 = jnp.bfloat16


def nt(a, b):
    return lax.dot_general(a, b, (((1,), (1,)), ((), ())), preferred_element_type=F32)


def tn(a, b):
    return lax.dot_general(a, b, (((0,), (0,)), ((), ())), preferred_element_type=F32)


def nn(a, b):
    return jnp.dot(a, b, preferred_element_type=F32)


HBM = pl.BlockSpec(memory_space=pl.ANY)
WHOLE = pl.BlockSpec(memory_space=pltpu.VMEM)
SCALARS = pl.BlockSpec(memory_space=pltpu.SMEM)


class Copies:
    def __init__(self, sems):
        self.sems, self.used = sems, 0
        self.pending = []

    def start(self, src, dst):
        copy = pltpu.make_async_copy(src, dst, self.sems.at[self.used])
        self.used += 1
        copy.start()
        return copy

    def out(self, src, dst):
        self.pending.append(self.start(src, dst))

    def drain(self):
        for copy in self.pending:
            copy.wait()


def call(kernel, name, inputs, outputs, scratch, copies, cost=1000):
    in_specs = [spec for spec, _ in inputs]
    return pl.pallas_call(
        kernel,
        name=name,
        in_specs=in_specs,
        out_specs=tuple(spec for spec, _ in outputs),
        out_shape=tuple(shape for _, shape in outputs),
        scratch_shapes=list(scratch) + [pltpu.SemaphoreType.DMA((copies,))],
        cost_estimate=pl.CostEstimate(flops=cost, transcendentals=0, bytes_accessed=0),
    )(*[value for _, value in inputs])


def shape(dims, dtype):
    return jax.ShapeDtypeStruct(dims, dtype)


def block(i, size):
    return pl.ds(pl.multiple_of(i * size, size), size)


def unit_norm(v):
    middle = jnp.mean(v, axis=-1, keepdims=True)
    centred = v - middle
    inverse = lax.rsqrt(jnp.mean(centred * centred, axis=-1, keepdims=True) + epsilon)
    return centred * inverse, inverse


def norm_grad(scaled, unit, inverse):
    mean_one = jnp.mean(scaled, axis=-1, keepdims=True)
    mean_two = jnp.mean(scaled * unit, axis=-1, keepdims=True)
    return inverse * (scaled - mean_one - unit * mean_two)


STEP = 128


def row_of(part, meta_ref, kind):
    return 2 * jnp.bitwise_xor(part, meta_ref[meta_ref.shape[0] - 1]) + kind


def attend_pair(x, plen, w_pair, smalls, meta, acc=None, vectors=None):
    rows, model = x.shape
    passages = rows // plen
    width = w_pair[0].shape[0] // 4
    heads = width // DH
    units = smalls[0].shape[1] - 3 * width
    last = acc is not None

    def kernel(meta_ref, x_hbm, wa, wb, bias_a, bias_b, *rest):
        if last:
            acc_hbm, b_out, gain, shift = rest[:4]
            qkv_hbm, ctx_hbm, p_hbm, unit_hbm, inv_hbm, low_hbm = rest[4:10]
            x_s, w_s, qkv_s, ctx_s, p_s, acc_s, inv_s, low_s, sems = rest[10:]
        else:
            qkv_hbm, ctx_hbm, p_hbm, acc_out = rest[:4]
            x_s, w_s, qkv_s, ctx_s, p_s, acc_s, sems = rest[4:]
        copies = Copies(sems)
        first = [copies.start(x_hbm, x_s), copies.start(wa, w_s.at[0])]
        second = [copies.start(wb, w_s.at[1])]
        if last:
            held = copies.start(acc_hbm, acc_s)
        for j, waits, bias in ((0, first, bias_a), (1, second, bias_b)):
            for copy in waits:
                copy.wait()
            qkv_s[j] = (nt(x_s[...], w_s[j, : 3 * width, :]) + bias[0:1, units:]).astype(BF16)
            copies.out(qkv_s.at[j], qkv_hbm.at[j])

            def one(g, carry, j=j):
                at = block(g, plen)
                qkv = qkv_s[j, at, :]
                keep = lax.broadcasted_iota(jnp.int32, (plen, 1), 0) < meta_ref[g]
                ctx = []
                for h in range(heads):
                    q = qkv[:, h * DH : (h + 1) * DH] * (1.0 / math.sqrt(DH))
                    k = qkv[:, width + h * DH : width + (h + 1) * DH]
                    v = qkv[:, 2 * width + h * DH : 2 * width + (h + 1) * DH]
                    s = jnp.where(keep, nt(k, q.astype(BF16)), -1000000000.0)
                    e = jnp.exp(s - jnp.max(s, axis=0, keepdims=True))
                    p = (e * (1.0 / jnp.sum(e, axis=0, keepdims=True))).astype(BF16)
                    p_s[j, g * heads + h] = p
                    ctx.append(tn(v, p))
                ctx_s[j, at, :] = jnp.concatenate(ctx, axis=0).T.astype(BF16)
                return carry

            lax.fori_loop(0, passages, one, 0, unroll=True)
            copies.out(ctx_s.at[j], ctx_hbm.at[j])
            copies.out(p_s.at[j], p_hbm.at[j])
            term = nn(ctx_s[j], w_s[j, 3 * width :, :])
            if last and j == 0:
                held.wait()
            acc_s[...] = term if j == 0 and not last else acc_s[...] + term
        if last:

            def finish(i, carry):
                at = block(i, STEP)
                v = x_s[at, :].astype(F32) + acc_s[at, :] + b_out[...]
                unit, inverse = unit_norm(v)
                acc_s[at, :] = unit
                inv_s[at, :] = jnp.broadcast_to(inverse, (STEP, 128))
                low_s[at, :] = (unit * gain[...] + shift[...]).astype(BF16)
                return carry

            lax.fori_loop(0, rows // STEP, finish, 0)
            copies.out(acc_s, unit_hbm)
            copies.out(inv_s, inv_hbm)
            copies.out(low_s, low_hbm)
        else:
            copies.out(acc_s, acc_out)
        copies.drain()

    inputs = [(SCALARS, meta), (HBM, x), (HBM, w_pair[0]), (HBM, w_pair[1])]
    inputs += [(WHOLE, v) for v in smalls]
    dims = [(2, rows, 3 * width), (2, rows, width), (2, passages * heads, plen, plen)]
    outputs = [(HBM, shape(d, BF16)) for d in dims]
    scratch = [pltpu.VMEM((rows, model), BF16), pltpu.VMEM((2, 4 * width, model), BF16)]
    scratch += [pltpu.VMEM(d, BF16) for d in dims]
    scratch += [pltpu.VMEM((rows, model), F32)]
    if last:
        inputs += [(HBM, acc)] + [(WHOLE, v) for v in vectors]
        outputs += [(HBM, shape((rows, model), F32)), (HBM, shape((rows, 128), F32))]
        outputs += [(HBM, shape((rows, model), BF16))]
        scratch += [pltpu.VMEM((rows, 128), F32), pltpu.VMEM((rows, model), BF16)]
    else:
        outputs += [(HBM, shape((rows, model), F32))]
    return call(kernel, "attend_pair", inputs, outputs, scratch, 16, 1000 if last else 200 * 10**9)


def feed(j, low_s, i_s, b_s, bias, act_s, slope_s):
    units = act_s.shape[2]
    for c in range(0, units, 256):
        cols = slice(c, c + 256)
        t = nn(low_s[...], i_s[j, :, cols]) + bias[0:1, cols]
        cdf = 0.5 * (1.0 + lax.erf(t * (1.0 / math.sqrt(2.0))))
        pdf = jnp.exp(-0.5 * t * t) * (1.0 / math.sqrt(2.0 * math.pi))
        act_s[j, :, cols] = (t * cdf).astype(BF16)
        slope_s[j, :, cols] = (cdf + t * pdf).astype(BF16)
    return nn(act_s[j], b_s[j])


def feed_pair(low, in_pair, back_pair, smalls):
    rows, model = low.shape
    units = in_pair[0].shape[1]

    def kernel(low_hbm, ia, ib, ba, bb, bias_a, bias_b, *rest):
        act_hbm, slope_hbm, acc_hbm, low_s, i_s, b_s, act_s, slope_s, acc_s, sems = rest
        copies = Copies(sems)
        first = [copies.start(low_hbm, low_s), copies.start(ia, i_s.at[0]), copies.start(ba, b_s.at[0])]
        second = [copies.start(ib, i_s.at[1]), copies.start(bb, b_s.at[1])]
        for j, waits, bias in ((0, first, bias_a), (1, second, bias_b)):
            for copy in waits:
                copy.wait()
            term = feed(j, low_s, i_s, b_s, bias, act_s, slope_s)
            copies.out(act_s.at[j], act_hbm.at[j])
            copies.out(slope_s.at[j], slope_hbm.at[j])
            acc_s[...] = acc_s[...] + term if j else term
        copies.out(acc_s, acc_hbm)
        copies.drain()

    inputs = [(HBM, v) for v in (low, *in_pair, *back_pair)] + [(WHOLE, v) for v in smalls]
    outputs = [(HBM, shape((2, rows, units), BF16))] * 2 + [(HBM, shape((rows, model), F32))]
    scratch = [pltpu.VMEM((rows, model), BF16), pltpu.VMEM((2, model, units), BF16)]
    scratch += [pltpu.VMEM((2, units, model), BF16)] + [pltpu.VMEM((2, rows, units), BF16)] * 2
    scratch += [pltpu.VMEM((rows, model), F32)]
    return call(kernel, "feed_pair", inputs, outputs, scratch, 12)


def turn_pair(low, in_pair, back_pair, smalls, unit, acc, dy, meta, vectors, plen):
    rows, model = low.shape
    units = in_pair[0].shape[1]

    def kernel(meta_ref, low_hbm, ia, ib, ba, bb, unit_hbm, acc_hbm, dy_hbm, bias_a, bias_b, *rest):
        gain_one, shift_one, b_back, gain_two, shift_two = rest[:5]
        out_hbm, grad_hbm, ffn_hbm, sum_ref, slope_hbm, oa, ob = rest[5:12]
        low_s, i_s, b_s, act_s, slope_s, acc_s, unit_s, dy_s, out_s, grad_s, ffn_s, g_s, sems = rest[12:]
        copies = Copies(sems)
        first = [copies.start(low_hbm, low_s), copies.start(ia, i_s.at[0]), copies.start(ba, b_s.at[0])]
        second = [copies.start(ib, i_s.at[1]), copies.start(bb, b_s.at[1]), copies.start(acc_hbm, acc_s)]
        third = [copies.start(unit_hbm, unit_s), copies.start(dy_hbm, dy_s)]
        for copy in first:
            copy.wait()
        term = feed(0, low_s, i_s, b_s, bias_a, act_s, slope_s)
        copies.out(slope_s.at[0], slope_hbm.at[0])
        for copy in second:
            copy.wait()
        acc_s[...] = acc_s[...] + term
        acc_s[...] = acc_s[...] + feed(1, low_s, i_s, b_s, bias_b, act_s, slope_s)
        copies.out(slope_s.at[1], slope_hbm.at[1])
        for copy in third:
            copy.wait()
        sum_ref[...] = jnp.zeros_like(sum_ref)

        def step(i, carry):
            at = block(i, STEP)
            normed = unit_s[at, :] * gain_one[...] + shift_one[...]
            u, inverse = unit_norm(normed + acc_s[at, :] + b_back[...])
            out_s[at, :] = (u * gain_two[...] + shift_two[...]).astype(BF16)
            slot = lax.broadcasted_iota(jnp.int32, (STEP, 1), 0) + (i * STEP) % plen
            keep = slot < meta_ref[(i * STEP) // plen]
            grad_y = jnp.where(keep, dy_s[at, :].astype(F32), 0.0)
            grad = norm_grad(grad_y * gain_two[...], u, inverse)
            grad_s[at, :] = grad
            ffn_s[at, :] = grad.astype(BF16)
            sum_ref[8:9, :] += jnp.sum(grad_y * u, axis=0, keepdims=True)
            sum_ref[9:10, :] += jnp.sum(grad_y, axis=0, keepdims=True)
            sum_ref[10:11, :] += jnp.sum(grad, axis=0, keepdims=True)
            return carry

        lax.fori_loop(0, rows // STEP, step, 0)
        copies.out(out_s, out_hbm)
        copies.out(grad_s, grad_hbm)
        copies.out(ffn_s, ffn_hbm)
        for j, out in ((1, ob), (0, oa)):
            g_s[j] = tn(act_s[j], ffn_s[...]).astype(BF16)
            copies.out(g_s.at[j], out)
        copies.drain()

    inputs = [(SCALARS, meta)] + [(HBM, v) for v in (low, *in_pair, *back_pair, unit, acc, dy)]
    inputs += [(WHOLE, v) for v in (*smalls, *vectors)]
    outputs = [(HBM, shape((rows, model), d)) for d in (BF16, F32, BF16)]
    outputs += [(WHOLE, shape((16, model), F32)), (HBM, shape((2, rows, units), BF16))]
    outputs += [(HBM, shape((units, model), BF16))] * 2
    scratch = [pltpu.VMEM((rows, model), BF16), pltpu.VMEM((2, model, units), BF16)]
    scratch += [pltpu.VMEM((2, units, model), BF16)] + [pltpu.VMEM((2, rows, units), BF16)] * 2
    scratch += [pltpu.VMEM((rows, model), d) for d in (F32, F32, BF16, BF16, F32, BF16)]
    scratch += [pltpu.VMEM((2, units, model), BF16)]
    return call(kernel, "turn_pair", inputs, outputs, scratch, 20)


def outer_pair(acts, grad_ffn):
    _, rows, units = acts.shape
    model = grad_ffn.shape[1]

    def kernel(act_hbm, g_hbm, oa, ob, act_s, g_s, out_s, sems):
        copies = Copies(sems)
        whole = copies.start(g_hbm, g_s)
        waits = [copies.start(act_hbm.at[j], act_s.at[j]) for j in (1, 0)]
        whole.wait()
        for j, wait, out in ((1, waits[0], ob), (0, waits[1], oa)):
            wait.wait()
            out_s[j] = tn(act_s[j], g_s[...]).astype(BF16)
            copies.out(out_s.at[j], out)
        copies.drain()

    inputs = [(HBM, acts), (HBM, grad_ffn)]
    outputs = [(HBM, shape((units, model), BF16))] * 2
    scratch = [pltpu.VMEM((2, rows, units), BF16), pltpu.VMEM((rows, model), BF16)]
    scratch += [pltpu.VMEM((2, units, model), BF16)]
    return call(kernel, "outer_pair", inputs, outputs, scratch, 8, 200 * 10**9)


def feed_back_pair(grad_ffn, slopes, which, in_pair, back_pair, low, start, parts, sums, meta, unit=None, inverse=None, gain=None):
    rows, model = grad_ffn.shape
    units = slopes[0].shape[2]
    last = unit is not None

    def kernel(meta_ref, before, g_hbm, sa, sb, ia, ib, ba, bb, low_hbm, start_hbm, *rest):
        if last:
            unit_hbm, inv_hbm, gain_ref = rest[:3]
            rest = rest[3:]
            oa, ob, sum_ref, one_hbm, attn_hbm = rest[:5]
            g_s, slope_s, i_s, b_s, low_s, acc_s, pre_s, out_s, line, unit_s, inv_s, attn_s, sems = rest[5:]
        else:
            oa, ob, sum_ref, acc_out = rest[:4]
            g_s, slope_s, i_s, b_s, low_s, acc_s, pre_s, out_s, line, sems = rest[4:]
        copies = Copies(sems)
        sum_ref[...] = before[...]
        weights = {1: (bb, ib, sb.at[which]), 0: (ba, ia, sa.at[which])}
        early = copies.start(g_hbm, g_s)
        waits, later = {}, {}
        for j in (1, 0):
            waits[j] = [copies.start(weights[j][0], b_s.at[j]), copies.start(weights[j][2], slope_s.at[j])]
            later[j] = [copies.start(weights[j][1], i_s.at[j])]
            if j == 1:
                later[j] += [copies.start(low_hbm, low_s), copies.start(start_hbm, acc_s)]
        if last:
            late = [copies.start(unit_hbm, unit_s), copies.start(inv_hbm, inv_s)]
        early.wait()
        for j, out in ((1, ob), (0, oa)):
            for wait in waits[j]:
                wait.wait()
            for c in range(0, units, 256):
                cols = slice(c, c + 256)
                pre = nt(g_s[...], b_s[j, cols, :]) * slope_s[j, :, cols].astype(F32)
                pre = pre.astype(BF16)
                pre_s[:, cols] = pre
                line[:, cols] = jnp.sum(pre.astype(F32), axis=0, keepdims=True)
            sum_ref[pl.ds(row_of(parts[j], meta_ref, 0), 1), :] = line[...]
            for wait in later[j]:
                wait.wait()
            acc_s[...] = acc_s[...] + nt(pre_s[...], i_s[j])
            out_s[j] = tn(low_s[...], pre_s[...]).astype(BF16)
            copies.out(out_s.at[j], out)
        if last:
            for wait in late:
                wait.wait()

            def finish(i, carry):
                at = block(i, STEP)
                normed = acc_s[at, :]
                u = unit_s[at, :]
                grad = norm_grad(normed * gain_ref[0:1, :], u, inv_s[at, 0:1])
                sum_ref[11:12, :] += jnp.sum(grad, axis=0, keepdims=True)
                sum_ref[12:13, :] += jnp.sum(normed * u, axis=0, keepdims=True)
                sum_ref[13:14, :] += jnp.sum(normed, axis=0, keepdims=True)
                acc_s[at, :] = grad
                attn_s[at, :] = grad.astype(BF16)
                return carry

            lax.fori_loop(0, rows // STEP, finish, 0)
            copies.out(acc_s, one_hbm)
            copies.out(attn_s, attn_hbm)
        else:
            copies.out(acc_s, acc_out)
        copies.drain()

    inputs = [(SCALARS, meta), (WHOLE, sums)]
    inputs += [(HBM, v) for v in (grad_ffn, *slopes, *in_pair, *back_pair, low, start)]
    outputs = [(HBM, shape((model, units), BF16))] * 2 + [(WHOLE, shape((16, model), F32))]
    outputs += [(HBM, shape((rows, model), F32))]
    scratch = [pltpu.VMEM((rows, model), BF16), pltpu.VMEM((2, rows, units), BF16)]
    scratch += [pltpu.VMEM((2, model, units), BF16), pltpu.VMEM((2, units, model), BF16)]
    scratch += [pltpu.VMEM((rows, model), BF16), pltpu.VMEM((rows, model), F32)]
    scratch += [pltpu.VMEM((rows, units), BF16), pltpu.VMEM((2, model, units), BF16)]
    scratch += [pltpu.VMEM((1, units), F32)]
    if last:
        inputs += [(HBM, unit), (HBM, inverse), (WHOLE, gain)]
        outputs += [(HBM, shape((rows, model), BF16))]
        scratch += [pltpu.VMEM((rows, model), F32), pltpu.VMEM((rows, 128), F32)]
        scratch += [pltpu.VMEM((rows, model), BF16)]
    return call(kernel, "feed_back_pair", inputs, outputs, scratch, 20, 200 * 10**9)


def attend_back_pair(x, plen, grad_attn, qkvs, ctxs, probs, which, w_pair, start, parts, sums, meta):
    rows, model = x.shape
    passages = rows // plen
    width = ctxs[0].shape[2]
    heads = width // DH

    def kernel(meta_ref, before, x_hbm, g_hbm, qa, qb, ca, cb, pa, pb, wa, wb, start_hbm, *rest):
        oa, ob, sum_ref, acc_out = rest[:4]
        x_s, g_s, qkv_s, ctx_s, p_s, w_s, acc_s, grow_s, out_s, gc_s, sems = rest[4:]
        copies = Copies(sems)
        sum_ref[...] = before[...]
        early = [copies.start(g_hbm, g_s)]
        of = {0: (wa, ca, qa, pa), 1: (wb, cb, qb, pb)}
        waits, middle, later = {}, {}, {}
        for j in (1, 0):
            waits[j] = [copies.start(of[j][0], w_s.at[j]), copies.start(of[j][1].at[which], ctx_s.at[j])]
            middle[j] = [copies.start(of[j][2].at[which], qkv_s.at[j]), copies.start(of[j][3].at[which], p_s.at[j])]
            later[j] = []
            if j == 1:
                later[j] = [copies.start(x_hbm, x_s), copies.start(start_hbm, acc_s)]
        for wait in early:
            wait.wait()
        for j, out in ((1, ob), (0, oa)):
            for wait in waits[j]:
                wait.wait()
            gc_s[...] = nt(g_s[...], w_s[j, 3 * width :, :]).astype(BF16)
            out_s[j, 3 * width :, :] = tn(ctx_s[j], g_s[...]).astype(BF16)
            for wait in middle[j]:
                wait.wait()

            def one(g, carry, j=j):
                at = block(g, plen)
                qkv = qkv_s[j, at, :]
                grad_ctx = gc_s[at, :]
                gq, gk, gv = [], [], []
                for h in range(heads):
                    q = qkv[:, h * DH : (h + 1) * DH]
                    k = qkv[:, width + h * DH : width + (h + 1) * DH]
                    v = qkv[:, 2 * width + h * DH : 2 * width + (h + 1) * DH]
                    gc = grad_ctx[:, h * DH : (h + 1) * DH]
                    low = p_s[j, g * heads + h]
                    p = low.astype(F32)
                    gp = nt(v, gc)
                    delta = jnp.sum(p * gp, axis=0, keepdims=True)
                    gs = (p * (gp - delta)).astype(BF16)
                    gq.append(tn(k, gs) * (1.0 / math.sqrt(DH)))
                    gk.append(nn(gs, q) * (1.0 / math.sqrt(DH)))
                    gv.append(nn(low, gc))
                gq = jnp.concatenate(gq, axis=0).T
                grow = jnp.concatenate([gq] + gk + gv, axis=1).astype(BF16)
                grow_s[at, :] = grow
                return carry + jnp.sum(grow.astype(F32), axis=0, keepdims=True)

            line = lax.fori_loop(0, passages, one, jnp.zeros((1, 3 * width), F32), unroll=True)
            line = jnp.concatenate([line, jnp.zeros((1, model - 3 * width), F32)], axis=1)
            sum_ref[pl.ds(row_of(parts[j], meta_ref, 1), 1), :] = line
            for wait in later[j]:
                wait.wait()
            out_s[j, : 3 * width, :] = tn(grow_s[...], x_s[...]).astype(BF16)
            copies.out(out_s.at[j], out)
            acc_s[...] = acc_s[...] + nn(grow_s[...], w_s[j, : 3 * width, :])
        copies.out(acc_s, acc_out)
        copies.drain()

    inputs = [(SCALARS, meta), (WHOLE, sums)]
    inputs += [(HBM, v) for v in (x, grad_attn, *qkvs, *ctxs, *probs, *w_pair, start)]
    outputs = [(HBM, shape((4 * width, model), BF16))] * 2
    outputs += [(WHOLE, shape((16, model), F32)), (HBM, shape((rows, model), F32))]
    scratch = [pltpu.VMEM((rows, model), BF16), pltpu.VMEM((rows, model), BF16)]
    scratch += [pltpu.VMEM(v[0].shape, BF16) for v in (qkvs, ctxs, probs)]
    scratch += [pltpu.VMEM((2, 4 * width, model), BF16), pltpu.VMEM((rows, model), F32)]
    scratch += [pltpu.VMEM((rows, 3 * width), BF16), pltpu.VMEM((2, 4 * width, model), BF16)]
    scratch += [pltpu.VMEM((rows, width), BF16)]
    return call(kernel, "attend_back_pair", inputs, outputs, scratch, 20, 200 * 10**9)


def tie(value, *others):
    return lax.optimization_barrier((value, *others))[0]


def flat_perm(move):
    pairs = []
    for z in range(4):
        for y in range(2):
            for x in range(2):
                for c in range(2):
                    z2, y2, x2, c2 = move(z, y, x, c)
                    pairs.append((((z * 2 + y) * 2 + x) * 2 + c, ((z2 * 2 + y2) * 2 + x2) * 2 + c2))
    return pairs


def add(*terms):
    return sum(term.astype(F32) for term in terms).astype(BF16)


ORDER = "svibusvisubvsuivsuvibuvsui"


class GridMoves:
    def __init__(self):
        self.row = lax.axis_index("batch") % 2
        self.layer = lax.axis_index("batch") // 2 % 2
        self.side = (self.row + self.layer) % 2
        self.to_core = flat_perm(lambda z, y, x, c: (z, y, x, 1 - c))
        self.to_x = flat_perm(lambda z, y, x, c: (z, y, 1 - x, c))
        self.to_y = flat_perm(lambda z, y, x, c: (z, 1 - y, x, c))
        self.to_z = flat_perm(lambda z, y, x, c: (z ^ 1, y, x, c))
        self.to_zz = flat_perm(lambda z, y, x, c: (z ^ 2, y, x, c))
        self.mark = None

    def send(self, value, pairs):
        return lax.ppermute(value, AXES, pairs)

    def half(self, value, which):
        if isinstance(value, tuple):
            return jnp.where(which == 0, value[0], value[1])
        if isinstance(value, dict):
            rows = value["rows"] // 2
            at = value["at"] + which * rows
            return lax.dynamic_slice_in_dim(value["of"], at, rows, axis=0)
        if isinstance(value, list):
            return add(*(self.half(term, which) for term in value))
        rows = value.shape[0] // 2
        return lax.dynamic_slice_in_dim(value, which * rows, rows, axis=0)

    def order(self, mine, other, bit):
        low = jnp.where(bit == 0, mine, other)
        high = jnp.where(bit == 0, other, mine)
        return jnp.concatenate([low, high], axis=0)

    def after(self, value):
        if self.mark is not None:
            value = tie(value, self.mark)
        return value

    def pieces(self, mine):
        first, second = self.halves(mine)
        return [self.send(first, self.to_y), self.send(second, self.to_z)]

    def whole(self, mine, pieces):
        return self.order(mine, jnp.concatenate(pieces, axis=0), self.side)

    def halves(self, value):
        rows = value.shape[0] // 2
        return value[:rows], value[rows:]

    def sums(self, one, two):
        return [add(a, b) for a, b in zip(self.halves(one), self.halves(two))]

    def chain(self, near, got):
        got = tuple(self.after(part) for part in got)
        got = got if len(got) == 2 else got[0]
        pass_on = self.half([*near, got], 1 - self.row)
        keep = self.half([*near, got], self.row)
        got = self.send(pass_on, self.to_y)
        yield pass_on
        yield from self.chain_z(add(keep, self.after(got)))

    def chain_zy(self, near, got):
        got = tuple(self.after(part) for part in got)
        pass_on = self.half([*near, got], 1 - self.layer)
        keep = self.half([*near, got], self.layer)
        got = self.send(pass_on, self.to_z)
        yield pass_on
        keep = add(keep, self.after(got))
        pass_on = self.half(keep, 1 - self.row)
        keep = self.half(keep, self.row)
        got = self.send(pass_on, self.to_y)
        yield pass_on
        keep = add(keep, self.after(got))
        got = self.send(keep, self.to_zz)
        yield keep
        keep = add(keep, self.after(got))
        got = self.send(keep, self.to_y)
        yield keep
        keep = self.order(keep, self.after(got), self.row)
        got = self.send(keep, self.to_z)
        yield keep
        yield self.order(keep, self.after(got), self.layer).astype(F32)

    def chain_y(self, near, far):
        pass_on = jnp.concatenate(
            [self.half(term, 1 - self.row) for term in (near, far)], axis=0
        )
        got = self.send(pass_on, self.to_y)
        yield pass_on
        got = self.halves(self.after(got))
        far = add(*(self.half(term, self.row) for term in far), got[1])
        keep = add(*(self.half(term, self.row) for term in near), got[0])
        got = self.send(far, self.to_x)
        yield far
        yield from self.chain_z(add(keep, self.after(got)))

    def chain_z(self, keep):
        pass_on = self.half(keep, 1 - self.layer)
        keep = self.half(keep, self.layer)
        got = self.send(pass_on, self.to_z)
        yield pass_on
        keep = add(keep, self.after(got))
        got = self.send(keep, self.to_zz)
        yield keep
        keep = add(keep, self.after(got))
        got = self.send(keep, self.to_z)
        yield keep
        keep = self.order(keep, self.after(got), self.layer)
        got = self.send(keep, self.to_y)
        yield keep
        yield self.order(keep, self.after(got), self.row).astype(F32)

    def chain_small(self, value):
        for pairs in (self.to_core, self.to_x, self.to_y, self.to_z, self.to_zz):
            got = self.send(value, pairs)
            yield value
            value = value + self.after(got)
        yield value

    def step(self, chain):
        self.mark = next(chain)
        return self.mark


def body(
    tokens,
    passage_lengths,
    cotangent,
    w_qkv,
    b_query,
    b_value,
    w_out,
    b_out,
    gain_one,
    shift_one,
    w_in,
    b_in,
    w_back,
    b_back,
    gain_two,
    shift_two,
):
    micro_count, own_rows, model = tokens.shape
    tp_count = lax.axis_size("tp")
    batch_count = lax.axis_size("batch")
    plen = own_rows * tp_count // passage_lengths.shape[1]
    own_passages = own_rows // plen
    assert own_passages * plen == own_rows and tp_count == 4
    grid = (batch_count, tp_count) == (8, 4)
    width = w_qkv.shape[2]
    rows = micro_count * own_rows
    position = lax.axis_index("tp")

    vector = lambda v: v.reshape(1, -1)
    x = tokens.reshape(rows, model)
    dy = cotangent.reshape(rows, model)
    lengths = lax.dynamic_slice_in_dim(
        passage_lengths, position * own_passages, own_passages, axis=1
    ).reshape(micro_count * own_passages)
    meta = jnp.concatenate([lengths, (position if grid else 0 * position).reshape(1)])
    qkvo = jnp.concatenate([jnp.transpose(w_qkv, (1, 2, 0)).reshape(3 * width, model), w_out], axis=0)
    small = vector(jnp.concatenate([b_in.astype(F32), b_query, jnp.zeros_like(b_query), b_value]))
    if grid:
        m = moves = GridMoves()
        x_att = m.send(m.half(qkvo, m.side), m.to_x)
        c_att = m.send(qkvo, m.to_core)
        c_small = m.send(small, m.to_core)
        x_small = m.send(small, m.to_x)
        half_in = m.half(w_in, m.side)
        meta = tie(meta, half_in)
        att, smalls = [qkvo, c_att], [small, c_small]
    else:
        att, smalls, ins, backs = [
            list(lax.all_gather(v, "tp", axis=0)) for v in (qkvo, small, w_in, w_back)
        ]
    qkv_near, ctx_near, p_near, acc = attend_pair(x, plen, att[:2], smalls[:2], meta)
    y = x
    if grid:
        x_att, x_small = tie(x_att, acc), tie(x_small, acc)
        y_att = m.send(x_att, m.to_y)
        half_back = m.half(w_back, m.side)
        x_in = m.send(tie(half_in, x_att), m.to_x)
        smalls += [x_small, m.send(x_small, m.to_core)]
        y_att = tie(y_att, half_back, smalls[3])
        f_att = m.order(x_att, y_att, m.side)
        att += [f_att, m.send(f_att, m.to_core)]
        c_in = m.send(tie(w_in, f_att), m.to_core)
        c_back = m.send(tie(w_back, f_att), m.to_core)
        x_in = tie(x_in, f_att)
        y_in = m.send(x_in, m.to_y)
        x_back = m.send(tie(half_back, x_in), m.to_x)
        y = tie(x, x_in)
    qkv_far, ctx_far, p_far, unit, inverse, low = attend_pair(
        y, plen, att[2:], smalls[2:], meta, acc, [vector(v) for v in (b_out, gain_one, shift_one)]
    )
    if grid:
        y_in = tie(y_in, low)
        f_in = m.order(x_in, y_in, m.side)
        ins = [w_in, c_in, f_in, m.send(f_in, m.to_core)]
        x_back = tie(x_back, f_in)
        p_back = m.pieces(x_back)
        backs = [w_back, c_back]
        low = tie(low, x_back)
    act_near, slope_near, feed_near = feed_pair(low, ins[:2], backs[:2], smalls[:2])
    if grid:
        p_back[0] = tie(p_back[0], feed_near)
        f_back = m.whole(x_back, p_back)
        backs += [f_back, m.send(f_back, m.to_core)]
    layer_out, grad_two, grad_ffn, sums, slope_far, b_far, b_farc = turn_pair(
        low,
        ins[2:],
        backs[2:],
        smalls[2:],
        unit,
        feed_near,
        dy,
        meta,
        [vector(v) for v in (gain_one, shift_one, b_back, gain_two, shift_two)],
        plen,
    )
    if grid:
        got_b3 = m.send(b_farc, m.to_core)
    b_own, b_core = outer_pair(act_near, grad_ffn)
    if grid:
        got_b1 = m.send(b_core, m.to_core)
        b_far = m.sums(b_far, tie(got_b3, b_own))
        got_bx = [m.send(part, m.to_x) for part in b_far]
        grad_ffn = tie(grad_ffn, *b_far)
    slopes = (slope_near, slope_far)
    feed_sent = [(v[1], v[3]) for v in (ins, backs)]
    feed_kept = [(v[0], v[2]) for v in (ins, backs)]
    i_core, i_farc, sums, normed = feed_back_pair(
        grad_ffn, slopes, 1, *feed_sent, low, grad_two, (1, 3), sums, meta
    )
    if grid:
        got_i1, got_i3 = [m.send(v, m.to_core) for v in (i_core, i_farc)]
        b_near = [b_own, tie(got_b1, normed)]
        got_bx[0] = tie(got_bx[0], normed)
        normed = tie(normed, got_bx[0])
    i_own, i_far, sums, grad_one, grad_attn = feed_back_pair(
        grad_ffn,
        slopes,
        0,
        *feed_kept,
        low,
        normed,
        (0, 2),
        sums,
        meta,
        unit,
        inverse,
        vector(gain_one),
    )
    if grid:
        i_far = m.sums(i_far, tie(got_i3, grad_attn))
        got_ix = [m.send(part, m.to_x) for part in i_far]
        m.mark = i_far[0]
        chain_b = m.chain(b_near, got_bx)
        m.step(chain_b)
        grad_attn = tie(grad_attn, m.mark)
    kept = [(qkv_near, qkv_far), (ctx_near, ctx_far), (p_near, p_far)]
    a_core, a_farc, sums, grad_x = attend_back_pair(
        x, plen, grad_attn, *kept, 1, (att[1], att[3]), grad_one, (1, 3), sums, meta
    )
    if grid:
        got_a1, got_a3 = [m.send(v, m.to_core) for v in (a_core, a_farc)]
        i_near = [i_own, got_i1]
        m.mark = grad_x
        m.step(chain_b)
        got_ix[0] = m.after(got_ix[0])
        grad_x = tie(grad_x, got_ix[0])
    a_own, a_far, packed, grad_x = attend_back_pair(
        x, plen, grad_attn, *kept, 0, (att[0], att[2]), grad_x, (0, 2), sums, meta
    )
    if grid:
        m.mark = grad_x
        got_a3 = m.after(got_a3)
        rows_a = a_far.shape[0] // 2
        low_far = [v[:rows_a] for v in (a_far, got_a3)]
        low_far = add(*low_far)
        got_ax = m.send(low_far, m.to_x)
        m.mark = low_far
        got_a1 = m.after(got_a1)
        view = lambda v, at: {"of": v, "at": at, "rows": rows_a}
        low_near = [view(v, 0) for v in (a_own, got_a1)]
        high_near = [view(v, rows_a) for v in (a_own, got_a1)]
        high_far = [view(v, rows_a) for v in (a_far, got_a3)]
        chains = {"b": chain_b, "i": m.chain_zy(i_near, got_ix), "v": m.chain_y(high_near, high_far)}
        done = {}
        for key in "vib":
            done[key] = m.step(chains[key])
        chains["u"] = m.chain(low_near, [got_ax])
        chains["s"] = m.chain_small(m.after(packed))
        for key in ORDER:
            done[key] = m.step(chains[key])
        g_back, g_in, packed = done["b"], done["i"], done["s"]
        g_att = jnp.concatenate([done["u"], done["v"]], axis=0)
    else:
        g_back, g_in, g_att = [
            lax.psum(
                lax.psum_scatter(jnp.stack(parts).astype(F32), "tp", scatter_dimension=0), "batch"
            )
            for parts in (
                (b_own, b_core, b_far, b_farc),
                (i_own, i_core, i_far, i_farc),
                (a_own, a_core, a_far, a_farc),
            )
        ]
        packed = lax.psum(packed, AXES)
    mine = lax.dynamic_slice_in_dim(packed, 2 * position, 2, axis=0)
    return (
        layer_out.reshape(tokens.shape),
        grad_x.reshape(tokens.shape),
        jnp.transpose(g_att[: 3 * width].reshape(3, width, model), (2, 0, 1)),
        mine[1, :width],
        mine[1, 2 * width : 3 * width],
        g_att[3 * width :],
        packed[11],
        packed[12],
        packed[13],
        g_in,
        mine[0],
        g_back,
        packed[10],
        packed[8],
        packed[9],
    )


def solution(mesh):
    in_specs = (
        P(None, ("batch", "tp"), None),
        P(None, "batch"),
        P(None, ("batch", "tp"), None),
        P(None, None, "tp"),
        P("tp"),
        P("tp"),
        P("tp", None),
        P(),
        P(),
        P(),
        P(None, "tp"),
        P("tp"),
        P("tp", None),
        P(),
        P(),
        P(),
    )
    out_specs = (
        P(None, ("batch", "tp"), None),
        P(None, ("batch", "tp"), None),
        P(None, None, "tp"),
        P("tp"),
        P("tp"),
        P("tp", None),
        P(),
        P(),
        P(),
        P(None, "tp"),
        P("tp"),
        P("tp", None),
        P(),
        P(),
        P(),
    )
    return jax.shard_map(body, mesh=mesh, in_specs=in_specs, out_specs=out_specs, check_vma=False)
```

```python
import math

import jax
import jax.numpy as jnp
from jax import lax
from jax.experimental import pallas as pl
from jax.experimental.pallas import tpu as pltpu
from jax.sharding import PartitionSpec as P

DH = 64
AXES = ("batch", "tp")
epsilon = 1e-05
F32 = jnp.float32
BF16 = jnp.bfloat16


def nt(a, b):
    return lax.dot_general(a, b, (((1,), (1,)), ((), ())), preferred_element_type=F32)


def tn(a, b):
    return lax.dot_general(a, b, (((0,), (0,)), ((), ())), preferred_element_type=F32)


def nn(a, b):
    return jnp.dot(a, b, preferred_element_type=F32)


HBM = pl.BlockSpec(memory_space=pl.ANY)
WHOLE = pl.BlockSpec(memory_space=pltpu.VMEM)
SCALARS = pl.BlockSpec(memory_space=pltpu.SMEM)


class Copies:
    def __init__(self, sems):
        self.sems, self.used = sems, 0
        self.pending = []

    def start(self, src, dst):
        copy = pltpu.make_async_copy(src, dst, self.sems.at[self.used])
        self.used += 1
        copy.start()
        return copy

    def out(self, src, dst):
        self.pending.append(self.start(src, dst))

    def drain(self):
        for copy in self.pending:
            copy.wait()


def call(kernel, name, inputs, outputs, scratch, copies, cost=1000):
    in_specs = [spec for spec, _ in inputs]
    return pl.pallas_call(
        kernel,
        name=name,
        in_specs=in_specs,
        out_specs=tuple(spec for spec, _ in outputs),
        out_shape=tuple(shape for _, shape in outputs),
        scratch_shapes=list(scratch) + [pltpu.SemaphoreType.DMA((copies,))],
        cost_estimate=pl.CostEstimate(flops=cost, transcendentals=0, bytes_accessed=0),
    )(*[value for _, value in inputs])


def shape(dims, dtype):
    return jax.ShapeDtypeStruct(dims, dtype)


def block(i, size):
    return pl.ds(pl.multiple_of(i * size, size), size)


def unit_norm(v):
    middle = jnp.mean(v, axis=-1, keepdims=True)
    centred = v - middle
    inverse = lax.rsqrt(jnp.mean(centred * centred, axis=-1, keepdims=True) + epsilon)
    return centred * inverse, inverse


def norm_grad(scaled, unit, inverse):
    mean_one = jnp.mean(scaled, axis=-1, keepdims=True)
    mean_two = jnp.mean(scaled * unit, axis=-1, keepdims=True)
    return inverse * (scaled - mean_one - unit * mean_two)


STEP = 128


def row_of(part, meta_ref, kind):
    return 2 * jnp.bitwise_xor(part, meta_ref[meta_ref.shape[0] - 1]) + kind


def attend_pair(x, plen, w_pair, smalls, meta, acc=None, vectors=None):
    rows, model = x.shape
    passages = rows // plen
    width = w_pair[0].shape[0] // 4
    heads = width // DH
    units = smalls[0].shape[1] - 3 * width
    last = acc is not None

    def kernel(meta_ref, x_hbm, wa, wb, bias_a, bias_b, *rest):
        if last:
            acc_hbm, b_out, gain, shift = rest[:4]
            qkv_hbm, ctx_hbm, p_hbm, unit_hbm, inv_hbm, low_hbm = rest[4:10]
            x_s, w_s, qkv_s, ctx_s, p_s, acc_s, inv_s, low_s, sems = rest[10:]
        else:
            qkv_hbm, ctx_hbm, p_hbm, acc_out = rest[:4]
            x_s, w_s, qkv_s, ctx_s, p_s, acc_s, sems = rest[4:]
        copies = Copies(sems)
        first = [copies.start(x_hbm, x_s), copies.start(wa, w_s.at[0])]
        second = [copies.start(wb, w_s.at[1])]
        if last:
            held = copies.start(acc_hbm, acc_s)
        for j, waits, bias in ((0, first, bias_a), (1, second, bias_b)):
            for copy in waits:
                copy.wait()
            qkv_s[j] = (nt(x_s[...], w_s[j, : 3 * width, :]) + bias[0:1, units:]).astype(BF16)
            copies.out(qkv_s.at[j], qkv_hbm.at[j])

            def one(g, carry, j=j):
                at = block(g, plen)
                qkv = qkv_s[j, at, :]
                keep = lax.broadcasted_iota(jnp.int32, (plen, 1), 0) < meta_ref[g]
                ctx = []
                for h in range(heads):
                    q = qkv[:, h * DH : (h + 1) * DH] * (1.0 / math.sqrt(DH))
                    k = qkv[:, width + h * DH : width + (h + 1) * DH]
                    v = qkv[:, 2 * width + h * DH : 2 * width + (h + 1) * DH]
                    s = jnp.where(keep, nt(k, q.astype(BF16)), -1000000000.0)
                    e = jnp.exp(s - jnp.max(s, axis=0, keepdims=True))
                    p = (e * (1.0 / jnp.sum(e, axis=0, keepdims=True))).astype(BF16)
                    p_s[j, g * heads + h] = p
                    ctx.append(tn(v, p))
                ctx_s[j, at, :] = jnp.concatenate(ctx, axis=0).T.astype(BF16)
                return carry

            lax.fori_loop(0, passages, one, 0, unroll=True)
            copies.out(ctx_s.at[j], ctx_hbm.at[j])
            copies.out(p_s.at[j], p_hbm.at[j])
            term = nn(ctx_s[j], w_s[j, 3 * width :, :])
            if last and j == 0:
                held.wait()
            acc_s[...] = term if j == 0 and not last else acc_s[...] + term
        if last:

            def finish(i, carry):
                at = block(i, STEP)
                v = x_s[at, :].astype(F32) + acc_s[at, :] + b_out[...]
                unit, inverse = unit_norm(v)
                acc_s[at, :] = unit
                inv_s[at, :] = jnp.broadcast_to(inverse, (STEP, 128))
                low_s[at, :] = (unit * gain[...] + shift[...]).astype(BF16)
                return carry

            lax.fori_loop(0, rows // STEP, finish, 0)
            copies.out(acc_s, unit_hbm)
            copies.out(inv_s, inv_hbm)
            copies.out(low_s, low_hbm)
        else:
            copies.out(acc_s, acc_out)
        copies.drain()

    inputs = [(SCALARS, meta), (HBM, x), (HBM, w_pair[0]), (HBM, w_pair[1])]
    inputs += [(WHOLE, v) for v in smalls]
    dims = [(2, rows, 3 * width), (2, rows, width), (2, passages * heads, plen, plen)]
    outputs = [(HBM, shape(d, BF16)) for d in dims]
    scratch = [pltpu.VMEM((rows, model), BF16), pltpu.VMEM((2, 4 * width, model), BF16)]
    scratch += [pltpu.VMEM(d, BF16) for d in dims]
    scratch += [pltpu.VMEM((rows, model), F32)]
    if last:
        inputs += [(HBM, acc)] + [(WHOLE, v) for v in vectors]
        outputs += [(HBM, shape((rows, model), F32)), (HBM, shape((rows, 128), F32))]
        outputs += [(HBM, shape((rows, model), BF16))]
        scratch += [pltpu.VMEM((rows, 128), F32), pltpu.VMEM((rows, model), BF16)]
    else:
        outputs += [(HBM, shape((rows, model), F32))]
    return call(kernel, "attend_pair", inputs, outputs, scratch, 16, 1000 if last else 200 * 10**9)


def feed(j, low_s, i_s, b_s, bias, act_s, slope_s):
    units = act_s.shape[2]
    for c in range(0, units, 256):
        cols = slice(c, c + 256)
        t = nn(low_s[...], i_s[j, :, cols]) + bias[0:1, cols]
        cdf = 0.5 * (1.0 + lax.erf(t * (1.0 / math.sqrt(2.0))))
        pdf = jnp.exp(-0.5 * t * t) * (1.0 / math.sqrt(2.0 * math.pi))
        act_s[j, :, cols] = (t * cdf).astype(BF16)
        slope_s[j, :, cols] = (cdf + t * pdf).astype(BF16)
    return nn(act_s[j], b_s[j])


def feed_pair(low, in_pair, back_pair, smalls):
    rows, model = low.shape
    units = in_pair[0].shape[1]

    def kernel(low_hbm, ia, ib, ba, bb, bias_a, bias_b, *rest):
        act_hbm, slope_hbm, acc_hbm, low_s, i_s, b_s, act_s, slope_s, acc_s, sems = rest
        copies = Copies(sems)
        first = [copies.start(low_hbm, low_s), copies.start(ia, i_s.at[0]), copies.start(ba, b_s.at[0])]
        second = [copies.start(ib, i_s.at[1]), copies.start(bb, b_s.at[1])]
        for j, waits, bias in ((0, first, bias_a), (1, second, bias_b)):
            for copy in waits:
                copy.wait()
            term = feed(j, low_s, i_s, b_s, bias, act_s, slope_s)
            copies.out(act_s.at[j], act_hbm.at[j])
            copies.out(slope_s.at[j], slope_hbm.at[j])
            acc_s[...] = acc_s[...] + term if j else term
        copies.out(acc_s, acc_hbm)
        copies.drain()

    inputs = [(HBM, v) for v in (low, *in_pair, *back_pair)] + [(WHOLE, v) for v in smalls]
    outputs = [(HBM, shape((2, rows, units), BF16))] * 2 + [(HBM, shape((rows, model), F32))]
    scratch = [pltpu.VMEM((rows, model), BF16), pltpu.VMEM((2, model, units), BF16)]
    scratch += [pltpu.VMEM((2, units, model), BF16)] + [pltpu.VMEM((2, rows, units), BF16)] * 2
    scratch += [pltpu.VMEM((rows, model), F32)]
    return call(kernel, "feed_pair", inputs, outputs, scratch, 12, 200 * 10**9)


def turn_pair(low, in_pair, back_pair, smalls, unit, acc, dy, meta, vectors, plen):
    rows, model = low.shape
    units = in_pair[0].shape[1]

    def kernel(meta_ref, low_hbm, ia, ib, ba, bb, unit_hbm, acc_hbm, dy_hbm, bias_a, bias_b, *rest):
        gain_one, shift_one, b_back, gain_two, shift_two = rest[:5]
        out_hbm, grad_hbm, ffn_hbm, sum_ref, slope_hbm, oa, ob = rest[5:12]
        low_s, i_s, b_s, act_s, slope_s, acc_s, unit_s, dy_s, out_s, grad_s, ffn_s, g_s, sems = rest[12:]
        copies = Copies(sems)
        first = [copies.start(low_hbm, low_s), copies.start(ia, i_s.at[0]), copies.start(ba, b_s.at[0])]
        second = [copies.start(ib, i_s.at[1]), copies.start(bb, b_s.at[1]), copies.start(acc_hbm, acc_s)]
        third = [copies.start(unit_hbm, unit_s), copies.start(dy_hbm, dy_s)]
        for copy in first:
            copy.wait()
        term = feed(0, low_s, i_s, b_s, bias_a, act_s, slope_s)
        copies.out(slope_s.at[0], slope_hbm.at[0])
        for copy in second:
            copy.wait()
        acc_s[...] = acc_s[...] + term
        acc_s[...] = acc_s[...] + feed(1, low_s, i_s, b_s, bias_b, act_s, slope_s)
        copies.out(slope_s.at[1], slope_hbm.at[1])
        for copy in third:
            copy.wait()
        sum_ref[...] = jnp.zeros_like(sum_ref)

        def step(i, carry):
            at = block(i, STEP)
            normed = unit_s[at, :] * gain_one[...] + shift_one[...]
            u, inverse = unit_norm(normed + acc_s[at, :] + b_back[...])
            out_s[at, :] = (u * gain_two[...] + shift_two[...]).astype(BF16)
            slot = lax.broadcasted_iota(jnp.int32, (STEP, 1), 0) + (i * STEP) % plen
            keep = slot < meta_ref[(i * STEP) // plen]
            grad_y = jnp.where(keep, dy_s[at, :].astype(F32), 0.0)
            grad = norm_grad(grad_y * gain_two[...], u, inverse)
            grad_s[at, :] = grad
            ffn_s[at, :] = grad.astype(BF16)
            sum_ref[8:9, :] += jnp.sum(grad_y * u, axis=0, keepdims=True)
            sum_ref[9:10, :] += jnp.sum(grad_y, axis=0, keepdims=True)
            sum_ref[10:11, :] += jnp.sum(grad, axis=0, keepdims=True)
            return carry

        lax.fori_loop(0, rows // STEP, step, 0)
        copies.out(out_s, out_hbm)
        copies.out(grad_s, grad_hbm)
        copies.out(ffn_s, ffn_hbm)
        for j, out in ((1, ob), (0, oa)):
            g_s[j] = tn(act_s[j], ffn_s[...]).astype(BF16)
            copies.out(g_s.at[j], out)
        copies.drain()

    inputs = [(SCALARS, meta)] + [(HBM, v) for v in (low, *in_pair, *back_pair, unit, acc, dy)]
    inputs += [(WHOLE, v) for v in (*smalls, *vectors)]
    outputs = [(HBM, shape((rows, model), d)) for d in (BF16, F32, BF16)]
    outputs += [(WHOLE, shape((16, model), F32)), (HBM, shape((2, rows, units), BF16))]
    outputs += [(HBM, shape((units, model), BF16))] * 2
    scratch = [pltpu.VMEM((rows, model), BF16), pltpu.VMEM((2, model, units), BF16)]
    scratch += [pltpu.VMEM((2, units, model), BF16)] + [pltpu.VMEM((2, rows, units), BF16)] * 2
    scratch += [pltpu.VMEM((rows, model), d) for d in (F32, F32, BF16, BF16, F32, BF16)]
    scratch += [pltpu.VMEM((2, units, model), BF16)]
    return call(kernel, "turn_pair", inputs, outputs, scratch, 20)


def outer_pair(acts, grad_ffn):
    _, rows, units = acts.shape
    model = grad_ffn.shape[1]

    def kernel(act_hbm, g_hbm, oa, ob, act_s, g_s, out_s, sems):
        copies = Copies(sems)
        whole = copies.start(g_hbm, g_s)
        waits = [copies.start(act_hbm.at[j], act_s.at[j]) for j in (1, 0)]
        whole.wait()
        for j, wait, out in ((1, waits[0], ob), (0, waits[1], oa)):
            wait.wait()
            out_s[j] = tn(act_s[j], g_s[...]).astype(BF16)
            copies.out(out_s.at[j], out)
        copies.drain()

    inputs = [(HBM, acts), (HBM, grad_ffn)]
    outputs = [(HBM, shape((units, model), BF16))] * 2
    scratch = [pltpu.VMEM((2, rows, units), BF16), pltpu.VMEM((rows, model), BF16)]
    scratch += [pltpu.VMEM((2, units, model), BF16)]
    return call(kernel, "outer_pair", inputs, outputs, scratch, 8, 200 * 10**9)


def feed_back_pair(grad_ffn, slopes, which, in_pair, back_pair, low, start, parts, sums, meta, unit=None, inverse=None, gain=None):
    rows, model = grad_ffn.shape
    units = slopes[0].shape[2]
    last = unit is not None

    def kernel(meta_ref, before, g_hbm, sa, sb, ia, ib, ba, bb, low_hbm, start_hbm, *rest):
        if last:
            unit_hbm, inv_hbm, gain_ref = rest[:3]
            rest = rest[3:]
            oa, ob, sum_ref, one_hbm, attn_hbm = rest[:5]
            g_s, slope_s, i_s, b_s, low_s, acc_s, pre_s, out_s, line, unit_s, inv_s, attn_s, sems = rest[5:]
        else:
            oa, ob, sum_ref, acc_out = rest[:4]
            g_s, slope_s, i_s, b_s, low_s, acc_s, pre_s, out_s, line, sems = rest[4:]
        copies = Copies(sems)
        sum_ref[...] = before[...]
        weights = {1: (bb, ib, sb.at[which]), 0: (ba, ia, sa.at[which])}
        early = copies.start(g_hbm, g_s)
        waits, later = {}, {}
        for j in (1, 0):
            waits[j] = [copies.start(weights[j][0], b_s.at[j]), copies.start(weights[j][2], slope_s.at[j])]
            later[j] = [copies.start(weights[j][1], i_s.at[j])]
            if j == 1:
                later[j] += [copies.start(low_hbm, low_s), copies.start(start_hbm, acc_s)]
        if last:
            late = [copies.start(unit_hbm, unit_s), copies.start(inv_hbm, inv_s)]
        early.wait()
        for j, out in ((1, ob), (0, oa)):
            for wait in waits[j]:
                wait.wait()
            for c in range(0, units, 256):
                cols = slice(c, c + 256)
                pre = nt(g_s[...], b_s[j, cols, :]) * slope_s[j, :, cols].astype(F32)
                pre = pre.astype(BF16)
                pre_s[:, cols] = pre
                line[:, cols] = jnp.sum(pre.astype(F32), axis=0, keepdims=True)
            sum_ref[pl.ds(row_of(parts[j], meta_ref, 0), 1), :] = line[...]
            for wait in later[j]:
                wait.wait()
            acc_s[...] = acc_s[...] + nt(pre_s[...], i_s[j])
            out_s[j] = tn(low_s[...], pre_s[...]).astype(BF16)
            copies.out(out_s.at[j], out)
        if last:
            for wait in late:
                wait.wait()

            def finish(i, carry):
                at = block(i, STEP)
                normed = acc_s[at, :]
                u = unit_s[at, :]
                grad = norm_grad(normed * gain_ref[0:1, :], u, inv_s[at, 0:1])
                sum_ref[11:12, :] += jnp.sum(grad, axis=0, keepdims=True)
                sum_ref[12:13, :] += jnp.sum(normed * u, axis=0, keepdims=True)
                sum_ref[13:14, :] += jnp.sum(normed, axis=0, keepdims=True)
                acc_s[at, :] = grad
                attn_s[at, :] = grad.astype(BF16)
                return carry

            lax.fori_loop(0, rows // STEP, finish, 0)
            copies.out(acc_s, one_hbm)
            copies.out(attn_s, attn_hbm)
        else:
            copies.out(acc_s, acc_out)
        copies.drain()

    inputs = [(SCALARS, meta), (WHOLE, sums)]
    inputs += [(HBM, v) for v in (grad_ffn, *slopes, *in_pair, *back_pair, low, start)]
    outputs = [(HBM, shape((model, units), BF16))] * 2 + [(WHOLE, shape((16, model), F32))]
    outputs += [(HBM, shape((rows, model), F32))]
    scratch = [pltpu.VMEM((rows, model), BF16), pltpu.VMEM((2, rows, units), BF16)]
    scratch += [pltpu.VMEM((2, model, units), BF16), pltpu.VMEM((2, units, model), BF16)]
    scratch += [pltpu.VMEM((rows, model), BF16), pltpu.VMEM((rows, model), F32)]
    scratch += [pltpu.VMEM((rows, units), BF16), pltpu.VMEM((2, model, units), BF16)]
    scratch += [pltpu.VMEM((1, units), F32)]
    if last:
        inputs += [(HBM, unit), (HBM, inverse), (WHOLE, gain)]
        outputs += [(HBM, shape((rows, model), BF16))]
        scratch += [pltpu.VMEM((rows, model), F32), pltpu.VMEM((rows, 128), F32)]
        scratch += [pltpu.VMEM((rows, model), BF16)]
    return call(kernel, "feed_back_pair", inputs, outputs, scratch, 20, 200 * 10**9)


def attend_back_pair(x, plen, grad_attn, qkvs, ctxs, probs, which, w_pair, start, parts, sums, meta):
    rows, model = x.shape
    passages = rows // plen
    width = ctxs[0].shape[2]
    heads = width // DH

    def kernel(meta_ref, before, x_hbm, g_hbm, qa, qb, ca, cb, pa, pb, wa, wb, start_hbm, *rest):
        oa, ob, sum_ref, acc_out = rest[:4]
        x_s, g_s, qkv_s, ctx_s, p_s, w_s, acc_s, grow_s, out_s, gc_s, sems = rest[4:]
        copies = Copies(sems)
        sum_ref[...] = before[...]
        early = [copies.start(g_hbm, g_s)]
        of = {0: (wa, ca, qa, pa), 1: (wb, cb, qb, pb)}
        waits, middle, later = {}, {}, {}
        for j in (1, 0):
            waits[j] = [copies.start(of[j][0], w_s.at[j]), copies.start(of[j][1].at[which], ctx_s.at[j])]
            middle[j] = [copies.start(of[j][2].at[which], qkv_s.at[j]), copies.start(of[j][3].at[which], p_s.at[j])]
            later[j] = []
            if j == 1:
                later[j] = [copies.start(x_hbm, x_s), copies.start(start_hbm, acc_s)]
        for wait in early:
            wait.wait()
        for j, out in ((1, ob), (0, oa)):
            for wait in waits[j]:
                wait.wait()
            gc_s[...] = nt(g_s[...], w_s[j, 3 * width :, :]).astype(BF16)
            out_s[j, 3 * width :, :] = tn(ctx_s[j], g_s[...]).astype(BF16)
            for wait in middle[j]:
                wait.wait()

            def one(g, carry, j=j):
                at = block(g, plen)
                qkv = qkv_s[j, at, :]
                grad_ctx = gc_s[at, :]
                gq, gk, gv = [], [], []
                for h in range(heads):
                    q = qkv[:, h * DH : (h + 1) * DH]
                    k = qkv[:, width + h * DH : width + (h + 1) * DH]
                    v = qkv[:, 2 * width + h * DH : 2 * width + (h + 1) * DH]
                    gc = grad_ctx[:, h * DH : (h + 1) * DH]
                    low = p_s[j, g * heads + h]
                    p = low.astype(F32)
                    gp = nt(v, gc)
                    delta = jnp.sum(p * gp, axis=0, keepdims=True)
                    gs = (p * (gp - delta)).astype(BF16)
                    gq.append(tn(k, gs) * (1.0 / math.sqrt(DH)))
                    gk.append(nn(gs, q) * (1.0 / math.sqrt(DH)))
                    gv.append(nn(low, gc))
                gq = jnp.concatenate(gq, axis=0).T
                grow = jnp.concatenate([gq] + gk + gv, axis=1).astype(BF16)
                grow_s[at, :] = grow
                return carry + jnp.sum(grow.astype(F32), axis=0, keepdims=True)

            line = lax.fori_loop(0, passages, one, jnp.zeros((1, 3 * width), F32), unroll=True)
            line = jnp.concatenate([line, jnp.zeros((1, model - 3 * width), F32)], axis=1)
            sum_ref[pl.ds(row_of(parts[j], meta_ref, 1), 1), :] = line
            for wait in later[j]:
                wait.wait()
            out_s[j, : 3 * width, :] = tn(grow_s[...], x_s[...]).astype(BF16)
            copies.out(out_s.at[j], out)
            acc_s[...] = acc_s[...] + nn(grow_s[...], w_s[j, : 3 * width, :])
        copies.out(acc_s, acc_out)
        copies.drain()

    inputs = [(SCALARS, meta), (WHOLE, sums)]
    inputs += [(HBM, v) for v in (x, grad_attn, *qkvs, *ctxs, *probs, *w_pair, start)]
    outputs = [(HBM, shape((4 * width, model), BF16))] * 2
    outputs += [(WHOLE, shape((16, model), F32)), (HBM, shape((rows, model), F32))]
    scratch = [pltpu.VMEM((rows, model), BF16), pltpu.VMEM((rows, model), BF16)]
    scratch += [pltpu.VMEM(v[0].shape, BF16) for v in (qkvs, ctxs, probs)]
    scratch += [pltpu.VMEM((2, 4 * width, model), BF16), pltpu.VMEM((rows, model), F32)]
    scratch += [pltpu.VMEM((rows, 3 * width), BF16), pltpu.VMEM((2, 4 * width, model), BF16)]
    scratch += [pltpu.VMEM((rows, width), BF16)]
    return call(kernel, "attend_back_pair", inputs, outputs, scratch, 20, 200 * 10**9)


def tie(value, *others):
    return lax.optimization_barrier((value, *others))[0]


def flat_perm(move):
    pairs = []
    for z in range(4):
        for y in range(2):
            for x in range(2):
                for c in range(2):
                    z2, y2, x2, c2 = move(z, y, x, c)
                    pairs.append((((z * 2 + y) * 2 + x) * 2 + c, ((z2 * 2 + y2) * 2 + x2) * 2 + c2))
    return pairs


def add(*terms):
    return sum(term.astype(F32) for term in terms).astype(BF16)


ORDER = "svibusvisubvsuivsuvibuvsui"


class GridMoves:
    def __init__(self):
        self.row = lax.axis_index("batch") % 2
        self.layer = lax.axis_index("batch") // 2 % 2
        self.side = (self.row + self.layer) % 2
        self.to_core = flat_perm(lambda z, y, x, c: (z, y, x, 1 - c))
        self.to_x = flat_perm(lambda z, y, x, c: (z, y, 1 - x, c))
        self.to_y = flat_perm(lambda z, y, x, c: (z, 1 - y, x, c))
        self.to_z = flat_perm(lambda z, y, x, c: (z ^ 1, y, x, c))
        self.to_zz = flat_perm(lambda z, y, x, c: (z ^ 2, y, x, c))
        self.mark = None

    def send(self, value, pairs):
        return lax.ppermute(value, AXES, pairs)

    def half(self, value, which):
        if isinstance(value, tuple):
            return jnp.where(which == 0, value[0], value[1])
        if isinstance(value, dict):
            rows = value["rows"] // 2
            at = value["at"] + which * rows
            return lax.dynamic_slice_in_dim(value["of"], at, rows, axis=0)
        if isinstance(value, list):
            return add(*(self.half(term, which) for term in value))
        rows = value.shape[0] // 2
        return lax.dynamic_slice_in_dim(value, which * rows, rows, axis=0)

    def order(self, mine, other, bit):
        low = jnp.where(bit == 0, mine, other)
        high = jnp.where(bit == 0, other, mine)
        return jnp.concatenate([low, high], axis=0)

    def after(self, value):
        if self.mark is not None:
            value = tie(value, self.mark)
        return value

    def pieces(self, mine):
        first, second = self.halves(mine)
        return [self.send(first, self.to_y), self.send(second, self.to_z)]

    def whole(self, mine, pieces):
        parts = list(zip(self.halves(mine), pieces))
        low = [jnp.where(self.side == 0, one, two) for one, two in parts]
        high = [jnp.where(self.side == 0, two, one) for one, two in parts]
        return jnp.concatenate(low + high, axis=0)

    def halves(self, value):
        rows = value.shape[0] // 2
        return value[:rows], value[rows:]

    def sums(self, one, two):
        return [add(a, b) for a, b in zip(self.halves(one), self.halves(two))]

    def chain(self, near, got):
        got = tuple(self.after(part) for part in got)
        got = got if len(got) == 2 else got[0]
        pass_on = self.half([*near, got], 1 - self.row)
        keep = self.half([*near, got], self.row)
        got = self.send(pass_on, self.to_y)
        yield pass_on
        yield from self.chain_z(add(keep, self.after(got)))

    def chain_zy(self, near, got):
        got = tuple(self.after(part) for part in got)
        pass_on = self.half([*near, got], 1 - self.layer)
        keep = self.half([*near, got], self.layer)
        got = self.send(pass_on, self.to_z)
        yield pass_on
        keep = add(keep, self.after(got))
        pass_on = self.half(keep, 1 - self.row)
        keep = self.half(keep, self.row)
        got = self.send(pass_on, self.to_y)
        yield pass_on
        keep = add(keep, self.after(got))
        got = self.send(keep, self.to_zz)
        yield keep
        keep = add(keep, self.after(got))
        got = self.send(keep, self.to_y)
        yield keep
        keep = self.order(keep, self.after(got), self.row)
        got = self.send(keep, self.to_z)
        yield keep
        yield self.order(keep, self.after(got), self.layer).astype(F32)

    def chain_y(self, near, far):
        pass_on = jnp.concatenate(
            [self.half(term, 1 - self.row) for term in (near, far)], axis=0
        )
        got = self.send(pass_on, self.to_y)
        yield pass_on
        got = self.halves(self.after(got))
        far = add(*(self.half(term, self.row) for term in far), got[1])
        keep = add(*(self.half(term, self.row) for term in near), got[0])
        got = self.send(far, self.to_x)
        yield far
        yield from self.chain_z(add(keep, self.after(got)))

    def chain_z(self, keep):
        pass_on = self.half(keep, 1 - self.layer)
        keep = self.half(keep, self.layer)
        got = self.send(pass_on, self.to_z)
        yield pass_on
        keep = add(keep, self.after(got))
        got = self.send(keep, self.to_zz)
        yield keep
        keep = add(keep, self.after(got))
        got = self.send(keep, self.to_z)
        yield keep
        keep = self.order(keep, self.after(got), self.layer)
        got = self.send(keep, self.to_y)
        yield keep
        yield self.order(keep, self.after(got), self.row).astype(F32)

    def chain_small(self, value):
        for pairs in (self.to_core, self.to_x, self.to_y, self.to_z, self.to_zz):
            got = self.send(value, pairs)
            yield value
            value = value + self.after(got)
        yield value

    def step(self, chain):
        self.mark = next(chain)
        return self.mark


def body(
    tokens,
    passage_lengths,
    cotangent,
    w_qkv,
    b_query,
    b_value,
    w_out,
    b_out,
    gain_one,
    shift_one,
    w_in,
    b_in,
    w_back,
    b_back,
    gain_two,
    shift_two,
):
    micro_count, own_rows, model = tokens.shape
    tp_count = lax.axis_size("tp")
    batch_count = lax.axis_size("batch")
    plen = own_rows * tp_count // passage_lengths.shape[1]
    own_passages = own_rows // plen
    assert own_passages * plen == own_rows and tp_count == 4
    grid = (batch_count, tp_count) == (8, 4)
    width = w_qkv.shape[2]
    rows = micro_count * own_rows
    position = lax.axis_index("tp")

    vector = lambda v: v.reshape(1, -1)
    x = tokens.reshape(rows, model)
    dy = cotangent.reshape(rows, model)
    lengths = lax.dynamic_slice_in_dim(
        passage_lengths, position * own_passages, own_passages, axis=1
    ).reshape(micro_count * own_passages)
    meta = jnp.concatenate([lengths, (position if grid else 0 * position).reshape(1)])
    qkvo = jnp.concatenate([jnp.transpose(w_qkv, (1, 2, 0)).reshape(3 * width, model), w_out], axis=0)
    small = vector(jnp.concatenate([b_in.astype(F32), b_query, jnp.zeros_like(b_query), b_value]))
    if grid:
        m = moves = GridMoves()
        x_att = m.send(m.half(qkvo, m.side), m.to_x)
        c_att = m.send(qkvo, m.to_core)
        c_small = m.send(small, m.to_core)
        x_small = m.send(small, m.to_x)
        half_in = m.half(w_in, m.side)
        meta = tie(meta, half_in)
        att, smalls = [qkvo, c_att], [small, c_small]
    else:
        att, smalls, ins, backs = [
            list(lax.all_gather(v, "tp", axis=0)) for v in (qkvo, small, w_in, w_back)
        ]
    qkv_near, ctx_near, p_near, acc = attend_pair(x, plen, att[:2], smalls[:2], meta)
    y = x
    if grid:
        x_att, x_small = tie(x_att, acc), tie(x_small, acc)
        y_att = m.send(x_att, m.to_y)
        half_back = m.half(w_back, m.side)
        x_in = m.send(tie(half_in, x_att), m.to_x)
        smalls += [x_small, m.send(x_small, m.to_core)]
        y_att = tie(y_att, half_back, smalls[3])
        f_att = m.order(x_att, y_att, m.side)
        att += [f_att, m.send(f_att, m.to_core)]
        c_in = m.send(tie(w_in, f_att), m.to_core)
        c_back = m.send(tie(w_back, f_att), m.to_core)
        x_in = tie(x_in, f_att)
        y_in = m.send(x_in, m.to_y)
        x_back = m.send(tie(half_back, x_in), m.to_x)
        y = tie(x, x_in)
    qkv_far, ctx_far, p_far, unit, inverse, low = attend_pair(
        y, plen, att[2:], smalls[2:], meta, acc, [vector(v) for v in (b_out, gain_one, shift_one)]
    )
    if grid:
        y_in = tie(y_in, low)
        f_in = m.order(x_in, y_in, m.side)
        ins = [w_in, c_in, f_in, m.send(f_in, m.to_core)]
        x_back = tie(x_back, f_in)
        p_back = m.pieces(x_back)
        backs = [w_back, c_back]
        low = tie(low, x_back)
    act_near, slope_near, feed_near = feed_pair(low, ins[:2], backs[:2], smalls[:2])
    if grid:
        p_back = lax.optimization_barrier((*p_back, feed_near))[:2]
        f_back = m.whole(x_back, p_back)
        backs += [f_back, m.send(f_back, m.to_core)]
    layer_out, grad_two, grad_ffn, sums, slope_far, b_far, b_farc = turn_pair(
        low,
        ins[2:],
        backs[2:],
        smalls[2:],
        unit,
        feed_near,
        dy,
        meta,
        [vector(v) for v in (gain_one, shift_one, b_back, gain_two, shift_two)],
        plen,
    )
    if grid:
        got_b3 = m.send(b_farc, m.to_core)
    b_own, b_core = outer_pair(act_near, grad_ffn)
    if grid:
        got_b1 = m.send(b_core, m.to_core)
        b_far = m.sums(b_far, tie(got_b3, b_own))
        got_bx = [m.send(part, m.to_x) for part in b_far]
        grad_ffn = tie(grad_ffn, *b_far)
    slopes = (slope_near, slope_far)
    feed_sent = [(v[1], v[3]) for v in (ins, backs)]
    feed_kept = [(v[0], v[2]) for v in (ins, backs)]
    i_core, i_farc, sums, normed = feed_back_pair(
        grad_ffn, slopes, 1, *feed_sent, low, grad_two, (1, 3), sums, meta
    )
    if grid:
        got_i1, got_i3 = [m.send(v, m.to_core) for v in (i_core, i_farc)]
        b_near = [b_own, tie(got_b1, normed)]
        got_bx[0] = tie(got_bx[0], normed)
        normed = tie(normed, got_bx[0])
    i_own, i_far, sums, grad_one, grad_attn = feed_back_pair(
        grad_ffn,
        slopes,
        0,
        *feed_kept,
        low,
        normed,
        (0, 2),
        sums,
        meta,
        unit,
        inverse,
        vector(gain_one),
    )
    if grid:
        i_far = m.sums(i_far, tie(got_i3, grad_attn))
        got_ix = [m.send(part, m.to_x) for part in i_far]
        m.mark = i_far[0]
        chain_b = m.chain(b_near, got_bx)
        m.step(chain_b)
        grad_attn = tie(grad_attn, m.mark)
    kept = [(qkv_near, qkv_far), (ctx_near, ctx_far), (p_near, p_far)]
    a_core, a_farc, sums, grad_x = attend_back_pair(
        x, plen, grad_attn, *kept, 1, (att[1], att[3]), grad_one, (1, 3), sums, meta
    )
    if grid:
        got_a1, got_a3 = [m.send(v, m.to_core) for v in (a_core, a_farc)]
        i_near = [i_own, got_i1]
        m.mark = grad_x
        m.step(chain_b)
        got_ix[0] = m.after(got_ix[0])
        grad_x = tie(grad_x, got_ix[0])
    a_own, a_far, packed, grad_x = attend_back_pair(
        x, plen, grad_attn, *kept, 0, (att[0], att[2]), grad_x, (0, 2), sums, meta
    )
    if grid:
        m.mark = grad_x
        got_a3 = m.after(got_a3)
        rows_a = a_far.shape[0] // 2
        low_far = [v[:rows_a] for v in (a_far, got_a3)]
        low_far = add(*low_far)
        got_ax = m.send(low_far, m.to_x)
        m.mark = low_far
        got_a1 = m.after(got_a1)
        view = lambda v, at: {"of": v, "at": at, "rows": rows_a}
        low_near = [view(v, 0) for v in (a_own, got_a1)]
        high_near = [view(v, rows_a) for v in (a_own, got_a1)]
        high_far = [view(v, rows_a) for v in (a_far, got_a3)]
        chains = {"b": chain_b, "i": m.chain_zy(i_near, got_ix), "v": m.chain_y(high_near, high_far)}
        done = {}
        for key in "vib":
            done[key] = m.step(chains[key])
        chains["u"] = m.chain(low_near, [got_ax])
        chains["s"] = m.chain_small(m.after(packed))
        for key in ORDER:
            done[key] = m.step(chains[key])
        g_back, g_in, packed = done["b"], done["i"], done["s"]
        g_att = jnp.concatenate([done["u"], done["v"]], axis=0)
    else:
        g_back, g_in, g_att = [
            lax.psum(
                lax.psum_scatter(jnp.stack(parts).astype(F32), "tp", scatter_dimension=0), "batch"
            )
            for parts in (
                (b_own, b_core, b_far, b_farc),
                (i_own, i_core, i_far, i_farc),
                (a_own, a_core, a_far, a_farc),
            )
        ]
        packed = lax.psum(packed, AXES)
    mine = lax.dynamic_slice_in_dim(packed, 2 * position, 2, axis=0)
    return (
        layer_out.reshape(tokens.shape),
        grad_x.reshape(tokens.shape),
        jnp.transpose(g_att[: 3 * width].reshape(3, width, model), (2, 0, 1)),
        mine[1, :width],
        mine[1, 2 * width : 3 * width],
        g_att[3 * width :],
        packed[11],
        packed[12],
        packed[13],
        g_in,
        mine[0],
        g_back,
        packed[10],
        packed[8],
        packed[9],
    )


def solution(mesh):
    in_specs = (
        P(None, ("batch", "tp"), None),
        P(None, "batch"),
        P(None, ("batch", "tp"), None),
        P(None, None, "tp"),
        P("tp"),
        P("tp"),
        P("tp", None),
        P(),
        P(),
        P(),
        P(None, "tp"),
        P("tp"),
        P("tp", None),
        P(),
        P(),
        P(),
    )
    out_specs = (
        P(None, ("batch", "tp"), None),
        P(None, ("batch", "tp"), None),
        P(None, None, "tp"),
        P("tp"),
        P("tp"),
        P("tp", None),
        P(),
        P(),
        P(),
        P(None, "tp"),
        P("tp"),
        P("tp", None),
        P(),
        P(),
        P(),
    )
    return jax.shard_map(body, mesh=mesh, in_specs=in_specs, out_specs=out_specs, check_vma=False)
```

```python
import math

import jax
import jax.numpy as jnp
from jax import lax
from jax.experimental import pallas as pl
from jax.experimental.pallas import tpu as pltpu
from jax.sharding import PartitionSpec as P

DH = 64
AXES = ("batch", "tp")
epsilon = 1e-05
F32 = jnp.float32
BF16 = jnp.bfloat16


def nt(a, b):
    return lax.dot_general(a, b, (((1,), (1,)), ((), ())), preferred_element_type=F32)


def tn(a, b):
    return lax.dot_general(a, b, (((0,), (0,)), ((), ())), preferred_element_type=F32)


def nn(a, b):
    return jnp.dot(a, b, preferred_element_type=F32)


HBM = pl.BlockSpec(memory_space=pl.ANY)
WHOLE = pl.BlockSpec(memory_space=pltpu.VMEM)
SCALARS = pl.BlockSpec(memory_space=pltpu.SMEM)


class Copies:
    def __init__(self, sems):
        self.sems, self.used = sems, 0
        self.pending = []

    def start(self, src, dst):
        copy = pltpu.make_async_copy(src, dst, self.sems.at[self.used])
        self.used += 1
        copy.start()
        return copy

    def out(self, src, dst):
        self.pending.append(self.start(src, dst))

    def drain(self):
        for copy in self.pending:
            copy.wait()


def call(kernel, name, inputs, outputs, scratch, copies, cost=1000):
    in_specs = [spec for spec, _ in inputs]
    return pl.pallas_call(
        kernel,
        name=name,
        in_specs=in_specs,
        out_specs=tuple(spec for spec, _ in outputs),
        out_shape=tuple(shape for _, shape in outputs),
        scratch_shapes=list(scratch) + [pltpu.SemaphoreType.DMA((copies,))],
        cost_estimate=pl.CostEstimate(flops=cost, transcendentals=0, bytes_accessed=0),
    )(*[value for _, value in inputs])


def shape(dims, dtype):
    return jax.ShapeDtypeStruct(dims, dtype)


def block(i, size):
    return pl.ds(pl.multiple_of(i * size, size), size)


def unit_norm(v):
    middle = jnp.mean(v, axis=-1, keepdims=True)
    centred = v - middle
    inverse = lax.rsqrt(jnp.mean(centred * centred, axis=-1, keepdims=True) + epsilon)
    return centred * inverse, inverse


def norm_grad(scaled, unit, inverse):
    mean_one = jnp.mean(scaled, axis=-1, keepdims=True)
    mean_two = jnp.mean(scaled * unit, axis=-1, keepdims=True)
    return inverse * (scaled - mean_one - unit * mean_two)


STEP = 256


def row_of(part, meta_ref, kind):
    return 2 * jnp.bitwise_xor(part, meta_ref[meta_ref.shape[0] - 1]) + kind


def attend_pair(x, plen, w_pair, smalls, meta, acc=None, vectors=None):
    rows, model = x.shape
    passages = rows // plen
    width = w_pair[0].shape[0] // 4
    heads = width // DH
    units = smalls[0].shape[1] - 3 * width
    last = acc is not None

    def kernel(meta_ref, x_hbm, wa, wb, bias_a, bias_b, *rest):
        if last:
            acc_hbm, b_out, gain, shift = rest[:4]
            qkv_hbm, ctx_hbm, p_hbm, unit_hbm, inv_hbm, low_hbm = rest[4:10]
            x_s, w_s, qkv_s, ctx_s, p_s, acc_s, inv_s, low_s, sems = rest[10:]
        else:
            qkv_hbm, ctx_hbm, p_hbm, acc_out = rest[:4]
            x_s, w_s, qkv_s, ctx_s, p_s, acc_s, sems = rest[4:]
        copies = Copies(sems)
        first = [copies.start(x_hbm, x_s), copies.start(wa, w_s.at[0])]
        second = [copies.start(wb, w_s.at[1])]
        if last:
            held = copies.start(acc_hbm, acc_s)
        for j, waits, bias in ((0, first, bias_a), (1, second, bias_b)):
            for copy in waits:
                copy.wait()
            qkv_s[j] = (nt(x_s[...], w_s[j, : 3 * width, :]) + bias[0:1, units:]).astype(BF16)
            copies.out(qkv_s.at[j], qkv_hbm.at[j])

            def one(g, carry, j=j):
                at = block(g, plen)
                qkv = qkv_s[j, at, :]
                keep = lax.broadcasted_iota(jnp.int32, (plen, 1), 0) < meta_ref[g]
                ctx = []
                for h in range(heads):
                    q = qkv[:, h * DH : (h + 1) * DH] * (1.0 / math.sqrt(DH))
                    k = qkv[:, width + h * DH : width + (h + 1) * DH]
                    v = qkv[:, 2 * width + h * DH : 2 * width + (h + 1) * DH]
                    s = jnp.where(keep, nt(k, q.astype(BF16)), -1000000000.0)
                    e = jnp.exp(s - jnp.max(s, axis=0, keepdims=True))
                    p = (e * (1.0 / jnp.sum(e, axis=0, keepdims=True))).astype(BF16)
                    p_s[j, g * heads + h] = p
                    ctx.append(tn(v, p))
                ctx_s[j, at, :] = jnp.concatenate(ctx, axis=0).T.astype(BF16)
                return carry

            lax.fori_loop(0, passages, one, 0, unroll=True)
            copies.out(ctx_s.at[j], ctx_hbm.at[j])
            copies.out(p_s.at[j], p_hbm.at[j])
            term = nn(ctx_s[j], w_s[j, 3 * width :, :])
            if last and j == 0:
                held.wait()
            acc_s[...] = term if j == 0 and not last else acc_s[...] + term
        if last:

            def finish(i, carry):
                at = block(i, STEP)
                v = x_s[at, :].astype(F32) + acc_s[at, :] + b_out[...]
                unit, inverse = unit_norm(v)
                acc_s[at, :] = unit
                inv_s[at, :] = jnp.broadcast_to(inverse, (STEP, 128))
                low_s[at, :] = (unit * gain[...] + shift[...]).astype(BF16)
                return carry

            lax.fori_loop(0, rows // STEP, finish, 0)
            copies.out(acc_s, unit_hbm)
            copies.out(inv_s, inv_hbm)
            copies.out(low_s, low_hbm)
        else:
            copies.out(acc_s, acc_out)
        copies.drain()

    inputs = [(SCALARS, meta), (HBM, x), (HBM, w_pair[0]), (HBM, w_pair[1])]
    inputs += [(WHOLE, v) for v in smalls]
    dims = [(2, rows, 3 * width), (2, rows, width), (2, passages * heads, plen, plen)]
    outputs = [(HBM, shape(d, BF16)) for d in dims]
    scratch = [pltpu.VMEM((rows, model), BF16), pltpu.VMEM((2, 4 * width, model), BF16)]
    scratch += [pltpu.VMEM(d, BF16) for d in dims]
    scratch += [pltpu.VMEM((rows, model), F32)]
    if last:
        inputs += [(HBM, acc)] + [(WHOLE, v) for v in vectors]
        outputs += [(HBM, shape((rows, model), F32)), (HBM, shape((rows, 128), F32))]
        outputs += [(HBM, shape((rows, model), BF16))]
        scratch += [pltpu.VMEM((rows, 128), F32), pltpu.VMEM((rows, model), BF16)]
    else:
        outputs += [(HBM, shape((rows, model), F32))]
    return call(kernel, "attend_pair", inputs, outputs, scratch, 16, 1000 if last else 200 * 10**9)


def feed(j, low_s, i_s, b_s, bias, act_s, slope_s):
    units = act_s.shape[2]
    for c in range(0, units, 256):
        cols = slice(c, c + 256)
        t = nn(low_s[...], i_s[j, :, cols]) + bias[0:1, cols]
        cdf = 0.5 * (1.0 + lax.erf(t * (1.0 / math.sqrt(2.0))))
        pdf = jnp.exp(-0.5 * t * t) * (1.0 / math.sqrt(2.0 * math.pi))
        act_s[j, :, cols] = (t * cdf).astype(BF16)
        slope_s[j, :, cols] = (cdf + t * pdf).astype(BF16)
    return nn(act_s[j], b_s[j])


def feed_pair(low, in_pair, back_pair, smalls):
    rows, model = low.shape
    units = in_pair[0].shape[1]

    def kernel(low_hbm, ia, ib, ba, bb, bias_a, bias_b, *rest):
        act_hbm, slope_hbm, acc_hbm, low_s, i_s, b_s, act_s, slope_s, acc_s, sems = rest
        copies = Copies(sems)
        first = [copies.start(low_hbm, low_s), copies.start(ia, i_s.at[0]), copies.start(ba, b_s.at[0])]
        second = [copies.start(ib, i_s.at[1]), copies.start(bb, b_s.at[1])]
        for j, waits, bias in ((0, first, bias_a), (1, second, bias_b)):
            for copy in waits:
                copy.wait()
            term = feed(j, low_s, i_s, b_s, bias, act_s, slope_s)
            copies.out(act_s.at[j], act_hbm.at[j])
            copies.out(slope_s.at[j], slope_hbm.at[j])
            acc_s[...] = acc_s[...] + term if j else term
        copies.out(acc_s, acc_hbm)
        copies.drain()

    inputs = [(HBM, v) for v in (low, *in_pair, *back_pair)] + [(WHOLE, v) for v in smalls]
    outputs = [(HBM, shape((2, rows, units), BF16))] * 2 + [(HBM, shape((rows, model), F32))]
    scratch = [pltpu.VMEM((rows, model), BF16), pltpu.VMEM((2, model, units), BF16)]
    scratch += [pltpu.VMEM((2, units, model), BF16)] + [pltpu.VMEM((2, rows, units), BF16)] * 2
    scratch += [pltpu.VMEM((rows, model), F32)]
    return call(kernel, "feed_pair", inputs, outputs, scratch, 12, 200 * 10**9)


def turn_pair(low, in_pair, back_pair, smalls, unit, acc, dy, meta, vectors, plen):
    rows, model = low.shape
    units = in_pair[0].shape[1]

    def kernel(meta_ref, low_hbm, ia, ib, ba, bb, unit_hbm, acc_hbm, dy_hbm, bias_a, bias_b, *rest):
        gain_one, shift_one, b_back, gain_two, shift_two = rest[:5]
        out_hbm, grad_hbm, ffn_hbm, sum_ref, slope_hbm, oa, ob = rest[5:12]
        low_s, i_s, b_s, act_s, slope_s, acc_s, unit_s, dy_s, out_s, grad_s, ffn_s, g_s, sems = rest[12:]
        copies = Copies(sems)
        first = [copies.start(low_hbm, low_s), copies.start(ia, i_s.at[0]), copies.start(ba, b_s.at[0])]
        second = [copies.start(ib, i_s.at[1]), copies.start(bb, b_s.at[1]), copies.start(acc_hbm, acc_s)]
        third = [copies.start(unit_hbm, unit_s), copies.start(dy_hbm, dy_s)]
        for copy in first:
            copy.wait()
        term = feed(0, low_s, i_s, b_s, bias_a, act_s, slope_s)
        copies.out(slope_s.at[0], slope_hbm.at[0])
        for copy in second:
            copy.wait()
        acc_s[...] = acc_s[...] + term
        acc_s[...] = acc_s[...] + feed(1, low_s, i_s, b_s, bias_b, act_s, slope_s)
        copies.out(slope_s.at[1], slope_hbm.at[1])
        for copy in third:
            copy.wait()
        sum_ref[...] = jnp.zeros_like(sum_ref)

        def step(i, carry):
            at = block(i, STEP)
            normed = unit_s[at, :] * gain_one[...] + shift_one[...]
            u, inverse = unit_norm(normed + acc_s[at, :] + b_back[...])
            out_s[at, :] = (u * gain_two[...] + shift_two[...]).astype(BF16)
            slot = lax.broadcasted_iota(jnp.int32, (STEP, 1), 0) + (i * STEP) % plen
            keep = slot < meta_ref[(i * STEP) // plen]
            grad_y = jnp.where(keep, dy_s[at, :].astype(F32), 0.0)
            grad = norm_grad(grad_y * gain_two[...], u, inverse)
            grad_s[at, :] = grad
            ffn_s[at, :] = grad.astype(BF16)
            sum_ref[8:9, :] += jnp.sum(grad_y * u, axis=0, keepdims=True)
            sum_ref[9:10, :] += jnp.sum(grad_y, axis=0, keepdims=True)
            sum_ref[10:11, :] += jnp.sum(grad, axis=0, keepdims=True)
            return carry

        lax.fori_loop(0, rows // STEP, step, 0)
        copies.out(out_s, out_hbm)
        copies.out(grad_s, grad_hbm)
        copies.out(ffn_s, ffn_hbm)
        for j, out in ((1, ob), (0, oa)):
            g_s[j] = tn(act_s[j], ffn_s[...]).astype(BF16)
            copies.out(g_s.at[j], out)
        copies.drain()

    inputs = [(SCALARS, meta)] + [(HBM, v) for v in (low, *in_pair, *back_pair, unit, acc, dy)]
    inputs += [(WHOLE, v) for v in (*smalls, *vectors)]
    outputs = [(HBM, shape((rows, model), d)) for d in (BF16, F32, BF16)]
    outputs += [(WHOLE, shape((16, model), F32)), (HBM, shape((2, rows, units), BF16))]
    outputs += [(HBM, shape((units, model), BF16))] * 2
    scratch = [pltpu.VMEM((rows, model), BF16), pltpu.VMEM((2, model, units), BF16)]
    scratch += [pltpu.VMEM((2, units, model), BF16)] + [pltpu.VMEM((2, rows, units), BF16)] * 2
    scratch += [pltpu.VMEM((rows, model), d) for d in (F32, F32, BF16, BF16, F32, BF16)]
    scratch += [pltpu.VMEM((2, units, model), BF16)]
    return call(kernel, "turn_pair", inputs, outputs, scratch, 20)


def outer_pair(acts, grad_ffn):
    _, rows, units = acts.shape
    model = grad_ffn.shape[1]

    def kernel(act_hbm, g_hbm, oa, ob, act_s, g_s, out_s, sems):
        copies = Copies(sems)
        whole = copies.start(g_hbm, g_s)
        waits = [copies.start(act_hbm.at[j], act_s.at[j]) for j in (1, 0)]
        whole.wait()
        for j, wait, out in ((1, waits[0], ob), (0, waits[1], oa)):
            wait.wait()
            out_s[j] = tn(act_s[j], g_s[...]).astype(BF16)
            copies.out(out_s.at[j], out)
        copies.drain()

    inputs = [(HBM, acts), (HBM, grad_ffn)]
    outputs = [(HBM, shape((units, model), BF16))] * 2
    scratch = [pltpu.VMEM((2, rows, units), BF16), pltpu.VMEM((rows, model), BF16)]
    scratch += [pltpu.VMEM((2, units, model), BF16)]
    return call(kernel, "outer_pair", inputs, outputs, scratch, 8, 200 * 10**9)


def feed_back_pair(grad_ffn, slopes, which, in_pair, back_pair, low, start, parts, sums, meta, unit=None, inverse=None, gain=None):
    rows, model = grad_ffn.shape
    units = slopes[0].shape[2]
    last = unit is not None

    def kernel(meta_ref, before, g_hbm, sa, sb, ia, ib, ba, bb, low_hbm, start_hbm, *rest):
        if last:
            unit_hbm, inv_hbm, gain_ref = rest[:3]
            rest = rest[3:]
            oa, ob, sum_ref, one_hbm, attn_hbm = rest[:5]
            g_s, slope_s, i_s, b_s, low_s, acc_s, pre_s, out_s, line, unit_s, inv_s, attn_s, sems = rest[5:]
        else:
            oa, ob, sum_ref, acc_out = rest[:4]
            g_s, slope_s, i_s, b_s, low_s, acc_s, pre_s, out_s, line, sems = rest[4:]
        copies = Copies(sems)
        sum_ref[...] = before[...]
        weights = {1: (bb, ib, sb.at[which]), 0: (ba, ia, sa.at[which])}
        early = copies.start(g_hbm, g_s)
        waits, later = {}, {}
        for j in (1, 0):
            waits[j] = [copies.start(weights[j][0], b_s.at[j]), copies.start(weights[j][2], slope_s.at[j])]
            later[j] = [copies.start(weights[j][1], i_s.at[j])]
            if j == 1:
                later[j] += [copies.start(low_hbm, low_s), copies.start(start_hbm, acc_s)]
        if last:
            late = [copies.start(unit_hbm, unit_s), copies.start(inv_hbm, inv_s)]
        early.wait()
        for j, out in ((1, ob), (0, oa)):
            for wait in waits[j]:
                wait.wait()
            for c in range(0, units, 256):
                cols = slice(c, c + 256)
                pre = nt(g_s[...], b_s[j, cols, :]) * slope_s[j, :, cols].astype(F32)
                pre = pre.astype(BF16)
                pre_s[:, cols] = pre
                line[:, cols] = jnp.sum(pre.astype(F32), axis=0, keepdims=True)
            sum_ref[pl.ds(row_of(parts[j], meta_ref, 0), 1), :] = line[...]
            for wait in later[j]:
                wait.wait()
            acc_s[...] = acc_s[...] + nt(pre_s[...], i_s[j])
            out_s[j] = tn(low_s[...], pre_s[...]).astype(BF16)
            copies.out(out_s.at[j], out)
        if last:
            for wait in late:
                wait.wait()

            def finish(i, carry):
                at = block(i, STEP)
                normed = acc_s[at, :]
                u = unit_s[at, :]
                grad = norm_grad(normed * gain_ref[0:1, :], u, inv_s[at, 0:1])
                sum_ref[11:12, :] += jnp.sum(grad, axis=0, keepdims=True)
                sum_ref[12:13, :] += jnp.sum(normed * u, axis=0, keepdims=True)
                sum_ref[13:14, :] += jnp.sum(normed, axis=0, keepdims=True)
                acc_s[at, :] = grad
                attn_s[at, :] = grad.astype(BF16)
                return carry

            lax.fori_loop(0, rows // STEP, finish, 0)
            copies.out(acc_s, one_hbm)
            copies.out(attn_s, attn_hbm)
        else:
            copies.out(acc_s, acc_out)
        copies.drain()

    inputs = [(SCALARS, meta), (WHOLE, sums)]
    inputs += [(HBM, v) for v in (grad_ffn, *slopes, *in_pair, *back_pair, low, start)]
    outputs = [(HBM, shape((model, units), BF16))] * 2 + [(WHOLE, shape((16, model), F32))]
    outputs += [(HBM, shape((rows, model), F32))]
    scratch = [pltpu.VMEM((rows, model), BF16), pltpu.VMEM((2, rows, units), BF16)]
    scratch += [pltpu.VMEM((2, model, units), BF16), pltpu.VMEM((2, units, model), BF16)]
    scratch += [pltpu.VMEM((rows, model), BF16), pltpu.VMEM((rows, model), F32)]
    scratch += [pltpu.VMEM((rows, units), BF16), pltpu.VMEM((2, model, units), BF16)]
    scratch += [pltpu.VMEM((1, units), F32)]
    if last:
        inputs += [(HBM, unit), (HBM, inverse), (WHOLE, gain)]
        outputs += [(HBM, shape((rows, model), BF16))]
        scratch += [pltpu.VMEM((rows, model), F32), pltpu.VMEM((rows, 128), F32)]
        scratch += [pltpu.VMEM((rows, model), BF16)]
    return call(kernel, "feed_back_pair", inputs, outputs, scratch, 20, 200 * 10**9)


def attend_back_pair(x, plen, grad_attn, qkvs, ctxs, probs, which, w_pair, start, parts, sums, meta):
    rows, model = x.shape
    passages = rows // plen
    width = ctxs[0].shape[2]
    heads = width // DH

    def kernel(meta_ref, before, x_hbm, g_hbm, qa, qb, ca, cb, pa, pb, wa, wb, start_hbm, *rest):
        oa, ob, sum_ref, acc_out = rest[:4]
        x_s, g_s, qkv_s, ctx_s, p_s, w_s, acc_s, grow_s, out_s, gc_s, sems = rest[4:]
        copies = Copies(sems)
        sum_ref[...] = before[...]
        early = [copies.start(g_hbm, g_s)]
        of = {0: (wa, ca, qa, pa), 1: (wb, cb, qb, pb)}
        waits, middle, later = {}, {}, {}
        for j in (1, 0):
            waits[j] = [copies.start(of[j][0], w_s.at[j]), copies.start(of[j][1].at[which], ctx_s.at[j])]
            middle[j] = [copies.start(of[j][2].at[which], qkv_s.at[j]), copies.start(of[j][3].at[which], p_s.at[j])]
            later[j] = []
            if j == 1:
                later[j] = [copies.start(x_hbm, x_s), copies.start(start_hbm, acc_s)]
        for wait in early:
            wait.wait()
        for j, out in ((1, ob), (0, oa)):
            for wait in waits[j]:
                wait.wait()
            gc_s[...] = nt(g_s[...], w_s[j, 3 * width :, :]).astype(BF16)
            out_s[j, 3 * width :, :] = tn(ctx_s[j], g_s[...]).astype(BF16)
            for wait in middle[j]:
                wait.wait()

            def one(g, carry, j=j):
                at = block(g, plen)
                qkv = qkv_s[j, at, :]
                grad_ctx = gc_s[at, :]
                gq, gk, gv = [], [], []
                for h in range(heads):
                    q = qkv[:, h * DH : (h + 1) * DH]
                    k = qkv[:, width + h * DH : width + (h + 1) * DH]
                    v = qkv[:, 2 * width + h * DH : 2 * width + (h + 1) * DH]
                    gc = grad_ctx[:, h * DH : (h + 1) * DH]
                    low = p_s[j, g * heads + h]
                    p = low.astype(F32)
                    gp = nt(v, gc)
                    delta = jnp.sum(p * gp, axis=0, keepdims=True)
                    gs = (p * (gp - delta)).astype(BF16)
                    gq.append(tn(k, gs) * (1.0 / math.sqrt(DH)))
                    gk.append(nn(gs, q) * (1.0 / math.sqrt(DH)))
                    gv.append(nn(low, gc))
                gq = jnp.concatenate(gq, axis=0).T
                grow = jnp.concatenate([gq] + gk + gv, axis=1).astype(BF16)
                grow_s[at, :] = grow
                return carry + jnp.sum(grow.astype(F32), axis=0, keepdims=True)

            line = lax.fori_loop(0, passages, one, jnp.zeros((1, 3 * width), F32), unroll=True)
            line = jnp.concatenate([line, jnp.zeros((1, model - 3 * width), F32)], axis=1)
            sum_ref[pl.ds(row_of(parts[j], meta_ref, 1), 1), :] = line
            for wait in later[j]:
                wait.wait()
            out_s[j, : 3 * width, :] = tn(grow_s[...], x_s[...]).astype(BF16)
            copies.out(out_s.at[j], out)
            acc_s[...] = acc_s[...] + nn(grow_s[...], w_s[j, : 3 * width, :])
        copies.out(acc_s, acc_out)
        copies.drain()

    inputs = [(SCALARS, meta), (WHOLE, sums)]
    inputs += [(HBM, v) for v in (x, grad_attn, *qkvs, *ctxs, *probs, *w_pair, start)]
    outputs = [(HBM, shape((4 * width, model), BF16))] * 2
    outputs += [(WHOLE, shape((16, model), F32)), (HBM, shape((rows, model), F32))]
    scratch = [pltpu.VMEM((rows, model), BF16), pltpu.VMEM((rows, model), BF16)]
    scratch += [pltpu.VMEM(v[0].shape, BF16) for v in (qkvs, ctxs, probs)]
    scratch += [pltpu.VMEM((2, 4 * width, model), BF16), pltpu.VMEM((rows, model), F32)]
    scratch += [pltpu.VMEM((rows, 3 * width), BF16), pltpu.VMEM((2, 4 * width, model), BF16)]
    scratch += [pltpu.VMEM((rows, width), BF16)]
    return call(kernel, "attend_back_pair", inputs, outputs, scratch, 20, 200 * 10**9)


def tie(value, *others):
    return lax.optimization_barrier((value, *others))[0]


def flat_perm(move):
    pairs = []
    for z in range(4):
        for y in range(2):
            for x in range(2):
                for c in range(2):
                    z2, y2, x2, c2 = move(z, y, x, c)
                    pairs.append((((z * 2 + y) * 2 + x) * 2 + c, ((z2 * 2 + y2) * 2 + x2) * 2 + c2))
    return pairs


def add(*terms):
    return sum(term.astype(F32) for term in terms).astype(BF16)


ORDER = "svibusvisbuvsuivsuvibuvsui"


class GridMoves:
    def __init__(self):
        self.row = lax.axis_index("batch") % 2
        self.layer = lax.axis_index("batch") // 2 % 2
        self.side = (self.row + self.layer) % 2
        self.to_core = flat_perm(lambda z, y, x, c: (z, y, x, 1 - c))
        self.to_x = flat_perm(lambda z, y, x, c: (z, y, 1 - x, c))
        self.to_y = flat_perm(lambda z, y, x, c: (z, 1 - y, x, c))
        self.to_z = flat_perm(lambda z, y, x, c: (z ^ 1, y, x, c))
        self.to_zz = flat_perm(lambda z, y, x, c: (z ^ 2, y, x, c))
        self.mark = None

    def send(self, value, pairs):
        return lax.ppermute(value, AXES, pairs)

    def half(self, value, which):
        if isinstance(value, tuple):
            return jnp.where(which == 0, value[0], value[1])
        if isinstance(value, dict):
            rows = value["rows"] // 2
            at = value["at"] + which * rows
            return lax.dynamic_slice_in_dim(value["of"], at, rows, axis=0)
        if isinstance(value, list):
            return add(*(self.half(term, which) for term in value))
        rows = value.shape[0] // 2
        return lax.dynamic_slice_in_dim(value, which * rows, rows, axis=0)

    def order(self, mine, other, bit):
        low = jnp.where(bit == 0, mine, other)
        high = jnp.where(bit == 0, other, mine)
        return jnp.concatenate([low, high], axis=0)

    def after(self, value):
        if self.mark is not None:
            value = tie(value, self.mark)
        return value

    def pieces(self, mine):
        first, second = self.halves(mine)
        return [self.send(first, self.to_y), self.send(second, self.to_z)]

    def whole(self, mine, pieces):
        parts = list(zip(self.halves(mine), pieces))
        low = [jnp.where(self.side == 0, one, two) for one, two in parts]
        high = [jnp.where(self.side == 0, two, one) for one, two in parts]
        return jnp.concatenate(low + high, axis=0)

    def halves(self, value):
        rows = value.shape[0] // 2
        return value[:rows], value[rows:]

    def sums(self, one, two):
        return [add(a, b) for a, b in zip(self.halves(one), self.halves(two))]

    def chain(self, near, got):
        got = tuple(self.after(part) for part in got)
        got = got if len(got) == 2 else got[0]
        pass_on = self.half([*near, got], 1 - self.row)
        keep = self.half([*near, got], self.row)
        got = self.send(pass_on, self.to_y)
        yield pass_on
        yield from self.chain_z(add(keep, self.after(got)))

    def chain_zy(self, near, got):
        got = tuple(self.after(part) for part in got)
        pass_on = self.half([*near, got], 1 - self.layer)
        keep = self.half([*near, got], self.layer)
        got = self.send(pass_on, self.to_z)
        yield pass_on
        keep = add(keep, self.after(got))
        pass_on = self.half(keep, 1 - self.row)
        keep = self.half(keep, self.row)
        got = self.send(pass_on, self.to_y)
        yield pass_on
        keep = add(keep, self.after(got))
        got = self.send(keep, self.to_zz)
        yield keep
        keep = add(keep, self.after(got))
        got = self.send(keep, self.to_y)
        yield keep
        keep = self.order(keep, self.after(got), self.row)
        got = self.send(keep, self.to_z)
        yield keep
        yield self.order(keep, self.after(got), self.layer).astype(F32)

    def chain_y(self, near, far):
        pass_on = jnp.concatenate(
            [self.half(term, 1 - self.row) for term in (near, far)], axis=0
        )
        got = self.send(pass_on, self.to_y)
        yield pass_on
        got = self.halves(self.after(got))
        far = add(*(self.half(term, self.row) for term in far), got[1])
        keep = add(*(self.half(term, self.row) for term in near), got[0])
        got = self.send(far, self.to_x)
        yield far
        yield from self.chain_z(add(keep, self.after(got)))

    def chain_z(self, keep):
        pass_on = self.half(keep, 1 - self.layer)
        keep = self.half(keep, self.layer)
        got = self.send(pass_on, self.to_z)
        yield pass_on
        keep = add(keep, self.after(got))
        got = self.send(keep, self.to_zz)
        yield keep
        keep = add(keep, self.after(got))
        got = self.send(keep, self.to_z)
        yield keep
        keep = self.order(keep, self.after(got), self.layer)
        got = self.send(keep, self.to_y)
        yield keep
        yield self.order(keep, self.after(got), self.row).astype(F32)

    def chain_small(self, value):
        for pairs in (self.to_core, self.to_x, self.to_y, self.to_z, self.to_zz):
            got = self.send(value, pairs)
            yield value
            value = value + self.after(got)
        yield value

    def step(self, chain):
        self.mark = next(chain)
        return self.mark


def body(
    tokens,
    passage_lengths,
    cotangent,
    w_qkv,
    b_query,
    b_value,
    w_out,
    b_out,
    gain_one,
    shift_one,
    w_in,
    b_in,
    w_back,
    b_back,
    gain_two,
    shift_two,
):
    micro_count, own_rows, model = tokens.shape
    tp_count = lax.axis_size("tp")
    batch_count = lax.axis_size("batch")
    plen = own_rows * tp_count // passage_lengths.shape[1]
    own_passages = own_rows // plen
    assert own_passages * plen == own_rows and tp_count == 4
    grid = (batch_count, tp_count) == (8, 4)
    width = w_qkv.shape[2]
    rows = micro_count * own_rows
    position = lax.axis_index("tp")

    vector = lambda v: v.reshape(1, -1)
    x = tokens.reshape(rows, model)
    dy = cotangent.reshape(rows, model)
    lengths = lax.dynamic_slice_in_dim(
        passage_lengths, position * own_passages, own_passages, axis=1
    ).reshape(micro_count * own_passages)
    meta = jnp.concatenate([lengths, (position if grid else 0 * position).reshape(1)])
    qkvo = jnp.concatenate([jnp.transpose(w_qkv, (1, 2, 0)).reshape(3 * width, model), w_out], axis=0)
    small = vector(jnp.concatenate([b_in.astype(F32), b_query, jnp.zeros_like(b_query), b_value]))
    if grid:
        m = moves = GridMoves()
        x_att = m.send(m.half(qkvo, m.side), m.to_x)
        c_att = m.send(qkvo, m.to_core)
        c_small = m.send(small, m.to_core)
        x_small = m.send(small, m.to_x)
        half_in = m.half(w_in, m.side)
        meta = tie(meta, half_in)
        att, smalls = [qkvo, c_att], [small, c_small]
    else:
        att, smalls, ins, backs = [
            list(lax.all_gather(v, "tp", axis=0)) for v in (qkvo, small, w_in, w_back)
        ]
    qkv_near, ctx_near, p_near, acc = attend_pair(x, plen, att[:2], smalls[:2], meta)
    y = x
    if grid:
        x_att, x_small = tie(x_att, acc), tie(x_small, acc)
        y_att = m.send(x_att, m.to_y)
        half_back = m.half(w_back, m.side)
        x_in = m.send(tie(half_in, x_att), m.to_x)
        smalls += [x_small, m.send(x_small, m.to_core)]
        y_att = tie(y_att, half_back, smalls[3])
        f_att = m.order(x_att, y_att, m.side)
        att += [f_att, m.send(f_att, m.to_core)]
        c_in = m.send(tie(w_in, f_att), m.to_core)
        c_back = m.send(tie(w_back, f_att), m.to_core)
        x_in = tie(x_in, f_att)
        y_in = m.send(x_in, m.to_y)
        x_back = m.send(tie(half_back, x_in), m.to_x)
        y = tie(x, x_in)
    qkv_far, ctx_far, p_far, unit, inverse, low = attend_pair(
        y, plen, att[2:], smalls[2:], meta, acc, [vector(v) for v in (b_out, gain_one, shift_one)]
    )
    if grid:
        y_in = tie(y_in, low)
        f_in = m.order(x_in, y_in, m.side)
        ins = [w_in, c_in, f_in, m.send(f_in, m.to_core)]
        x_back = tie(x_back, f_in)
        p_back = m.pieces(x_back)
        backs = [w_back, c_back]
        low = tie(low, x_back)
    act_near, slope_near, feed_near = feed_pair(low, ins[:2], backs[:2], smalls[:2])
    if grid:
        p_back = lax.optimization_barrier((*p_back, feed_near))[:2]
        f_back = m.whole(x_back, p_back)
        backs += [f_back, m.send(f_back, m.to_core)]
    layer_out, grad_two, grad_ffn, sums, slope_far, b_far, b_farc = turn_pair(
        low,
        ins[2:],
        backs[2:],
        smalls[2:],
        unit,
        feed_near,
        dy,
        meta,
        [vector(v) for v in (gain_one, shift_one, b_back, gain_two, shift_two)],
        plen,
    )
    if grid:
        got_b3 = m.send(b_farc, m.to_core)
    b_own, b_core = outer_pair(act_near, grad_ffn)
    if grid:
        got_b1 = m.send(b_core, m.to_core)
        b_far = m.sums(b_far, tie(got_b3, b_own))
        got_bx = [m.send(part, m.to_x) for part in b_far]
        grad_ffn = tie(grad_ffn, *b_far)
    slopes = (slope_near, slope_far)
    feed_sent = [(v[1], v[3]) for v in (ins, backs)]
    feed_kept = [(v[0], v[2]) for v in (ins, backs)]
    i_core, i_farc, sums, normed = feed_back_pair(
        grad_ffn, slopes, 1, *feed_sent, low, grad_two, (1, 3), sums, meta
    )
    if grid:
        got_i1, got_i3 = [m.send(v, m.to_core) for v in (i_core, i_farc)]
        b_near = [b_own, tie(got_b1, normed)]
        got_bx[0] = tie(got_bx[0], normed)
        normed = tie(normed, got_bx[0])
    i_own, i_far, sums, grad_one, grad_attn = feed_back_pair(
        grad_ffn,
        slopes,
        0,
        *feed_kept,
        low,
        normed,
        (0, 2),
        sums,
        meta,
        unit,
        inverse,
        vector(gain_one),
    )
    if grid:
        i_far = m.sums(i_far, tie(got_i3, grad_attn))
        got_ix = [m.send(part, m.to_x) for part in i_far]
        m.mark = i_far[0]
        chain_b = m.chain(b_near, got_bx)
        m.step(chain_b)
        grad_attn = tie(grad_attn, m.mark)
    kept = [(qkv_near, qkv_far), (ctx_near, ctx_far), (p_near, p_far)]
    a_core, a_farc, sums, grad_x = attend_back_pair(
        x, plen, grad_attn, *kept, 1, (att[1], att[3]), grad_one, (1, 3), sums, meta
    )
    if grid:
        got_a1, got_a3 = [m.send(v, m.to_core) for v in (a_core, a_farc)]
        i_near = [i_own, got_i1]
        m.mark = grad_x
        m.step(chain_b)
        got_ix[0] = m.after(got_ix[0])
        grad_x = tie(grad_x, got_ix[0])
    a_own, a_far, packed, grad_x = attend_back_pair(
        x, plen, grad_attn, *kept, 0, (att[0], att[2]), grad_x, (0, 2), sums, meta
    )
    if grid:
        m.mark = grad_x
        got_a3 = m.after(got_a3)
        rows_a = a_far.shape[0] // 2
        low_far = [v[:rows_a] for v in (a_far, got_a3)]
        low_far = add(*low_far)
        got_ax = m.send(low_far, m.to_x)
        m.mark = low_far
        got_a1 = m.after(got_a1)
        view = lambda v, at: {"of": v, "at": at, "rows": rows_a}
        low_near = [view(v, 0) for v in (a_own, got_a1)]
        high_near = [view(v, rows_a) for v in (a_own, got_a1)]
        high_far = [view(v, rows_a) for v in (a_far, got_a3)]
        chains = {"b": chain_b, "i": m.chain_zy(i_near, got_ix), "v": m.chain_y(high_near, high_far)}
        done = {}
        for key in "vib":
            done[key] = m.step(chains[key])
        chains["u"] = m.chain(low_near, [got_ax])
        chains["s"] = m.chain_small(m.after(packed))
        for key in ORDER:
            done[key] = m.step(chains[key])
        g_back, g_in, packed = done["b"], done["i"], done["s"]
        g_att = jnp.concatenate([done["u"], done["v"]], axis=0)
    else:
        g_back, g_in, g_att = [
            lax.psum(
                lax.psum_scatter(jnp.stack(parts).astype(F32), "tp", scatter_dimension=0), "batch"
            )
            for parts in (
                (b_own, b_core, b_far, b_farc),
                (i_own, i_core, i_far, i_farc),
                (a_own, a_core, a_far, a_farc),
            )
        ]
        packed = lax.psum(packed, AXES)
    mine = lax.dynamic_slice_in_dim(packed, 2 * position, 2, axis=0)
    return (
        layer_out.reshape(tokens.shape),
        grad_x.reshape(tokens.shape),
        jnp.transpose(g_att[: 3 * width].reshape(3, width, model), (2, 0, 1)),
        mine[1, :width],
        mine[1, 2 * width : 3 * width],
        g_att[3 * width :],
        packed[11],
        packed[12],
        packed[13],
        g_in,
        mine[0],
        g_back,
        packed[10],
        packed[8],
        packed[9],
    )


def solution(mesh):
    in_specs = (
        P(None, ("batch", "tp"), None),
        P(None, "batch"),
        P(None, ("batch", "tp"), None),
        P(None, None, "tp"),
        P("tp"),
        P("tp"),
        P("tp", None),
        P(),
        P(),
        P(),
        P(None, "tp"),
        P("tp"),
        P("tp", None),
        P(),
        P(),
        P(),
    )
    out_specs = (
        P(None, ("batch", "tp"), None),
        P(None, ("batch", "tp"), None),
        P(None, None, "tp"),
        P("tp"),
        P("tp"),
        P("tp", None),
        P(),
        P(),
        P(),
        P(None, "tp"),
        P("tp"),
        P("tp", None),
        P(),
        P(),
        P(),
    )
    return jax.shard_map(body, mesh=mesh, in_specs=in_specs, out_specs=out_specs, check_vma=False)
```
